32 devices in a mesh: seq: 8 (over z, y), fsdp: 4 (over x, core).
Axes of the slice: x: 2, y: 2, z: 4, core: 2. Of those that a mesh axis runs over, the one named last changes fastest.
Arguments:
- tokens: bfloat16 [4, 16384, 768], P('fsdp', 'seq'), may hold values from -6 to 6
- first_gain: bfloat16 [768], P('fsdp'), may hold values from 0.099609375 to 1.8984375
- first_shift: bfloat16 [768], P('fsdp'), may hold values from -3 to 3
- project_in: bfloat16 [768, 2304], P('fsdp'), may hold values from -0.21875 to 0.21875
- project_out: bfloat16 [768, 768], P('fsdp'), may hold values from -2 to 2
- second_gain: bfloat16 [768], P('fsdp'), may hold values from 0.099609375 to 1.8984375
- second_shift: bfloat16 [768], P('fsdp'), may hold values from -3 to 3
- up_weight: bfloat16 [768, 3072], P('fsdp'), may hold values from -0.21875 to 0.21875
- down_weight: bfloat16 [3072, 768], P('fsdp'), may hold values from -0.15625 to 0.15625
- valid_mask: int32 [4, 16384], P('fsdp', 'seq'), may hold values from 0 to 1, as said below
- cotangent: bfloat16 [4, 16384, 768], P('fsdp', 'seq'), may hold values from -6 to 6
Outputs:
- mixed: bfloat16 [4, 16384, 768], P('fsdp', 'seq')
- tokens_back: float32 [4, 16384, 768], P('fsdp', 'seq')
- first_gain_back: float32 [768], P('fsdp')
- first_shift_back: float32 [768], P('fsdp')
- project_in_back: float32 [768, 2304], P('fsdp')
- project_out_back: float32 [768, 768], P('fsdp')
- second_gain_back: float32 [768], P('fsdp')
- second_shift_back: float32 [768], P('fsdp')
- up_weight_back: float32 [768, 3072], P('fsdp')
- down_weight_back: float32 [3072, 768], P('fsdp')
The draws below stay inside these ranges and needn't reach their ends.
Inputs may be any that keep to these rules, and one draw needn't show every extreme that they name: `valid_mask`: positions of a stream come in blocks of 16384; each slide covers one or more whole blocks, and its valid positions are a prefix of it that ends inside its last block after 2 * 1024 or more of that block's positions; the last block of every stream ends in padding.
All inputs are finite; a program needn't handle non-finite values.
Results may differ from the reference program's by a relative error of at most 0.014.
Values may be sent and summed in bfloat16 or wider, within the bound.
A program may use at most 384 MiB of HBM per device.

```python
import jax
import jax.numpy as jnp
from jax import lax

D = 768
FF = 3072
HEADS = 16
HEAD_DIM = 48
SEG = 1024
BRANCHES = 5
STREAM = 16384
BATCH = 4


def draw_valid_mask(key, part):
    key = jax.random.fold_in(key, 7)
    first_key, second_key = jax.random.split(key)
    blocks = STREAM // (16 * SEG)
    starts = jax.random.randint(first_key, (BATCH, blocks), 0, 2)
    closing = jnp.concatenate([starts[:, 1:], jnp.ones((BATCH, 1), jnp.int32)], axis=1)
    tails = jax.random.randint(second_key, (BATCH, blocks), 2 * SEG, 16 * SEG)
    places = jnp.arange(16 * SEG, dtype=jnp.int32)
    inside = places[None, None, :] < tails[:, :, None]
    valid = jnp.where(closing[:, :, None] == 1, inside, True)
    return valid.astype(jnp.int32).reshape(BATCH, STREAM)


def shard_levels(stream_key, shape, cuts, low, largest):
    level = 1.0
    for dim, shards_of in cuts:
        heights = jax.random.uniform(jax.random.fold_in(jax.random.fold_in(stream_key, 6), dim), (shards_of,), jnp.float32, low / len(cuts), largest / len(cuts))
        level = level * jnp.repeat(jnp.exp(heights), shape[dim] // shards_of).reshape((-1,) + (1,) * (len(shape) - 1 - dim))
    return level


def noise(rng, shape, width, bound, shards=(), kind=jnp.bfloat16):
    factor_of = shard_levels(rng, shape, shards, -0.22, 0.18) if shards else 1.0
    drawn = jax.random.normal(rng, shape, jnp.float32) * width * factor_of
    return jnp.minimum(jnp.maximum(drawn, -bound), bound).astype(kind)


def setup_inputs(seed: int = 0) -> dict:
    streams_of = jax.random.split(jax.random.key(seed), 12)
    tokens = noise(streams_of[0], (BATCH, STREAM, D), 1.0, 6.0, ((0, 4), (1, 8)))
    first_gain = jnp.clip(1.0 + 0.18 * jax.random.normal(streams_of[1], (D,), jnp.float32), 0.099609375, 1.8984375).astype(jnp.bfloat16)
    first_shift = noise(streams_of[2], (D,), 0.5, 3.0, ((0, 4),))
    project_in = noise(streams_of[3], (D, 3 * D), D ** -0.5, 0.21875, ((0, 4),))
    project_out = noise(streams_of[4], (D, D), (max(D * 32 // (3 * SEG), 1)) ** -0.5, 2.0, ((0, 4),))
    second_gain = jnp.clip(1.0 + 0.18 * jax.random.normal(streams_of[5], (D,), jnp.float32), 0.099609375, 1.8984375).astype(jnp.bfloat16)
    second_shift = noise(streams_of[6], (D,), 0.5, 3.0, ((0, 4),))
    up_weight = noise(streams_of[7], (D, FF), D ** -0.5, 0.21875, ((0, 4),))
    down_weight = noise(streams_of[8], (FF, D), (FF // 2) ** -0.5, 0.15625, ((0, 4),))
    valid_mask = draw_valid_mask(jax.random.fold_in(streams_of[11], 71), 0)
    cotangent = noise(streams_of[10], (BATCH, STREAM, D), 1.0, 6.0, ((0, 4), (1, 8)))
    return dict(tokens=tokens, first_gain=first_gain, first_shift=first_shift, project_in=project_in, project_out=project_out, second_gain=second_gain, second_shift=second_shift, up_weight=up_weight, down_weight=down_weight, valid_mask=valid_mask, cotangent=cotangent)


@jax.custom_vjp
def low(v):
    return lax.optimization_barrier(v.astype(jnp.bfloat16)).astype(jnp.float32)

@jax.custom_vjp
def low_back(v):
    return v

def low_keep(v):
    return (low(v), None)

def low_pass(kept, grad):
    return (grad,)

def back_keep(v):
    return (v, None)

def back_low(kept, grad):
    return (low(grad),)
low.defvjp(low_keep, low_pass)
low_back.defvjp(back_keep, back_low)
EPS = 1e-05
NEG = -1e+30

def matmul(left, right):
    return jnp.dot(left, right, precision=lax.Precision.HIGHEST)

def normalize(values, gain, shift):
    mean = lax.optimization_barrier(jnp.mean(values, axis=-1, keepdims=True))
    centred = values - mean
    spread = lax.optimization_barrier(jnp.mean(centred * centred, axis=-1, keepdims=True))
    return centred * lax.rsqrt(spread + EPS) * gain + shift

def gelu_exact(values):
    return 0.5 * values * (1.0 + lax.erf(values * 0.7071067811865476))

def segment_attend(block):
    queries, keys, values, keeping = block
    raw = jnp.einsum('hqd,hkd->hqk', queries, keys, precision=lax.Precision.HIGHEST) * HEAD_DIM ** (-0.5)
    scores = low_back(jnp.where(keeping[:, None, :] > 0.5, raw, NEG))
    top = lax.optimization_barrier(jnp.max(scores, axis=-1, keepdims=True))
    lse = top + jnp.log(lax.optimization_barrier(jnp.sum(jnp.exp(scores - top), axis=-1, keepdims=True)))
    probs = low(jnp.exp(scores - lse))
    result = low_back(jnp.einsum('hqk,hkd->hqd', probs, values, precision=lax.Precision.HIGHEST))
    return (result, lse[..., 0])

def stream_forward(stream, keep_row, params):
    first_gain, first_shift, project_in, project_out, second_gain, second_shift, up_weight, down_weight = params
    length = stream.shape[0]
    inner = low(normalize(stream, first_gain, first_shift))
    mixed_qkv = low_back(low(matmul(inner, project_in)))
    split = mixed_qkv.reshape(length, 3, HEADS, HEAD_DIM)
    queries, keys, values = (split[:, 0], split[:, 1], split[:, 2])
    keep_heads = jnp.broadcast_to(keep_row[:, None, None], (length, HEADS, 1))
    heads_iota = jnp.arange(HEADS, dtype=jnp.int32)
    outs = []
    lses = []
    for level in range(BRANCHES):
        ratio = 2 ** level
        count = length // (SEG * ratio)
        pick = jnp.arange(ratio, dtype=jnp.int32)[:, None] == (heads_iota % ratio)[None, :]

        def select(array):
            shaped = array.reshape(count, SEG, ratio, HEADS, array.shape[-1])
            chosen = lax.optimization_barrier(jnp.sum(jnp.where(pick[None, None, :, :, None], shaped, 0.0), axis=2))
            return chosen.transpose(0, 2, 1, 3)
        block_out, block_lse = lax.map(jax.checkpoint(segment_attend), (select(queries), select(keys), select(values), select(keep_heads)[..., 0]))
        full_out = jnp.where(pick[None, None, :, :, None], block_out.transpose(0, 2, 1, 3)[:, :, None], 0.0)
        full_lse = jnp.where(pick[None, None, :, :], block_lse.transpose(0, 2, 1)[:, :, None], NEG)
        outs.append(full_out.reshape(length, HEADS, HEAD_DIM))
        lses.append(full_lse.reshape(length, HEADS))
    stacked = jnp.stack(lses)
    top = lax.optimization_barrier(jnp.max(stacked, axis=0))
    total = top + jnp.log(lax.optimization_barrier(jnp.sum(jnp.exp(stacked - top), axis=0)))
    shares = jnp.exp(stacked - total)
    merged = shares[0][..., None] * outs[0]
    for level in range(1, BRANCHES):
        merged = merged + shares[level][..., None] * outs[level]
    attended = low_back(low(merged.reshape(length, D) * keep_row[:, None]))
    middle = stream + low_back(matmul(attended, project_out))
    hidden = low(normalize(middle, second_gain, second_shift))
    upper = low_back(matmul(hidden, up_weight))
    active = low(gelu_exact(upper))
    return middle + low_back(matmul(active, down_weight))

def reference(tokens, first_gain, first_shift, project_in, project_out, second_gain, second_shift, up_weight, down_weight, valid_mask, cotangent):
    params = tuple((w.astype(jnp.float32) for w in (first_gain, first_shift, project_in, project_out, second_gain, second_shift, up_weight, down_weight)))
    keep = valid_mask.astype(jnp.float32)

    def whole(streams, *weights):
        return lax.map(lambda pair: stream_forward(pair[0], pair[1], weights), (streams, keep))
    result, pullback = jax.vjp(whole, tokens.astype(jnp.float32), *params)
    grads = pullback(cotangent.astype(jnp.float32))
    return (result.astype(jnp.bfloat16), grads[0], grads[1], grads[2], grads[3], grads[4], grads[5], grads[6], grads[7], grads[8])
```

```python
import functools
import math

import jax
import jax.numpy as jnp
import ml_dtypes
import numpy as np
from jax import lax
from jax.experimental import pallas as pl
from jax.experimental.pallas import tpu as pltpu
from jax.sharding import PartitionSpec as P

HEADS = 16
HEAD_DIM = 48
SEG = 1024
BRANCHES = 5
RES = 16
RUN = SEG // RES
D = HEADS * HEAD_DIM

EPS = 1e-05
NEG = -1e30
ROOT_HALF = 0.7071067811865476
INV_ROOT_TWO_PI = 0.3989422804014327
F32 = jnp.float32
BF16 = jnp.bfloat16
QUERY_SCALE = math.log2(math.e) * HEAD_DIM ** (-0.5)
VMEM_LIMIT = 56 * 1024 * 1024


def dotg(left, right, left_dim, right_dim):
    return lax.dot_general(
        left, right, (((left_dim,), (right_dim,)), ((), ())), preferred_element_type=F32
    )


def normalize(values, gain, shift):
    mean = jnp.mean(values, axis=-1, keepdims=True)
    centred = values - mean
    spread = jnp.mean(centred * centred, axis=-1, keepdims=True)
    inverse = lax.rsqrt(spread + EPS)
    normed = centred * inverse
    return (normed * gain + shift, normed, inverse)


def normalize_back(grad, normed, inverse, gain):
    scaled = grad * gain
    first = jnp.mean(scaled, axis=-1, keepdims=True)
    second = jnp.mean(scaled * normed, axis=-1, keepdims=True)
    return (
        inverse * (scaled - first - normed * second),
        jnp.sum(grad * normed, axis=0),
        jnp.sum(grad, axis=0),
    )


def reorder(array):
    rows, cols = array.shape
    split = array.reshape(rows // SEG, RUN, 2, 2, 2, 2, cols)
    return split.transpose(0, 5, 4, 3, 2, 1, 6).reshape(rows, cols)


def restore(array):
    rows, cols = array.shape
    split = array.reshape(rows // SEG, 2, 2, 2, 2, RUN, cols)
    return split.transpose(0, 5, 4, 3, 2, 1, 6).reshape(rows, cols)


def reversed_bits(head):
    return ((head & 1) << 3) | ((head & 2) << 1) | ((head & 4) >> 1) | ((head & 8) >> 3)


def near_class(head, low_bits, length):
    lane = lax.broadcasted_iota(jnp.int32, (1, length), 1)
    rho = lax.rem(lane // RUN, 1 << low_bits)
    return rho ^ (reversed_bits(head) & ((1 << low_bits) - 1))


def class_rows(near, length):
    row = lax.broadcasted_iota(jnp.int32, (16, length), 0)
    step = lax.rem(row + 3, 4) + 1
    bound = jnp.where((row >= 5) & (row <= 12), lax.shift_right_logical(RES, step), 0)
    return row, near < bound


def query_rows(head, length, neg_lse=None):
    near = near_class(head, 4, length)
    row, inside = class_rows(near, length)
    out = jnp.where(inside, 1.0, 0.0)
    out = jnp.where(row == 0, 1.0, out)
    out = jnp.where(row == 4, jnp.where(near < 1, 0.0, NEG), out)
    if neg_lse is not None:
        high = neg_lse.astype(BF16).astype(F32)
        rest = neg_lse - high
        mid = rest.astype(BF16).astype(F32)
        low = rest - mid
        out = jnp.where(row == 1, high, jnp.where(row == 2, mid, jnp.where(row == 3, low, out)))
    return out.astype(BF16)


def weight_of(level, step):
    return math.log2((step - level + 1) / (step - level)) if step > level else 0.0


def key_rows(head, level, low_bits, length, keep):
    near = near_class(head, low_bits, length)
    row, inside = class_rows(near, length)
    weight = jnp.zeros((16, length), F32)
    for step in range(level + 1, BRANCHES):
        value = weight_of(level, step)
        high = float(np.asarray(value, ml_dtypes.bfloat16))
        weight = jnp.where(row == 4 + step, high, weight)
        weight = jnp.where(row == 8 + step, value - high, weight)
    out = jnp.where(inside, weight, 0.0)
    out = jnp.where((row >= 1) & (row <= 3), 1.0, out)
    out = jnp.where(row == 0, jnp.where(keep > 0.5, 0.0, NEG), out)
    if level == BRANCHES - 1:
        out = jnp.where(row == 4, 1.0, out)
    return out.astype(BF16)


def value_rows(length):
    row = lax.broadcasted_iota(jnp.int32, (16, length), 0)
    return jnp.where(row < 2, 1.0, 0.0).astype(BF16)


def join(rows, extra):
    return jnp.concatenate([rows, extra], axis=0)


def kept_start(head, level, seg):
    size = SEG >> level
    block = reversed_bits(head) >> (4 - level)
    return pl.multiple_of(seg * SEG + block * size, min(size, 128))


def attend_tiles(query, key, value, tile, acc, top):
    key_t = key.T
    for start in range(0, key.shape[1], tile):
        scores = dotg(key_t[start : start + tile], query, 1, 0)
        here = jnp.max(scores, axis=0, keepdims=True)
        new_top = here if top is None else jnp.maximum(top, here)
        probs = jnp.exp2(scores - new_top).astype(BF16)
        part = dotg(value[:, start : start + tile], probs, 1, 0)
        acc = part if top is None else acc * jnp.exp2(top - new_top) + part
        top = new_top
    return acc, top


def local_forward(nseg, q_ref, k_ref, v_ref, keep_ref, o_ref, l_ref, m_ref, qa, ka, va):
    head = pl.program_id(0)
    length = nseg * SEG
    qa[...] = join(q_ref[0], query_rows(head, length))
    va[...] = join(v_ref[0], value_rows(length))
    ka[0] = join(k_ref[0], key_rows(head, 0, 4, length, keep_ref[...]))
    if nseg == 2:
        ka[1] = join(k_ref[0], key_rows(head, 1, 4, length, keep_ref[...]))
    for seg in range(nseg):
        lanes = slice(seg * SEG, (seg + 1) * SEG)
        acc, top = attend_tiles(qa[:, lanes], ka[0, :, lanes], va[:, lanes], 256, None, None)
        o_ref[:, lanes] = acc[:HEAD_DIM]
        l_ref[0, :, lanes] = acc[HEAD_DIM : HEAD_DIM + 1]
        m_ref[0, :, lanes] = top
    if nseg == 2:
        for seg in range(2):
            mine = pl.ds(kept_start(head, 1, seg), SEG // 2)
            other = pl.ds(kept_start(head, 1, 1 - seg), SEG // 2)
            merge_level(qa[:, mine], ka[1, :, other], va[:, other], mine, o_ref, l_ref, m_ref)


def merge_level(query, key, value, mine, o_ref, l_ref, m_ref):
    acc = jnp.concatenate([o_ref[:, mine], jnp.broadcast_to(l_ref[0, :, mine], (16, query.shape[1]))])
    acc, top = attend_tiles(query, key, value, 256, acc, m_ref[0, :, mine])
    o_ref[:, mine] = acc[:HEAD_DIM]
    l_ref[0, :, mine] = acc[HEAD_DIM : HEAD_DIM + 1]
    m_ref[0, :, mine] = top


def remote_keys(head, level, pack, nseg):
    k_ref, v_ref, mask_ref = pack
    length = k_ref.shape[1]
    row = lax.broadcasted_iota(jnp.int32, (16, length), 0)
    keep = jnp.sum(jnp.where(row == head, mask_ref[...].astype(F32), 0.0), axis=0, keepdims=True)
    key = join(k_ref[...], key_rows(head, level, 4 - level, length, keep))
    return key, join(v_ref[...], value_rows(length))


def remote_plan(first):
    return [(level,) for level in range(first, 3)] + [(3, 4)]


def remote_forward(nseg, first, q_ref, keep_ref, o_in, l_in, m_in, *refs):
    head = pl.program_id(0)
    levels = range(first, BRANCHES)
    packs = {level: refs[3 * i : 3 * i + 3] for i, level in enumerate(levels)}
    att_ref, lse_ref, o_ref, l_ref, m_ref, qa = refs[3 * len(levels) :]
    length = nseg * SEG
    qa[...] = join(q_ref[0], query_rows(head, length))
    o_ref[...] = o_in[...]
    l_ref[...] = l_in[...]
    m_ref[...] = m_in[...]
    for group in remote_plan(first):
        pairs = [remote_keys(head, level, packs[level], nseg) for level in group]
        key = jnp.concatenate([pair[0] for pair in pairs], axis=1)
        value = jnp.concatenate([pair[1] for pair in pairs], axis=1)
        for seg in range(nseg):
            mine = pl.ds(kept_start(head, group[0], seg), SEG >> group[0])
            merge_level(qa[:, mine], key, value, mine, o_ref, l_ref, m_ref)
    weight = keep_ref[...] / l_ref[0]
    att_ref[...] = (o_ref[...] * weight).astype(BF16)
    lse_ref[0] = m_ref[0] + jnp.log2(l_ref[0])


def back_tile(query_t, grad_t, query, grad, key, value, dq, dk_ref, dv_ref, lanes, first):
    scores = dotg(query_t, key, 1, 0)
    slope = dotg(grad_t, value, 1, 0)
    probs = jnp.exp2(scores)
    dscore = (probs * slope).astype(BF16)
    probs = probs.astype(BF16)
    part = dotg(key[:HEAD_DIM], dscore, 1, 1)
    dq = part if dq is None else dq + part
    dv = dotg(grad[:HEAD_DIM], probs, 1, 0)
    dk = dotg(query[:HEAD_DIM], dscore, 1, 0)
    if first:
        dv_ref[:, lanes] = dv
        dk_ref[:, lanes] = dk
    else:
        dv_ref[:, lanes] += dv
        dk_ref[:, lanes] += dk
    return dq


def grad_rows(grad, slope):
    length = grad.shape[1]
    row = lax.broadcasted_iota(jnp.int32, (16, length), 0)
    high = (-slope).astype(BF16).astype(F32)
    low = -slope - high
    extra = jnp.where(row == 0, high, jnp.where(row == 1, low, 0.0)).astype(BF16)
    return join(grad, extra)


def back_pair(query, grad, key_ref, value_ref, key_lanes, tile, dk_ref, dv_ref, start_lane, fresh):
    out = []
    for start in range(0, query.shape[1], tile):
        size = min(tile, query.shape[1])
        q_tile, g_tile = query[:, start : start + size], grad[:, start : start + size]
        q_t, g_t = q_tile.T, g_tile.T
        dq = None
        for lanes in key_lanes:
            dq = back_tile(
                q_t, g_t, q_tile, g_tile, key_ref[:, lanes], value_ref[:, lanes], dq,
                dk_ref, dv_ref, lanes, fresh and start == 0,
            )
        out.append(dq)
    return jnp.concatenate(out, axis=1) if len(out) > 1 else out[0]


DQ_SCALE = HEAD_DIM ** (-0.5)
DK_SCALE = math.log(2.0)


def neg_total(lse, keep):
    return jnp.where(keep > 0.5, -lse, NEG)


def local_backward(nseg, first, q_ref, k_ref, v_ref, g_ref, lse_ref, slope_ref, keep_ref, dqr_ref, out_ref, qa, ga, ka, va, dk, dv):
    head = pl.program_id(0)
    length = nseg * SEG
    keep = keep_ref[...]
    qa[...] = join(q_ref[0], query_rows(head, length, neg_total(lse_ref[0], keep)))
    ga[...] = grad_rows(g_ref[...], slope_ref[0])
    va[...] = join(v_ref[0], value_rows(length))
    ka[0] = join(k_ref[0], key_rows(head, 0, 4, length, keep))
    if nseg == 2:
        ka[1] = join(k_ref[0], key_rows(head, 1, 4, length, keep))
    for seg in range(nseg):
        lanes = slice(seg * SEG, (seg + 1) * SEG)
        tiles = [slice(seg * SEG + 256 * i, seg * SEG + 256 * (i + 1)) for i in range(4)]
        dq = back_pair(qa[:, lanes], ga[:, lanes], ka.at[0], va, tiles, 256, dk, dv, 0, True)
        out_ref[0, :, lanes] = dq * DQ_SCALE
    if nseg == 2:
        for seg in range(2):
            mine = pl.ds(kept_start(head, 1, seg), SEG // 2)
            base = kept_start(head, 1, 1 - seg)
            tiles = [pl.ds(pl.multiple_of(base + 256 * i, 256), 256) for i in range(2)]
            dq = back_pair(qa[:, mine], ga[:, mine], ka.at[1], va, tiles, 256, dk, dv, 0, False)
            out_ref[0, :, mine] += dq * DQ_SCALE
    size = SEG >> first
    for seg in range(nseg):
        mine = pl.ds(kept_start(head, first, seg), size)
        out_ref[0, :, mine] += dqr_ref[:, seg * size : (seg + 1) * size]
    out_ref[1] = dk[...] * DK_SCALE
    out_ref[2] = dv[...]


def remote_backward(nseg, first, q_ref, g_ref, lse_ref, slope_ref, keep_ref, *refs):
    head = pl.program_id(0)
    levels = range(first, BRANCHES)
    n = len(levels)
    packs = {level: refs[3 * i : 3 * i + 3] for i, level in enumerate(levels)}
    dqr_ref = refs[3 * n]
    outs = {level: refs[3 * n + 1 + i] for i, level in enumerate(levels)}
    qa, ga, ka, va, dk, dv = refs[4 * n + 1 :]
    length = nseg * SEG
    qa[...] = join(q_ref[0], query_rows(head, length, neg_total(lse_ref[0], keep_ref[...])))
    ga[...] = grad_rows(g_ref[...], slope_ref[0])
    full = SEG >> first
    for group in remote_plan(first):
        for i, level in enumerate(group):
            key, value = remote_keys(head, level, packs[level], nseg)
            ka[:, i * 512 : (i + 1) * 512] = key
            va[:, i * 512 : (i + 1) * 512] = value
        size = SEG >> group[0]
        mine = [pl.ds(kept_start(head, group[0], seg), size) for seg in range(nseg)]
        query = jnp.concatenate([qa[:, m] for m in mine], axis=1)
        grad = jnp.concatenate([ga[:, m] for m in mine], axis=1)
        tiles = [slice(256 * i, 256 * (i + 1)) for i in range(2 * len(group))]
        dq = back_pair(query, grad, ka, va, tiles, 256, dk, dv, 0, True) * DQ_SCALE
        for seg in range(nseg):
            piece = dq[:, seg * size : (seg + 1) * size]
            if group[0] == first:
                dqr_ref[:, seg * full : (seg + 1) * full] = piece
            else:
                inner = (reversed_bits(head) >> (4 - group[0])) & ((1 << (group[0] - first)) - 1)
                lanes = pl.ds(pl.multiple_of(seg * full + inner * size, 128), size)
                dqr_ref[:, lanes] += piece
        for i, level in enumerate(group):
            lanes = slice(i * 512, (i + 1) * 512)
            outs[level][0] = (dk[:, lanes] * DK_SCALE).astype(BF16)
            outs[level][1] = dv[:, lanes].astype(BF16)


def row_block(length):
    return pl.BlockSpec((1, 1, length), lambda h: (h, 0, 0))


def head_block(length):
    return pl.BlockSpec((HEAD_DIM, length), lambda h: (h, 0))


def part_block(part, length):
    return pl.BlockSpec((1, HEAD_DIM, length), lambda h: (part, h, 0))


def keep_block(length):
    return pl.BlockSpec((1, length), lambda h: (0, 0))


def pack_specs(length):
    return [
        pl.BlockSpec((HEAD_DIM, length), lambda h: (h, 0)),
        pl.BlockSpec((HEAD_DIM, length), lambda h: (HEADS + h, 0)),
        pl.BlockSpec((16, length), lambda h: (2 * D // 16, 0)),
    ]


PARAMS = pltpu.CompilerParams(vmem_limit_bytes=VMEM_LIMIT)


def shape(dims, dtype):
    return jax.ShapeDtypeStruct(dims, dtype)


def call_local_forward(nseg, qkv, keep):
    length = nseg * SEG
    return pl.pallas_call(
        functools.partial(local_forward, nseg),
        grid=(HEADS,),
        in_specs=[part_block(0, length), part_block(1, length), part_block(2, length), keep_block(length)],
        out_specs=[head_block(length), row_block(length), row_block(length)],
        out_shape=[shape((D, length), F32), shape((HEADS, 1, length), F32), shape((HEADS, 1, length), F32)],
        scratch_shapes=[
            pltpu.VMEM((64, length), BF16),
            pltpu.VMEM((nseg, 64, length), BF16),
            pltpu.VMEM((64, length), BF16),
        ],
        compiler_params=PARAMS,
        name="local_forward",
    )(qkv, qkv, qkv, keep)


def call_remote_forward(nseg, first, qkv, keep, o_part, l_part, m_part, packs):
    length = nseg * SEG
    args, specs = [], []
    for pack in packs:
        args += [pack] * 3
        specs += pack_specs(pack.shape[1])
    return pl.pallas_call(
        functools.partial(remote_forward, nseg, first),
        grid=(HEADS,),
        in_specs=[part_block(0, length), keep_block(length), head_block(length), row_block(length), row_block(length)]
        + specs,
        out_specs=[head_block(length), row_block(length)],
        out_shape=[shape((D, length), BF16), shape((HEADS, 1, length), F32)],
        scratch_shapes=[
            pltpu.VMEM((HEAD_DIM, length), F32),
            pltpu.VMEM((1, 1, length), F32),
            pltpu.VMEM((1, 1, length), F32),
            pltpu.VMEM((64, length), BF16),
        ],
        compiler_params=PARAMS,
        name="remote_forward",
    )(qkv, keep, o_part, l_part, m_part, *args)


def call_remote_backward(nseg, first, qkv, grad, lse, slope, keep, packs):
    length = nseg * SEG
    args, specs = [], []
    for pack in packs:
        args += [pack] * 3
        specs += pack_specs(pack.shape[1])
    kept = nseg * (SEG >> first)
    return pl.pallas_call(
        functools.partial(remote_backward, nseg, first),
        grid=(HEADS,),
        in_specs=[part_block(0, length), head_block(length), row_block(length), row_block(length), keep_block(length)]
        + specs,
        out_specs=[head_block(kept)]
        + [pl.BlockSpec((2, HEAD_DIM, pack.shape[1]), lambda h: (0, h, 0)) for pack in packs],
        out_shape=[shape((D, kept), F32)] + [shape((2, D, pack.shape[1]), BF16) for pack in packs],
        scratch_shapes=[
            pltpu.VMEM((64, length), BF16),
            pltpu.VMEM((64, length), BF16),
            pltpu.VMEM((64, 1024), BF16),
            pltpu.VMEM((64, 1024), BF16),
            pltpu.VMEM((HEAD_DIM, 1024), F32),
            pltpu.VMEM((HEAD_DIM, 1024), F32),
        ],
        compiler_params=PARAMS,
        name="remote_backward",
    )(qkv, grad, lse, slope, keep, *args)


def call_local_backward(nseg, first, qkv, grad, lse, slope, keep, dq_remote):
    length = nseg * SEG
    return pl.pallas_call(
        functools.partial(local_backward, nseg, first),
        grid=(HEADS,),
        in_specs=[part_block(0, length), part_block(1, length), part_block(2, length), head_block(length),
                  row_block(length), row_block(length), keep_block(length), head_block(dq_remote.shape[1])],
        out_specs=pl.BlockSpec((3, HEAD_DIM, length), lambda h: (0, h, 0)),
        out_shape=shape((3, D, length), F32),
        scratch_shapes=[
            pltpu.VMEM((64, length), BF16),
            pltpu.VMEM((64, length), BF16),
            pltpu.VMEM((nseg, 64, length), BF16),
            pltpu.VMEM((64, length), BF16),
            pltpu.VMEM((HEAD_DIM, length), F32),
            pltpu.VMEM((HEAD_DIM, length), F32),
        ],
        compiler_params=PARAMS,
        name="local_backward",
    )(qkv, qkv, qkv, grad, lse, slope, keep, dq_remote)


def pack_kernel(nseg, first, kv_ref, keep_ref, *outs):
    for i, level in enumerate(range(first, BRANCHES)):
        size = SEG >> level
        for head in range(HEADS):
            start = (reversed_bits(head) >> (4 - level)) * size
            for part in range(2):
                src = pl.ds((part + 1) * D + head * HEAD_DIM, HEAD_DIM)
                dst = pl.ds(part * D + head * HEAD_DIM, HEAD_DIM)
                for seg in range(nseg):
                    outs[i][dst, seg * size : (seg + 1) * size] = kv_ref[
                        src, seg * SEG + start : seg * SEG + start + size
                    ]
        rows = []
        for head in range(HEADS):
            start = (reversed_bits(head) >> (4 - level)) * size
            rows.append(
                jnp.concatenate([keep_ref[:, seg * SEG + start : seg * SEG + start + size] for seg in range(nseg)], axis=1)
            )
        outs[i][2 * D :, :] = jnp.concatenate(rows, axis=0).astype(BF16)


def call_pack(nseg, first, qkv, keep):
    return pl.pallas_call(
        functools.partial(pack_kernel, nseg, first),
        out_shape=[shape((2 * D + 16, nseg * (SEG >> level)), BF16) for level in range(first, BRANCHES)],
        compiler_params=PARAMS,
        name="pack",
    )(qkv.reshape(3 * D, nseg * SEG), keep)


def exchange(array, distance):
    size = lax.axis_size("seq")
    return lax.ppermute(array, "seq", [(i, i ^ distance) for i in range(size)])


def fetch_level(pack, group):
    pieces = exchange(pack, group)
    step = 1
    while step < group:
        pieces = jnp.concatenate([pieces, exchange(pieces, step)], axis=-1)
        step *= 2
    return pieces


def return_level(grads, group):
    step = group // 2
    while step >= 1:
        half = grads.shape[-1] // 2
        other = exchange(grads[..., half:], step)
        grads = (grads[..., :half].astype(F32) + other.astype(F32)).astype(BF16)
        step //= 2
    return exchange(grads, group)


def spread_level(grads, level, nseg):
    size = SEG >> level
    shaped = grads.astype(F32).reshape(2, HEADS, HEAD_DIM, nseg, 1, size)
    head = jnp.arange(HEADS, dtype=jnp.int32)
    block = reversed_bits(head) >> (4 - level)
    hit = block[:, None] == jnp.arange(1 << level, dtype=jnp.int32)[None, :]
    full = jnp.where(hit[None, :, None, None, :, None], shaped, 0.0)
    return full.reshape(2, D, nseg * SEG)


def scatter_sum(term):
    part = lax.psum_scatter(term.astype(BF16), "fsdp", scatter_dimension=0, tiled=True)
    piece = lax.psum_scatter(part, "seq", scatter_dimension=0, tiled=True)
    return lax.all_gather(piece, "seq", axis=0, tiled=True).astype(F32)


def per_device(
    tokens,
    first_gain,
    first_shift,
    project_in,
    project_out,
    second_gain,
    second_shift,
    up_weight,
    down_weight,
    valid_mask,
    cotangent,
):
    length = tokens.shape[1]
    nseg = length // SEG
    first = nseg.bit_length()

    def gather(weight):
        return lax.all_gather(weight, "fsdp", axis=0, tiled=True)

    weight_in = gather(project_in)
    small = gather(jnp.stack([first_gain, first_shift, second_gain, second_shift], axis=1)).astype(F32)
    gain_attend, shift_attend, gain_feed, shift_feed = (small[:, i] for i in range(4))
    weight_out = gather(project_out)
    weight_up = gather(up_weight)
    weight_down = gather(down_weight)

    stream = reorder(tokens[0]).astype(F32)
    keep = reorder(valid_mask[0][:, None])[:, 0].astype(F32)[None, :]
    normed_in, unit_first, inverse_first = normalize(stream, gain_attend, shift_attend)
    inner = normed_in.astype(BF16)
    column_scale = jnp.where(jnp.arange(3 * D) < D, QUERY_SCALE, 1.0).astype(F32)
    qkv = (dotg(weight_in, inner, 0, 1) * column_scale[:, None]).astype(BF16).reshape(3, D, length)

    sends = call_pack(nseg, first, qkv, keep)
    packs = [
        fetch_level(send, (SEG << (level - 1)) // length)
        for level, send in zip(range(first, BRANCHES), sends)
    ]
    o_part, l_part, m_part = call_local_forward(nseg, qkv, keep)
    attended, lse = call_remote_forward(nseg, first, qkv, keep, o_part, l_part, m_part, packs)

    middle = stream + dotg(attended, weight_out, 0, 0)
    normed_mid, unit_second, inverse_second = normalize(middle, gain_feed, shift_feed)
    hidden = normed_mid.astype(BF16)
    upper = jnp.dot(hidden, weight_up, preferred_element_type=F32)
    active = (0.5 * upper * (1.0 + lax.erf(upper * ROOT_HALF))).astype(BF16)
    final = middle + jnp.dot(active, weight_down, preferred_element_type=F32)
    mixed = restore(final.astype(BF16))[None]

    grad_final = reorder(cotangent[0])
    grad_down = dotg(active, grad_final, 0, 0)
    grad_active = dotg(grad_final, weight_down, 1, 1)
    slope = (
        0.5 * (1.0 + lax.erf(upper * ROOT_HALF))
        + upper * jnp.exp(-0.5 * upper * upper) * INV_ROOT_TWO_PI
    )
    grad_upper = (grad_active * slope).astype(BF16)
    grad_up = dotg(hidden, grad_upper, 0, 0)
    grad_hidden = dotg(grad_upper, weight_up, 1, 1)
    grad_mid_norm, grad_gain_feed, grad_shift_feed = normalize_back(
        grad_hidden, unit_second, inverse_second, gain_feed
    )
    grad_middle = grad_final.astype(F32) + grad_mid_norm
    grad_branch = grad_middle.astype(BF16)
    grad_out_proj = dotg(attended, grad_branch, 1, 0)
    grad_merged = (dotg(weight_out, grad_branch, 1, 1) * keep).astype(BF16)
    along = jnp.sum(
        (grad_merged.astype(F32) * attended.astype(F32)).reshape(HEADS, HEAD_DIM, length), axis=1
    )[:, None, :]

    dq_remote, *sent = call_remote_backward(nseg, first, qkv, grad_merged, lse, along, keep, packs)
    returned = [
        return_level(part, (SEG << (level - 1)) // length)
        for level, part in zip(range(first, BRANCHES), sent)
    ]
    local = call_local_backward(nseg, first, qkv, grad_merged, lse, along, keep, dq_remote)
    key_value = local[1:]
    for level, part in zip(range(first, BRANCHES), returned):
        key_value = key_value + spread_level(part, level, nseg)
    grad_mixed = jnp.concatenate([local[:1], key_value], axis=0).astype(BF16).reshape(3 * D, length)

    grad_in = dotg(inner, grad_mixed, 0, 1)
    grad_inner = dotg(grad_mixed, weight_in, 0, 1)
    grad_in_norm, grad_gain_attend, grad_shift_attend = normalize_back(
        grad_inner, unit_first, inverse_first, gain_attend
    )
    tokens_back = restore(grad_middle + grad_in_norm)[None]

    vectors = jnp.stack([grad_gain_attend, grad_shift_attend, grad_gain_feed, grad_shift_feed], axis=1)
    vectors = scatter_sum(vectors)
    return (
        mixed,
        tokens_back,
        vectors[:, 0],
        vectors[:, 1],
        scatter_sum(grad_in),
        scatter_sum(grad_out_proj),
        vectors[:, 2],
        vectors[:, 3],
        scatter_sum(grad_up),
        scatter_sum(grad_down),
    )


def solution(mesh):
    in_specs = (
        P("fsdp", "seq", None),
        P("fsdp"),
        P("fsdp"),
        P("fsdp", None),
        P("fsdp", None),
        P("fsdp"),
        P("fsdp"),
        P("fsdp", None),
        P("fsdp", None),
        P("fsdp", "seq"),
        P("fsdp", "seq", None),
    )
    out_specs = (
        P("fsdp", "seq", None),
        P("fsdp", "seq", None),
        P("fsdp"),
        P("fsdp"),
        P("fsdp", None),
        P("fsdp", None),
        P("fsdp"),
        P("fsdp"),
        P("fsdp", None),
        P("fsdp", None),
    )
    return jax.shard_map(
        per_device, mesh=mesh, in_specs=in_specs, out_specs=out_specs, check_vma=False
    )
```

```python
import functools
import math

import jax
import jax.numpy as jnp
import ml_dtypes
import numpy as np
from jax import lax
from jax.experimental import pallas as pl
from jax.experimental.pallas import tpu as pltpu
from jax.sharding import PartitionSpec as P

HEADS = 16
HEAD_DIM = 48
SEG = 1024
BRANCHES = 5
RES = 16
RUN = SEG // RES
D = HEADS * HEAD_DIM

EPS = 1e-05
NEG = -1e30
ROOT_HALF = 0.7071067811865476
INV_ROOT_TWO_PI = 0.3989422804014327
F32 = jnp.float32
BF16 = jnp.bfloat16
QUERY_SCALE = math.log2(math.e) * HEAD_DIM ** (-0.5)
VMEM_LIMIT = 56 * 1024 * 1024


def dotg(left, right, left_dim, right_dim):
    return lax.dot_general(
        left, right, (((left_dim,), (right_dim,)), ((), ())), preferred_element_type=F32
    )


def normalize(values, gain, shift):
    mean = jnp.mean(values, axis=-1, keepdims=True)
    centred = values - mean
    spread = jnp.mean(centred * centred, axis=-1, keepdims=True)
    inverse = lax.rsqrt(spread + EPS)
    normed = centred * inverse
    return (normed * gain + shift, normed, inverse)


def normalize_back(grad, normed, inverse, gain):
    scaled = grad * gain
    first = jnp.mean(scaled, axis=-1, keepdims=True)
    second = jnp.mean(scaled * normed, axis=-1, keepdims=True)
    return (
        inverse * (scaled - first - normed * second),
        jnp.sum(grad * normed, axis=0),
        jnp.sum(grad, axis=0),
    )


def reversed_bits(head):
    return ((head & 1) << 3) | ((head & 2) << 1) | ((head & 4) >> 1) | ((head & 8) >> 3)


def near_class(head, low_bits, length):
    lane = lax.broadcasted_iota(jnp.int32, (1, length), 1)
    rho = lax.rem(lane // RUN, 1 << low_bits)
    return rho ^ (reversed_bits(head) & ((1 << low_bits) - 1))


def class_rows(near, length):
    row = lax.broadcasted_iota(jnp.int32, (16, length), 0)
    step = lax.rem(row + 3, 4) + 1
    bound = jnp.where((row >= 5) & (row <= 12), lax.shift_right_logical(RES, step), 0)
    return row, near < bound


def query_rows(head, length, neg_lse=None):
    near = near_class(head, 4, length)
    row, inside = class_rows(near, length)
    out = jnp.where(inside, 1.0, 0.0)
    out = jnp.where(row == 0, 1.0, out)
    out = jnp.where(row == 4, jnp.where(near < 1, 0.0, NEG), out)
    if neg_lse is not None:
        high = neg_lse.astype(BF16).astype(F32)
        rest = neg_lse - high
        mid = rest.astype(BF16).astype(F32)
        low = rest - mid
        out = jnp.where(row == 1, high, jnp.where(row == 2, mid, jnp.where(row == 3, low, out)))
    return out.astype(BF16)


def residue_of(rho):
    return reversed_bits(rho)


def local_keep(count, length):
    lane = lax.broadcasted_iota(jnp.int32, (1, length), 1)
    rho = lax.rem(lane // RUN, RES)
    position = lane // SEG * SEG + lax.rem(lane, RUN) * RES + residue_of(rho)
    return position < count


def remote_keep(head, level, nseg, mine, limit, length):
    size = SEG >> level
    group = (SEG << (level - 1)) // (nseg * SEG)
    lane = lax.broadcasted_iota(jnp.int32, (1, length), 1)
    owner = mine ^ (group + lane // (nseg * size))
    inside = lax.rem(lane, nseg * size)
    rho = (reversed_bits(head) >> (4 - level)) * (size // RUN) + lax.rem(inside, size) // RUN
    position = (
        owner * (nseg * SEG) + inside // size * SEG + lax.rem(inside, RUN) * RES + residue_of(rho)
    )
    return position < limit


def weight_of(level, step):
    return math.log2((step - level + 1) / (step - level)) if step > level else 0.0


def key_rows(head, level, low_bits, length, keep):
    near = near_class(head, low_bits, length)
    row, inside = class_rows(near, length)
    weight = jnp.zeros((16, length), F32)
    for step in range(level + 1, BRANCHES):
        value = weight_of(level, step)
        high = float(np.asarray(value, ml_dtypes.bfloat16))
        weight = jnp.where(row == 4 + step, high, weight)
        weight = jnp.where(row == 8 + step, value - high, weight)
    out = jnp.where(inside, weight, 0.0)
    out = jnp.where((row >= 1) & (row <= 3), 1.0, out)
    out = jnp.where(row == 0, jnp.where(keep, 0.0, NEG), out)
    if level == BRANCHES - 1:
        out = jnp.where(row == 4, 1.0, out)
    return out.astype(BF16)


def value_rows(length):
    row = lax.broadcasted_iota(jnp.int32, (16, length), 0)
    return jnp.where(row < 2, 1.0, 0.0).astype(BF16)


def join(rows, extra):
    return jnp.concatenate([rows, extra], axis=0)


def kept_start(head, level, seg):
    size = SEG >> level
    block = reversed_bits(head) >> (4 - level)
    return pl.multiple_of(seg * SEG + block * size, min(size, 128))


def attend_tiles(query, key, value, tile, acc, top):
    key_t = key.T
    for start in range(0, key.shape[1], tile):
        scores = dotg(key_t[start : start + tile], query, 1, 0)
        here = jnp.max(scores, axis=0, keepdims=True)
        new_top = here if top is None else jnp.maximum(top, here)
        probs = jnp.exp2(scores - new_top).astype(BF16)
        part = dotg(value[:, start : start + tile], probs, 1, 0)
        acc = part if top is None else acc * jnp.exp2(top - new_top) + part
        top = new_top
    return acc, top


def local_forward(nseg, mask_ref, q_ref, k_ref, v_ref, o_ref, l_ref, m_ref, qa, ka, va):
    head = pl.program_id(0)
    length = nseg * SEG
    keep = local_keep(mask_ref[0], length)
    qa[...] = join(q_ref[0], query_rows(head, length))
    va[...] = join(v_ref[0], value_rows(length))
    ka[0] = join(k_ref[0], key_rows(head, 0, 4, length, keep))
    if nseg == 2:
        ka[1] = join(k_ref[0], key_rows(head, 1, 4, length, keep))
    for seg in range(nseg):
        lanes = slice(seg * SEG, (seg + 1) * SEG)
        acc, top = attend_tiles(qa[:, lanes], ka[0, :, lanes], va[:, lanes], 256, None, None)
        o_ref[:, lanes] = acc[:HEAD_DIM]
        l_ref[0, :, lanes] = acc[HEAD_DIM : HEAD_DIM + 1]
        m_ref[0, :, lanes] = top
    if nseg == 2:
        for seg in range(2):
            mine = pl.ds(kept_start(head, 1, seg), SEG // 2)
            other = pl.ds(kept_start(head, 1, 1 - seg), SEG // 2)
            merge_level(qa[:, mine], ka[1, :, other], va[:, other], mine, o_ref, l_ref, m_ref)


def merge_level(query, key, value, mine, o_ref, l_ref, m_ref):
    acc = jnp.concatenate([o_ref[:, mine], jnp.broadcast_to(l_ref[0, :, mine], (16, query.shape[1]))])
    acc, top = attend_tiles(query, key, value, 256, acc, m_ref[0, :, mine])
    o_ref[:, mine] = acc[:HEAD_DIM]
    l_ref[0, :, mine] = acc[HEAD_DIM : HEAD_DIM + 1]
    m_ref[0, :, mine] = top


def remote_keys(head, level, pack, nseg, mask_ref):
    k_ref, v_ref = pack
    length = k_ref.shape[1]
    keep = remote_keep(head, level, nseg, mask_ref[1], mask_ref[2], length)
    key = join(k_ref[...], key_rows(head, level, 4 - level, length, keep))
    return key, join(v_ref[...], value_rows(length))


def remote_plan(first):
    return [(level,) for level in range(first, 3)] + [(3, 4)]


def remote_forward(nseg, first, mask_ref, q_ref, o_in, l_in, m_in, *refs):
    head = pl.program_id(0)
    levels = range(first, BRANCHES)
    packs = {level: refs[2 * i : 2 * i + 2] for i, level in enumerate(levels)}
    att_ref, lse_ref, o_ref, l_ref, m_ref, qa = refs[2 * len(levels) :]
    length = nseg * SEG
    qa[...] = join(q_ref[0], query_rows(head, length))
    o_ref[...] = o_in[...]
    l_ref[...] = l_in[...]
    m_ref[...] = m_in[...]
    for group in remote_plan(first):
        pairs = [remote_keys(head, level, packs[level], nseg, mask_ref) for level in group]
        key = jnp.concatenate([pair[0] for pair in pairs], axis=1)
        value = jnp.concatenate([pair[1] for pair in pairs], axis=1)
        for seg in range(nseg):
            mine = pl.ds(kept_start(head, group[0], seg), SEG >> group[0])
            merge_level(qa[:, mine], key, value, mine, o_ref, l_ref, m_ref)
    weight = jnp.where(local_keep(mask_ref[0], length), 1.0, 0.0) / l_ref[0]
    att_ref[...] = (o_ref[...] * weight).astype(BF16)
    lse_ref[0] = m_ref[0] + jnp.log2(l_ref[0])


def back_tile(query_t, grad_t, query, grad, key, value, dq, dk_ref, dv_ref, lanes, first):
    scores = dotg(query_t, key, 1, 0)
    slope = dotg(grad_t, value, 1, 0)
    probs = jnp.exp2(scores)
    dscore = (probs * slope).astype(BF16)
    probs = probs.astype(BF16)
    part = dotg(key[:HEAD_DIM], dscore, 1, 1)
    dq = part if dq is None else dq + part
    dv = dotg(grad[:HEAD_DIM], probs, 1, 0)
    dk = dotg(query[:HEAD_DIM], dscore, 1, 0)
    if first:
        dv_ref[:, lanes] = dv
        dk_ref[:, lanes] = dk
    else:
        dv_ref[:, lanes] += dv
        dk_ref[:, lanes] += dk
    return dq


def grad_rows(grad, slope):
    length = grad.shape[1]
    row = lax.broadcasted_iota(jnp.int32, (16, length), 0)
    high = (-slope).astype(BF16).astype(F32)
    low = -slope - high
    extra = jnp.where(row == 0, high, jnp.where(row == 1, low, 0.0)).astype(BF16)
    return join(grad, extra)


def back_pair(query, grad, key_ref, value_ref, key_lanes, tile, dk_ref, dv_ref, start_lane, fresh):
    out = []
    for start in range(0, query.shape[1], tile):
        size = min(tile, query.shape[1])
        q_tile, g_tile = query[:, start : start + size], grad[:, start : start + size]
        q_t, g_t = q_tile.T, g_tile.T
        dq = None
        for lanes in key_lanes:
            dq = back_tile(
                q_t, g_t, q_tile, g_tile, key_ref[:, lanes], value_ref[:, lanes], dq,
                dk_ref, dv_ref, lanes, fresh and start == 0,
            )
        out.append(dq)
    return jnp.concatenate(out, axis=1) if len(out) > 1 else out[0]


DQ_SCALE = HEAD_DIM ** (-0.5)
DK_SCALE = math.log(2.0)


def neg_total(lse, keep):
    return jnp.where(keep, -lse, NEG)


def local_backward(nseg, first, mask_ref, q_ref, k_ref, v_ref, g_ref, lse_ref, slope_ref, dqr_ref, out_ref, qa, ga, ka, va, dk, dv):
    head = pl.program_id(0)
    length = nseg * SEG
    keep = local_keep(mask_ref[0], length)
    qa[...] = join(q_ref[0], query_rows(head, length, neg_total(lse_ref[0], keep)))
    ga[...] = grad_rows(g_ref[...], slope_ref[0])
    va[...] = join(v_ref[0], value_rows(length))
    ka[0] = join(k_ref[0], key_rows(head, 0, 4, length, keep))
    if nseg == 2:
        ka[1] = join(k_ref[0], key_rows(head, 1, 4, length, keep))
    for seg in range(nseg):
        lanes = slice(seg * SEG, (seg + 1) * SEG)
        tiles = [slice(seg * SEG + 256 * i, seg * SEG + 256 * (i + 1)) for i in range(4)]
        dq = back_pair(qa[:, lanes], ga[:, lanes], ka.at[0], va, tiles, 256, dk, dv, 0, True)
        out_ref[0, :, lanes] = dq * DQ_SCALE
    if nseg == 2:
        for seg in range(2):
            mine = pl.ds(kept_start(head, 1, seg), SEG // 2)
            base = kept_start(head, 1, 1 - seg)
            tiles = [pl.ds(pl.multiple_of(base + 256 * i, 256), 256) for i in range(2)]
            dq = back_pair(qa[:, mine], ga[:, mine], ka.at[1], va, tiles, 256, dk, dv, 0, False)
            out_ref[0, :, mine] += dq * DQ_SCALE
    size = SEG >> first
    for seg in range(nseg):
        mine = pl.ds(kept_start(head, first, seg), size)
        out_ref[0, :, mine] += dqr_ref[:, seg * size : (seg + 1) * size]
    out_ref[1] = dk[...] * DK_SCALE
    out_ref[2] = dv[...]


def remote_backward(nseg, first, mask_ref, q_ref, g_ref, lse_ref, slope_ref, *refs):
    head = pl.program_id(0)
    levels = range(first, BRANCHES)
    n = len(levels)
    packs = {level: refs[2 * i : 2 * i + 2] for i, level in enumerate(levels)}
    dqr_ref = refs[2 * n]
    outs = {level: refs[2 * n + 1 + i] for i, level in enumerate(levels)}
    qa, ga, ka, va, dk, dv = refs[3 * n + 1 :]
    length = nseg * SEG
    qa[...] = join(q_ref[0], query_rows(head, length, neg_total(lse_ref[0], local_keep(mask_ref[0], length))))
    ga[...] = grad_rows(g_ref[...], slope_ref[0])
    full = SEG >> first
    for group in remote_plan(first):
        for i, level in enumerate(group):
            key, value = remote_keys(head, level, packs[level], nseg, mask_ref)
            ka[:, i * 512 : (i + 1) * 512] = key
            va[:, i * 512 : (i + 1) * 512] = value
        size = SEG >> group[0]
        mine = [pl.ds(kept_start(head, group[0], seg), size) for seg in range(nseg)]
        query = jnp.concatenate([qa[:, m] for m in mine], axis=1)
        grad = jnp.concatenate([ga[:, m] for m in mine], axis=1)
        tiles = [slice(256 * i, 256 * (i + 1)) for i in range(2 * len(group))]
        dq = back_pair(query, grad, ka, va, tiles, 256, dk, dv, 0, True) * DQ_SCALE
        for seg in range(nseg):
            piece = dq[:, seg * size : (seg + 1) * size]
            if group[0] == first:
                dqr_ref[:, seg * full : (seg + 1) * full] = piece
            else:
                inner = (reversed_bits(head) >> (4 - group[0])) & ((1 << (group[0] - first)) - 1)
                lanes = pl.ds(pl.multiple_of(seg * full + inner * size, 128), size)
                dqr_ref[:, lanes] += piece
        for i, level in enumerate(group):
            lanes = slice(i * 512, (i + 1) * 512)
            outs[level][0] = (dk[:, lanes] * DK_SCALE).astype(BF16)
            outs[level][1] = dv[:, lanes].astype(BF16)


def row_block(length):
    return pl.BlockSpec((1, 1, length), lambda h: (h, 0, 0))


def head_block(length):
    return pl.BlockSpec((HEAD_DIM, length), lambda h: (h, 0))


def part_block(part, length):
    return pl.BlockSpec((1, HEAD_DIM, length), lambda h: (part, h, 0))


MASK_BLOCK = pl.BlockSpec(memory_space=pltpu.SMEM)


def pack_specs(length):
    return [
        pl.BlockSpec((HEAD_DIM, length), lambda h: (h, 0)),
        pl.BlockSpec((HEAD_DIM, length), lambda h: (HEADS + h, 0)),
    ]


PARAMS = pltpu.CompilerParams(vmem_limit_bytes=VMEM_LIMIT)


def shape(dims, dtype):
    return jax.ShapeDtypeStruct(dims, dtype)


def cost(seconds):
    return pl.CostEstimate(flops=int(seconds * 1.1e15), transcendentals=0, bytes_accessed=0)


def call_local_forward(nseg, qkv, mask):
    length = nseg * SEG
    return pl.pallas_call(
        functools.partial(local_forward, nseg),
        grid=(HEADS,),
        in_specs=[MASK_BLOCK, part_block(0, length), part_block(1, length), part_block(2, length)],
        out_specs=[head_block(length), row_block(length), row_block(length)],
        out_shape=[shape((D, length), F32), shape((HEADS, 1, length), F32), shape((HEADS, 1, length), F32)],
        scratch_shapes=[
            pltpu.VMEM((64, length), BF16),
            pltpu.VMEM((nseg, 64, length), BF16),
            pltpu.VMEM((64, length), BF16),
        ],
        compiler_params=PARAMS,
        cost_estimate=cost(nseg * 37e-6),
        name="local_forward",
    )(mask, qkv, qkv, qkv)


def call_remote_forward(nseg, first, qkv, mask, o_part, l_part, m_part, packs):
    length = nseg * SEG
    args, specs = [], []
    for pack in packs:
        args += [pack] * 2
        specs += pack_specs(pack.shape[1])
    return pl.pallas_call(
        functools.partial(remote_forward, nseg, first),
        grid=(HEADS,),
        in_specs=[MASK_BLOCK, part_block(0, length), head_block(length), row_block(length), row_block(length)]
        + specs,
        out_specs=[head_block(length), row_block(length)],
        out_shape=[shape((D, length), BF16), shape((HEADS, 1, length), F32)],
        scratch_shapes=[
            pltpu.VMEM((HEAD_DIM, length), F32),
            pltpu.VMEM((1, 1, length), F32),
            pltpu.VMEM((1, 1, length), F32),
            pltpu.VMEM((64, length), BF16),
        ],
        compiler_params=PARAMS,
        cost_estimate=cost(nseg * 24e-6),
        name="remote_forward",
    )(mask, qkv, o_part, l_part, m_part, *args)


def call_remote_backward(nseg, first, qkv, grad, lse, slope, mask, packs):
    length = nseg * SEG
    args, specs = [], []
    for pack in packs:
        args += [pack] * 2
        specs += pack_specs(pack.shape[1])
    kept = nseg * (SEG >> first)
    return pl.pallas_call(
        functools.partial(remote_backward, nseg, first),
        grid=(HEADS,),
        in_specs=[MASK_BLOCK, part_block(0, length), head_block(length), row_block(length), row_block(length)]
        + specs,
        out_specs=[head_block(kept)]
        + [pl.BlockSpec((2, HEAD_DIM, pack.shape[1]), lambda h: (0, h, 0)) for pack in packs],
        out_shape=[shape((D, kept), F32)] + [shape((2, D, pack.shape[1]), BF16) for pack in packs],
        scratch_shapes=[
            pltpu.VMEM((64, length), BF16),
            pltpu.VMEM((64, length), BF16),
            pltpu.VMEM((64, 1024), BF16),
            pltpu.VMEM((64, 1024), BF16),
            pltpu.VMEM((HEAD_DIM, 1024), F32),
            pltpu.VMEM((HEAD_DIM, 1024), F32),
        ],
        compiler_params=PARAMS,
        cost_estimate=cost(nseg * 20e-6),
        name="remote_backward",
    )(mask, qkv, grad, lse, slope, *args)


def call_local_backward(nseg, first, qkv, grad, lse, slope, mask, dq_remote):
    length = nseg * SEG
    return pl.pallas_call(
        functools.partial(local_backward, nseg, first),
        grid=(HEADS,),
        in_specs=[MASK_BLOCK, part_block(0, length), part_block(1, length), part_block(2, length), head_block(length),
                  row_block(length), row_block(length), head_block(dq_remote.shape[1])],
        out_specs=pl.BlockSpec((3, HEAD_DIM, length), lambda h: (0, h, 0)),
        out_shape=shape((3, D, length), F32),
        scratch_shapes=[
            pltpu.VMEM((64, length), BF16),
            pltpu.VMEM((64, length), BF16),
            pltpu.VMEM((nseg, 64, length), BF16),
            pltpu.VMEM((64, length), BF16),
            pltpu.VMEM((HEAD_DIM, length), F32),
            pltpu.VMEM((HEAD_DIM, length), F32),
        ],
        compiler_params=PARAMS,
        cost_estimate=cost(nseg * 72e-6),
        name="local_backward",
    )(mask, qkv, qkv, qkv, grad, lse, slope, dq_remote)


HALF = D // 2


def const_block(dims):
    return pl.BlockSpec(dims, lambda i: (0,) * len(dims), pipeline_mode=pl.Buffered(1))


def rev4(value):
    return int(reversed_bits(value))


TILES = D // 128


def put_rows(tiled, start, array):
    for tile in range(TILES):
        tiled[tile, start : start + array.shape[0], :] = array[:, tile * 128 : (tile + 1) * 128]


def get_rows(tiled, start, size):
    return jnp.concatenate([tiled[tile, start : start + size, :] for tile in range(TILES)], axis=1)


def get_residue(tiled, start):
    return jnp.concatenate(
        [tiled[tile, pl.ds(start, RUN, stride=RES), :] for tile in range(TILES)], axis=1
    )


def put_residue(tiled, start, array):
    for tile in range(TILES):
        tiled[tile, pl.ds(start, RUN, stride=RES), :] = array[:, tile * 128 : (tile + 1) * 128]


def project_kernel(nseg, first, tok_ref, gain_ref, shift_ref, w_ref, qkv_ref, xp_ref, inner_ref, *refs):
    *packs, xs = refs
    step = pl.program_id(0)

    @pl.when(step == 0)
    def _():
        for seg in range(nseg):
            put_rows(xs, 0, tok_ref[seg * SEG : (seg + 1) * SEG, :].astype(F32))
            for pair in range(RES // 2):
                rows = jnp.concatenate(
                    [get_residue(xs, rev4(2 * pair + i)) for i in range(2)], axis=0
                )
                normed = normalize(rows, gain_ref[...], shift_ref[...])[0].astype(BF16)
                at = slice(seg * SEG + pair * 2 * RUN, seg * SEG + (pair + 1) * 2 * RUN)
                xp_ref[at, :] = rows.astype(BF16)
                inner_ref[:, at] = normed.T

    scale = jnp.where(step < 2, QUERY_SCALE, 1.0)
    for start in range(0, nseg * SEG, 512):
        lanes = slice(start, start + 512)
        qkv_ref[0, :, lanes] = (dotg(w_ref[...], inner_ref[:, lanes], 0, 0) * scale).astype(BF16)

    @pl.when(step >= 2)
    def _():
        upper = lax.rem(step, 2) == 1
        for pack, level in zip(packs, range(first, BRANCHES)):
            size = SEG >> level
            for head in range(HEADS // 2):
                rows = slice(head * HEAD_DIM, (head + 1) * HEAD_DIM)
                pieces = []
                for seg in range(nseg):
                    start = seg * SEG + (rev4(head) >> (4 - level)) * size
                    if level < 4:
                        pieces.append(qkv_ref[0, rows, start : start + size])
                    else:
                        both = qkv_ref[0, rows, start : start + 2 * size]
                        pieces.append(jnp.where(upper, both[:, size:], both[:, :size]))
                pack[rows, :] = jnp.concatenate(pieces, axis=1) if nseg > 1 else pieces[0]


def call_project(nseg, first, tokens, gain, shift, weight):
    length = nseg * SEG
    kept = [nseg * (SEG >> level) for level in range(first, BRANCHES)]
    return pl.pallas_call(
        functools.partial(project_kernel, nseg, first),
        grid=(6,),
        in_specs=[
            const_block((length, D)),
            const_block((1, D)),
            const_block((1, D)),
            pl.BlockSpec((D, HALF), lambda i: (0, i)),
        ],
        out_specs=[
            pl.BlockSpec((1, HALF, length), lambda i: (i // 2, i % 2, 0)),
            const_block((length, D)),
            const_block((D, length)),
        ]
        + [pl.BlockSpec((HALF, size), lambda i: (jnp.maximum(i - 2, 0), 0)) for size in kept],
        out_shape=[
            shape((3, D, length), BF16),
            shape((length, D), BF16),
            shape((D, length), BF16),
        ]
        + [shape((2 * D, size), BF16) for size in kept],
        scratch_shapes=[pltpu.VMEM((TILES, SEG, 128), F32)],
        compiler_params=PARAMS,
        cost_estimate=cost(nseg * 10e-6),
        name="project",
    )(tokens, gain, shift, weight)


ROWS = 256
UP_ROWS = 4 * 192
STACK = UP_ROWS + 192 + D


def feed_kernel(
    nseg, mask_ref, att_ref, x_ref, cot_ref, wout_ref, up_ref, down_ref, gain_ref, shift_ref,
    mixed_ref, gmid_ref, gm_ref, along_ref, vec_ref, grads_ref,
    cs, out_acc, up_acc, down_acc, stage, sems,
):
    step = pl.program_id(0)
    quarter = lax.rem(step, 4)
    low = (quarter >> 1) | ((quarter & 1) << 1)

    @pl.when(step == 0)
    def _():
        out_acc[...] = jnp.zeros_like(out_acc)
        up_acc[...] = jnp.zeros_like(up_acc)
        down_acc[...] = jnp.zeros_like(down_acc)
        vec_ref[...] = jnp.zeros_like(vec_ref)

    @pl.when(quarter == 0)
    def _():
        put_rows(cs, 0, cot_ref[...].astype(F32))

    grad = jnp.concatenate([get_residue(cs, rev4(i) + low) for i in range(4)], axis=0)
    grad_b = grad.astype(BF16)
    att = att_ref[...]
    middle = x_ref[...].astype(F32) + dotg(att, wout_ref[...], 0, 0)
    gain = gain_ref[...]
    normed, unit, inverse = normalize(middle, gain, shift_ref[...])
    hidden = normed.astype(BF16)
    hidden_t = hidden.T
    final = middle
    grad_hidden = jnp.zeros((ROWS, D), F32)
    for start in range(0, 4 * D, D):
        cols = slice(start, start + D)
        upper = dotg(hidden, up_ref[:, cols], 1, 0)
        grad_active = dotg(grad_b, down_ref[cols, :], 1, 1)
        half = 0.5 * (1.0 + lax.erf(upper * ROOT_HALF))
        slope = half + upper * jnp.exp(-0.5 * upper * upper) * INV_ROOT_TWO_PI
        active = (upper * half).astype(BF16)
        grad_upper = (grad_active * slope).astype(BF16)
        final = final + dotg(active, down_ref[cols, :], 1, 0)
        grad_hidden = grad_hidden + dotg(grad_upper, up_ref[:, cols], 1, 1)
        up_acc[:, cols] += dotg(hidden_t, grad_upper, 1, 0)
        down_acc[cols, :] += dotg(active, grad_b, 0, 0)
    for i in range(4):
        put_residue(cs, rev4(i) + low, final[i * RUN : (i + 1) * RUN])

    @pl.when(quarter == 3)
    def _():
        mixed_ref[...] = get_rows(cs, 0, SEG).astype(BF16)

    back, gain_back, shift_back = normalize_back(grad_hidden, unit, inverse, gain)
    vec_ref[0:1, :] += gain_back[None, :]
    vec_ref[1:2, :] += shift_back[None, :]
    grad_middle = grad + back
    gmid_ref[...] = grad_middle
    branch = grad_middle.astype(BF16)
    out_acc[...] += dotg(att, branch, 1, 0)
    lane = lax.broadcasted_iota(jnp.int32, (1, ROWS), 1)
    position = step // 4 * SEG + lax.rem(lane, RUN) * RES + residue_of(lane // RUN) + low
    keep = position < mask_ref[0]
    merged = jnp.where(keep, dotg(wout_ref[...], branch, 1, 1), 0.0).astype(BF16)
    gm_ref[...] = merged
    product = merged.astype(F32) * att.astype(F32)
    for head in range(HEADS):
        rows = slice(head * HEAD_DIM, (head + 1) * HEAD_DIM)
        along_ref[head] = jnp.sum(product[rows], axis=0, keepdims=True)

    @pl.when(step == pl.num_programs(0) - 1)
    def _():
        copies = []
        for owner in range(4):
            for piece in range(3):
                count = owner * 3 + piece
                slot = count % 2
                if count >= 2:
                    copies[count - 2].wait()
                if piece == 0:
                    rows = slice(owner * 192, (owner + 1) * 192)
                    for col in range(4):
                        stage[slot, col * 192 : (col + 1) * 192, :] = up_acc[
                            rows, col * D : (col + 1) * D
                        ].astype(BF16)
                    offset, size = 0, UP_ROWS
                elif piece == 1:
                    stage[slot, :192, :] = out_acc[owner * 192 : (owner + 1) * 192, :].astype(BF16)
                    offset, size = UP_ROWS, 192
                else:
                    stage[slot, :D, :] = down_acc[owner * D : (owner + 1) * D, :].astype(BF16)
                    offset, size = UP_ROWS + 192, D
                copy = pltpu.make_async_copy(
                    stage.at[slot, pl.ds(0, size), :],
                    grads_ref.at[owner, pl.ds(offset, size), :],
                    sems.at[slot],
                )
                copy.start()
                copies.append(copy)
        copies[-2].wait()
        copies[-1].wait()


def call_feed(nseg, mask, att, x, cot, wout, up, down, gain, shift):
    length = nseg * SEG
    return pl.pallas_call(
        functools.partial(feed_kernel, nseg),
        grid=(length // ROWS,),
        in_specs=[
            MASK_BLOCK,
            pl.BlockSpec((D, ROWS), lambda i: (0, i)),
            pl.BlockSpec((ROWS, D), lambda i: (i, 0)),
            pl.BlockSpec((SEG, D), lambda i: (i // 4, 0)),
            const_block((D, D)),
            const_block((D, 4 * D)),
            const_block((4 * D, D)),
            const_block((1, D)),
            const_block((1, D)),
        ],
        out_specs=[
            pl.BlockSpec((SEG, D), lambda i: (i // 4, 0)),
            pl.BlockSpec((ROWS, D), lambda i: (i, 0)),
            pl.BlockSpec((D, ROWS), lambda i: (0, i)),
            pl.BlockSpec((HEADS, 1, ROWS), lambda i: (0, 0, i)),
            pl.BlockSpec((2, D), lambda i: (0, 0)),
            pl.BlockSpec(memory_space=pl.ANY),
        ],
        out_shape=[
            shape((length, D), BF16),
            shape((length, D), F32),
            shape((D, length), BF16),
            shape((HEADS, 1, length), F32),
            shape((2, D), F32),
            shape((4, STACK, D), BF16),
        ],
        scratch_shapes=[
            pltpu.VMEM((TILES, SEG, 128), F32),
            pltpu.VMEM((D, D), F32),
            pltpu.VMEM((D, 4 * D), F32),
            pltpu.VMEM((4 * D, D), F32),
            pltpu.VMEM((2, D, D), BF16),
            pltpu.SemaphoreType.DMA((2,)),
        ],
        compiler_params=pltpu.CompilerParams(vmem_limit_bytes=62 * 1024 * 1024),
        cost_estimate=cost(nseg * 45e-6),
        name="feed",
    )(mask, att, x, cot, wout, up, down, gain, shift)


def inner_back_kernel(nseg, first, local_ref, inner_ref, w_ref, x_ref, gmid_ref, gain_ref, *refs):
    n = BRANCHES - first
    packs, (grad_in_ref, back_ref, vec_ref), (acc, mixed, order) = refs[:n], refs[n : n + 3], refs[n + 3 :]
    step = pl.program_id(0)
    length = nseg * SEG

    @pl.when(step < 2)
    def _():
        mixed[...] = local_ref[0].astype(BF16)

    @pl.when(step >= 2)
    def _():
        upper = lax.rem(step, 2) == 1
        for pack, level in zip(packs, range(first, BRANCHES)):
            size = SEG >> level
            for head in range(HEADS // 2):
                rows = slice(head * HEAD_DIM, (head + 1) * HEAD_DIM)
                for seg in range(nseg):
                    start = seg * SEG + (rev4(head) >> (4 - level)) * size
                    piece = pack[0, rows, seg * size : (seg + 1) * size].astype(F32)
                    if level == 4:
                        zero = jnp.zeros_like(piece)
                        piece = jnp.concatenate(
                            [jnp.where(upper, zero, piece), jnp.where(upper, piece, zero)], axis=1
                        )
                    local_ref[0, rows, start : start + piece.shape[1]] += piece
        mixed[...] = local_ref[0].astype(BF16)

    grad_in_ref[...] = dotg(inner_ref[...], mixed[...], 1, 1).astype(BF16)
    for start in range(0, length, 512):
        lanes = slice(start, start + 512)
        part = dotg(w_ref[...], mixed[:, lanes], 1, 0)

        @pl.when(step == 0)
        def _():
            acc[:, lanes] = part

        @pl.when(step > 0)
        def _():
            acc[:, lanes] += part

    @pl.when(step == pl.num_programs(0) - 1)
    def _():
        gain = gain_ref[...]
        gain_back = jnp.zeros((1, D), F32)
        shift_back = jnp.zeros((1, D), F32)
        for seg in range(nseg):
            for pair in range(RES // 2):
                at = slice(seg * SEG + pair * 2 * RUN, seg * SEG + (pair + 1) * 2 * RUN)
                grad = acc[:, at].T
                _, unit, inverse = normalize(x_ref[at, :].astype(F32), gain, gain)
                back, gain_part, shift_part = normalize_back(grad, unit, inverse, gain)
                gain_back = gain_back + gain_part[None, :]
                shift_back = shift_back + shift_part[None, :]
                total = gmid_ref[at, :] + back
                for i in range(2):
                    put_residue(order, rev4(2 * pair + i), total[i * RUN : (i + 1) * RUN])
            back_ref[seg * SEG : (seg + 1) * SEG, :] = get_rows(order, 0, SEG)
        vec_ref[0:1, :] = gain_back
        vec_ref[1:2, :] = shift_back


def call_inner_back(nseg, first, local, inner, weight, x, gmid, gain, packs):
    length = nseg * SEG
    return pl.pallas_call(
        functools.partial(inner_back_kernel, nseg, first),
        grid=(6,),
        in_specs=[
            pl.BlockSpec((1, HALF, length), lambda i: (i // 2, i % 2, 0)),
            const_block((D, length)),
            pl.BlockSpec((D, HALF), lambda i: (0, i)),
            const_block((length, D)),
            const_block((length, D)),
            const_block((1, D)),
        ]
        + [
            pl.BlockSpec((1, HALF, pack.shape[2]), lambda i: (jnp.maximum(i // 2 - 1, 0), i % 2, 0))
            for pack in packs
        ],
        out_specs=[
            pl.BlockSpec((D, HALF), lambda i: (0, i)),
            const_block((length, D)),
            const_block((2, D)),
        ],
        out_shape=[shape((D, 3 * D), BF16), shape((length, D), F32), shape((2, D), F32)],
        scratch_shapes=[
            pltpu.VMEM((D, length), F32),
            pltpu.VMEM((HALF, length), BF16),
            pltpu.VMEM((TILES, SEG, 128), F32),
        ],
        compiler_params=PARAMS,
        cost_estimate=cost(nseg * 15e-6),
        name="inner_back",
    )(local, inner, weight, x, gmid, gain, *packs)


def exchange(array, distance):
    size = lax.axis_size("seq")
    return lax.ppermute(array, "seq", [(i, i ^ distance) for i in range(size)])


def fetch_level(pack, group):
    pieces = exchange(pack, group)
    step = 1
    while step < group:
        pieces = jnp.concatenate([pieces, exchange(pieces, step)], axis=-1)
        step *= 2
    return pieces


def return_level(grads, group):
    step = group // 2
    while step >= 1:
        half = grads.shape[-1] // 2
        other = exchange(grads[..., half:], step)
        grads = (grads[..., :half].astype(F32) + other.astype(F32)).astype(BF16)
        step //= 2
    return exchange(grads, group)


def per_device(
    tokens,
    first_gain,
    first_shift,
    project_in,
    project_out,
    second_gain,
    second_shift,
    up_weight,
    down_weight,
    valid_mask,
    cotangent,
):
    length = tokens.shape[1]
    nseg = length // SEG
    first = nseg.bit_length()
    levels = range(first, BRANCHES)
    group_of = {level: (SEG << (level - 1)) // length for level in levels}

    def gather(weight):
        return lax.all_gather(weight, "fsdp", axis=0, tiled=True)

    weight_in = gather(project_in)
    small = gather(jnp.stack([first_gain, first_shift, second_gain, second_shift], axis=1)).astype(F32)
    gain_attend, shift_attend, gain_feed, shift_feed = (small[:, i][None, :] for i in range(4))
    weight_out = gather(project_out)
    weight_up = gather(up_weight)
    weight_down = gather(down_weight)

    block_devices = (RES * SEG) // length
    place = lax.axis_index("seq")
    count = jnp.sum(valid_mask[0])
    counts = lax.all_gather(count.astype(F32), "seq")
    same = jnp.arange(counts.shape[0], dtype=jnp.int32) // block_devices == place // block_devices
    limit = jnp.sum(jnp.where(same, counts, 0.0)).astype(jnp.int32)
    local_mask = count[None]
    mask = jnp.stack([count, place, limit + place // block_devices * (RES * SEG)])

    qkv, x, inner, *sends = call_project(nseg, first, tokens[0], gain_attend, shift_attend, weight_in)
    packs = [fetch_level(send, group_of[level]) for level, send in zip(levels, sends)]
    o_part, l_part, m_part = call_local_forward(nseg, qkv, local_mask)
    attended, lse = call_remote_forward(nseg, first, qkv, mask, o_part, l_part, m_part, packs)

    mixed, grad_middle, grad_merged, along, feed_vec, feed_grads = call_feed(
        nseg, local_mask, attended, x, cotangent[0], weight_out, weight_up, weight_down, gain_feed, shift_feed
    )
    feed_part = lax.psum_scatter(feed_grads, "fsdp", scatter_dimension=0, tiled=True)
    feed_sum = lax.psum(feed_part, "seq")[0]

    dq_remote, *sent = call_remote_backward(nseg, first, qkv, grad_merged, lse, along, mask, packs)
    returned = [return_level(part, group_of[level]) for level, part in zip(levels, sent)]
    local = call_local_backward(nseg, first, qkv, grad_merged, lse, along, local_mask, dq_remote)
    grad_in, tokens_back, attend_vec = call_inner_back(
        nseg, first, local, inner, weight_in, x, grad_middle, gain_attend, returned
    )
    in_part = lax.psum_scatter(grad_in, "fsdp", scatter_dimension=0, tiled=True)
    in_part, feed_sum = lax.optimization_barrier((in_part, feed_sum))
    in_sum = lax.psum(in_part, "seq")
    vectors = lax.psum(jnp.concatenate([attend_vec, feed_vec], axis=0), ("fsdp", "seq"))
    quarter = D // lax.axis_size("fsdp")
    vectors = lax.dynamic_slice_in_dim(vectors, lax.axis_index("fsdp") * quarter, quarter, 1)
    up_rows = feed_sum[:UP_ROWS].reshape(4, 192, D)
    return (
        mixed[None],
        tokens_back[None],
        vectors[0],
        vectors[1],
        in_sum.astype(F32),
        feed_sum[UP_ROWS : UP_ROWS + 192].astype(F32),
        vectors[2],
        vectors[3],
        jnp.concatenate([up_rows[i] for i in range(4)], axis=1).astype(F32),
        feed_sum[UP_ROWS + 192 :].astype(F32),
    )


def solution(mesh):
    in_specs = (
        P("fsdp", "seq", None),
        P("fsdp"),
        P("fsdp"),
        P("fsdp", None),
        P("fsdp", None),
        P("fsdp"),
        P("fsdp"),
        P("fsdp", None),
        P("fsdp", None),
        P("fsdp", "seq"),
        P("fsdp", "seq", None),
    )
    out_specs = (
        P("fsdp", "seq", None),
        P("fsdp", "seq", None),
        P("fsdp"),
        P("fsdp"),
        P("fsdp", None),
        P("fsdp", None),
        P("fsdp"),
        P("fsdp"),
        P("fsdp", None),
        P("fsdp", None),
    )
    return jax.shard_map(
        per_device, mesh=mesh, in_specs=in_specs, out_specs=out_specs, check_vma=False
    )
```

```python
import functools
import math

import jax
import jax.numpy as jnp
import ml_dtypes
import numpy as np
from jax import lax
from jax.experimental import pallas as pl
from jax.experimental.pallas import tpu as pltpu
from jax.sharding import PartitionSpec as P

HEADS = 16
HEAD_DIM = 48
SEG = 1024
BRANCHES = 5
RES = 16
RUN = SEG // RES
D = HEADS * HEAD_DIM

EPS = 1e-05
NEG = -1e30
ROOT_HALF = 0.7071067811865476
INV_ROOT_TWO_PI = 0.3989422804014327
F32 = jnp.float32
BF16 = jnp.bfloat16
QUERY_SCALE = math.log2(math.e) * HEAD_DIM ** (-0.5)
VMEM_LIMIT = 56 * 1024 * 1024


def dotg(left, right, left_dim, right_dim):
    return lax.dot_general(
        left, right, (((left_dim,), (right_dim,)), ((), ())), preferred_element_type=F32
    )


def normalize(values, gain, shift):
    mean = jnp.mean(values, axis=-1, keepdims=True)
    centred = values - mean
    spread = jnp.mean(centred * centred, axis=-1, keepdims=True)
    inverse = lax.rsqrt(spread + EPS)
    normed = centred * inverse
    return (normed * gain + shift, normed, inverse)


def normalize_back(grad, normed, inverse, gain):
    scaled = grad * gain
    first = jnp.mean(scaled, axis=-1, keepdims=True)
    second = jnp.mean(scaled * normed, axis=-1, keepdims=True)
    return (
        inverse * (scaled - first - normed * second),
        jnp.sum(grad * normed, axis=0),
        jnp.sum(grad, axis=0),
    )


def reversed_bits(head):
    return ((head & 1) << 3) | ((head & 2) << 1) | ((head & 4) >> 1) | ((head & 8) >> 3)


def near_class(head, low_bits, length):
    lane = lax.broadcasted_iota(jnp.int32, (1, length), 1)
    rho = lax.rem(lane // RUN, 1 << low_bits)
    return rho ^ (reversed_bits(head) & ((1 << low_bits) - 1))


def class_rows(near, length):
    row = lax.broadcasted_iota(jnp.int32, (16, length), 0)
    step = lax.rem(row + 3, 4) + 1
    bound = jnp.where((row >= 5) & (row <= 12), lax.shift_right_logical(RES, step), 0)
    return row, near < bound


def query_rows(head, length, neg_lse=None):
    near = near_class(head, 4, length)
    row, inside = class_rows(near, length)
    out = jnp.where(inside, 1.0, 0.0)
    out = jnp.where(row == 0, 1.0, out)
    out = jnp.where(row == 4, jnp.where(near < 1, 0.0, NEG), out)
    if neg_lse is not None:
        high = neg_lse.astype(BF16).astype(F32)
        rest = neg_lse - high
        mid = rest.astype(BF16).astype(F32)
        low = rest - mid
        out = jnp.where(row == 1, high, jnp.where(row == 2, mid, jnp.where(row == 3, low, out)))
    return out.astype(BF16)


def residue_of(rho):
    return reversed_bits(rho)


def local_keep(count, length):
    lane = lax.broadcasted_iota(jnp.int32, (1, length), 1)
    rho = lax.rem(lane // RUN, RES)
    position = lane // SEG * SEG + lax.rem(lane, RUN) * RES + residue_of(rho)
    return position < count


def packed_keep(count, level, nseg):
    size = SEG >> level
    dims = (HEADS, nseg * size)
    head = lax.broadcasted_iota(jnp.int32, dims, 0)
    lane = lax.broadcasted_iota(jnp.int32, dims, 1)
    rho = (reversed_bits(head) >> (4 - level)) * (size // RUN) + lax.rem(lane, size) // RUN
    position = lane // size * SEG + lax.rem(lane, RUN) * RES + residue_of(rho)
    return jnp.where(position < count, 1.0, 0.0).astype(BF16)


def weight_of(level, step):
    return math.log2((step - level + 1) / (step - level)) if step > level else 0.0


def key_rows(head, level, low_bits, length, keep):
    near = near_class(head, low_bits, length)
    row, inside = class_rows(near, length)
    weight = jnp.zeros((16, length), F32)
    for step in range(level + 1, BRANCHES):
        value = weight_of(level, step)
        high = float(np.asarray(value, ml_dtypes.bfloat16))
        weight = jnp.where(row == 4 + step, high, weight)
        weight = jnp.where(row == 8 + step, value - high, weight)
    out = jnp.where(inside, weight, 0.0)
    out = jnp.where((row >= 1) & (row <= 3), 1.0, out)
    out = jnp.where(row == 0, jnp.where(keep, 0.0, NEG), out)
    if level == BRANCHES - 1:
        out = jnp.where(row == 4, 1.0, out)
    return out.astype(BF16)


def value_rows(length):
    row = lax.broadcasted_iota(jnp.int32, (16, length), 0)
    return jnp.where(row < 2, 1.0, 0.0).astype(BF16)


def join(rows, extra):
    return jnp.concatenate([rows, extra], axis=0)


def kept_start(head, level, seg):
    size = SEG >> level
    block = reversed_bits(head) >> (4 - level)
    return pl.multiple_of(seg * SEG + block * size, min(size, 128))


def partner(axis, distance):
    place = lax.axis_index(axis)
    return {axis: place + distance * (1 - 2 * lax.rem(lax.div(place, distance), 2))}


def seq_bits():
    return lax.axis_size("seq").bit_length() - 1


def meet(peers):
    barrier = pltpu.get_barrier_semaphore()
    for axis, distance in peers:
        pl.semaphore_signal(
            barrier, inc=1, device_id=partner(axis, distance), device_id_type=pl.DeviceIdType.MESH
        )
    pl.semaphore_wait(barrier, len(peers))


class Sends:
    def __init__(self, send_sems, recv_sems):
        self.send_sems, self.recv_sems, self.made = send_sems, recv_sems, {}

    def copy(self, key, source, target, axis, distance):
        index = self.made.setdefault(key, len(self.made))
        return pltpu.make_async_remote_copy(
            src_ref=source,
            dst_ref=target,
            send_sem=self.send_sems.at[index],
            recv_sem=self.recv_sems.at[index],
            device_id=partner(axis, distance),
            device_id_type=pl.DeviceIdType.MESH,
        )


class Gather:
    def __init__(self, nseg, first, packs, gathered, sends):
        self.hops, self.distances = [], set()
        for level, pack, into in zip(range(first, BRANCHES), packs, gathered):
            group = (SEG << (level - 1)) // (nseg * SEG)
            hops = [((level, 0), pack, into.at[0], group)]
            step = 1
            while step < group:
                hops.append(((level, step), into.at[pl.ds(0, step)], into.at[pl.ds(step, step)], step))
                step *= 2
            self.hops.append([sends.copy(k, a, b, "seq", d) for k, a, b, d in hops])
            self.distances |= {hop[3] for hop in hops}

    def peers(self):
        return [("seq", distance) for distance in sorted(self.distances)]

    def start(self):
        for hops in self.hops:
            hops[0].start()

    def pass_on(self, turn):
        for hops in self.hops:
            if turn < len(hops):
                hops[turn - 1].wait_recv()
                hops[turn].start()

    def finish(self):
        for hops in self.hops:
            for hop in hops:
                hop.wait_send()
            hops[-1].wait_recv()

    def turns(self):
        return max(len(hops) for hops in self.hops)


class Return:
    def __init__(self, nseg, first, sent, returned, bufs, recvs, local_sems, sends):
        self.plans = []
        for i, level in enumerate(range(first, BRANCHES)):
            group = (SEG << (level - 1)) // (nseg * SEG)
            plan = []
            if group == 1:
                plan.append((None, sends.copy((level, 0), sent[i].at[0], returned[i], "seq", group)))
                self.plans.append((plan, None))
                continue
            buf, recv = bufs.pop(0), recvs.pop(0)
            step = group // 2
            load = pltpu.make_async_copy(sent[i].at[pl.ds(0, step)], buf, local_sems.at[i])
            source, at, add = sent[i].at[pl.ds(step, step)], 0, None
            while step >= 1:
                into = recv.at[pl.ds(at, step)]
                plan.append((add, sends.copy((level, step), source, into, "seq", step)))
                add = (buf, recv, at, step)
                at += step
                step //= 2
                if step:
                    source = buf.at[pl.ds(step, step)]
            plan.append((add, sends.copy((level, 0), buf.at[0], returned[i], "seq", group)))
            self.plans.append((plan, load))

    def start(self):
        for plan, load in self.plans:
            if load is not None:
                load.start()
            plan[0][1].start()

    def turn(self, number):
        for plan, load in self.plans:
            if number < len(plan):
                plan[number - 1][1].wait_recv()
                if number == 1 and load is not None:
                    load.wait()
                buf, recv, at, step = plan[number][0]
                for i in range(step):
                    buf[i] = (buf[i].astype(F32) + recv[at + i].astype(F32)).astype(BF16)
                plan[number][1].start()

    def finish(self):
        for plan, load in self.plans:
            for _, copy in plan:
                copy.wait_send()
            plan[-1][1].wait_recv()

    def turns(self):
        return max(len(plan) for plan, _ in self.plans)


def add_blocks(into, at, other, start, count):
    unit = max(u for u in range(1, 13) if count % u == 0)

    def body(i, carry):
        rows = pl.ds(at + i * unit, unit)
        part = other[pl.ds(start + i * unit, unit)].astype(F32)
        into[rows] = (into[rows].astype(F32) + part).astype(BF16)
        return carry

    lax.fori_loop(0, count // unit, body, 0)


def copy_blocks(into, other, at, count):
    unit = max(u for u in range(1, 13) if count % u == 0)

    def body(i, carry):
        rows = pl.ds(at + i * unit, unit)
        into[rows] = other[rows]
        return carry

    lax.fori_loop(0, count // unit, body, 0)


class Reduce:
    def __init__(self, chunks, blocks, source, terms, own, recv_core, recv_x, recv_seq, total, sends, loads=None):
        self.chunks, self.blocks, self.source, self.terms, self.own = chunks, blocks, source, terms, own
        self.recv_core, self.recv_x, self.recv_seq, self.total = recv_core, recv_x, recv_seq, total
        self.sends, self.loads = sends, loads
        fsdp = lax.axis_index("fsdp")
        self.core, self.x = lax.rem(fsdp, 2), lax.div(fsdp, 2)
        self.bits = seq_bits()
        seq = lax.axis_index("seq")
        self.low = [0]
        self.given = []
        for j in range(self.bits):
            bit = lax.rem(lax.div(seq, 2**j), 2)
            half = blocks >> (j + 1)
            self.given.append(self.low[j] + (1 - bit) * half)
            self.low.append(self.low[j] + bit * half)

    def peers(self):
        return [("fsdp", 1), ("fsdp", 2)] + [("seq", 2**j) for j in range(self.bits)]

    def stages(self):
        return 2 + 2 * self.bits

    def core_copy(self, chunk, xo):
        rows = pl.ds(chunk * self.blocks, self.blocks)
        owner = 2 * xo + 1 - self.core
        return self.sends.copy(
            ("core", chunk, xo), self.source.at[owner, rows], self.recv_core.at[xo, rows], "fsdp", 1
        )

    def load_copy(self, chunk, xo):
        rows = pl.ds(chunk * self.blocks, self.blocks)
        return pltpu.make_async_copy(
            self.source.at[2 * xo + self.core, rows], self.terms.at[xo, rows], self.loads.at[2 * chunk + xo]
        )

    def x_copy(self, chunk):
        rows = pl.ds(chunk * self.blocks, self.blocks)
        return self.sends.copy(
            ("x", chunk), self.terms.at[self.own(1 - self.x), rows], self.recv_x.at[rows], "fsdp", 2
        )

    def down_copy(self, chunk, j):
        half = self.blocks >> (j + 1)
        base = chunk * self.blocks
        rows = pl.ds(base + self.given[j], half)
        into = pl.ds(base + self.blocks - (self.blocks >> j), half)
        return self.sends.copy(
            ("down", chunk, j), self.terms.at[self.own(self.x), rows], self.recv_seq.at[into], "seq", 2**j
        )

    def up_copy(self, chunk, j):
        rows = pl.ds(chunk * self.blocks + self.low[j + 1], self.blocks >> (j + 1))
        return self.sends.copy(("up", chunk, j), self.total.at[rows], self.total.at[rows], "seq", 2**j)

    def begin(self, chunk):
        for xo in range(2):
            if self.loads is not None:
                self.load_copy(chunk, xo).start()
            self.core_copy(chunk, xo).start()

    def event(self, stage, chunk):
        base = chunk * self.blocks
        if stage == 0:
            for xo in range(2):
                self.core_copy(chunk, xo).wait_recv()
                if self.loads is not None:
                    self.load_copy(chunk, xo).wait()
                add_blocks(self.terms.at[self.own(xo)], base, self.recv_core.at[xo], base, self.blocks)
            self.x_copy(chunk).start()
        elif stage < 2 + self.bits:
            j = stage - 2
            mine = self.terms.at[self.own(self.x)]
            if stage == 1:
                self.x_copy(chunk).wait_recv()
                add_blocks(mine, base, self.recv_x, base, self.blocks)
            else:
                self.down_copy(chunk, j).wait_recv()
                half = self.blocks >> (j + 1)
                add_blocks(
                    mine, base + self.low[j + 1], self.recv_seq, base + self.blocks - (self.blocks >> j), half
                )
            if j + 1 < self.bits:
                self.down_copy(chunk, j + 1).start()
            else:
                copy_blocks(self.total, mine, base + self.low[self.bits], self.blocks >> self.bits)
                self.up_copy(chunk, self.bits - 1).start()
        else:
            j = 2 * self.bits + 1 - stage
            self.up_copy(chunk, j).wait_recv()
            if j:
                self.up_copy(chunk, j - 1).start()

    def finish(self):
        for chunk in range(self.chunks):
            for xo in range(2):
                self.core_copy(chunk, xo).wait_send()
            self.x_copy(chunk).wait_send()
            for j in range(self.bits):
                self.down_copy(chunk, j).wait_send()
                self.up_copy(chunk, j).wait_send()

    def copies(self):
        return self.chunks * (3 + 2 * self.bits)


def run_schedule(step, last, events):
    due = {}
    for when, call in events:
        due.setdefault(min(when, last), []).append(call)
    for when in sorted(due):

        @pl.when(step == when)
        def _():
            for call in due[when]:
                call()


def attend_tiles(query, key, value, tile, acc, top):
    key_t = key.T
    for start in range(0, key.shape[1], tile):
        scores = dotg(key_t[start : start + tile], query, 1, 0)
        here = jnp.max(scores, axis=0, keepdims=True)
        new_top = here if top is None else jnp.maximum(top, here)
        probs = jnp.exp2(scores - new_top).astype(BF16)
        part = dotg(value[:, start : start + tile], probs, 1, 0)
        acc = part if top is None else acc * jnp.exp2(top - new_top) + part
        top = new_top
    return acc, top


def local_forward(nseg, first, mask_ref, q_ref, k_ref, v_ref, *refs):
    n = BRANCHES - first
    packs, (o_ref, l_ref, m_ref), gathered = refs[:n], refs[n : n + 3], refs[n + 3 : 2 * n + 3]
    qa, ka, va, send_sems, recv_sems = refs[2 * n + 3 :]
    head = pl.program_id(0)
    length = nseg * SEG
    gather = Gather(nseg, first, packs, gathered, Sends(send_sems, recv_sems))

    def begin():
        meet(gather.peers())
        gather.start()

    events = [(0, begin)]
    for turn in range(1, gather.turns()):
        events.append((2 + 4 * turn, functools.partial(gather.pass_on, turn)))
    run_schedule(head, HEADS - 1, events)

    keep = local_keep(mask_ref[0], length)
    qa[...] = join(q_ref[0], query_rows(head, length))
    va[...] = join(v_ref[0], value_rows(length))
    ka[0] = join(k_ref[0], key_rows(head, 0, 4, length, keep))
    if nseg == 2:
        ka[1] = join(k_ref[0], key_rows(head, 1, 4, length, keep))
    for seg in range(nseg):
        lanes = slice(seg * SEG, (seg + 1) * SEG)
        acc, top = attend_tiles(qa[:, lanes], ka[0, :, lanes], va[:, lanes], 256, None, None)
        o_ref[:, lanes] = acc[:HEAD_DIM]
        l_ref[0, :, lanes] = acc[HEAD_DIM : HEAD_DIM + 1]
        m_ref[0, :, lanes] = top
    if nseg == 2:
        for seg in range(2):
            mine = pl.ds(kept_start(head, 1, seg), SEG // 2)
            other = pl.ds(kept_start(head, 1, 1 - seg), SEG // 2)
            merge_level(qa[:, mine], ka[1, :, other], va[:, other], mine, o_ref, l_ref, m_ref)

    run_schedule(head, HEADS - 1, [(HEADS - 1, gather.finish)])


def merge_level(query, key, value, mine, o_ref, l_ref, m_ref):
    acc = jnp.concatenate([o_ref[:, mine], jnp.broadcast_to(l_ref[0, :, mine], (16, query.shape[1]))])
    acc, top = attend_tiles(query, key, value, 256, acc, m_ref[0, :, mine])
    o_ref[:, mine] = acc[:HEAD_DIM]
    l_ref[0, :, mine] = acc[HEAD_DIM : HEAD_DIM + 1]
    m_ref[0, :, mine] = top


def remote_keys(head, level, pack):
    k_ref, v_ref, mask_ref = pack
    pieces = range(k_ref.shape[0])
    key, value, mask = (
        jnp.concatenate([ref[i] for i in pieces], axis=1) for ref in (k_ref, v_ref, mask_ref)
    )
    length = key.shape[1]
    row = lax.broadcasted_iota(jnp.int32, (16, length), 0)
    keep = jnp.sum(jnp.where(row == head, mask.astype(F32), 0.0), axis=0, keepdims=True) > 0.5
    return join(key, key_rows(head, level, 4 - level, length, keep)), join(value, value_rows(length))


def remote_plan(first):
    return [(level,) for level in range(first, 3)] + [(3, 4)]


def remote_forward(nseg, first, mask_ref, q_ref, o_in, l_in, m_in, *refs):
    head = pl.program_id(0)
    levels = range(first, BRANCHES)
    packs = {level: refs[3 * i : 3 * i + 3] for i, level in enumerate(levels)}
    att_ref, lse_ref, o_ref, l_ref, m_ref, qa = refs[3 * len(levels) :]
    length = nseg * SEG
    qa[...] = join(q_ref[0], query_rows(head, length))
    o_ref[...] = o_in[...]
    l_ref[...] = l_in[...]
    m_ref[...] = m_in[...]
    for group in remote_plan(first):
        pairs = [remote_keys(head, level, packs[level]) for level in group]
        key = jnp.concatenate([pair[0] for pair in pairs], axis=1)
        value = jnp.concatenate([pair[1] for pair in pairs], axis=1)
        for seg in range(nseg):
            mine = pl.ds(kept_start(head, group[0], seg), SEG >> group[0])
            merge_level(qa[:, mine], key, value, mine, o_ref, l_ref, m_ref)
    weight = jnp.where(local_keep(mask_ref[0], length), 1.0, 0.0) / l_ref[0]
    att_ref[...] = (o_ref[...] * weight).astype(BF16)
    lse_ref[0] = m_ref[0] + jnp.log2(l_ref[0])


def back_tile(query_t, grad_t, query, grad, key, value, dq, dk_ref, dv_ref, lanes, first):
    scores = dotg(query_t, key, 1, 0)
    slope = dotg(grad_t, value, 1, 0)
    probs = jnp.exp2(scores)
    dscore = (probs * slope).astype(BF16)
    probs = probs.astype(BF16)
    part = dotg(key[:HEAD_DIM], dscore, 1, 1)
    dq = part if dq is None else dq + part
    dv = dotg(grad[:HEAD_DIM], probs, 1, 0)
    dk = dotg(query[:HEAD_DIM], dscore, 1, 0)
    if first:
        dv_ref[:, lanes] = dv
        dk_ref[:, lanes] = dk
    else:
        dv_ref[:, lanes] += dv
        dk_ref[:, lanes] += dk
    return dq


def grad_rows(grad, slope):
    length = grad.shape[1]
    row = lax.broadcasted_iota(jnp.int32, (16, length), 0)
    high = (-slope).astype(BF16).astype(F32)
    low = -slope - high
    extra = jnp.where(row == 0, high, jnp.where(row == 1, low, 0.0)).astype(BF16)
    return join(grad, extra)


def back_pair(query, grad, key_ref, value_ref, key_lanes, tile, dk_ref, dv_ref, start_lane, fresh):
    out = []
    for start in range(0, query.shape[1], tile):
        size = min(tile, query.shape[1])
        q_tile, g_tile = query[:, start : start + size], grad[:, start : start + size]
        q_t, g_t = q_tile.T, g_tile.T
        dq = None
        for lanes in key_lanes:
            dq = back_tile(
                q_t, g_t, q_tile, g_tile, key_ref[:, lanes], value_ref[:, lanes], dq,
                dk_ref, dv_ref, lanes, fresh and start == 0,
            )
        out.append(dq)
    return jnp.concatenate(out, axis=1) if len(out) > 1 else out[0]


DQ_SCALE = HEAD_DIM ** (-0.5)
DK_SCALE = math.log(2.0)


def neg_total(lse, keep):
    return jnp.where(keep, -lse, NEG)


def local_backward(nseg, first, mask_ref, q_ref, k_ref, v_ref, g_ref, lse_ref, slope_ref, dqr_ref, *refs):
    n = BRANCHES - first
    sent, feed_ref, out_ref = refs[:n], refs[n], refs[n + 1]
    returned, (up_ref, proj_ref, down_ref) = refs[n + 2 : 2 * n + 2], refs[2 * n + 2 : 2 * n + 5]
    qa, ga, ka, va, dk, dv = refs[2 * n + 5 : 2 * n + 11]
    rest = list(refs[2 * n + 11 :])
    back_send, back_recv, back_load, red_send, red_recv, red_load = rest[-6:]
    terms, recv_core, recv_x, recv_seq, total = rest[-11:-6]
    bufs, recvs = rest[: (len(rest) - 11) // 2], rest[(len(rest) - 11) // 2 : -11]
    head = pl.program_id(0)
    last = HEADS - 1
    length = nseg * SEG

    back = Return(nseg, first, sent, returned, bufs, recvs, back_load, Sends(back_send, back_recv))
    blocks = terms.shape[1] // CHUNKS
    reduce = Reduce(
        CHUNKS, blocks, feed_ref, terms, lambda xo: xo, recv_core, recv_x, recv_seq, total,
        Sends(red_send, red_recv), red_load,
    )

    def begin():
        meet(reduce.peers())
        back.start()
        for chunk in range(CHUNKS):
            reduce.begin(chunk)

    events = [(2 * turn, functools.partial(back.turn, turn)) for turn in range(1, back.turns())]
    for chunk in range(CHUNKS):
        for stage in range(reduce.stages()):
            if stage == 0:
                when = 1 + (chunk + 1) // 2
            else:
                when = 3 + 2 * chunk + stage + (stage >= 2) + (stage == reduce.stages() - 1)
            events.append((when, functools.partial(reduce.event, stage, chunk)))
    run_schedule(head, last, [(0, begin)] + sorted(events, key=lambda event: event[0]))

    keep = local_keep(mask_ref[0], length)
    qa[...] = join(q_ref[0], query_rows(head, length, neg_total(lse_ref[0], keep)))
    ga[...] = grad_rows(g_ref[...], slope_ref[0])
    va[...] = join(v_ref[0], value_rows(length))
    ka[0] = join(k_ref[0], key_rows(head, 0, 4, length, keep))
    if nseg == 2:
        ka[1] = join(k_ref[0], key_rows(head, 1, 4, length, keep))
    for seg in range(nseg):
        lanes = slice(seg * SEG, (seg + 1) * SEG)
        tiles = [slice(seg * SEG + 256 * i, seg * SEG + 256 * (i + 1)) for i in range(4)]
        dq = back_pair(qa[:, lanes], ga[:, lanes], ka.at[0], va, tiles, 256, dk, dv, 0, True)
        out_ref[0, :, lanes] = dq * DQ_SCALE
    if nseg == 2:
        for seg in range(2):
            mine = pl.ds(kept_start(head, 1, seg), SEG // 2)
            base = kept_start(head, 1, 1 - seg)
            tiles = [pl.ds(pl.multiple_of(base + 256 * i, 256), 256) for i in range(2)]
            dq = back_pair(qa[:, mine], ga[:, mine], ka.at[1], va, tiles, 256, dk, dv, 0, False)
            out_ref[0, :, mine] += dq * DQ_SCALE
    size = SEG >> first
    for seg in range(nseg):
        mine = pl.ds(kept_start(head, first, seg), size)
        out_ref[0, :, mine] += dqr_ref[:, seg * size : (seg + 1) * size]
    out_ref[1] = dk[...] * DK_SCALE
    out_ref[2] = dv[...]

    @pl.when(head == last)
    def _():
        back.finish()
        reduce.finish()
        for tile in range(TILES):
            cols = slice(tile * 128, (tile + 1) * 128)
            for col in range(4):
                at = col * 72 + tile * 12
                up_ref[:, col * D + tile * 128 : col * D + (tile + 1) * 128] = rows_of(total, at, 12)
            proj_ref[:, cols] = rows_of(total, 288 + tile * 12, 12)
            down_ref[:, cols] = rows_of(total, 360 + tile * 48, 48)


def rows_of(total, at, count):
    return total[at : at + count].astype(F32).reshape(count * 16, 128)


def remote_backward(nseg, first, mask_ref, q_ref, g_ref, lse_ref, slope_ref, *refs):
    head = pl.program_id(0)
    levels = range(first, BRANCHES)
    n = len(levels)
    packs = {level: refs[3 * i : 3 * i + 3] for i, level in enumerate(levels)}
    dqr_ref = refs[3 * n]
    outs = {level: refs[3 * n + 1 + i] for i, level in enumerate(levels)}
    qa, ga, ka, va, dk, dv = refs[4 * n + 1 :]
    length = nseg * SEG
    qa[...] = join(q_ref[0], query_rows(head, length, neg_total(lse_ref[0], local_keep(mask_ref[0], length))))
    ga[...] = grad_rows(g_ref[...], slope_ref[0])
    full = SEG >> first
    for group in remote_plan(first):
        for i, level in enumerate(group):
            key, value = remote_keys(head, level, packs[level])
            ka[:, i * 512 : (i + 1) * 512] = key
            va[:, i * 512 : (i + 1) * 512] = value
        size = SEG >> group[0]
        mine = [pl.ds(kept_start(head, group[0], seg), size) for seg in range(nseg)]
        query = jnp.concatenate([qa[:, m] for m in mine], axis=1)
        grad = jnp.concatenate([ga[:, m] for m in mine], axis=1)
        tiles = [slice(256 * i, 256 * (i + 1)) for i in range(2 * len(group))]
        dq = back_pair(query, grad, ka, va, tiles, 256, dk, dv, 0, True) * DQ_SCALE
        for seg in range(nseg):
            piece = dq[:, seg * size : (seg + 1) * size]
            if group[0] == first:
                dqr_ref[:, seg * full : (seg + 1) * full] = piece
            else:
                inner = (reversed_bits(head) >> (4 - group[0])) & ((1 << (group[0] - first)) - 1)
                lanes = pl.ds(pl.multiple_of(seg * full + inner * size, 128), size)
                dqr_ref[:, lanes] += piece
        for i, level in enumerate(group):
            pieces, _, _, size = outs[level].shape
            for piece in range(pieces):
                lanes = slice(i * 512 + piece * size, i * 512 + (piece + 1) * size)
                outs[level][piece, 0] = (dk[:, lanes] * DK_SCALE).astype(BF16)
                outs[level][piece, 1] = dv[:, lanes].astype(BF16)


def row_block(length):
    return pl.BlockSpec((1, 1, length), lambda h: (h, 0, 0))


def head_block(length):
    return pl.BlockSpec((HEAD_DIM, length), lambda h: (h, 0))


def part_block(part, length):
    return pl.BlockSpec((1, HEAD_DIM, length), lambda h: (part, h, 0))


MASK_BLOCK = pl.BlockSpec(memory_space=pltpu.SMEM)


def pack_specs(pack):
    group, _, length = pack.shape
    return [
        pl.BlockSpec((group, HEAD_DIM, length), lambda h: (0, h, 0)),
        pl.BlockSpec((group, HEAD_DIM, length), lambda h: (0, HEADS + h, 0)),
        pl.BlockSpec((group, 16, length), lambda h: (0, 2 * D // 16, 0)),
    ]


ANY_BLOCK = pl.BlockSpec(memory_space=pl.ANY)


def sems(count):
    return pltpu.SemaphoreType.DMA((count,))


def talking(collective_id):
    return pltpu.CompilerParams(
        vmem_limit_bytes=VMEM_LIMIT, collective_id=collective_id, has_side_effects=True
    )


PARAMS = pltpu.CompilerParams(vmem_limit_bytes=VMEM_LIMIT)


def shape(dims, dtype):
    return jax.ShapeDtypeStruct(dims, dtype)


def cost(seconds):
    return pl.CostEstimate(flops=int(seconds * 1.1e15), transcendentals=0, bytes_accessed=0)


def call_local_forward(nseg, first, qkv, mask, packs):
    length = nseg * SEG
    n = len(packs)
    groups = [(SEG << (level - 1)) // length for level in range(first, BRANCHES)]
    hops = sum(group.bit_length() for group in groups)
    o_part, l_part, m_part, *gathered = pl.pallas_call(
        functools.partial(local_forward, nseg, first),
        grid=(HEADS,),
        in_specs=[MASK_BLOCK, part_block(0, length), part_block(1, length), part_block(2, length)]
        + [ANY_BLOCK] * n,
        out_specs=[head_block(length), row_block(length), row_block(length)] + [ANY_BLOCK] * n,
        out_shape=[shape((D, length), F32), shape((HEADS, 1, length), F32), shape((HEADS, 1, length), F32)]
        + [shape((group,) + pack.shape, BF16) for group, pack in zip(groups, packs)],
        scratch_shapes=[
            pltpu.VMEM((64, length), BF16),
            pltpu.VMEM((nseg, 64, length), BF16),
            pltpu.VMEM((64, length), BF16),
            sems(hops),
            sems(hops),
        ],
        compiler_params=talking(1),
        cost_estimate=cost(nseg * 37e-6),
        name="local_forward",
    )(mask, qkv, qkv, qkv, *packs)
    return o_part, l_part, m_part, gathered


def call_remote_forward(nseg, first, qkv, mask, o_part, l_part, m_part, packs):
    length = nseg * SEG
    args, specs = [], []
    for pack in packs:
        args += [pack] * 3
        specs += pack_specs(pack)
    return pl.pallas_call(
        functools.partial(remote_forward, nseg, first),
        grid=(HEADS,),
        in_specs=[MASK_BLOCK, part_block(0, length), head_block(length), row_block(length), row_block(length)]
        + specs,
        out_specs=[head_block(length), row_block(length)],
        out_shape=[shape((D, length), BF16), shape((HEADS, 1, length), F32)],
        scratch_shapes=[
            pltpu.VMEM((HEAD_DIM, length), F32),
            pltpu.VMEM((1, 1, length), F32),
            pltpu.VMEM((1, 1, length), F32),
            pltpu.VMEM((64, length), BF16),
        ],
        compiler_params=PARAMS,
        cost_estimate=cost(nseg * 24e-6),
        name="remote_forward",
    )(mask, qkv, o_part, l_part, m_part, *args)


def call_remote_backward(nseg, first, qkv, grad, lse, slope, mask, packs):
    length = nseg * SEG
    args, specs = [], []
    for pack in packs:
        args += [pack] * 3
        specs += pack_specs(pack)
    kept = nseg * (SEG >> first)
    return pl.pallas_call(
        functools.partial(remote_backward, nseg, first),
        grid=(HEADS,),
        in_specs=[MASK_BLOCK, part_block(0, length), head_block(length), row_block(length), row_block(length)]
        + specs,
        out_specs=[head_block(kept)]
        + [
            pl.BlockSpec((pack.shape[0], 2, HEAD_DIM, pack.shape[2]), lambda h: (0, 0, h, 0))
            for pack in packs
        ],
        out_shape=[shape((D, kept), F32)]
        + [shape((pack.shape[0], 2, D, pack.shape[2]), BF16) for pack in packs],
        scratch_shapes=[
            pltpu.VMEM((64, length), BF16),
            pltpu.VMEM((64, length), BF16),
            pltpu.VMEM((64, 1024), BF16),
            pltpu.VMEM((64, 1024), BF16),
            pltpu.VMEM((HEAD_DIM, 1024), F32),
            pltpu.VMEM((HEAD_DIM, 1024), F32),
        ],
        compiler_params=PARAMS,
        cost_estimate=cost(nseg * 20e-6),
        name="remote_backward",
    )(mask, qkv, grad, lse, slope, *args)


CHUNKS = 3
FEED_BLOCKS = (4 * D + D + 4 * D) * D // (4 * 16 * 128)
IN_BLOCKS = 3 * D * D // (4 * 16 * 128)


def padded(blocks):
    unit = CHUNKS * lax.axis_size("seq")
    return (blocks + unit - 1) // unit * unit


def reduce_copies():
    return CHUNKS * (3 + 2 * seq_bits())


def call_local_backward(nseg, first, qkv, grad, lse, slope, mask, dq_remote, sent, feed_grads):
    length = nseg * SEG
    n = len(sent)
    groups = [part.shape[0] for part in sent]
    hops = sum(group.bit_length() for group in groups)
    blocks = feed_grads.shape[1]
    bufs = [pltpu.VMEM((g // 2,) + part.shape[1:], BF16) for g, part in zip(groups, sent) if g > 1]
    recvs = [pltpu.VMEM((g - 1,) + part.shape[1:], BF16) for g, part in zip(groups, sent) if g > 1]
    local, *rest = pl.pallas_call(
        functools.partial(local_backward, nseg, first),
        grid=(HEADS,),
        in_specs=[MASK_BLOCK, part_block(0, length), part_block(1, length), part_block(2, length), head_block(length),
                  row_block(length), row_block(length), head_block(dq_remote.shape[1])]
        + [ANY_BLOCK] * (n + 1),
        out_specs=[pl.BlockSpec((3, HEAD_DIM, length), lambda h: (0, h, 0))]
        + [ANY_BLOCK] * n
        + [const_block((192, 4 * D)), const_block((192, D)), const_block((D, D))],
        out_shape=[shape((3, D, length), F32)]
        + [shape(part.shape[1:], BF16) for part in sent]
        + [shape((192, 4 * D), F32), shape((192, D), F32), shape((D, D), F32)],
        scratch_shapes=[
            pltpu.VMEM((64, length), BF16),
            pltpu.VMEM((64, length), BF16),
            pltpu.VMEM((nseg, 64, length), BF16),
            pltpu.VMEM((64, length), BF16),
            pltpu.VMEM((HEAD_DIM, length), F32),
            pltpu.VMEM((HEAD_DIM, length), F32),
        ]
        + bufs
        + recvs
        + [
            pltpu.VMEM((2, blocks, 16, 128), BF16),
            pltpu.VMEM((2, blocks, 16, 128), BF16),
            pltpu.VMEM((blocks, 16, 128), BF16),
            pltpu.VMEM((blocks, 16, 128), BF16),
            pltpu.VMEM((blocks, 16, 128), BF16),
            sems(hops),
            sems(hops),
            sems(n),
            sems(reduce_copies()),
            sems(reduce_copies()),
            sems(2 * CHUNKS),
        ],
        compiler_params=talking(2),
        cost_estimate=cost(nseg * 72e-6),
        name="local_backward",
    )(mask, qkv, qkv, qkv, grad, lse, slope, dq_remote, *sent, feed_grads)
    return local, rest[:n], rest[n:]


HALF = D // 2


def const_block(dims):
    return pl.BlockSpec(dims, lambda i: (0,) * len(dims), pipeline_mode=pl.Buffered(1))


def rev4(value):
    return int(reversed_bits(value))


TILES = D // 128


def put_rows(tiled, start, array):
    for tile in range(TILES):
        tiled[tile, start : start + array.shape[0], :] = array[:, tile * 128 : (tile + 1) * 128]


def get_rows(tiled, start, size):
    return jnp.concatenate([tiled[tile, start : start + size, :] for tile in range(TILES)], axis=1)


def get_residue(tiled, start):
    return jnp.concatenate(
        [tiled[tile, pl.ds(start, RUN, stride=RES), :] for tile in range(TILES)], axis=1
    )


def put_residue(tiled, start, array):
    for tile in range(TILES):
        tiled[tile, pl.ds(start, RUN, stride=RES), :] = array[:, tile * 128 : (tile + 1) * 128]


def project_kernel(nseg, first, mask_ref, tok_ref, gain_ref, shift_ref, w_ref, qkv_ref, xp_ref, inner_ref, *refs):
    *packs, xs = refs
    step = pl.program_id(0)

    @pl.when(step == 0)
    def _():
        for seg in range(nseg):
            put_rows(xs, 0, tok_ref[seg * SEG : (seg + 1) * SEG, :].astype(F32))
            for pair in range(RES // 2):
                rows = jnp.concatenate(
                    [get_residue(xs, rev4(2 * pair + i)) for i in range(2)], axis=0
                )
                normed = normalize(rows, gain_ref[...], shift_ref[...])[0].astype(BF16)
                at = slice(seg * SEG + pair * 2 * RUN, seg * SEG + (pair + 1) * 2 * RUN)
                xp_ref[at, :] = rows.astype(BF16)
                inner_ref[:, at] = normed.T
        for pack, level in zip(packs, range(first, BRANCHES)):
            pack[2 * D :, :] = packed_keep(mask_ref[0], level, nseg)

    scale = jnp.where(step < 2, QUERY_SCALE, 1.0)
    for start in range(0, nseg * SEG, 512):
        lanes = slice(start, start + 512)
        qkv_ref[0, :, lanes] = (dotg(w_ref[...], inner_ref[:, lanes], 0, 0) * scale).astype(BF16)

    @pl.when(step >= 2)
    def _():
        upper = lax.rem(step, 2) == 1
        for pack, level in zip(packs, range(first, BRANCHES)):
            size = SEG >> level
            for head in range(HEADS // 2):
                rows = slice(head * HEAD_DIM, (head + 1) * HEAD_DIM)
                pieces = []
                for seg in range(nseg):
                    start = seg * SEG + (rev4(head) >> (4 - level)) * size
                    if level < 4:
                        pieces.append(qkv_ref[0, rows, start : start + size])
                    else:
                        both = qkv_ref[0, rows, start : start + 2 * size]
                        pieces.append(jnp.where(upper, both[:, size:], both[:, :size]))
                into = pl.ds(pl.multiple_of((step - 2) * HALF + head * HEAD_DIM, 16), HEAD_DIM)
                pack[into, :] = jnp.concatenate(pieces, axis=1) if nseg > 1 else pieces[0]


def call_project(nseg, first, mask, tokens, gain, shift, weight):
    length = nseg * SEG
    kept = [nseg * (SEG >> level) for level in range(first, BRANCHES)]
    return pl.pallas_call(
        functools.partial(project_kernel, nseg, first),
        grid=(6,),
        in_specs=[
            MASK_BLOCK,
            const_block((length, D)),
            const_block((1, D)),
            const_block((1, D)),
            pl.BlockSpec((D, HALF), lambda i: (0, i)),
        ],
        out_specs=[
            pl.BlockSpec((1, HALF, length), lambda i: (i // 2, i % 2, 0)),
            const_block((length, D)),
            const_block((D, length)),
        ]
        + [const_block((2 * D + 16, size)) for size in kept],
        out_shape=[
            shape((3, D, length), BF16),
            shape((length, D), BF16),
            shape((D, length), BF16),
        ]
        + [shape((2 * D + 16, size), BF16) for size in kept],
        scratch_shapes=[pltpu.VMEM((TILES, SEG, 128), F32)],
        compiler_params=PARAMS,
        cost_estimate=cost(nseg * 10e-6),
        name="project",
    )(mask, tokens, gain, shift, weight)


ROWS = 256


def blocks_of(ref, rows, col):
    part = ref[rows, col * 128 : (col + 1) * 128].astype(BF16)
    return part.reshape(part.shape[0] // 16, 16, 128)


def feed_kernel(
    nseg, mask_ref, att_ref, x_ref, cot_ref, wout_ref, up_ref, down_ref, gain_ref, shift_ref,
    mixed_ref, gmid_ref, gm_ref, along_ref, vec_ref, grads_ref,
    cs, out_acc, up_acc, down_acc, stage, sems,
):
    step = pl.program_id(0)
    quarter = lax.rem(step, 4)
    low = (quarter >> 1) | ((quarter & 1) << 1)

    @pl.when(step == 0)
    def _():
        out_acc[...] = jnp.zeros_like(out_acc)
        up_acc[...] = jnp.zeros_like(up_acc)
        down_acc[...] = jnp.zeros_like(down_acc)
        vec_ref[...] = jnp.zeros_like(vec_ref)

    @pl.when(quarter == 0)
    def _():
        put_rows(cs, 0, cot_ref[...].astype(F32))

    grad = jnp.concatenate([get_residue(cs, rev4(i) + low) for i in range(4)], axis=0)
    grad_b = grad.astype(BF16)
    att = att_ref[...]
    middle = x_ref[...].astype(F32) + dotg(att, wout_ref[...], 0, 0)
    gain = gain_ref[...]
    normed, unit, inverse = normalize(middle, gain, shift_ref[...])
    hidden = normed.astype(BF16)
    hidden_t = hidden.T
    final = middle
    grad_hidden = jnp.zeros((ROWS, D), F32)
    for start in range(0, 4 * D, D):
        cols = slice(start, start + D)
        upper = dotg(hidden, up_ref[:, cols], 1, 0)
        grad_active = dotg(grad_b, down_ref[cols, :], 1, 1)
        half = 0.5 * (1.0 + lax.erf(upper * ROOT_HALF))
        slope = half + upper * jnp.exp(-0.5 * upper * upper) * INV_ROOT_TWO_PI
        active = (upper * half).astype(BF16)
        grad_upper = (grad_active * slope).astype(BF16)
        final = final + dotg(active, down_ref[cols, :], 1, 0)
        grad_hidden = grad_hidden + dotg(grad_upper, up_ref[:, cols], 1, 1)
        up_acc[:, cols] += dotg(hidden_t, grad_upper, 1, 0)
        down_acc[cols, :] += dotg(active, grad_b, 0, 0)
    for i in range(4):
        put_residue(cs, rev4(i) + low, final[i * RUN : (i + 1) * RUN])

    @pl.when(quarter == 3)
    def _():
        mixed_ref[...] = get_rows(cs, 0, SEG).astype(BF16)

    back, gain_back, shift_back = normalize_back(grad_hidden, unit, inverse, gain)
    vec_ref[0:1, :] += gain_back[None, :]
    vec_ref[1:2, :] += shift_back[None, :]
    grad_middle = grad + back
    gmid_ref[...] = grad_middle
    branch = grad_middle.astype(BF16)
    out_acc[...] += dotg(att, branch, 1, 0)
    lane = lax.broadcasted_iota(jnp.int32, (1, ROWS), 1)
    position = step // 4 * SEG + lax.rem(lane, RUN) * RES + residue_of(lane // RUN) + low
    keep = position < mask_ref[0]
    merged = jnp.where(keep, dotg(wout_ref[...], branch, 1, 1), 0.0).astype(BF16)
    gm_ref[...] = merged
    product = merged.astype(F32) * att.astype(F32)
    for head in range(HEADS):
        rows = slice(head * HEAD_DIM, (head + 1) * HEAD_DIM)
        along_ref[head] = jnp.sum(product[rows], axis=0, keepdims=True)

    @pl.when(step == pl.num_programs(0) - 1)
    def _():
        copies = []
        for owner in range(4):
            for piece in range(3):
                count = owner * 3 + piece
                slot = count % 2
                if count >= 2:
                    copies[count - 2].wait()
                if piece == 0:
                    rows, offset, size = slice(owner * 192, (owner + 1) * 192), 0, 288
                    for col in range(4 * TILES):
                        stage[slot, col * 12 : (col + 1) * 12] = blocks_of(up_acc, rows, col)
                elif piece == 1:
                    rows, offset, size = slice(owner * 192, (owner + 1) * 192), 288, 72
                    for col in range(TILES):
                        stage[slot, col * 12 : (col + 1) * 12] = blocks_of(out_acc, rows, col)
                else:
                    rows, offset, size = slice(owner * D, (owner + 1) * D), 360, 288
                    for col in range(TILES):
                        stage[slot, col * 48 : (col + 1) * 48] = blocks_of(down_acc, rows, col)
                copy = pltpu.make_async_copy(
                    stage.at[slot, pl.ds(0, size)],
                    grads_ref.at[owner, pl.ds(offset, size)],
                    sems.at[slot],
                )
                copy.start()
                copies.append(copy)
        copies[-2].wait()
        copies[-1].wait()


def call_feed(nseg, mask, att, x, cot, wout, up, down, gain, shift):
    length = nseg * SEG
    return pl.pallas_call(
        functools.partial(feed_kernel, nseg),
        grid=(length // ROWS,),
        in_specs=[
            MASK_BLOCK,
            pl.BlockSpec((D, ROWS), lambda i: (0, i)),
            pl.BlockSpec((ROWS, D), lambda i: (i, 0)),
            pl.BlockSpec((SEG, D), lambda i: (i // 4, 0)),
            const_block((D, D)),
            const_block((D, 4 * D)),
            const_block((4 * D, D)),
            const_block((1, D)),
            const_block((1, D)),
        ],
        out_specs=[
            pl.BlockSpec((SEG, D), lambda i: (i // 4, 0)),
            pl.BlockSpec((ROWS, D), lambda i: (i, 0)),
            pl.BlockSpec((D, ROWS), lambda i: (0, i)),
            pl.BlockSpec((HEADS, 1, ROWS), lambda i: (0, 0, i)),
            pl.BlockSpec((2, D), lambda i: (0, 0)),
            pl.BlockSpec(memory_space=pl.ANY),
        ],
        out_shape=[
            shape((length, D), BF16),
            shape((length, D), F32),
            shape((D, length), BF16),
            shape((HEADS, 1, length), F32),
            shape((2, D), F32),
            shape((4, padded(FEED_BLOCKS), 16, 128), BF16),
        ],
        scratch_shapes=[
            pltpu.VMEM((TILES, SEG, 128), F32),
            pltpu.VMEM((D, D), F32),
            pltpu.VMEM((D, 4 * D), F32),
            pltpu.VMEM((4 * D, D), F32),
            pltpu.VMEM((2, 288, 16, 128), BF16),
            pltpu.SemaphoreType.DMA((2,)),
        ],
        compiler_params=pltpu.CompilerParams(vmem_limit_bytes=62 * 1024 * 1024),
        cost_estimate=cost(nseg * 45e-6),
        name="feed",
    )(mask, att, x, cot, wout, up, down, gain, shift)


STEPS = 6


def inner_back_kernel(nseg, first, local_ref, inner_ref, w_ref, x_ref, gmid_ref, gain_ref, feed_vec_ref, *refs):
    n = BRANCHES - first
    packs, (weight_ref, back_ref, vec_ref) = refs[:n], refs[n : n + 3]
    acc, mixed, order, terms, recv_core, recv_x, recv_seq, total, vecs, vec_recv = refs[n + 3 : n + 13]
    red_send, red_recv, vec_send, vec_recv_sems = refs[n + 13 :]
    step = pl.program_id(0)
    last = pl.num_programs(0) - 1
    length = nseg * SEG
    end = STEPS + length // ROWS
    blocks = terms.shape[1] // CHUNKS
    core = lax.rem(lax.axis_index("fsdp"), 2)
    reduce = Reduce(
        CHUNKS, blocks, terms, terms, lambda xo: 2 * xo + core, recv_core, recv_x, recv_seq, total,
        Sends(red_send, red_recv),
    )
    vec_sends = Sends(vec_send, vec_recv_sems)

    def vec_copy(i):
        return vec_sends.copy(i, vecs.at[i], vec_recv.at[i], *reduce.peers()[i])

    def vec_event(i):
        vec_copy(i).wait_recv()
        vecs[i + 1] = vecs[i] + vec_recv[i]
        if i + 1 < len(reduce.peers()):
            vec_copy(i + 1).start()

    def vec_start():
        vec_copy(0).start()

    @pl.when(step == 0)
    def _():
        meet(reduce.peers())
        vecs[0] = jnp.concatenate([jnp.zeros((2, D), F32), feed_vec_ref[...], jnp.zeros((4, D), F32)], axis=0)

    @pl.when(step < 2)
    def _():
        mixed[...] = local_ref[0].astype(BF16)

    @pl.when((step >= 2) & (step < STEPS))
    def _():
        upper = lax.rem(step, 2) == 1
        for pack, level in zip(packs, range(first, BRANCHES)):
            size = SEG >> level
            for head in range(HEADS // 2):
                rows = slice(head * HEAD_DIM, (head + 1) * HEAD_DIM)
                for seg in range(nseg):
                    start = seg * SEG + (rev4(head) >> (4 - level)) * size
                    piece = pack[0, rows, seg * size : (seg + 1) * size].astype(F32)
                    if level == 4:
                        zero = jnp.zeros_like(piece)
                        piece = jnp.concatenate(
                            [jnp.where(upper, zero, piece), jnp.where(upper, piece, zero)], axis=1
                        )
                    local_ref[0, rows, start : start + piece.shape[1]] += piece
        mixed[...] = local_ref[0].astype(BF16)

    @pl.when(step < STEPS)
    def _():
        grad_in = dotg(inner_ref[...], mixed[...], 1, 1).astype(BF16)
        base = lax.div(step, 2) * blocks + lax.rem(step, 2) * 36
        for col in range(3):
            part = grad_in[:, col * 128 : (col + 1) * 128].reshape(4, 12, 16, 128)
            for owner in range(4):
                terms[owner, pl.ds(base + col * 12, 12)] = part[owner]
        for start in range(0, length, 512):
            lanes = slice(start, start + 512)
            part = dotg(w_ref[...], mixed[:, lanes], 1, 0)

            @pl.when(step == 0)
            def _():
                acc[:, lanes] = part

            @pl.when(step > 0)
            def _():
                acc[:, lanes] += part

    events = []
    for chunk in range(CHUNKS):
        begin = 2 * chunk + 1
        events.append((begin, functools.partial(reduce.begin, chunk)))
        for stage in range(reduce.stages()):
            when = begin + 1 + stage + (1 if stage else 0) + max(0, stage - 1 - chunk)
            events.append((when, functools.partial(reduce.event, stage, chunk)))
    events.append((end - 1, vec_start))
    for i in range(len(reduce.peers())):
        events.append((end + i, functools.partial(vec_event, i)))
    events.sort(key=lambda event: event[0])

    @pl.when((step >= STEPS) & (step < end))
    def _():
        turn = step - STEPS
        quarter = lax.rem(turn, 4)
        low = (quarter >> 1) | ((quarter & 1) << 1)
        gain = gain_ref[...]
        grad = acc[:, pl.ds(pl.multiple_of(turn * ROWS, ROWS), ROWS)].T
        _, unit, inverse = normalize(x_ref[...].astype(F32), gain, gain)
        back, gain_part, shift_part = normalize_back(grad, unit, inverse, gain)
        vecs[0, 0:1, :] += gain_part[None, :]
        vecs[0, 1:2, :] += shift_part[None, :]
        total_back = gmid_ref[...] + back
        for i in range(4):
            put_residue(order, rev4(i) + low, total_back[i * RUN : (i + 1) * RUN])

        @pl.when(quarter == 3)
        def _():
            back_ref[...] = get_rows(order, 0, SEG)

    run_schedule(step, last, events)

    @pl.when(step == last)
    def _():
        reduce.finish()
        for i in range(len(reduce.peers())):
            vec_copy(i).wait_send()
        vec_ref[...] = vecs[len(reduce.peers())]
        for part in range(STEPS):
            for col in range(3):
                at = part // 2 * blocks + part % 2 * 36 + col * 12
                weight_ref[:, part * HALF + col * 128 : part * HALF + (col + 1) * 128] = rows_of(total, at, 12)


def call_inner_back(nseg, first, local, inner, weight, x, gmid, gain, feed_vec, packs):
    length = nseg * SEG
    turns = length // ROWS
    blocks = padded(IN_BLOCKS)
    if blocks // CHUNKS < 72:
        raise ValueError("blocks")
    peers = 2 + seq_bits()

    def at(i):
        return jnp.minimum(i, STEPS - 1)

    def turn(i):
        return jnp.clip(i - STEPS, 0, turns - 1)

    return pl.pallas_call(
        functools.partial(inner_back_kernel, nseg, first),
        grid=(STEPS + turns + 1,),
        in_specs=[
            pl.BlockSpec((1, HALF, length), lambda i: (at(i) // 2, at(i) % 2, 0)),
            const_block((D, length)),
            pl.BlockSpec((D, HALF), lambda i: (0, at(i))),
            pl.BlockSpec((ROWS, D), lambda i: (turn(i), 0)),
            pl.BlockSpec((ROWS, D), lambda i: (turn(i), 0)),
            const_block((1, D)),
            const_block((2, D)),
        ]
        + [
            pl.BlockSpec((1, HALF, pack.shape[2]), lambda i: (jnp.maximum(at(i) // 2 - 1, 0), at(i) % 2, 0))
            for pack in packs
        ],
        out_specs=[
            const_block((192, 3 * D)),
            pl.BlockSpec((SEG, D), lambda i: (turn(i) // 4, 0)),
            const_block((8, D)),
        ],
        out_shape=[shape((192, 3 * D), F32), shape((length, D), F32), shape((8, D), F32)],
        scratch_shapes=[
            pltpu.VMEM((D, length), F32),
            pltpu.VMEM((HALF, length), BF16),
            pltpu.VMEM((TILES, SEG, 128), F32),
            pltpu.VMEM((4, blocks, 16, 128), BF16),
            pltpu.VMEM((2, blocks, 16, 128), BF16),
            pltpu.VMEM((blocks, 16, 128), BF16),
            pltpu.VMEM((blocks, 16, 128), BF16),
            pltpu.VMEM((blocks, 16, 128), BF16),
            pltpu.VMEM((peers + 1, 8, D), F32),
            pltpu.VMEM((peers, 8, D), F32),
            sems(reduce_copies()),
            sems(reduce_copies()),
            sems(peers),
            sems(peers),
        ],
        compiler_params=talking(3),
        cost_estimate=cost(nseg * 15e-6),
        name="inner_back",
    )(local, inner, weight, x, gmid, gain, feed_vec, *packs)


def per_device(
    tokens,
    first_gain,
    first_shift,
    project_in,
    project_out,
    second_gain,
    second_shift,
    up_weight,
    down_weight,
    valid_mask,
    cotangent,
):
    length = tokens.shape[1]
    nseg = length // SEG
    first = nseg.bit_length()

    def gather(weight):
        return lax.all_gather(weight, "fsdp", axis=0, tiled=True)

    weight_in = gather(project_in)
    small = gather(jnp.stack([first_gain, first_shift, second_gain, second_shift], axis=1)).astype(F32)
    gain_attend, shift_attend, gain_feed, shift_feed = (small[:, i][None, :] for i in range(4))
    weight_out = gather(project_out)
    weight_up = gather(up_weight)
    weight_down = gather(down_weight)

    mask = jnp.sum(valid_mask[0])[None]

    qkv, x, inner, *packs = call_project(nseg, first, mask, tokens[0], gain_attend, shift_attend, weight_in)
    o_part, l_part, m_part, gathered = call_local_forward(nseg, first, qkv, mask, packs)
    attended, lse = call_remote_forward(nseg, first, qkv, mask, o_part, l_part, m_part, gathered)

    mixed, grad_middle, grad_merged, along, feed_vec, feed_grads = call_feed(
        nseg, mask, attended, x, cotangent[0], weight_out, weight_up, weight_down, gain_feed, shift_feed
    )

    dq_remote, *sent = call_remote_backward(nseg, first, qkv, grad_merged, lse, along, mask, gathered)
    local, returned, (grad_up, grad_out, grad_down) = call_local_backward(
        nseg, first, qkv, grad_merged, lse, along, mask, dq_remote, sent, feed_grads
    )
    grad_in, tokens_back, vectors = call_inner_back(
        nseg, first, local, inner, weight_in, x, grad_middle, gain_attend, feed_vec, returned
    )
    quarter = D // lax.axis_size("fsdp")
    vectors = lax.dynamic_slice_in_dim(vectors, lax.axis_index("fsdp") * quarter, quarter, 1)
    return (
        mixed[None],
        tokens_back[None],
        vectors[0],
        vectors[1],
        grad_in,
        grad_out,
        vectors[2],
        vectors[3],
        grad_up,
        grad_down,
    )


def solution(mesh):
    in_specs = (
        P("fsdp", "seq", None),
        P("fsdp"),
        P("fsdp"),
        P("fsdp", None),
        P("fsdp", None),
        P("fsdp"),
        P("fsdp"),
        P("fsdp", None),
        P("fsdp", None),
        P("fsdp", "seq"),
        P("fsdp", "seq", None),
    )
    out_specs = (
        P("fsdp", "seq", None),
        P("fsdp", "seq", None),
        P("fsdp"),
        P("fsdp"),
        P("fsdp", None),
        P("fsdp", None),
        P("fsdp"),
        P("fsdp"),
        P("fsdp", None),
        P("fsdp", None),
    )
    return jax.shard_map(
        per_device, mesh=mesh, in_specs=in_specs, out_specs=out_specs, check_vma=False
    )
```

```python
import functools
import math

import jax
import jax.numpy as jnp
import ml_dtypes
import numpy as np
from jax import lax
from jax.experimental import pallas as pl
from jax.experimental.pallas import tpu as pltpu
from jax.sharding import PartitionSpec as P

HEADS = 16
HEAD_DIM = 48
SEG = 1024
BRANCHES = 5
RES = 16
RUN = SEG // RES
D = HEADS * HEAD_DIM

EPS = 1e-05
NEG = -1e30
ROOT_HALF = 0.7071067811865476
INV_ROOT_TWO_PI = 0.3989422804014327
F32 = jnp.float32
BF16 = jnp.bfloat16
QUERY_SCALE = math.log2(math.e) * HEAD_DIM ** (-0.5)
VMEM_LIMIT = 56 * 1024 * 1024


def dotg(left, right, left_dim, right_dim):
    return lax.dot_general(
        left, right, (((left_dim,), (right_dim,)), ((), ())), preferred_element_type=F32
    )


def normalize(values, gain, shift):
    mean = jnp.mean(values, axis=-1, keepdims=True)
    centred = values - mean
    spread = jnp.mean(centred * centred, axis=-1, keepdims=True)
    inverse = lax.rsqrt(spread + EPS)
    normed = centred * inverse
    return (normed * gain + shift, normed, inverse)


def normalize_back(grad, normed, inverse, gain):
    scaled = grad * gain
    first = jnp.mean(scaled, axis=-1, keepdims=True)
    second = jnp.mean(scaled * normed, axis=-1, keepdims=True)
    return (
        inverse * (scaled - first - normed * second),
        jnp.sum(grad * normed, axis=0),
        jnp.sum(grad, axis=0),
    )


def reversed_bits(head):
    return ((head & 1) << 3) | ((head & 2) << 1) | ((head & 4) >> 1) | ((head & 8) >> 3)


def near_class(head, low_bits, length):
    lane = lax.broadcasted_iota(jnp.int32, (1, length), 1)
    rho = lax.rem(lane // RUN, 1 << low_bits)
    return rho ^ (reversed_bits(head) & ((1 << low_bits) - 1))


def class_rows(near, length):
    row = lax.broadcasted_iota(jnp.int32, (16, length), 0)
    step = lax.rem(row + 3, 4) + 1
    bound = jnp.where((row >= 5) & (row <= 12), lax.shift_right_logical(RES, step), 0)
    return row, near < bound


def query_rows(head, length, neg_lse=None):
    near = near_class(head, 4, length)
    row, inside = class_rows(near, length)
    out = jnp.where(inside, 1.0, 0.0)
    out = jnp.where(row == 0, 1.0, out)
    out = jnp.where(row == 4, jnp.where(near < 1, 0.0, NEG), out)
    if neg_lse is not None:
        high = neg_lse.astype(BF16).astype(F32)
        rest = neg_lse - high
        mid = rest.astype(BF16).astype(F32)
        low = rest - mid
        out = jnp.where(row == 1, high, jnp.where(row == 2, mid, jnp.where(row == 3, low, out)))
    return out.astype(BF16)


def residue_of(rho):
    return reversed_bits(rho)


def local_keep(count, length):
    lane = lax.broadcasted_iota(jnp.int32, (1, length), 1)
    rho = lax.rem(lane // RUN, RES)
    position = lane // SEG * SEG + lax.rem(lane, RUN) * RES + residue_of(rho)
    return position < count


def packed_keep(count, level, nseg):
    size = SEG >> level
    dims = (HEADS, nseg * size)
    head = lax.broadcasted_iota(jnp.int32, dims, 0)
    lane = lax.broadcasted_iota(jnp.int32, dims, 1)
    rho = (reversed_bits(head) >> (4 - level)) * (size // RUN) + lax.rem(lane, size) // RUN
    position = lane // size * SEG + lax.rem(lane, RUN) * RES + residue_of(rho)
    return jnp.where(position < count, 1.0, 0.0).astype(BF16)


def weight_of(level, step):
    return math.log2((step - level + 1) / (step - level)) if step > level else 0.0


def key_rows(head, level, low_bits, length, keep):
    near = near_class(head, low_bits, length)
    row, inside = class_rows(near, length)
    weight = jnp.zeros((16, length), F32)
    for step in range(level + 1, BRANCHES):
        value = weight_of(level, step)
        high = float(np.asarray(value, ml_dtypes.bfloat16))
        weight = jnp.where(row == 4 + step, high, weight)
        weight = jnp.where(row == 8 + step, value - high, weight)
    out = jnp.where(inside, weight, 0.0)
    out = jnp.where((row >= 1) & (row <= 3), 1.0, out)
    out = jnp.where(row == 0, jnp.where(keep, 0.0, NEG), out)
    if level == BRANCHES - 1:
        out = jnp.where(row == 4, 1.0, out)
    return out.astype(BF16)


def value_rows(length):
    row = lax.broadcasted_iota(jnp.int32, (16, length), 0)
    return jnp.where(row < 2, 1.0, 0.0).astype(BF16)


def join(rows, extra):
    return jnp.concatenate([rows, extra], axis=0)


def kept_start(head, level, seg):
    size = SEG >> level
    block = reversed_bits(head) >> (4 - level)
    return pl.multiple_of(seg * SEG + block * size, min(size, 128))


def partner(axis, distance):
    place = lax.axis_index(axis)
    return {axis: place + distance * (1 - 2 * lax.rem(lax.div(place, distance), 2))}


def seq_bits():
    return lax.axis_size("seq").bit_length() - 1


def meet(peers):
    barrier = pltpu.get_barrier_semaphore()
    for axis, distance in peers:
        pl.semaphore_signal(
            barrier, inc=1, device_id=partner(axis, distance), device_id_type=pl.DeviceIdType.MESH
        )
    pl.semaphore_wait(barrier, len(peers))


class Sends:
    def __init__(self, send_sems, recv_sems):
        self.send_sems, self.recv_sems, self.made = send_sems, recv_sems, {}

    def copy(self, key, source, target, axis, distance):
        index = self.made.setdefault(key, len(self.made))
        return pltpu.make_async_remote_copy(
            src_ref=source,
            dst_ref=target,
            send_sem=self.send_sems.at[index],
            recv_sem=self.recv_sems.at[index],
            device_id=partner(axis, distance),
            device_id_type=pl.DeviceIdType.MESH,
        )


class Gather:
    def __init__(self, nseg, first, packs, gathered, sends):
        self.hops, self.distances = [], set()
        for level, pack, into in zip(range(first, BRANCHES), packs, gathered):
            group = (SEG << (level - 1)) // (nseg * SEG)
            hops = [((level, 0), pack, into.at[0], group)]
            step = 1
            while step < group:
                hops.append(((level, step), into.at[pl.ds(0, step)], into.at[pl.ds(step, step)], step))
                step *= 2
            self.hops.append([sends.copy(k, a, b, "seq", d) for k, a, b, d in hops])
            self.distances |= {hop[3] for hop in hops}

    def peers(self):
        return [("seq", distance) for distance in sorted(self.distances)]

    def start(self):
        for hops in self.hops:
            hops[0].start()

    def pass_on(self, turn):
        for hops in self.hops:
            if turn < len(hops):
                hops[turn - 1].wait_recv()
                hops[turn].start()

    def finish(self):
        for hops in self.hops:
            for hop in hops:
                hop.wait_send()
            hops[-1].wait_recv()

    def turns(self):
        return max(len(hops) for hops in self.hops)


class Return:
    def __init__(self, nseg, first, sent, returned, bufs, recvs, local_sems, sends):
        self.plans = []
        for i, level in enumerate(range(first, BRANCHES)):
            group = (SEG << (level - 1)) // (nseg * SEG)
            plan = []
            if group == 1:
                plan.append((None, sends.copy((level, 0), sent[i].at[0], returned[i], "seq", group)))
                self.plans.append((plan, None))
                continue
            buf, recv = bufs.pop(0), recvs.pop(0)
            step = group // 2
            load = pltpu.make_async_copy(sent[i].at[pl.ds(0, step)], buf, local_sems.at[i])
            source, at, add = sent[i].at[pl.ds(step, step)], 0, None
            while step >= 1:
                into = recv.at[pl.ds(at, step)]
                plan.append((add, sends.copy((level, step), source, into, "seq", step)))
                add = (buf, recv, at, step)
                at += step
                step //= 2
                if step:
                    source = buf.at[pl.ds(step, step)]
            plan.append((add, sends.copy((level, 0), buf.at[0], returned[i], "seq", group)))
            self.plans.append((plan, load))

    def start(self):
        for plan, load in self.plans:
            if load is not None:
                load.start()
            plan[0][1].start()

    def turn(self, number):
        for plan, load in self.plans:
            if number < len(plan):
                plan[number - 1][1].wait_recv()
                if number == 1 and load is not None:
                    load.wait()
                buf, recv, at, step = plan[number][0]
                for i in range(step):
                    buf[i] = (buf[i].astype(F32) + recv[at + i].astype(F32)).astype(BF16)
                plan[number][1].start()

    def finish(self):
        for plan, load in self.plans:
            for _, copy in plan:
                copy.wait_send()
            plan[-1][1].wait_recv()

    def turns(self):
        return max(len(plan) for plan, _ in self.plans)


def add_blocks(into, at, other, start, count):
    unit = max(u for u in range(1, 13) if count % u == 0)

    def body(i, carry):
        rows = pl.ds(at + i * unit, unit)
        part = other[pl.ds(start + i * unit, unit)].astype(F32)
        into[rows] = (into[rows].astype(F32) + part).astype(BF16)
        return carry

    lax.fori_loop(0, count // unit, body, 0)


def copy_blocks(into, other, at, count):
    unit = max(u for u in range(1, 13) if count % u == 0)

    def body(i, carry):
        rows = pl.ds(at + i * unit, unit)
        into[rows] = other[rows]
        return carry

    lax.fori_loop(0, count // unit, body, 0)


class Reduce:
    def __init__(self, chunks, blocks, source, terms, own, recv_core, recv_x, recv_seq, total, sends, loads=None):
        self.chunks, self.blocks, self.source, self.terms, self.own = chunks, blocks, source, terms, own
        self.recv_core, self.recv_x, self.recv_seq, self.total = recv_core, recv_x, recv_seq, total
        self.sends, self.loads = sends, loads
        fsdp = lax.axis_index("fsdp")
        self.core, self.x = lax.rem(fsdp, 2), lax.div(fsdp, 2)
        self.bits = seq_bits()
        seq = lax.axis_index("seq")
        self.low = [0]
        self.given = []
        for j in range(self.bits):
            bit = lax.rem(lax.div(seq, 2**j), 2)
            half = blocks >> (j + 1)
            self.given.append(self.low[j] + (1 - bit) * half)
            self.low.append(self.low[j] + bit * half)

    def peers(self):
        return [("fsdp", 1), ("fsdp", 2)] + [("seq", 2**j) for j in range(self.bits)]

    def stages(self):
        return 2 + 2 * self.bits

    def core_copy(self, chunk, xo):
        rows = pl.ds(chunk * self.blocks, self.blocks)
        owner = 2 * xo + 1 - self.core
        return self.sends.copy(
            ("core", chunk, xo), self.source.at[owner, rows], self.recv_core.at[xo, rows], "fsdp", 1
        )

    def load_copy(self, chunk, xo):
        rows = pl.ds(chunk * self.blocks, self.blocks)
        return pltpu.make_async_copy(
            self.source.at[2 * xo + self.core, rows], self.terms.at[xo, rows], self.loads.at[2 * chunk + xo]
        )

    def x_copy(self, chunk):
        rows = pl.ds(chunk * self.blocks, self.blocks)
        return self.sends.copy(
            ("x", chunk), self.terms.at[self.own(1 - self.x), rows], self.recv_x.at[rows], "fsdp", 2
        )

    def down_copy(self, chunk, j):
        half = self.blocks >> (j + 1)
        base = chunk * self.blocks
        rows = pl.ds(base + self.given[j], half)
        into = pl.ds(base + self.blocks - (self.blocks >> j), half)
        return self.sends.copy(
            ("down", chunk, j), self.terms.at[self.own(self.x), rows], self.recv_seq.at[into], "seq", 2**j
        )

    def up_copy(self, chunk, j):
        rows = pl.ds(chunk * self.blocks + self.low[j + 1], self.blocks >> (j + 1))
        return self.sends.copy(("up", chunk, j), self.total.at[rows], self.total.at[rows], "seq", 2**j)

    def begin(self, chunk):
        for xo in range(2):
            if self.loads is not None:
                self.load_copy(chunk, xo).start()
            self.core_copy(chunk, xo).start()

    def event(self, stage, chunk):
        base = chunk * self.blocks
        if stage == 0:
            for xo in range(2):
                self.core_copy(chunk, xo).wait_recv()
                if self.loads is not None:
                    self.load_copy(chunk, xo).wait()
                add_blocks(self.terms.at[self.own(xo)], base, self.recv_core.at[xo], base, self.blocks)
            self.x_copy(chunk).start()
        elif stage < 2 + self.bits:
            j = stage - 2
            mine = self.terms.at[self.own(self.x)]
            if stage == 1:
                self.x_copy(chunk).wait_recv()
                add_blocks(mine, base, self.recv_x, base, self.blocks)
            else:
                self.down_copy(chunk, j).wait_recv()
                half = self.blocks >> (j + 1)
                add_blocks(
                    mine, base + self.low[j + 1], self.recv_seq, base + self.blocks - (self.blocks >> j), half
                )
            if j + 1 < self.bits:
                self.down_copy(chunk, j + 1).start()
            else:
                copy_blocks(self.total, mine, base + self.low[self.bits], self.blocks >> self.bits)
                self.up_copy(chunk, self.bits - 1).start()
        else:
            j = 2 * self.bits + 1 - stage
            self.up_copy(chunk, j).wait_recv()
            if j:
                self.up_copy(chunk, j - 1).start()

    def finish(self):
        for chunk in range(self.chunks):
            for xo in range(2):
                self.core_copy(chunk, xo).wait_send()
            self.x_copy(chunk).wait_send()
            for j in range(self.bits):
                self.down_copy(chunk, j).wait_send()
                self.up_copy(chunk, j).wait_send()

    def copies(self):
        return self.chunks * (3 + 2 * self.bits)


def run_schedule(step, last, events):
    due = {}
    for when, call in events:
        due.setdefault(min(when, last), []).append(call)
    for when in sorted(due):

        @pl.when(step == when)
        def _():
            for call in due[when]:
                call()


FRONT = 3
KEY_TILE = 128


class State:
    def __init__(self, query, acc=None, top=None):
        self.query, self.acc, self.top = query, acc, top


def attend(items):
    items = list(items)
    ready = []
    for turn in range(len(items) + FRONT):
        if turn < len(items):
            state, key, _ = items[turn]
            ready.append(dotg(key, state.query, 1, 0))
        if turn >= FRONT:
            state, _, value = items[turn - FRONT]
            scores, ready[turn - FRONT] = ready[turn - FRONT], None
            top = jnp.max(scores, axis=0, keepdims=True)
            if state.top is not None:
                top = jnp.maximum(top, state.top)
            probs = jnp.exp2(scores - top).astype(BF16)
            part = dotg(value, probs, 1, 0)
            state.acc = part if state.top is None else state.acc * jnp.exp2(state.top - top) + part
            state.top = top


def key_items(state, key_t, value):
    size = key_t.shape[0]
    tile = min(KEY_TILE, size)
    for start in range(0, size, tile):
        yield state, key_t[start : start + tile], value[:, start : start + tile]


def load_state(query, mine, o_ref, l_ref, m_ref):
    acc = [jnp.concatenate([o_ref[:, at], jnp.broadcast_to(l_ref[0, :, at], (16, at.size))]) for at in mine]
    top = [m_ref[0, :, at] for at in mine]
    return State(query, jnp.concatenate(acc, axis=1), jnp.concatenate(top, axis=1))


def store_state(state, mine, o_ref, l_ref, m_ref):
    start = 0
    for at in mine:
        lanes = slice(start, start + at.size)
        o_ref[:, at] = state.acc[:HEAD_DIM, lanes]
        l_ref[0, :, at] = state.acc[HEAD_DIM : HEAD_DIM + 1, lanes]
        m_ref[0, :, at] = state.top[:, lanes]
        start += at.size


def local_forward(nseg, first, mask_ref, q_ref, k_ref, v_ref, *refs):
    n = BRANCHES - first
    packs, (o_ref, l_ref, m_ref), gathered = refs[:n], refs[n : n + 3], refs[n + 3 : 2 * n + 3]
    qa, ka, va, send_sems, recv_sems = refs[2 * n + 3 :]
    head = pl.program_id(0)
    length = nseg * SEG
    gather = Gather(nseg, first, packs, gathered, Sends(send_sems, recv_sems))

    def begin():
        meet(gather.peers())
        gather.start()

    events = [(0, begin)]
    for turn in range(1, gather.turns()):
        events.append((2 + 4 * turn, functools.partial(gather.pass_on, turn)))
    run_schedule(head, HEADS - 1, events)
    local_forward_core(nseg, mask_ref, q_ref, k_ref, v_ref, o_ref, l_ref, m_ref, qa, ka, va)
    run_schedule(head, HEADS - 1, [(HEADS - 1, gather.finish)])


def local_forward_scratch(nseg):
    length = nseg * SEG
    return [
        pltpu.VMEM((64, length), BF16),
        pltpu.VMEM((nseg, 64, length), BF16),
        pltpu.VMEM((64, length), BF16),
    ]


def local_forward_core(nseg, mask_ref, q_ref, k_ref, v_ref, o_ref, l_ref, m_ref, qa, ka, va):
    head = pl.program_id(0)
    length = nseg * SEG
    keep = local_keep(mask_ref[0], length)
    qa[...] = join(q_ref[0], query_rows(head, length))
    va[...] = join(v_ref[0], value_rows(length))
    ka[0] = join(k_ref[0], key_rows(head, 0, 4, length, keep))
    if nseg == 2:
        ka[1] = join(k_ref[0], key_rows(head, 1, 4, length, keep))
    states, items = [], []
    for seg in range(nseg):
        lanes = slice(seg * SEG, (seg + 1) * SEG)
        states.append(State(qa[:, lanes]))
        items += key_items(states[-1], ka[0, :, lanes].T, va[:, lanes])
    attend(items)
    for seg in range(nseg):
        store_state(states[seg], [pl.ds(seg * SEG, SEG)], o_ref, l_ref, m_ref)
    if nseg == 2:
        kept = [pl.ds(kept_start(head, 1, seg), SEG // 2) for seg in range(2)]
        states = [load_state(qa[:, at], [at], o_ref, l_ref, m_ref) for at in kept]
        items = []
        for seg in range(2):
            items += key_items(states[seg], ka[1, :, kept[1 - seg]].T, va[:, kept[1 - seg]])
        attend(items)
        for seg in range(2):
            store_state(states[seg], [kept[seg]], o_ref, l_ref, m_ref)


def remote_keys(head, level, pack):
    k_ref, v_ref, mask_ref = pack
    pieces = range(k_ref.shape[0])
    key, value, mask = (
        jnp.concatenate([ref[i] for i in pieces], axis=1) for ref in (k_ref, v_ref, mask_ref)
    )
    length = key.shape[1]
    row = lax.broadcasted_iota(jnp.int32, (16, length), 0)
    keep = jnp.sum(jnp.where(row == head, mask.astype(F32), 0.0), axis=0, keepdims=True) > 0.5
    return join(key, key_rows(head, level, 4 - level, length, keep)), join(value, value_rows(length))


def remote_plan(first):
    return [(level,) for level in range(first, 3)] + [(3, 4)]


def remote_forward(nseg, first, mask_ref, q_ref, o_in, l_in, m_in, *refs):
    head = pl.program_id(0)
    levels = range(first, BRANCHES)
    packs = {level: refs[3 * i : 3 * i + 3] for i, level in enumerate(levels)}
    att_ref, lse_ref, o_ref, l_ref, m_ref, qa = refs[3 * len(levels) :]
    length = nseg * SEG
    qa[...] = join(q_ref[0], query_rows(head, length))
    o_ref[...] = o_in[...]
    l_ref[...] = l_in[...]
    m_ref[...] = m_in[...]
    for group in remote_plan(first):
        pairs = [remote_keys(head, level, packs[level]) for level in group]
        key = jnp.concatenate([pair[0] for pair in pairs], axis=1)
        value = jnp.concatenate([pair[1] for pair in pairs], axis=1)
        mine = [pl.ds(kept_start(head, group[0], seg), SEG >> group[0]) for seg in range(nseg)]
        query = jnp.concatenate([qa[:, at] for at in mine], axis=1)
        state = load_state(query, mine, o_ref, l_ref, m_ref)
        attend(key_items(state, key.T, value))
        store_state(state, mine, o_ref, l_ref, m_ref)
    weight = jnp.where(local_keep(mask_ref[0], length), 1.0, 0.0) / l_ref[0]
    att_ref[...] = (o_ref[...] * weight).astype(BF16)
    lse_ref[0] = m_ref[0] + jnp.log2(l_ref[0])


def grad_rows(grad, slope):
    length = grad.shape[1]
    row = lax.broadcasted_iota(jnp.int32, (16, length), 0)
    high = (-slope).astype(BF16).astype(F32)
    low = -slope - high
    extra = jnp.where(row == 0, high, jnp.where(row == 1, low, 0.0)).astype(BF16)
    return join(grad, extra)


AHEAD = 2
QUERY_TILE = 256
BACK_KEYS = 256


class Side:
    def __init__(self, query, grad):
        self.query, self.grad = query[:HEAD_DIM], grad[:HEAD_DIM]
        self.query_t, self.grad_t = query.T, grad.T
        self.dq = None


def attend_back(items, dk_ref, dv_ref, written):
    items = list(items)
    ready = []
    for turn in range(len(items) + AHEAD):
        if turn < len(items):
            side, key, value, _, _ = items[turn]
            ready.append((dotg(side.query_t, key, 1, 0), dotg(side.grad_t, value, 1, 0)))
        if turn >= AHEAD:
            side, key, _, lanes, name = items[turn - AHEAD]
            scores, slope = ready[turn - AHEAD]
            ready[turn - AHEAD] = None
            probs = jnp.exp2(scores)
            dscore = (probs * slope).astype(BF16)
            dv = dotg(side.grad, probs.astype(BF16), 1, 0)
            dk = dotg(side.query, dscore, 1, 0)
            part = dotg(key[:HEAD_DIM], dscore, 1, 1)
            side.dq = part if side.dq is None else side.dq + part
            if name in written:
                dv_ref[:, lanes] += dv
                dk_ref[:, lanes] += dk
            else:
                written.add(name)
                dv_ref[:, lanes] = dv
                dk_ref[:, lanes] = dk


def sides_of(query, grad):
    tile = min(QUERY_TILE, query.shape[1])
    return [
        Side(query[:, start : start + tile], grad[:, start : start + tile])
        for start in range(0, query.shape[1], tile)
    ]


def pairs(sides, key_ref, value_ref, tiles):
    return [
        (side, key_ref[:, lanes], value_ref[:, lanes], lanes, name) for side in sides for name, lanes in tiles
    ]


def joined(sides):
    return jnp.concatenate([side.dq for side in sides], axis=1) if len(sides) > 1 else sides[0].dq


DQ_SCALE = HEAD_DIM ** (-0.5)
DK_SCALE = math.log(2.0)


def neg_total(lse, keep):
    return jnp.where(keep, -lse, NEG)


def local_backward(nseg, first, mask_ref, q_ref, k_ref, v_ref, g_ref, lse_ref, slope_ref, dqr_ref, *refs):
    n = BRANCHES - first
    sent, feed_ref, out_ref = refs[:n], refs[n], refs[n + 1]
    returned, (up_ref, proj_ref, down_ref) = refs[n + 2 : 2 * n + 2], refs[2 * n + 2 : 2 * n + 5]
    qa, ga, ka, va, dk, dv = refs[2 * n + 5 : 2 * n + 11]
    rest = list(refs[2 * n + 11 :])
    back_send, back_recv, back_load, red_send, red_recv, red_load = rest[-6:]
    terms, recv_core, recv_x, recv_seq, total = rest[-11:-6]
    bufs, recvs = rest[: (len(rest) - 11) // 2], rest[(len(rest) - 11) // 2 : -11]
    head = pl.program_id(0)
    last = HEADS - 1
    length = nseg * SEG

    back = Return(nseg, first, sent, returned, bufs, recvs, back_load, Sends(back_send, back_recv))
    blocks = terms.shape[1] // CHUNKS
    reduce = Reduce(
        CHUNKS, blocks, feed_ref, terms, lambda xo: xo, recv_core, recv_x, recv_seq, total,
        Sends(red_send, red_recv), red_load,
    )

    def begin():
        meet(reduce.peers())
        back.start()
        for chunk in range(CHUNKS):
            reduce.begin(chunk)

    events = [(2 * turn, functools.partial(back.turn, turn)) for turn in range(1, back.turns())]
    for chunk in range(CHUNKS):
        for stage in range(reduce.stages()):
            if stage == 0:
                when = 1 + (chunk + 1) // 2
            else:
                when = 3 + 2 * chunk + stage + (stage >= 2) + (stage == reduce.stages() - 1)
            events.append((when, functools.partial(reduce.event, stage, chunk)))
    run_schedule(head, last, [(0, begin)] + sorted(events, key=lambda event: event[0]))
    local_backward_core(
        nseg, first, mask_ref, q_ref, k_ref, v_ref, g_ref, lse_ref, slope_ref, dqr_ref, out_ref,
        qa, ga, ka, va, dk, dv,
    )

    @pl.when(head == last)
    def _():
        back.finish()
        reduce.finish()
        for tile in range(TILES):
            cols = slice(tile * 128, (tile + 1) * 128)
            for col in range(4):
                at = col * 72 + tile * 12
                up_ref[:, col * D + tile * 128 : col * D + (tile + 1) * 128] = rows_of(total, at, 12)
            proj_ref[:, cols] = rows_of(total, 288 + tile * 12, 12)
            down_ref[:, cols] = rows_of(total, 360 + tile * 48, 48)


def local_backward_scratch(nseg):
    length = nseg * SEG
    return [
        pltpu.VMEM((64, length), BF16),
        pltpu.VMEM((64, length), BF16),
        pltpu.VMEM((nseg, 64, length), BF16),
        pltpu.VMEM((64, length), BF16),
        pltpu.VMEM((HEAD_DIM, length), F32),
        pltpu.VMEM((HEAD_DIM, length), F32),
    ]


def local_backward_core(
    nseg, first, mask_ref, q_ref, k_ref, v_ref, g_ref, lse_ref, slope_ref, dqr_ref, out_ref,
    qa, ga, ka, va, dk, dv,
):
    head = pl.program_id(0)
    length = nseg * SEG
    keep = local_keep(mask_ref[0], length)
    qa[...] = join(q_ref[0], query_rows(head, length, neg_total(lse_ref[0], keep)))
    ga[...] = grad_rows(g_ref[...], slope_ref[0])
    va[...] = join(v_ref[0], value_rows(length))
    ka[0] = join(k_ref[0], key_rows(head, 0, 4, length, keep))
    if nseg == 2:
        ka[1] = join(k_ref[0], key_rows(head, 1, 4, length, keep))
    items, sides, written = [], [], set()
    for seg in range(nseg):
        lanes = slice(seg * SEG, (seg + 1) * SEG)
        tiles = [
            ((seg, i), slice(seg * SEG + BACK_KEYS * i, seg * SEG + BACK_KEYS * (i + 1)))
            for i in range(SEG // BACK_KEYS)
        ]
        sides.append(sides_of(qa[:, lanes], ga[:, lanes]))
        items += pairs(sides[-1], ka.at[0], va, tiles)
    attend_back(items, dk, dv, written)
    for seg in range(nseg):
        out_ref[0, :, seg * SEG : (seg + 1) * SEG] = joined(sides[seg]) * DQ_SCALE
    if nseg == 2:
        items, sides = [], []
        kept = [pl.ds(kept_start(head, 1, seg), SEG // 2) for seg in range(2)]
        for seg in range(2):
            base = kept_start(head, 1, 1 - seg)
            tile = min(BACK_KEYS, SEG // 2)
            tiles = [
                ((seg, i), pl.ds(pl.multiple_of(base + tile * i, tile), tile)) for i in range(SEG // 2 // tile)
            ]
            sides.append(sides_of(qa[:, kept[seg]], ga[:, kept[seg]]))
            items += pairs(sides[-1], ka.at[1], va, tiles)
        attend_back(items, dk, dv, set(item[4] for item in items))
        for seg in range(2):
            out_ref[0, :, kept[seg]] += joined(sides[seg]) * DQ_SCALE
    size = SEG >> first
    for seg in range(nseg):
        mine = pl.ds(kept_start(head, first, seg), size)
        out_ref[0, :, mine] += dqr_ref[:, seg * size : (seg + 1) * size]
    out_ref[1] = dk[...] * DK_SCALE
    out_ref[2] = dv[...]


def rows_of(total, at, count):
    return total[at : at + count].astype(F32).reshape(count * 16, 128)


def remote_backward(nseg, first, mask_ref, q_ref, g_ref, lse_ref, slope_ref, *refs):
    head = pl.program_id(0)
    levels = range(first, BRANCHES)
    n = len(levels)
    packs = {level: refs[3 * i : 3 * i + 3] for i, level in enumerate(levels)}
    dqr_ref = refs[3 * n]
    outs = {level: refs[3 * n + 1 + i] for i, level in enumerate(levels)}
    qa, ga, ka, va, dk, dv = refs[4 * n + 1 :]
    length = nseg * SEG
    qa[...] = join(q_ref[0], query_rows(head, length, neg_total(lse_ref[0], local_keep(mask_ref[0], length))))
    ga[...] = grad_rows(g_ref[...], slope_ref[0])
    full = SEG >> first
    for group in remote_plan(first):
        for i, level in enumerate(group):
            key, value = remote_keys(head, level, packs[level])
            ka[:, i * 512 : (i + 1) * 512] = key
            va[:, i * 512 : (i + 1) * 512] = value
        size = SEG >> group[0]
        mine = [pl.ds(kept_start(head, group[0], seg), size) for seg in range(nseg)]
        query = jnp.concatenate([qa[:, m] for m in mine], axis=1)
        grad = jnp.concatenate([ga[:, m] for m in mine], axis=1)
        tile = min(BACK_KEYS, 512)
        tiles = [(i, slice(tile * i, tile * (i + 1))) for i in range(512 // tile * len(group))]
        sides = sides_of(query, grad)
        attend_back(pairs(sides, ka, va, tiles), dk, dv, set())
        dq = joined(sides) * DQ_SCALE
        for seg in range(nseg):
            piece = dq[:, seg * size : (seg + 1) * size]
            if group[0] == first:
                dqr_ref[:, seg * full : (seg + 1) * full] = piece
            else:
                inner = (reversed_bits(head) >> (4 - group[0])) & ((1 << (group[0] - first)) - 1)
                lanes = pl.ds(pl.multiple_of(seg * full + inner * size, 128), size)
                dqr_ref[:, lanes] += piece
        for i, level in enumerate(group):
            pieces, _, _, size = outs[level].shape
            for piece in range(pieces):
                lanes = slice(i * 512 + piece * size, i * 512 + (piece + 1) * size)
                outs[level][piece, 0] = (dk[:, lanes] * DK_SCALE).astype(BF16)
                outs[level][piece, 1] = dv[:, lanes].astype(BF16)


def row_block(length):
    return pl.BlockSpec((1, 1, length), lambda h: (h, 0, 0))


def head_block(length):
    return pl.BlockSpec((HEAD_DIM, length), lambda h: (h, 0))


def part_block(part, length):
    return pl.BlockSpec((1, HEAD_DIM, length), lambda h: (part, h, 0))


MASK_BLOCK = pl.BlockSpec(memory_space=pltpu.SMEM)


def pack_specs(pack):
    group, _, length = pack.shape
    return [
        pl.BlockSpec((group, HEAD_DIM, length), lambda h: (0, h, 0)),
        pl.BlockSpec((group, HEAD_DIM, length), lambda h: (0, HEADS + h, 0)),
        pl.BlockSpec((group, 16, length), lambda h: (0, 2 * D // 16, 0)),
    ]


ANY_BLOCK = pl.BlockSpec(memory_space=pl.ANY)


def sems(count):
    return pltpu.SemaphoreType.DMA((count,))


def talking(collective_id):
    return pltpu.CompilerParams(
        vmem_limit_bytes=VMEM_LIMIT, collective_id=collective_id, has_side_effects=True
    )


PARAMS = pltpu.CompilerParams(vmem_limit_bytes=VMEM_LIMIT)


def shape(dims, dtype):
    return jax.ShapeDtypeStruct(dims, dtype)


def cost(seconds):
    return pl.CostEstimate(flops=int(seconds * 1.1e15), transcendentals=0, bytes_accessed=0)


def call_local_forward(nseg, first, qkv, mask, packs):
    length = nseg * SEG
    n = len(packs)
    groups = [(SEG << (level - 1)) // length for level in range(first, BRANCHES)]
    hops = sum(group.bit_length() for group in groups)
    o_part, l_part, m_part, *gathered = pl.pallas_call(
        functools.partial(local_forward, nseg, first),
        grid=(HEADS,),
        in_specs=[MASK_BLOCK, part_block(0, length), part_block(1, length), part_block(2, length)]
        + [ANY_BLOCK] * n,
        out_specs=[head_block(length), row_block(length), row_block(length)] + [ANY_BLOCK] * n,
        out_shape=[shape((D, length), F32), shape((HEADS, 1, length), F32), shape((HEADS, 1, length), F32)]
        + [shape((group,) + pack.shape, BF16) for group, pack in zip(groups, packs)],
        scratch_shapes=local_forward_scratch(nseg)
        + [
            sems(hops),
            sems(hops),
        ],
        compiler_params=talking(1),
        cost_estimate=cost(nseg * 37e-6),
        name="local_forward",
    )(mask, qkv, qkv, qkv, *packs)
    return o_part, l_part, m_part, gathered


def call_remote_forward(nseg, first, qkv, mask, o_part, l_part, m_part, packs):
    length = nseg * SEG
    args, specs = [], []
    for pack in packs:
        args += [pack] * 3
        specs += pack_specs(pack)
    return pl.pallas_call(
        functools.partial(remote_forward, nseg, first),
        grid=(HEADS,),
        in_specs=[MASK_BLOCK, part_block(0, length), head_block(length), row_block(length), row_block(length)]
        + specs,
        out_specs=[head_block(length), row_block(length)],
        out_shape=[shape((D, length), BF16), shape((HEADS, 1, length), F32)],
        scratch_shapes=[
            pltpu.VMEM((HEAD_DIM, length), F32),
            pltpu.VMEM((1, 1, length), F32),
            pltpu.VMEM((1, 1, length), F32),
            pltpu.VMEM((64, length), BF16),
        ],
        compiler_params=PARAMS,
        cost_estimate=cost(nseg * 24e-6),
        name="remote_forward",
    )(mask, qkv, o_part, l_part, m_part, *args)


def call_remote_backward(nseg, first, qkv, grad, lse, slope, mask, packs):
    length = nseg * SEG
    args, specs = [], []
    for pack in packs:
        args += [pack] * 3
        specs += pack_specs(pack)
    kept = nseg * (SEG >> first)
    return pl.pallas_call(
        functools.partial(remote_backward, nseg, first),
        grid=(HEADS,),
        in_specs=[MASK_BLOCK, part_block(0, length), head_block(length), row_block(length), row_block(length)]
        + specs,
        out_specs=[head_block(kept)]
        + [
            pl.BlockSpec((pack.shape[0], 2, HEAD_DIM, pack.shape[2]), lambda h: (0, 0, h, 0))
            for pack in packs
        ],
        out_shape=[shape((D, kept), F32)]
        + [shape((pack.shape[0], 2, D, pack.shape[2]), BF16) for pack in packs],
        scratch_shapes=[
            pltpu.VMEM((64, length), BF16),
            pltpu.VMEM((64, length), BF16),
            pltpu.VMEM((64, 1024), BF16),
            pltpu.VMEM((64, 1024), BF16),
            pltpu.VMEM((HEAD_DIM, 1024), F32),
            pltpu.VMEM((HEAD_DIM, 1024), F32),
        ],
        compiler_params=PARAMS,
        cost_estimate=cost(nseg * 20e-6),
        name="remote_backward",
    )(mask, qkv, grad, lse, slope, *args)


CHUNKS = 3
FEED_BLOCKS = (4 * D + D + 4 * D) * D // (4 * 16 * 128)
IN_BLOCKS = 3 * D * D // (4 * 16 * 128)


def padded(blocks):
    unit = CHUNKS * lax.axis_size("seq")
    return (blocks + unit - 1) // unit * unit


def reduce_copies():
    return CHUNKS * (3 + 2 * seq_bits())


def call_local_backward(nseg, first, qkv, grad, lse, slope, mask, dq_remote, sent, feed_grads):
    length = nseg * SEG
    n = len(sent)
    groups = [part.shape[0] for part in sent]
    hops = sum(group.bit_length() for group in groups)
    blocks = feed_grads.shape[1]
    bufs = [pltpu.VMEM((g // 2,) + part.shape[1:], BF16) for g, part in zip(groups, sent) if g > 1]
    recvs = [pltpu.VMEM((g - 1,) + part.shape[1:], BF16) for g, part in zip(groups, sent) if g > 1]
    local, *rest = pl.pallas_call(
        functools.partial(local_backward, nseg, first),
        grid=(HEADS,),
        in_specs=[MASK_BLOCK, part_block(0, length), part_block(1, length), part_block(2, length), head_block(length),
                  row_block(length), row_block(length), head_block(dq_remote.shape[1])]
        + [ANY_BLOCK] * (n + 1),
        out_specs=[pl.BlockSpec((3, HEAD_DIM, length), lambda h: (0, h, 0))]
        + [ANY_BLOCK] * n
        + [const_block((192, 4 * D)), const_block((192, D)), const_block((D, D))],
        out_shape=[shape((3, D, length), F32)]
        + [shape(part.shape[1:], BF16) for part in sent]
        + [shape((192, 4 * D), F32), shape((192, D), F32), shape((D, D), F32)],
        scratch_shapes=local_backward_scratch(nseg)
        + bufs
        + recvs
        + [
            pltpu.VMEM((2, blocks, 16, 128), BF16),
            pltpu.VMEM((2, blocks, 16, 128), BF16),
            pltpu.VMEM((blocks, 16, 128), BF16),
            pltpu.VMEM((blocks, 16, 128), BF16),
            pltpu.VMEM((blocks, 16, 128), BF16),
            sems(hops),
            sems(hops),
            sems(n),
            sems(reduce_copies()),
            sems(reduce_copies()),
            sems(2 * CHUNKS),
        ],
        compiler_params=talking(2),
        cost_estimate=cost(nseg * 72e-6),
        name="local_backward",
    )(mask, qkv, qkv, qkv, grad, lse, slope, dq_remote, *sent, feed_grads)
    return local, rest[:n], rest[n:]


HALF = D // 2


def const_block(dims):
    return pl.BlockSpec(dims, lambda i: (0,) * len(dims), pipeline_mode=pl.Buffered(1))


def rev4(value):
    return int(reversed_bits(value))


TILES = D // 128


def put_rows(tiled, start, array):
    for tile in range(TILES):
        tiled[tile, start : start + array.shape[0], :] = array[:, tile * 128 : (tile + 1) * 128]


def get_rows(tiled, start, size):
    return jnp.concatenate([tiled[tile, start : start + size, :] for tile in range(TILES)], axis=1)


def get_residue(tiled, start):
    return jnp.concatenate(
        [tiled[tile, pl.ds(start, RUN, stride=RES), :] for tile in range(TILES)], axis=1
    )


def put_residue(tiled, start, array):
    for tile in range(TILES):
        tiled[tile, pl.ds(start, RUN, stride=RES), :] = array[:, tile * 128 : (tile + 1) * 128]


COLUMN_CHUNKS = 3


def project_kernel(nseg, first, mask_ref, tok_ref, *refs):
    n = BRANCHES - first
    vectors, w_ref = refs[:4], refs[4]
    qkv_ref, xp_ref, inner_ref, weight_ref, gains_ref = refs[5:10]
    packs = refs[10 : 10 + n]
    xs, weight, gains, vec_send, vec_recv, w_send, w_recv, w_load, w_store = refs[10 + n :]
    step = pl.program_id(0)
    last = pl.num_programs(0) - 1
    me = lax.axis_index("fsdp")
    sibling = me + 1 - 2 * lax.rem(me, 2)
    across = lax.rem(me + 2, 4)
    sends = Sends(w_send, w_recv)

    def send(source, target, key, other):
        index = sends.made.setdefault(key, len(sends.made))
        return pltpu.make_async_remote_copy(
            src_ref=source, dst_ref=target, send_sem=w_send.at[index], recv_sem=w_recv.at[index],
            device_id={"fsdp": other}, device_id_type=pl.DeviceIdType.MESH,
        )

    def chunk_copies(chunk):
        cols = pl.ds(chunk * D, D)
        mine = w_ref.at[:, cols]
        load = pltpu.make_async_copy(mine, weight.at[me, :, cols], w_load.at[chunk])
        core = send(mine, weight.at[me, :, cols], ("core", chunk), sibling)
        x = send(mine, weight.at[me, :, cols], ("x", chunk), across)
        handed = weight.at[across, :, cols]
        return load, core, x, send(handed, handed, ("hand", chunk), sibling)

    def vec_copies():
        return [
            pltpu.make_async_remote_copy(
                src_ref=gains.at[me], dst_ref=gains.at[me], send_sem=vec_send.at[i], recv_sem=vec_recv.at[i],
                device_id={"fsdp": other}, device_id_type=pl.DeviceIdType.MESH,
            )
            for i, other in enumerate((sibling, across, 3 - me))
        ]

    store = pltpu.make_async_copy(weight, weight_ref, w_store.at[0])

    @pl.when(step == 0)
    def _():
        barrier = pltpu.get_barrier_semaphore()
        for other in (sibling, across, 3 - me):
            pl.semaphore_signal(
                barrier, inc=1, device_id={"fsdp": other}, device_id_type=pl.DeviceIdType.MESH
            )
        for i, vector in enumerate(vectors):
            gains[me, i : i + 1, :192] = vector[...].astype(F32)
        pl.semaphore_wait(barrier, 3)
        for copy in vec_copies():
            copy.start()
        for chunk in range(COLUMN_CHUNKS):
            for copy in chunk_copies(chunk)[:3]:
                copy.start()
        for copy in vec_copies():
            copy.wait_recv()
        full = [
            jnp.concatenate([gains[owner, i : i + 1, :192] for owner in range(4)], axis=1) for i in range(4)
        ]
        gains_ref[...] = jnp.concatenate(full + [jnp.zeros((4, D), F32)], axis=0)
        for seg in range(nseg):
            put_rows(xs, 0, tok_ref[seg * SEG : (seg + 1) * SEG, :].astype(F32))
            for pair in range(RES // 2):
                rows = jnp.concatenate([get_residue(xs, rev4(2 * pair + i)) for i in range(2)], axis=0)
                normed = normalize(rows, full[0], full[1])[0].astype(BF16)
                at = slice(seg * SEG + pair * 2 * RUN, seg * SEG + (pair + 1) * 2 * RUN)
                xp_ref[at, :] = rows.astype(BF16)
                inner_ref[:, at] = normed.T
        for pack, level in zip(packs, range(first, BRANCHES)):
            pack[2 * D :, :] = packed_keep(mask_ref[0], level, nseg)

    for chunk in range(COLUMN_CHUNKS):

        @pl.when(step == 2 * chunk)
        def _():
            load, core, x, hand = chunk_copies(chunk)
            x.wait_recv()
            hand.start()
            load.wait()
            core.wait_recv()
            hand.wait_recv()

    @pl.when(step == 4)
    def _():
        store.start()

    cols = pl.ds(pl.multiple_of(step * HALF, HALF), HALF)
    block = jnp.concatenate([weight[owner, :, cols] for owner in range(4)], axis=0)
    scale = jnp.where(step < 2, QUERY_SCALE, 1.0)
    for start in range(0, nseg * SEG, 512):
        lanes = slice(start, start + 512)
        qkv_ref[0, :, lanes] = (dotg(block, inner_ref[:, lanes], 0, 0) * scale).astype(BF16)

    @pl.when(step >= 2)
    def _():
        upper = lax.rem(step, 2) == 1
        for pack, level in zip(packs, range(first, BRANCHES)):
            size = SEG >> level
            for head in range(HEADS // 2):
                rows = slice(head * HEAD_DIM, (head + 1) * HEAD_DIM)
                pieces = []
                for seg in range(nseg):
                    start = seg * SEG + (rev4(head) >> (4 - level)) * size
                    if level < 4:
                        pieces.append(qkv_ref[0, rows, start : start + size])
                    else:
                        both = qkv_ref[0, rows, start : start + 2 * size]
                        pieces.append(jnp.where(upper, both[:, size:], both[:, :size]))
                into = pl.ds(pl.multiple_of((step - 2) * HALF + head * HEAD_DIM, 16), HEAD_DIM)
                pack[into, :] = jnp.concatenate(pieces, axis=1) if nseg > 1 else pieces[0]

    @pl.when(step == last)
    def _():
        for copy in vec_copies():
            copy.wait_send()
        for chunk in range(COLUMN_CHUNKS):
            for copy in chunk_copies(chunk)[1:]:
                copy.wait_send()
        store.wait()


def call_project(nseg, first, mask, tokens, vectors, weight):
    length = nseg * SEG
    kept = [nseg * (SEG >> level) for level in range(first, BRANCHES)]
    return pl.pallas_call(
        functools.partial(project_kernel, nseg, first),
        grid=(6,),
        in_specs=[MASK_BLOCK, const_block((length, D))] + [const_block((1, 192))] * 4 + [ANY_BLOCK],
        out_specs=[
            pl.BlockSpec((1, HALF, length), lambda i: (i // 2, i % 2, 0)),
            const_block((length, D)),
            const_block((D, length)),
            ANY_BLOCK,
            const_block((8, D)),
        ]
        + [const_block((2 * D + 16, size)) for size in kept],
        out_shape=[
            shape((3, D, length), BF16),
            shape((length, D), BF16),
            shape((D, length), BF16),
            shape((4, 192, 3 * D), BF16),
            shape((8, D), F32),
        ]
        + [shape((2 * D + 16, size), BF16) for size in kept],
        scratch_shapes=[
            pltpu.VMEM((TILES, SEG, 128), F32),
            pltpu.VMEM((4, 192, 3 * D), BF16),
            pltpu.VMEM((4, 8, 256), F32),
            sems(3),
            sems(3),
            sems(3 * COLUMN_CHUNKS),
            sems(3 * COLUMN_CHUNKS),
            sems(COLUMN_CHUNKS),
            sems(1),
        ],
        compiler_params=talking(4),
        cost_estimate=cost(nseg * 10e-6),
        name="project",
    )(mask, tokens, *vectors, weight)


ROWS = 256


def blocks_of(ref, rows, col):
    part = ref[rows, col * 128 : (col + 1) * 128].astype(BF16)
    return part.reshape(part.shape[0] // 16, 16, 128)


def feed_kernel(
    nseg, mask_ref, att_ref, x_ref, cot_ref, wout_ref, up_ref, down_ref, gains_ref,
    mixed_ref, gmid_ref, gm_ref, along_ref, vec_ref, grads_ref,
    cs, out_acc, up_acc, down_acc, stage, sems,
):
    step = pl.program_id(0)
    quarter = lax.rem(step, 4)
    low = (quarter >> 1) | ((quarter & 1) << 1)

    @pl.when(step == 0)
    def _():
        out_acc[...] = jnp.zeros_like(out_acc)
        up_acc[...] = jnp.zeros_like(up_acc)
        down_acc[...] = jnp.zeros_like(down_acc)
        vec_ref[...] = jnp.zeros_like(vec_ref)

    @pl.when(quarter == 0)
    def _():
        put_rows(cs, 0, cot_ref[...].astype(F32))

    grad = jnp.concatenate([get_residue(cs, rev4(i) + low) for i in range(4)], axis=0)
    grad_b = grad.astype(BF16)
    att = att_ref[...]
    middle = x_ref[...].astype(F32) + dotg(att, wout_ref[...], 0, 0)
    gain = gains_ref[2:3, :]
    normed, unit, inverse = normalize(middle, gain, gains_ref[3:4, :])
    hidden = normed.astype(BF16)
    hidden_t = hidden.T
    final = middle
    grad_hidden = jnp.zeros((ROWS, D), F32)
    for start in range(0, 4 * D, D):
        cols = slice(start, start + D)
        upper = dotg(hidden, up_ref[:, cols], 1, 0)
        grad_active = dotg(grad_b, down_ref[cols, :], 1, 1)
        half = 0.5 * (1.0 + lax.erf(upper * ROOT_HALF))
        slope = half + upper * jnp.exp(-0.5 * upper * upper) * INV_ROOT_TWO_PI
        active = (upper * half).astype(BF16)
        grad_upper = (grad_active * slope).astype(BF16)
        final = final + dotg(active, down_ref[cols, :], 1, 0)
        grad_hidden = grad_hidden + dotg(grad_upper, up_ref[:, cols], 1, 1)
        up_acc[:, cols] += dotg(hidden_t, grad_upper, 1, 0)
        down_acc[cols, :] += dotg(active, grad_b, 0, 0)
    for i in range(4):
        put_residue(cs, rev4(i) + low, final[i * RUN : (i + 1) * RUN])

    @pl.when(quarter == 3)
    def _():
        mixed_ref[...] = get_rows(cs, 0, SEG).astype(BF16)

    back, gain_back, shift_back = normalize_back(grad_hidden, unit, inverse, gain)
    vec_ref[0:1, :] += gain_back[None, :]
    vec_ref[1:2, :] += shift_back[None, :]
    grad_middle = grad + back
    gmid_ref[...] = grad_middle
    branch = grad_middle.astype(BF16)
    out_acc[...] += dotg(att, branch, 1, 0)
    lane = lax.broadcasted_iota(jnp.int32, (1, ROWS), 1)
    position = step // 4 * SEG + lax.rem(lane, RUN) * RES + residue_of(lane // RUN) + low
    keep = position < mask_ref[0]
    merged = jnp.where(keep, dotg(wout_ref[...], branch, 1, 1), 0.0).astype(BF16)
    gm_ref[...] = merged
    product = merged.astype(F32) * att.astype(F32)
    for head in range(HEADS):
        rows = slice(head * HEAD_DIM, (head + 1) * HEAD_DIM)
        along_ref[head] = jnp.sum(product[rows], axis=0, keepdims=True)

    @pl.when(step == pl.num_programs(0) - 1)
    def _():
        copies = []
        for owner in range(4):
            for piece in range(3):
                count = owner * 3 + piece
                slot = count % 2
                if count >= 2:
                    copies[count - 2].wait()
                if piece == 0:
                    rows, offset, size = slice(owner * 192, (owner + 1) * 192), 0, 288
                    for col in range(4 * TILES):
                        stage[slot, col * 12 : (col + 1) * 12] = blocks_of(up_acc, rows, col)
                elif piece == 1:
                    rows, offset, size = slice(owner * 192, (owner + 1) * 192), 288, 72
                    for col in range(TILES):
                        stage[slot, col * 12 : (col + 1) * 12] = blocks_of(out_acc, rows, col)
                else:
                    rows, offset, size = slice(owner * D, (owner + 1) * D), 360, 288
                    for col in range(TILES):
                        stage[slot, col * 48 : (col + 1) * 48] = blocks_of(down_acc, rows, col)
                copy = pltpu.make_async_copy(
                    stage.at[slot, pl.ds(0, size)],
                    grads_ref.at[owner, pl.ds(offset, size)],
                    sems.at[slot],
                )
                copy.start()
                copies.append(copy)
        copies[-2].wait()
        copies[-1].wait()


def call_feed(nseg, mask, att, x, cot, wout, up, down, gains):
    length = nseg * SEG
    return pl.pallas_call(
        functools.partial(feed_kernel, nseg),
        grid=(length // ROWS,),
        in_specs=[
            MASK_BLOCK,
            pl.BlockSpec((D, ROWS), lambda i: (0, i)),
            pl.BlockSpec((ROWS, D), lambda i: (i, 0)),
            pl.BlockSpec((SEG, D), lambda i: (i // 4, 0)),
            const_block((D, D)),
            const_block((D, 4 * D)),
            const_block((4 * D, D)),
            const_block((8, D)),
        ],
        out_specs=[
            pl.BlockSpec((SEG, D), lambda i: (i // 4, 0)),
            pl.BlockSpec((ROWS, D), lambda i: (i, 0)),
            pl.BlockSpec((D, ROWS), lambda i: (0, i)),
            pl.BlockSpec((HEADS, 1, ROWS), lambda i: (0, 0, i)),
            pl.BlockSpec((2, D), lambda i: (0, 0)),
            pl.BlockSpec(memory_space=pl.ANY),
        ],
        out_shape=[
            shape((length, D), BF16),
            shape((length, D), F32),
            shape((D, length), BF16),
            shape((HEADS, 1, length), F32),
            shape((2, D), F32),
            shape((4, padded(FEED_BLOCKS), 16, 128), BF16),
        ],
        scratch_shapes=[
            pltpu.VMEM((TILES, SEG, 128), F32),
            pltpu.VMEM((D, D), F32),
            pltpu.VMEM((D, 4 * D), F32),
            pltpu.VMEM((4 * D, D), F32),
            pltpu.VMEM((2, 288, 16, 128), BF16),
            pltpu.SemaphoreType.DMA((2,)),
        ],
        compiler_params=pltpu.CompilerParams(vmem_limit_bytes=62 * 1024 * 1024),
        cost_estimate=cost(nseg * 45e-6),
        name="feed",
    )(mask, att, x, cot, wout, up, down, gains)


STEPS = 6


def inner_back_kernel(nseg, first, local_ref, inner_ref, w_ref, x_ref, gmid_ref, gain_ref, feed_vec_ref, *refs):
    n = BRANCHES - first
    packs, (weight_ref, back_ref, vec_ref) = refs[:n], refs[n : n + 3]
    acc, mixed, order, terms, recv_core, recv_x, recv_seq, total, vecs, vec_recv = refs[n + 3 : n + 13]
    red_send, red_recv, vec_send, vec_recv_sems = refs[n + 13 :]
    step = pl.program_id(0)
    last = pl.num_programs(0) - 1
    length = nseg * SEG
    end = STEPS + length // ROWS
    blocks = terms.shape[1] // CHUNKS
    core = lax.rem(lax.axis_index("fsdp"), 2)
    reduce = Reduce(
        CHUNKS, blocks, terms, terms, lambda xo: 2 * xo + core, recv_core, recv_x, recv_seq, total,
        Sends(red_send, red_recv),
    )
    vec_sends = Sends(vec_send, vec_recv_sems)

    def vec_copy(i):
        return vec_sends.copy(i, vecs.at[i], vec_recv.at[i], *reduce.peers()[i])

    def vec_event(i):
        vec_copy(i).wait_recv()
        vecs[i + 1] = vecs[i] + vec_recv[i]
        if i + 1 < len(reduce.peers()):
            vec_copy(i + 1).start()

    def vec_start():
        vec_copy(0).start()

    @pl.when(step == 0)
    def _():
        meet(reduce.peers())
        vecs[0] = jnp.concatenate([jnp.zeros((2, D), F32), feed_vec_ref[...], jnp.zeros((4, D), F32)], axis=0)

    @pl.when(step < 2)
    def _():
        mixed[...] = local_ref[0].astype(BF16)

    @pl.when((step >= 2) & (step < STEPS))
    def _():
        upper = lax.rem(step, 2) == 1
        for pack, level in zip(packs, range(first, BRANCHES)):
            size = SEG >> level
            for head in range(HEADS // 2):
                rows = slice(head * HEAD_DIM, (head + 1) * HEAD_DIM)
                for seg in range(nseg):
                    start = seg * SEG + (rev4(head) >> (4 - level)) * size
                    piece = pack[0, rows, seg * size : (seg + 1) * size].astype(F32)
                    if level == 4:
                        zero = jnp.zeros_like(piece)
                        piece = jnp.concatenate(
                            [jnp.where(upper, zero, piece), jnp.where(upper, piece, zero)], axis=1
                        )
                    local_ref[0, rows, start : start + piece.shape[1]] += piece
        mixed[...] = local_ref[0].astype(BF16)

    @pl.when(step < STEPS)
    def _():
        grad_in = dotg(inner_ref[...], mixed[...], 1, 1).astype(BF16)
        base = lax.div(step, 2) * blocks + lax.rem(step, 2) * 36
        for col in range(3):
            part = grad_in[:, col * 128 : (col + 1) * 128].reshape(4, 12, 16, 128)
            for owner in range(4):
                terms[owner, pl.ds(base + col * 12, 12)] = part[owner]
        for start in range(0, length, 512):
            lanes = slice(start, start + 512)
            part = dotg(w_ref[...], mixed[:, lanes], 1, 0)

            @pl.when(step == 0)
            def _():
                acc[:, lanes] = part

            @pl.when(step > 0)
            def _():
                acc[:, lanes] += part

    events = []
    for chunk in range(CHUNKS):
        begin = 2 * chunk + 1
        events.append((begin, functools.partial(reduce.begin, chunk)))
        for stage in range(reduce.stages()):
            when = begin + 1 + stage + (1 if stage else 0) + max(0, stage - 1 - chunk)
            events.append((when, functools.partial(reduce.event, stage, chunk)))
    events.append((end - 1, vec_start))
    for i in range(len(reduce.peers())):
        events.append((end + i, functools.partial(vec_event, i)))
    events.sort(key=lambda event: event[0])

    @pl.when((step >= STEPS) & (step < end))
    def _():
        turn = step - STEPS
        quarter = lax.rem(turn, 4)
        low = (quarter >> 1) | ((quarter & 1) << 1)
        gain = gain_ref[0:1, :]
        grad = acc[:, pl.ds(pl.multiple_of(turn * ROWS, ROWS), ROWS)].T
        _, unit, inverse = normalize(x_ref[...].astype(F32), gain, gain)
        back, gain_part, shift_part = normalize_back(grad, unit, inverse, gain)
        vecs[0, 0:1, :] += gain_part[None, :]
        vecs[0, 1:2, :] += shift_part[None, :]
        total_back = gmid_ref[...] + back
        for i in range(4):
            put_residue(order, rev4(i) + low, total_back[i * RUN : (i + 1) * RUN])

        @pl.when(quarter == 3)
        def _():
            back_ref[...] = get_rows(order, 0, SEG)

    run_schedule(step, last, events)

    @pl.when(step == last)
    def _():
        reduce.finish()
        for i in range(len(reduce.peers())):
            vec_copy(i).wait_send()
        vec_ref[...] = vecs[len(reduce.peers())]
        for part in range(STEPS):
            for col in range(3):
                at = part // 2 * blocks + part % 2 * 36 + col * 12
                weight_ref[:, part * HALF + col * 128 : part * HALF + (col + 1) * 128] = rows_of(total, at, 12)


def call_inner_back(nseg, first, local, inner, weight, x, gmid, gain, feed_vec, packs):
    length = nseg * SEG
    turns = length // ROWS
    blocks = padded(IN_BLOCKS)
    if blocks // CHUNKS < 72:
        raise ValueError("blocks")
    peers = 2 + seq_bits()

    def at(i):
        return jnp.minimum(i, STEPS - 1)

    def turn(i):
        return jnp.clip(i - STEPS, 0, turns - 1)

    return pl.pallas_call(
        functools.partial(inner_back_kernel, nseg, first),
        grid=(STEPS + turns + 1,),
        in_specs=[
            pl.BlockSpec((1, HALF, length), lambda i: (at(i) // 2, at(i) % 2, 0)),
            const_block((D, length)),
            pl.BlockSpec((D, HALF), lambda i: (0, at(i))),
            pl.BlockSpec((ROWS, D), lambda i: (turn(i), 0)),
            pl.BlockSpec((ROWS, D), lambda i: (turn(i), 0)),
            const_block((8, D)),
            const_block((2, D)),
        ]
        + [
            pl.BlockSpec((1, HALF, pack.shape[2]), lambda i: (jnp.maximum(at(i) // 2 - 1, 0), at(i) % 2, 0))
            for pack in packs
        ],
        out_specs=[
            const_block((192, 3 * D)),
            pl.BlockSpec((SEG, D), lambda i: (turn(i) // 4, 0)),
            const_block((8, D)),
        ],
        out_shape=[shape((192, 3 * D), F32), shape((length, D), F32), shape((8, D), F32)],
        scratch_shapes=[
            pltpu.VMEM((D, length), F32),
            pltpu.VMEM((HALF, length), BF16),
            pltpu.VMEM((TILES, SEG, 128), F32),
            pltpu.VMEM((4, blocks, 16, 128), BF16),
            pltpu.VMEM((2, blocks, 16, 128), BF16),
            pltpu.VMEM((blocks, 16, 128), BF16),
            pltpu.VMEM((blocks, 16, 128), BF16),
            pltpu.VMEM((blocks, 16, 128), BF16),
            pltpu.VMEM((peers + 1, 8, D), F32),
            pltpu.VMEM((peers, 8, D), F32),
            sems(reduce_copies()),
            sems(reduce_copies()),
            sems(peers),
            sems(peers),
        ],
        compiler_params=talking(3),
        cost_estimate=cost(nseg * 15e-6),
        name="inner_back",
    )(local, inner, weight, x, gmid, gain, feed_vec, *packs)


def per_device(
    tokens,
    first_gain,
    first_shift,
    project_in,
    project_out,
    second_gain,
    second_shift,
    up_weight,
    down_weight,
    valid_mask,
    cotangent,
):
    length = tokens.shape[1]
    nseg = length // SEG
    first = nseg.bit_length()

    def gather(weight):
        return lax.all_gather(weight, "fsdp", axis=0, tiled=True)

    weight_out = gather(project_out)
    weight_up = gather(up_weight)
    weight_down = gather(down_weight)

    mask = jnp.sum(valid_mask[0])[None]

    vectors = [vector[None, :] for vector in (first_gain, first_shift, second_gain, second_shift)]
    qkv, x, inner, weight_in, gains, *packs = call_project(nseg, first, mask, tokens[0], vectors, project_in)
    weight_in = weight_in.reshape(D, 3 * D)
    o_part, l_part, m_part, gathered = call_local_forward(nseg, first, qkv, mask, packs)
    attended, lse = call_remote_forward(nseg, first, qkv, mask, o_part, l_part, m_part, gathered)

    mixed, grad_middle, grad_merged, along, feed_vec, feed_grads = call_feed(
        nseg, mask, attended, x, cotangent[0], weight_out, weight_up, weight_down, gains
    )

    dq_remote, *sent = call_remote_backward(nseg, first, qkv, grad_merged, lse, along, mask, gathered)
    local, returned, (grad_up, grad_out, grad_down) = call_local_backward(
        nseg, first, qkv, grad_merged, lse, along, mask, dq_remote, sent, feed_grads
    )
    grad_in, tokens_back, vectors = call_inner_back(
        nseg, first, local, inner, weight_in, x, grad_middle, gains, feed_vec, returned
    )
    quarter = D // lax.axis_size("fsdp")
    vectors = lax.dynamic_slice_in_dim(vectors, lax.axis_index("fsdp") * quarter, quarter, 1)
    return (
        mixed[None],
        tokens_back[None],
        vectors[0],
        vectors[1],
        grad_in,
        grad_out,
        vectors[2],
        vectors[3],
        grad_up,
        grad_down,
    )


def solution(mesh):
    in_specs = (
        P("fsdp", "seq", None),
        P("fsdp"),
        P("fsdp"),
        P("fsdp", None),
        P("fsdp", None),
        P("fsdp"),
        P("fsdp"),
        P("fsdp", None),
        P("fsdp", None),
        P("fsdp", "seq"),
        P("fsdp", "seq", None),
    )
    out_specs = (
        P("fsdp", "seq", None),
        P("fsdp", "seq", None),
        P("fsdp"),
        P("fsdp"),
        P("fsdp", None),
        P("fsdp", None),
        P("fsdp"),
        P("fsdp"),
        P("fsdp", None),
        P("fsdp", None),
    )
    return jax.shard_map(
        per_device, mesh=mesh, in_specs=in_specs, out_specs=out_specs, check_vma=False
    )
```

```python
import functools
import math

import jax
import jax.numpy as jnp
import ml_dtypes
import numpy as np
from jax import lax
from jax.experimental import pallas as pl
from jax.experimental.pallas import tpu as pltpu
from jax.sharding import PartitionSpec as P

HEADS = 16
HEAD_DIM = 48
SEG = 1024
BRANCHES = 5
RES = 16
RUN = SEG // RES
D = HEADS * HEAD_DIM

EPS = 1e-05
NEG = -1e30
ROOT_HALF = 0.7071067811865476
INV_ROOT_TWO_PI = 0.3989422804014327
F32 = jnp.float32
BF16 = jnp.bfloat16
QUERY_SCALE = math.log2(math.e) * HEAD_DIM ** (-0.5)
VMEM_LIMIT = 56 * 1024 * 1024


def dotg(left, right, left_dim, right_dim):
    return lax.dot_general(
        left, right, (((left_dim,), (right_dim,)), ((), ())), preferred_element_type=F32
    )


def normalize(values, gain, shift):
    mean = jnp.mean(values, axis=-1, keepdims=True)
    centred = values - mean
    spread = jnp.mean(centred * centred, axis=-1, keepdims=True)
    inverse = lax.rsqrt(spread + EPS)
    normed = centred * inverse
    return (normed * gain + shift, normed, inverse)


def normalize_back(grad, normed, inverse, gain):
    scaled = grad * gain
    first = jnp.mean(scaled, axis=-1, keepdims=True)
    second = jnp.mean(scaled * normed, axis=-1, keepdims=True)
    return (
        inverse * (scaled - first - normed * second),
        jnp.sum(grad * normed, axis=0),
        jnp.sum(grad, axis=0),
    )


def reversed_bits(head):
    return ((head & 1) << 3) | ((head & 2) << 1) | ((head & 4) >> 1) | ((head & 8) >> 3)


def near_class(head, low_bits, length):
    lane = lax.broadcasted_iota(jnp.int32, (1, length), 1)
    rho = lax.rem(lane // RUN, 1 << low_bits)
    return rho ^ (reversed_bits(head) & ((1 << low_bits) - 1))


def class_rows(near, length):
    row = lax.broadcasted_iota(jnp.int32, (16, length), 0)
    step = lax.rem(row + 3, 4) + 1
    bound = jnp.where((row >= 5) & (row <= 12), lax.shift_right_logical(RES, step), 0)
    return row, near < bound


def query_rows(head, length, neg_lse=None):
    near = near_class(head, 4, length)
    row, inside = class_rows(near, length)
    out = jnp.where(inside, 1.0, 0.0)
    out = jnp.where(row == 0, 1.0, out)
    out = jnp.where(row == 4, jnp.where(near < 1, 0.0, NEG), out)
    if neg_lse is not None:
        high = neg_lse.astype(BF16).astype(F32)
        rest = neg_lse - high
        mid = rest.astype(BF16).astype(F32)
        low = rest - mid
        out = jnp.where(row == 1, high, jnp.where(row == 2, mid, jnp.where(row == 3, low, out)))
    return out.astype(BF16)


def residue_of(rho):
    return reversed_bits(rho)


def local_keep(count, length):
    lane = lax.broadcasted_iota(jnp.int32, (1, length), 1)
    rho = lax.rem(lane // RUN, RES)
    position = lane // SEG * SEG + lax.rem(lane, RUN) * RES + residue_of(rho)
    return position < count


def packed_keep(count, level, nseg):
    size = SEG >> level
    dims = (HEADS, nseg * size)
    head = lax.broadcasted_iota(jnp.int32, dims, 0)
    lane = lax.broadcasted_iota(jnp.int32, dims, 1)
    rho = (reversed_bits(head) >> (4 - level)) * (size // RUN) + lax.rem(lane, size) // RUN
    position = lane // size * SEG + lax.rem(lane, RUN) * RES + residue_of(rho)
    return jnp.where(position < count, 1.0, 0.0).astype(BF16)


def weight_of(level, step):
    return math.log2((step - level + 1) / (step - level)) if step > level else 0.0


def key_rows(head, level, low_bits, length, keep):
    near = near_class(head, low_bits, length)
    row, inside = class_rows(near, length)
    weight = jnp.zeros((16, length), F32)
    for step in range(level + 1, BRANCHES):
        value = weight_of(level, step)
        high = float(np.asarray(value, ml_dtypes.bfloat16))
        weight = jnp.where(row == 4 + step, high, weight)
        weight = jnp.where(row == 8 + step, value - high, weight)
    out = jnp.where(inside, weight, 0.0)
    out = jnp.where((row >= 1) & (row <= 3), 1.0, out)
    out = jnp.where(row == 0, jnp.where(keep, 0.0, NEG), out)
    if level == BRANCHES - 1:
        out = jnp.where(row == 4, 1.0, out)
    return out.astype(BF16)


def value_rows(length):
    row = lax.broadcasted_iota(jnp.int32, (16, length), 0)
    return jnp.where(row < 2, 1.0, 0.0).astype(BF16)


def join(rows, extra):
    return jnp.concatenate([rows, extra], axis=0)


def kept_start(head, level, seg):
    size = SEG >> level
    block = reversed_bits(head) >> (4 - level)
    return pl.multiple_of(seg * SEG + block * size, min(size, 128))


def partner(axis, distance):
    place = lax.axis_index(axis)
    return {axis: place + distance * (1 - 2 * lax.rem(lax.div(place, distance), 2))}


def seq_bits():
    return lax.axis_size("seq").bit_length() - 1


def meet(peers):
    barrier = pltpu.get_barrier_semaphore()
    for axis, distance in peers:
        pl.semaphore_signal(
            barrier, inc=1, device_id=partner(axis, distance), device_id_type=pl.DeviceIdType.MESH
        )
    pl.semaphore_wait(barrier, len(peers))


class Sends:
    def __init__(self, send_sems, recv_sems):
        self.send_sems, self.recv_sems, self.made = send_sems, recv_sems, {}

    def copy(self, key, source, target, axis, distance):
        index = self.made.setdefault(key, len(self.made))
        return pltpu.make_async_remote_copy(
            src_ref=source,
            dst_ref=target,
            send_sem=self.send_sems.at[index],
            recv_sem=self.recv_sems.at[index],
            device_id=partner(axis, distance),
            device_id_type=pl.DeviceIdType.MESH,
        )


class Gather:
    def __init__(self, nseg, first, packs, gathered, sends):
        self.hops, self.distances = [], set()
        for level, pack, into in zip(range(first, BRANCHES), packs, gathered):
            group = (SEG << (level - 1)) // (nseg * SEG)
            hops = [((level, 0), pack, into.at[0], group)]
            step = 1
            while step < group:
                hops.append(((level, step), into.at[pl.ds(0, step)], into.at[pl.ds(step, step)], step))
                step *= 2
            self.hops.append([sends.copy(k, a, b, "seq", d) for k, a, b, d in hops])
            self.distances |= {hop[3] for hop in hops}

    def peers(self):
        return [("seq", distance) for distance in sorted(self.distances)]

    def start(self):
        for hops in reversed(self.hops):
            hops[0].start()

    def pass_on(self, index, turn):
        hops = self.hops[index]
        hops[turn - 1].wait_recv()
        hops[turn].start()

    def finish(self):
        for hops in self.hops:
            for hop in hops:
                hop.wait_send()
            hops[-1].wait_recv()

    def turns(self):
        events = []
        for index, hops in reversed(list(enumerate(self.hops))):
            for turn in range(1, len(hops)):
                when = 4 * turn + (2 if turn > 1 else 0) + (len(self.hops) - 1 - index)
                events.append((when, functools.partial(self.pass_on, index, turn)))
        return events


class Return:
    def __init__(self, nseg, first, sent, returned, bufs, recvs, local_sems, sends):
        self.plans = []
        for i, level in enumerate(range(first, BRANCHES)):
            group = (SEG << (level - 1)) // (nseg * SEG)
            plan = []
            if group == 1:
                plan.append((None, sends.copy((level, 0), sent[i].at[0], returned[i], "seq", group)))
                self.plans.append((plan, None))
                continue
            buf, recv = bufs.pop(0), recvs.pop(0)
            step = group // 2
            load = pltpu.make_async_copy(sent[i].at[pl.ds(0, step)], buf, local_sems.at[i])
            source, at, add = sent[i].at[pl.ds(step, step)], 0, None
            while step >= 1:
                into = recv.at[pl.ds(at, step)]
                plan.append((add, sends.copy((level, step), source, into, "seq", step)))
                add = (buf, recv, at, step)
                at += step
                step //= 2
                if step:
                    source = buf.at[pl.ds(step, step)]
            plan.append((add, sends.copy((level, 0), buf.at[0], returned[i], "seq", group)))
            self.plans.append((plan, load))

    def start(self, direct):
        for plan, load in reversed(self.plans):
            if direct == (load is None):
                if load is not None:
                    load.start()
                plan[0][1].start()

    def turn(self, number):
        for plan, load in reversed(self.plans):
            if number < len(plan):
                plan[number - 1][1].wait_recv()
                if number == 1 and load is not None:
                    load.wait()
                buf, recv, at, step = plan[number][0]
                for i in range(step):
                    buf[i] = (buf[i].astype(F32) + recv[at + i].astype(F32)).astype(BF16)
                plan[number][1].start()

    def finish(self):
        for plan, load in self.plans:
            for _, copy in plan:
                copy.wait_send()
            plan[-1][1].wait_recv()

    def turns(self):
        return max(len(plan) for plan, _ in self.plans)


def add_blocks(into, at, other, start, count):
    unit = max(u for u in range(1, 13) if count % u == 0)

    def body(i, carry):
        rows = pl.ds(at + i * unit, unit)
        part = other[pl.ds(start + i * unit, unit)].astype(F32)
        into[rows] = (into[rows].astype(F32) + part).astype(BF16)
        return carry

    lax.fori_loop(0, count // unit, body, 0)


def copy_blocks(into, at, other, start, count):
    unit = max(u for u in range(1, 13) if count % u == 0)

    def body(i, carry):
        into[pl.ds(at + i * unit, unit)] = other[pl.ds(start + i * unit, unit)]
        return carry

    lax.fori_loop(0, count // unit, body, 0)


def halving(blocks, order):
    seq = lax.axis_index("seq")
    low, given = [0], []
    for j, distance in enumerate(order):
        bit = lax.rem(lax.div(seq, distance), 2)
        half = blocks >> (j + 1)
        given.append(low[j] + (1 - bit) * half)
        low.append(low[j] + bit * half)
    return low, given


def orders():
    plain = [2**j for j in range(seq_bits())]
    return [plain] * (CHUNKS - 1) + [plain[1:] + plain[:1]]


def all_peers():
    return [("fsdp", 1), ("fsdp", 2)] + [("seq", 2**j) for j in range(seq_bits())]


class Reduce:
    def __init__(self, blocks, source, terms, own, recv_core, recv_x, recv_seq, sends, done, loads=None):
        self.blocks, self.source, self.terms, self.own, self.done = blocks, source, terms, own, done
        self.recv_core, self.recv_x, self.recv_seq = recv_core, recv_x, recv_seq
        self.sends, self.loads = sends, loads
        fsdp = lax.axis_index("fsdp")
        self.core, self.x = lax.rem(fsdp, 2), lax.div(fsdp, 2)
        self.bits = seq_bits()
        self.orders = orders()
        self.halves = [halving(blocks, order) for order in self.orders]

    def stages(self):
        return 2 + self.bits

    def core_copy(self, chunk, xo):
        rows = pl.ds(chunk * self.blocks, self.blocks)
        owner = 2 * xo + 1 - self.core
        return self.sends.copy(
            ("core", chunk, xo), self.source.at[owner, rows], self.recv_core.at[xo, rows], "fsdp", 1
        )

    def load_copy(self, chunk, xo):
        rows = pl.ds(chunk * self.blocks, self.blocks)
        return pltpu.make_async_copy(
            self.source.at[2 * xo + self.core, rows], self.terms.at[xo, rows], self.loads.at[2 * chunk + xo]
        )

    def x_copy(self, chunk):
        rows = pl.ds(chunk * self.blocks, self.blocks)
        return self.sends.copy(
            ("x", chunk), self.terms.at[self.own(1 - self.x), rows], self.recv_x.at[rows], "fsdp", 2
        )

    def down_copy(self, chunk, j):
        half = self.blocks >> (j + 1)
        base = chunk * self.blocks
        rows = pl.ds(base + self.halves[chunk][1][j], half)
        into = pl.ds(base + self.blocks - (self.blocks >> j), half)
        return self.sends.copy(
            ("down", chunk, j), self.terms.at[self.own(self.x), rows], self.recv_seq.at[into], "seq",
            self.orders[chunk][j],
        )

    def begin(self, chunk):
        for xo in range(2):
            if self.loads is not None:
                self.load_copy(chunk, xo).start()
            self.core_copy(chunk, xo).start()

    def event(self, stage, chunk):
        base = chunk * self.blocks
        low = self.halves[chunk][0]
        mine = self.terms.at[self.own(self.x)]
        if stage == 0:
            for xo in range(2):
                self.core_copy(chunk, xo).wait_recv()
                if self.loads is not None:
                    self.load_copy(chunk, xo).wait()
                add_blocks(self.terms.at[self.own(xo)], base, self.recv_core.at[xo], base, self.blocks)
            self.x_copy(chunk).start()
            return
        j = stage - 2
        if stage == 1:
            self.x_copy(chunk).wait_recv()
            add_blocks(mine, base, self.recv_x, base, self.blocks)
        else:
            self.down_copy(chunk, j).wait_recv()
            half = self.blocks >> (j + 1)
            add_blocks(mine, base + low[j + 1], self.recv_seq, base + self.blocks - (self.blocks >> j), half)
        if j + 1 < self.bits:
            self.down_copy(chunk, j + 1).start()
        else:
            self.done(chunk, mine, base + low[self.bits])

    def finish(self):
        for chunk in range(CHUNKS):
            for xo in range(2):
                self.core_copy(chunk, xo).wait_send()
            self.x_copy(chunk).wait_send()
            for j in range(self.bits):
                self.down_copy(chunk, j).wait_send()


class Spread:
    def __init__(self, blocks, total, sends):
        self.blocks, self.total, self.sends = blocks, total, sends
        self.bits = seq_bits()
        self.orders = orders()
        self.lows = [halving(blocks, order)[0] for order in self.orders]

    def stages(self):
        return self.bits

    def copy(self, chunk, j):
        rows = pl.ds(chunk * self.blocks + self.lows[chunk][j + 1], self.blocks >> (j + 1))
        here = self.total.at[rows]
        return self.sends.copy((chunk, j), here, here, "seq", self.orders[chunk][j])

    def begin(self, chunk, ref, start):
        size = self.blocks >> self.bits
        copy_blocks(self.total, chunk * self.blocks + self.lows[chunk][self.bits], ref, start, size)
        self.copy(chunk, self.bits - 1).start()

    def event(self, stage, chunk):
        j = self.bits - 1 - stage
        self.copy(chunk, j).wait_recv()
        if j:
            self.copy(chunk, j - 1).start()

    def finish(self):
        for chunk in range(CHUNKS):
            for j in range(self.bits):
                self.copy(chunk, j).wait_send()


def run_schedule(step, last, events):
    due = {}
    for when, call in events:
        due.setdefault(min(when, last), []).append(call)
    for when in sorted(due):

        @pl.when(step == when)
        def _():
            for call in due[when]:
                call()


FRONT = 3
KEY_TILE = 128


class State:
    def __init__(self, query, acc=None, top=None):
        self.query, self.acc, self.top = query, acc, top


def attend(items):
    items = list(items)
    ready = []
    for turn in range(len(items) + FRONT):
        if turn < len(items):
            state, key, _ = items[turn]
            ready.append(dotg(key, state.query, 1, 0))
        if turn >= FRONT:
            state, _, value = items[turn - FRONT]
            scores, ready[turn - FRONT] = ready[turn - FRONT], None
            top = jnp.max(scores, axis=0, keepdims=True)
            if state.top is not None:
                top = jnp.maximum(top, state.top)
            probs = jnp.exp2(scores - top).astype(BF16)
            part = dotg(value, probs, 1, 0)
            state.acc = part if state.top is None else state.acc * jnp.exp2(state.top - top) + part
            state.top = top


def key_items(state, key_t, value):
    size = key_t.shape[0]
    tile = min(KEY_TILE, size)
    for start in range(0, size, tile):
        yield state, key_t[start : start + tile], value[:, start : start + tile]


def load_state(query, mine, o_ref, l_ref, m_ref):
    acc = [jnp.concatenate([o_ref[:, at], jnp.broadcast_to(l_ref[0, :, at], (16, at.size))]) for at in mine]
    top = [m_ref[0, :, at] for at in mine]
    return State(query, jnp.concatenate(acc, axis=1), jnp.concatenate(top, axis=1))


def store_state(state, mine, o_ref, l_ref, m_ref):
    start = 0
    for at in mine:
        lanes = slice(start, start + at.size)
        o_ref[:, at] = state.acc[:HEAD_DIM, lanes]
        l_ref[0, :, at] = state.acc[HEAD_DIM : HEAD_DIM + 1, lanes]
        m_ref[0, :, at] = state.top[:, lanes]
        start += at.size


def local_forward(nseg, first, mask_ref, q_ref, k_ref, v_ref, *refs):
    n = BRANCHES - first
    packs, (o_ref, l_ref, m_ref), gathered = refs[:n], refs[n : n + 3], refs[n + 3 : 2 * n + 3]
    qa, ka, va, send_sems, recv_sems = refs[2 * n + 3 :]
    head = pl.program_id(0)
    length = nseg * SEG
    gather = Gather(nseg, first, packs, gathered, Sends(send_sems, recv_sems))

    def begin():
        meet(gather.peers())
        gather.start()

    run_schedule(head, HEADS - 1, [(0, begin)] + sorted(gather.turns(), key=lambda event: event[0]))
    local_forward_core(nseg, mask_ref, q_ref, k_ref, v_ref, o_ref, l_ref, m_ref, qa, ka, va)
    run_schedule(head, HEADS - 1, [(HEADS - 1, gather.finish)])


def local_forward_scratch(nseg):
    length = nseg * SEG
    return [
        pltpu.VMEM((64, length), BF16),
        pltpu.VMEM((nseg, 64, length), BF16),
        pltpu.VMEM((64, length), BF16),
    ]


def local_forward_core(nseg, mask_ref, q_ref, k_ref, v_ref, o_ref, l_ref, m_ref, qa, ka, va):
    head = pl.program_id(0)
    length = nseg * SEG
    keep = local_keep(mask_ref[0], length)
    qa[...] = join(q_ref[0], query_rows(head, length))
    va[...] = join(v_ref[0], value_rows(length))
    ka[0] = join(k_ref[0], key_rows(head, 0, 4, length, keep))
    if nseg == 2:
        ka[1] = join(k_ref[0], key_rows(head, 1, 4, length, keep))
    states, items = [], []
    for seg in range(nseg):
        lanes = slice(seg * SEG, (seg + 1) * SEG)
        states.append(State(qa[:, lanes]))
        items += key_items(states[-1], ka[0, :, lanes].T, va[:, lanes])
    attend(items)
    for seg in range(nseg):
        store_state(states[seg], [pl.ds(seg * SEG, SEG)], o_ref, l_ref, m_ref)
    if nseg == 2:
        kept = [pl.ds(kept_start(head, 1, seg), SEG // 2) for seg in range(2)]
        states = [load_state(qa[:, at], [at], o_ref, l_ref, m_ref) for at in kept]
        items = []
        for seg in range(2):
            items += key_items(states[seg], ka[1, :, kept[1 - seg]].T, va[:, kept[1 - seg]])
        attend(items)
        for seg in range(2):
            store_state(states[seg], [kept[seg]], o_ref, l_ref, m_ref)


def remote_keys(head, level, pack):
    k_ref, v_ref, mask_ref = pack
    pieces = range(k_ref.shape[0])
    key, value, mask = (
        jnp.concatenate([ref[i] for i in pieces], axis=1) for ref in (k_ref, v_ref, mask_ref)
    )
    length = key.shape[1]
    row = lax.broadcasted_iota(jnp.int32, (16, length), 0)
    keep = jnp.sum(jnp.where(row == head, mask.astype(F32), 0.0), axis=0, keepdims=True) > 0.5
    return join(key, key_rows(head, level, 4 - level, length, keep)), join(value, value_rows(length))


def remote_plan(first):
    return [(level,) for level in range(first, 3)] + [(3, 4)]


def remote_forward(nseg, first, mask_ref, q_ref, o_in, l_in, m_in, *refs):
    head = pl.program_id(0)
    levels = range(first, BRANCHES)
    packs = {level: refs[3 * i : 3 * i + 3] for i, level in enumerate(levels)}
    att_ref, lse_ref, o_ref, l_ref, m_ref, qa = refs[3 * len(levels) :]
    length = nseg * SEG
    qa[...] = join(q_ref[0], query_rows(head, length))
    o_ref[...] = o_in[...]
    l_ref[...] = l_in[...]
    m_ref[...] = m_in[...]
    for group in remote_plan(first):
        pairs = [remote_keys(head, level, packs[level]) for level in group]
        key = jnp.concatenate([pair[0] for pair in pairs], axis=1)
        value = jnp.concatenate([pair[1] for pair in pairs], axis=1)
        mine = [pl.ds(kept_start(head, group[0], seg), SEG >> group[0]) for seg in range(nseg)]
        query = jnp.concatenate([qa[:, at] for at in mine], axis=1)
        state = load_state(query, mine, o_ref, l_ref, m_ref)
        attend(key_items(state, key.T, value))
        store_state(state, mine, o_ref, l_ref, m_ref)
    weight = jnp.where(local_keep(mask_ref[0], length), 1.0, 0.0) / l_ref[0]
    att_ref[...] = (o_ref[...] * weight).astype(BF16)
    lse_ref[0] = m_ref[0] + jnp.log2(l_ref[0])


def grad_rows(grad, slope):
    length = grad.shape[1]
    row = lax.broadcasted_iota(jnp.int32, (16, length), 0)
    high = (-slope).astype(BF16).astype(F32)
    low = -slope - high
    extra = jnp.where(row == 0, high, jnp.where(row == 1, low, 0.0)).astype(BF16)
    return join(grad, extra)


AHEAD = 2
QUERY_TILE = 256
BACK_KEYS = 256


class Side:
    def __init__(self, query, grad):
        self.query, self.grad = query[:HEAD_DIM], grad[:HEAD_DIM]
        self.query_t, self.grad_t = query.T, grad.T
        self.dq = None


def attend_back(items, dk_ref, dv_ref, written):
    items = list(items)
    ready = []
    for turn in range(len(items) + AHEAD):
        if turn < len(items):
            side, key, value, _, _ = items[turn]
            ready.append((dotg(side.query_t, key, 1, 0), dotg(side.grad_t, value, 1, 0)))
        if turn >= AHEAD:
            side, key, _, lanes, name = items[turn - AHEAD]
            scores, slope = ready[turn - AHEAD]
            ready[turn - AHEAD] = None
            probs = jnp.exp2(scores)
            dscore = (probs * slope).astype(BF16)
            dv = dotg(side.grad, probs.astype(BF16), 1, 0)
            dk = dotg(side.query, dscore, 1, 0)
            part = dotg(key[:HEAD_DIM], dscore, 1, 1)
            side.dq = part if side.dq is None else side.dq + part
            if name in written:
                dv_ref[:, lanes] += dv
                dk_ref[:, lanes] += dk
            else:
                written.add(name)
                dv_ref[:, lanes] = dv
                dk_ref[:, lanes] = dk


def sides_of(query, grad):
    tile = min(QUERY_TILE, query.shape[1])
    return [
        Side(query[:, start : start + tile], grad[:, start : start + tile])
        for start in range(0, query.shape[1], tile)
    ]


def pairs(sides, key_ref, value_ref, tiles):
    return [
        (side, key_ref[:, lanes], value_ref[:, lanes], lanes, name) for side in sides for name, lanes in tiles
    ]


def joined(sides):
    return jnp.concatenate([side.dq for side in sides], axis=1) if len(sides) > 1 else sides[0].dq


DQ_SCALE = HEAD_DIM ** (-0.5)
DK_SCALE = math.log(2.0)


def neg_total(lse, keep):
    return jnp.where(keep, -lse, NEG)


def local_backward(nseg, first, mask_ref, q_ref, k_ref, v_ref, g_ref, lse_ref, slope_ref, dqr_ref, *refs):
    n = BRANCHES - first
    sent, feed_ref, out_ref = refs[:n], refs[n], refs[n + 1]
    returned, piece_ref = refs[n + 2 : 2 * n + 2], refs[2 * n + 2]
    qa, ga, ka, va, dk, dv = refs[2 * n + 3 : 2 * n + 9]
    rest = list(refs[2 * n + 9 :])
    back_send, back_recv, back_load, red_send, red_recv, red_load = rest[-6:]
    terms, recv_core, recv_x, recv_seq = rest[-10:-6]
    bufs, recvs = rest[: (len(rest) - 10) // 2], rest[(len(rest) - 10) // 2 : -10]
    head = pl.program_id(0)
    last = HEADS - 1

    back = Return(nseg, first, sent, returned, bufs, recvs, back_load, Sends(back_send, back_recv))
    blocks = terms.shape[1] // CHUNKS
    reduce = Reduce(
        blocks, feed_ref, terms, lambda xo: xo, recv_core, recv_x, recv_seq, Sends(red_send, red_recv),
        lambda chunk, ref, start: copy_blocks(piece_ref.at[chunk], 0, ref, start, blocks >> seq_bits()),
        red_load,
    )

    def begin():
        meet(all_peers())
        back.start(False)
        for chunk in range(CHUNKS):
            reduce.begin(chunk)

    events = [(3 * turn, functools.partial(back.turn, turn)) for turn in range(1, back.turns())]
    events.append((8, functools.partial(back.start, True)))
    for chunk in range(CHUNKS):
        for stage in range(reduce.stages()):
            when = 1 + (chunk + 1) // 2 if stage == 0 else 4 + 3 * chunk + 2 * (stage - 1)
            events.append((when, functools.partial(reduce.event, stage, chunk)))
    run_schedule(head, last, [(0, begin)] + sorted(events, key=lambda event: event[0]))
    local_backward_core(
        nseg, first, mask_ref, q_ref, k_ref, v_ref, g_ref, lse_ref, slope_ref, dqr_ref, out_ref,
        qa, ga, ka, va, dk, dv,
    )

    @pl.when(head == last)
    def _():
        back.finish()
        reduce.finish()


def local_backward_scratch(nseg):
    length = nseg * SEG
    return [
        pltpu.VMEM((64, length), BF16),
        pltpu.VMEM((64, length), BF16),
        pltpu.VMEM((nseg, 64, length), BF16),
        pltpu.VMEM((64, length), BF16),
        pltpu.VMEM((HEAD_DIM, length), F32),
        pltpu.VMEM((HEAD_DIM, length), F32),
    ]


def local_backward_core(
    nseg, first, mask_ref, q_ref, k_ref, v_ref, g_ref, lse_ref, slope_ref, dqr_ref, out_ref,
    qa, ga, ka, va, dk, dv,
):
    head = pl.program_id(0)
    length = nseg * SEG
    keep = local_keep(mask_ref[0], length)
    qa[...] = join(q_ref[0], query_rows(head, length, neg_total(lse_ref[0], keep)))
    ga[...] = grad_rows(g_ref[...], slope_ref[0])
    va[...] = join(v_ref[0], value_rows(length))
    ka[0] = join(k_ref[0], key_rows(head, 0, 4, length, keep))
    if nseg == 2:
        ka[1] = join(k_ref[0], key_rows(head, 1, 4, length, keep))
    items, sides, written = [], [], set()
    for seg in range(nseg):
        lanes = slice(seg * SEG, (seg + 1) * SEG)
        tiles = [
            ((seg, i), slice(seg * SEG + BACK_KEYS * i, seg * SEG + BACK_KEYS * (i + 1)))
            for i in range(SEG // BACK_KEYS)
        ]
        sides.append(sides_of(qa[:, lanes], ga[:, lanes]))
        items += pairs(sides[-1], ka.at[0], va, tiles)
    attend_back(items, dk, dv, written)
    for seg in range(nseg):
        out_ref[0, :, seg * SEG : (seg + 1) * SEG] = joined(sides[seg]) * DQ_SCALE
    if nseg == 2:
        items, sides = [], []
        kept = [pl.ds(kept_start(head, 1, seg), SEG // 2) for seg in range(2)]
        for seg in range(2):
            base = kept_start(head, 1, 1 - seg)
            tile = min(BACK_KEYS, SEG // 2)
            tiles = [
                ((seg, i), pl.ds(pl.multiple_of(base + tile * i, tile), tile)) for i in range(SEG // 2 // tile)
            ]
            sides.append(sides_of(qa[:, kept[seg]], ga[:, kept[seg]]))
            items += pairs(sides[-1], ka.at[1], va, tiles)
        attend_back(items, dk, dv, set(item[4] for item in items))
        for seg in range(2):
            out_ref[0, :, kept[seg]] += joined(sides[seg]) * DQ_SCALE
    size = SEG >> first
    for seg in range(nseg):
        mine = pl.ds(kept_start(head, first, seg), size)
        out_ref[0, :, mine] += dqr_ref[:, seg * size : (seg + 1) * size]
    out_ref[1] = dk[...] * DK_SCALE
    out_ref[2] = dv[...]


def rows_of(total, at, count):
    return total[at : at + count].reshape(count * 16, 128)


def remote_backward(nseg, first, mask_ref, q_ref, g_ref, lse_ref, slope_ref, *refs):
    head = pl.program_id(0)
    levels = range(first, BRANCHES)
    n = len(levels)
    packs = {level: refs[3 * i : 3 * i + 3] for i, level in enumerate(levels)}
    dqr_ref = refs[3 * n]
    outs = {level: refs[3 * n + 1 + i] for i, level in enumerate(levels)}
    qa, ga, ka, va, dk, dv = refs[4 * n + 1 :]
    length = nseg * SEG
    qa[...] = join(q_ref[0], query_rows(head, length, neg_total(lse_ref[0], local_keep(mask_ref[0], length))))
    ga[...] = grad_rows(g_ref[...], slope_ref[0])
    full = SEG >> first
    for group in remote_plan(first):
        for i, level in enumerate(group):
            key, value = remote_keys(head, level, packs[level])
            ka[:, i * 512 : (i + 1) * 512] = key
            va[:, i * 512 : (i + 1) * 512] = value
        size = SEG >> group[0]
        mine = [pl.ds(kept_start(head, group[0], seg), size) for seg in range(nseg)]
        query = jnp.concatenate([qa[:, m] for m in mine], axis=1)
        grad = jnp.concatenate([ga[:, m] for m in mine], axis=1)
        tile = min(BACK_KEYS, 512)
        tiles = [(i, slice(tile * i, tile * (i + 1))) for i in range(512 // tile * len(group))]
        sides = sides_of(query, grad)
        attend_back(pairs(sides, ka, va, tiles), dk, dv, set())
        dq = joined(sides) * DQ_SCALE
        for seg in range(nseg):
            piece = dq[:, seg * size : (seg + 1) * size]
            if group[0] == first:
                dqr_ref[:, seg * full : (seg + 1) * full] = piece
            else:
                inner = (reversed_bits(head) >> (4 - group[0])) & ((1 << (group[0] - first)) - 1)
                lanes = pl.ds(pl.multiple_of(seg * full + inner * size, 128), size)
                dqr_ref[:, lanes] += piece
        for i, level in enumerate(group):
            pieces, _, _, size = outs[level].shape
            for piece in range(pieces):
                lanes = slice(i * 512 + piece * size, i * 512 + (piece + 1) * size)
                outs[level][piece, 0] = (dk[:, lanes] * DK_SCALE).astype(BF16)
                outs[level][piece, 1] = dv[:, lanes].astype(BF16)


def row_block(length):
    return pl.BlockSpec((1, 1, length), lambda h: (h, 0, 0))


def head_block(length):
    return pl.BlockSpec((HEAD_DIM, length), lambda h: (h, 0))


def part_block(part, length):
    return pl.BlockSpec((1, HEAD_DIM, length), lambda h: (part, h, 0))


MASK_BLOCK = pl.BlockSpec(memory_space=pltpu.SMEM)


def pack_specs(pack):
    group, _, length = pack.shape
    return [
        pl.BlockSpec((group, HEAD_DIM, length), lambda h: (0, h, 0)),
        pl.BlockSpec((group, HEAD_DIM, length), lambda h: (0, HEADS + h, 0)),
        pl.BlockSpec((group, 16, length), lambda h: (0, 2 * D // 16, 0)),
    ]


ANY_BLOCK = pl.BlockSpec(memory_space=pl.ANY)


def sems(count):
    return pltpu.SemaphoreType.DMA((count,))


def talking(collective_id, mebibytes=56):
    return pltpu.CompilerParams(
        vmem_limit_bytes=mebibytes * 1024 * 1024, collective_id=collective_id, has_side_effects=True
    )


PARAMS = pltpu.CompilerParams(vmem_limit_bytes=VMEM_LIMIT)


def shape(dims, dtype):
    return jax.ShapeDtypeStruct(dims, dtype)


def cost(seconds):
    return pl.CostEstimate(flops=int(seconds * 1.1e15), transcendentals=0, bytes_accessed=0)


def call_local_forward(nseg, first, qkv, mask, packs):
    length = nseg * SEG
    n = len(packs)
    groups = [(SEG << (level - 1)) // length for level in range(first, BRANCHES)]
    hops = sum(group.bit_length() for group in groups)
    o_part, l_part, m_part, *gathered = pl.pallas_call(
        functools.partial(local_forward, nseg, first),
        grid=(HEADS,),
        in_specs=[MASK_BLOCK, part_block(0, length), part_block(1, length), part_block(2, length)]
        + [ANY_BLOCK] * n,
        out_specs=[head_block(length), row_block(length), row_block(length)] + [ANY_BLOCK] * n,
        out_shape=[shape((D, length), F32), shape((HEADS, 1, length), F32), shape((HEADS, 1, length), F32)]
        + [shape((group,) + pack.shape, BF16) for group, pack in zip(groups, packs)],
        scratch_shapes=local_forward_scratch(nseg)
        + [
            sems(hops),
            sems(hops),
        ],
        compiler_params=talking(1),
        cost_estimate=cost(nseg * 37e-6),
        name="local_forward",
    )(mask, qkv, qkv, qkv, *packs)
    return o_part, l_part, m_part, gathered


def call_remote_forward(nseg, first, qkv, mask, o_part, l_part, m_part, packs):
    length = nseg * SEG
    args, specs = [], []
    for pack in packs:
        args += [pack] * 3
        specs += pack_specs(pack)
    return pl.pallas_call(
        functools.partial(remote_forward, nseg, first),
        grid=(HEADS,),
        in_specs=[MASK_BLOCK, part_block(0, length), head_block(length), row_block(length), row_block(length)]
        + specs,
        out_specs=[head_block(length), row_block(length)],
        out_shape=[shape((D, length), BF16), shape((HEADS, 1, length), F32)],
        scratch_shapes=[
            pltpu.VMEM((HEAD_DIM, length), F32),
            pltpu.VMEM((1, 1, length), F32),
            pltpu.VMEM((1, 1, length), F32),
            pltpu.VMEM((64, length), BF16),
        ],
        compiler_params=PARAMS,
        cost_estimate=cost(nseg * 24e-6),
        name="remote_forward",
    )(mask, qkv, o_part, l_part, m_part, *args)


def call_remote_backward(nseg, first, qkv, grad, lse, slope, mask, packs):
    length = nseg * SEG
    args, specs = [], []
    for pack in packs:
        args += [pack] * 3
        specs += pack_specs(pack)
    kept = nseg * (SEG >> first)
    return pl.pallas_call(
        functools.partial(remote_backward, nseg, first),
        grid=(HEADS,),
        in_specs=[MASK_BLOCK, part_block(0, length), head_block(length), row_block(length), row_block(length)]
        + specs,
        out_specs=[head_block(kept)]
        + [
            pl.BlockSpec((pack.shape[0], 2, HEAD_DIM, pack.shape[2]), lambda h: (0, 0, h, 0))
            for pack in packs
        ],
        out_shape=[shape((D, kept), F32)]
        + [shape((pack.shape[0], 2, D, pack.shape[2]), BF16) for pack in packs],
        scratch_shapes=[
            pltpu.VMEM((64, length), BF16),
            pltpu.VMEM((64, length), BF16),
            pltpu.VMEM((64, 1024), BF16),
            pltpu.VMEM((64, 1024), BF16),
            pltpu.VMEM((HEAD_DIM, 1024), F32),
            pltpu.VMEM((HEAD_DIM, 1024), F32),
        ],
        compiler_params=PARAMS,
        cost_estimate=cost(nseg * 20e-6),
        name="remote_backward",
    )(mask, qkv, grad, lse, slope, *args)


CHUNKS = 3
FEED_BLOCKS = (4 * D + D + 4 * D) * D // (4 * 16 * 128)
IN_BLOCKS = 3 * D * D // (4 * 16 * 128)


def padded(blocks):
    unit = CHUNKS * lax.axis_size("seq")
    return (blocks + unit - 1) // unit * unit


def reduce_copies():
    return CHUNKS * (3 + seq_bits())


def call_local_backward(nseg, first, qkv, grad, lse, slope, mask, dq_remote, sent, feed_grads):
    length = nseg * SEG
    n = len(sent)
    groups = [part.shape[0] for part in sent]
    hops = sum(group.bit_length() for group in groups)
    blocks = feed_grads.shape[1]
    piece = (CHUNKS, blocks // CHUNKS >> seq_bits(), 16, 128)
    bufs = [pltpu.VMEM((g // 2,) + part.shape[1:], BF16) for g, part in zip(groups, sent) if g > 1]
    recvs = [pltpu.VMEM((g - 1,) + part.shape[1:], BF16) for g, part in zip(groups, sent) if g > 1]
    local, *rest = pl.pallas_call(
        functools.partial(local_backward, nseg, first),
        grid=(HEADS,),
        in_specs=[MASK_BLOCK, part_block(0, length), part_block(1, length), part_block(2, length), head_block(length),
                  row_block(length), row_block(length), head_block(dq_remote.shape[1])]
        + [ANY_BLOCK] * (n + 1),
        out_specs=[pl.BlockSpec((3, HEAD_DIM, length), lambda h: (0, h, 0))]
        + [ANY_BLOCK] * n
        + [const_block(piece)],
        out_shape=[shape((3, D, length), F32)]
        + [shape(part.shape[1:], BF16) for part in sent]
        + [shape(piece, BF16)],
        scratch_shapes=local_backward_scratch(nseg)
        + bufs
        + recvs
        + [
            pltpu.VMEM((2, blocks, 16, 128), BF16),
            pltpu.VMEM((2, blocks, 16, 128), BF16),
            pltpu.VMEM((blocks, 16, 128), BF16),
            pltpu.VMEM((blocks, 16, 128), BF16),
            sems(hops),
            sems(hops),
            sems(n),
            sems(reduce_copies()),
            sems(reduce_copies()),
            sems(2 * CHUNKS),
        ],
        compiler_params=talking(2),
        cost_estimate=cost(nseg * 72e-6),
        name="local_backward",
    )(mask, qkv, qkv, qkv, grad, lse, slope, dq_remote, *sent, feed_grads)
    return local, rest[:n], rest[n]


HALF = D // 2


def const_block(dims):
    return pl.BlockSpec(dims, lambda i: (0,) * len(dims), pipeline_mode=pl.Buffered(1))


def rev4(value):
    return int(reversed_bits(value))


TILES = D // 128


def put_rows(tiled, start, array):
    for tile in range(TILES):
        tiled[tile, start : start + array.shape[0], :] = array[:, tile * 128 : (tile + 1) * 128]


def get_rows(tiled, start, size):
    return jnp.concatenate([tiled[tile, start : start + size, :] for tile in range(TILES)], axis=1)


def get_residue(tiled, start):
    return jnp.concatenate(
        [tiled[tile, pl.ds(start, RUN, stride=RES), :] for tile in range(TILES)], axis=1
    )


def put_residue(tiled, start, array):
    for tile in range(TILES):
        tiled[tile, pl.ds(start, RUN, stride=RES), :] = array[:, tile * 128 : (tile + 1) * 128]


COLUMN_CHUNKS = 3


def project_kernel(nseg, first, mask_ref, tok_ref, *refs):
    n = BRANCHES - first
    vectors, w_ref = refs[:4], refs[4]
    qkv_ref, xp_ref, inner_ref, weight_ref, gains_ref = refs[5:10]
    packs = refs[10 : 10 + n]
    xs, weight, gains, vec_send, vec_recv, w_send, w_recv, w_load, w_store = refs[10 + n :]
    step = pl.program_id(0)
    last = pl.num_programs(0) - 1
    me = lax.axis_index("fsdp")
    sibling = me + 1 - 2 * lax.rem(me, 2)
    across = lax.rem(me + 2, 4)
    sends = Sends(w_send, w_recv)

    def send(source, target, key, other):
        index = sends.made.setdefault(key, len(sends.made))
        return pltpu.make_async_remote_copy(
            src_ref=source, dst_ref=target, send_sem=w_send.at[index], recv_sem=w_recv.at[index],
            device_id={"fsdp": other}, device_id_type=pl.DeviceIdType.MESH,
        )

    def chunk_copies(chunk):
        cols = pl.ds(chunk * D, D)
        mine = w_ref.at[:, cols]
        load = pltpu.make_async_copy(mine, weight.at[me, :, cols], w_load.at[chunk])
        core = send(mine, weight.at[me, :, cols], ("core", chunk), sibling)
        x = send(mine, weight.at[me, :, cols], ("x", chunk), across)
        handed = weight.at[across, :, cols]
        return load, core, x, send(handed, handed, ("hand", chunk), sibling)

    def vec_copies():
        return [
            pltpu.make_async_remote_copy(
                src_ref=gains.at[me], dst_ref=gains.at[me], send_sem=vec_send.at[i], recv_sem=vec_recv.at[i],
                device_id={"fsdp": other}, device_id_type=pl.DeviceIdType.MESH,
            )
            for i, other in enumerate((sibling, across, 3 - me))
        ]

    store = pltpu.make_async_copy(weight, weight_ref, w_store.at[0])

    @pl.when(step == 0)
    def _():
        barrier = pltpu.get_barrier_semaphore()
        for other in (sibling, across, 3 - me):
            pl.semaphore_signal(
                barrier, inc=1, device_id={"fsdp": other}, device_id_type=pl.DeviceIdType.MESH
            )
        for i, vector in enumerate(vectors):
            gains[me, i : i + 1, :192] = vector[...].astype(F32)
        pl.semaphore_wait(barrier, 3)
        for copy in vec_copies():
            copy.start()
        for chunk in range(COLUMN_CHUNKS):
            for copy in chunk_copies(chunk)[:3]:
                copy.start()
        for copy in vec_copies():
            copy.wait_recv()
        full = [
            jnp.concatenate([gains[owner, i : i + 1, :192] for owner in range(4)], axis=1) for i in range(4)
        ]
        gains_ref[...] = jnp.concatenate(full + [jnp.zeros((4, D), F32)], axis=0)
        for seg in range(nseg):
            put_rows(xs, 0, tok_ref[seg * SEG : (seg + 1) * SEG, :].astype(F32))
            for pair in range(RES // 2):
                rows = jnp.concatenate([get_residue(xs, rev4(2 * pair + i)) for i in range(2)], axis=0)
                normed = normalize(rows, full[0], full[1])[0].astype(BF16)
                at = slice(seg * SEG + pair * 2 * RUN, seg * SEG + (pair + 1) * 2 * RUN)
                xp_ref[at, :] = rows.astype(BF16)
                inner_ref[:, at] = normed.T
        for pack, level in zip(packs, range(first, BRANCHES)):
            pack[2 * D :, :] = packed_keep(mask_ref[0], level, nseg)

    for chunk in range(COLUMN_CHUNKS):

        @pl.when(step == 2 * chunk)
        def _():
            load, core, x, hand = chunk_copies(chunk)
            x.wait_recv()
            hand.start()
            load.wait()
            core.wait_recv()
            hand.wait_recv()

    @pl.when(step == 4)
    def _():
        store.start()

    cols = pl.ds(pl.multiple_of(step * HALF, HALF), HALF)
    block = jnp.concatenate([weight[owner, :, cols] for owner in range(4)], axis=0)
    scale = jnp.where(step < 2, QUERY_SCALE, 1.0)
    for start in range(0, nseg * SEG, 512):
        lanes = slice(start, start + 512)
        qkv_ref[0, :, lanes] = (dotg(block, inner_ref[:, lanes], 0, 0) * scale).astype(BF16)

    @pl.when(step >= 2)
    def _():
        upper = lax.rem(step, 2) == 1
        for pack, level in zip(packs, range(first, BRANCHES)):
            size = SEG >> level
            for head in range(HEADS // 2):
                rows = slice(head * HEAD_DIM, (head + 1) * HEAD_DIM)
                pieces = []
                for seg in range(nseg):
                    start = seg * SEG + (rev4(head) >> (4 - level)) * size
                    if level < 4:
                        pieces.append(qkv_ref[0, rows, start : start + size])
                    else:
                        both = qkv_ref[0, rows, start : start + 2 * size]
                        pieces.append(jnp.where(upper, both[:, size:], both[:, :size]))
                into = pl.ds(pl.multiple_of((step - 2) * HALF + head * HEAD_DIM, 16), HEAD_DIM)
                pack[into, :] = jnp.concatenate(pieces, axis=1) if nseg > 1 else pieces[0]

    @pl.when(step == last)
    def _():
        for copy in vec_copies():
            copy.wait_send()
        for chunk in range(COLUMN_CHUNKS):
            for copy in chunk_copies(chunk)[1:]:
                copy.wait_send()
        store.wait()


def call_project(nseg, first, mask, tokens, vectors, weight):
    length = nseg * SEG
    kept = [nseg * (SEG >> level) for level in range(first, BRANCHES)]
    return pl.pallas_call(
        functools.partial(project_kernel, nseg, first),
        grid=(6,),
        in_specs=[MASK_BLOCK, const_block((length, D))] + [const_block((1, 192))] * 4 + [ANY_BLOCK],
        out_specs=[
            pl.BlockSpec((1, HALF, length), lambda i: (i // 2, i % 2, 0)),
            const_block((length, D)),
            const_block((D, length)),
            ANY_BLOCK,
            const_block((8, D)),
        ]
        + [const_block((2 * D + 16, size)) for size in kept],
        out_shape=[
            shape((3, D, length), BF16),
            shape((length, D), BF16),
            shape((D, length), BF16),
            shape((4, 192, 3 * D), BF16),
            shape((8, D), F32),
        ]
        + [shape((2 * D + 16, size), BF16) for size in kept],
        scratch_shapes=[
            pltpu.VMEM((TILES, SEG, 128), F32),
            pltpu.VMEM((4, 192, 3 * D), BF16),
            pltpu.VMEM((4, 8, 256), F32),
            sems(3),
            sems(3),
            sems(3 * COLUMN_CHUNKS),
            sems(3 * COLUMN_CHUNKS),
            sems(COLUMN_CHUNKS),
            sems(1),
        ],
        compiler_params=talking(4),
        cost_estimate=cost(nseg * 10e-6),
        name="project",
    )(mask, tokens, *vectors, weight)


ROWS = 256


def blocks_of(ref, rows, col):
    part = ref[rows, col * 128 : (col + 1) * 128].astype(BF16)
    return part.reshape(part.shape[0] // 16, 16, 128)


def feed_kernel(
    nseg, mask_ref, att_ref, x_ref, cot_ref, wout_ref, up_ref, down_ref, gains_ref,
    mixed_ref, gmid_ref, gm_ref, along_ref, vec_ref, grads_ref,
    cs, out_acc, up_acc, down_acc, stage, sems,
):
    step = pl.program_id(0)
    quarter = lax.rem(step, 4)
    low = (quarter >> 1) | ((quarter & 1) << 1)

    @pl.when(step == 0)
    def _():
        out_acc[...] = jnp.zeros_like(out_acc)
        up_acc[...] = jnp.zeros_like(up_acc)
        down_acc[...] = jnp.zeros_like(down_acc)
        vec_ref[...] = jnp.zeros_like(vec_ref)

    @pl.when(quarter == 0)
    def _():
        put_rows(cs, 0, cot_ref[...].astype(F32))

    grad = jnp.concatenate([get_residue(cs, rev4(i) + low) for i in range(4)], axis=0)
    grad_b = grad.astype(BF16)
    att = att_ref[...]
    middle = x_ref[...].astype(F32) + dotg(att, wout_ref[...], 0, 0)
    gain = gains_ref[2:3, :]
    normed, unit, inverse = normalize(middle, gain, gains_ref[3:4, :])
    hidden = normed.astype(BF16)
    hidden_t = hidden.T
    final = middle
    grad_hidden = jnp.zeros((ROWS, D), F32)
    for start in range(0, 4 * D, D):
        cols = slice(start, start + D)
        upper = dotg(hidden, up_ref[:, cols], 1, 0)
        grad_active = dotg(grad_b, down_ref[cols, :], 1, 1)
        half = 0.5 * (1.0 + lax.erf(upper * ROOT_HALF))
        slope = half + upper * jnp.exp(-0.5 * upper * upper) * INV_ROOT_TWO_PI
        active = (upper * half).astype(BF16)
        grad_upper = (grad_active * slope).astype(BF16)
        final = final + dotg(active, down_ref[cols, :], 1, 0)
        grad_hidden = grad_hidden + dotg(grad_upper, up_ref[:, cols], 1, 1)
        up_acc[:, cols] += dotg(hidden_t, grad_upper, 1, 0)
        down_acc[cols, :] += dotg(active, grad_b, 0, 0)
    for i in range(4):
        put_residue(cs, rev4(i) + low, final[i * RUN : (i + 1) * RUN])

    @pl.when(quarter == 3)
    def _():
        mixed_ref[...] = get_rows(cs, 0, SEG).astype(BF16)

    back, gain_back, shift_back = normalize_back(grad_hidden, unit, inverse, gain)
    vec_ref[0:1, :] += gain_back[None, :]
    vec_ref[1:2, :] += shift_back[None, :]
    grad_middle = grad + back
    gmid_ref[...] = grad_middle
    branch = grad_middle.astype(BF16)
    out_acc[...] += dotg(att, branch, 1, 0)
    lane = lax.broadcasted_iota(jnp.int32, (1, ROWS), 1)
    position = step // 4 * SEG + lax.rem(lane, RUN) * RES + residue_of(lane // RUN) + low
    keep = position < mask_ref[0]
    merged = jnp.where(keep, dotg(wout_ref[...], branch, 1, 1), 0.0).astype(BF16)
    gm_ref[...] = merged
    product = merged.astype(F32) * att.astype(F32)
    for head in range(HEADS):
        rows = slice(head * HEAD_DIM, (head + 1) * HEAD_DIM)
        along_ref[head] = jnp.sum(product[rows], axis=0, keepdims=True)

    @pl.when(step == pl.num_programs(0) - 1)
    def _():
        copies = []
        for owner in range(4):
            for piece in range(3):
                count = owner * 3 + piece
                slot = count % 2
                if count >= 2:
                    copies[count - 2].wait()
                if piece == 0:
                    rows, offset, size = slice(owner * 192, (owner + 1) * 192), 0, 288
                    for col in range(4 * TILES):
                        stage[slot, col * 12 : (col + 1) * 12] = blocks_of(up_acc, rows, col)
                elif piece == 1:
                    rows, offset, size = slice(owner * 192, (owner + 1) * 192), 288, 72
                    for col in range(TILES):
                        stage[slot, col * 12 : (col + 1) * 12] = blocks_of(out_acc, rows, col)
                else:
                    rows, offset, size = slice(owner * D, (owner + 1) * D), 360, 288
                    for col in range(TILES):
                        stage[slot, col * 48 : (col + 1) * 48] = blocks_of(down_acc, rows, col)
                copy = pltpu.make_async_copy(
                    stage.at[slot, pl.ds(0, size)],
                    grads_ref.at[owner, pl.ds(offset, size)],
                    sems.at[slot],
                )
                copy.start()
                copies.append(copy)
        copies[-2].wait()
        copies[-1].wait()


def call_feed(nseg, mask, att, x, cot, wout, up, down, gains):
    length = nseg * SEG
    return pl.pallas_call(
        functools.partial(feed_kernel, nseg),
        grid=(length // ROWS,),
        in_specs=[
            MASK_BLOCK,
            pl.BlockSpec((D, ROWS), lambda i: (0, i)),
            pl.BlockSpec((ROWS, D), lambda i: (i, 0)),
            pl.BlockSpec((SEG, D), lambda i: (i // 4, 0)),
            const_block((D, D)),
            const_block((D, 4 * D)),
            const_block((4 * D, D)),
            const_block((8, D)),
        ],
        out_specs=[
            pl.BlockSpec((SEG, D), lambda i: (i // 4, 0)),
            pl.BlockSpec((ROWS, D), lambda i: (i, 0)),
            pl.BlockSpec((D, ROWS), lambda i: (0, i)),
            pl.BlockSpec((HEADS, 1, ROWS), lambda i: (0, 0, i)),
            pl.BlockSpec((2, D), lambda i: (0, 0)),
            pl.BlockSpec(memory_space=pl.ANY),
        ],
        out_shape=[
            shape((length, D), BF16),
            shape((length, D), F32),
            shape((D, length), BF16),
            shape((HEADS, 1, length), F32),
            shape((2, D), F32),
            shape((4, padded(FEED_BLOCKS), 16, 128), BF16),
        ],
        scratch_shapes=[
            pltpu.VMEM((TILES, SEG, 128), F32),
            pltpu.VMEM((D, D), F32),
            pltpu.VMEM((D, 4 * D), F32),
            pltpu.VMEM((4 * D, D), F32),
            pltpu.VMEM((2, 288, 16, 128), BF16),
            pltpu.SemaphoreType.DMA((2,)),
        ],
        compiler_params=pltpu.CompilerParams(vmem_limit_bytes=62 * 1024 * 1024),
        cost_estimate=cost(nseg * 45e-6),
        name="feed",
    )(mask, att, x, cot, wout, up, down, gains)


STEPS = 6


def inner_back_kernel(
    nseg, first, local_ref, inner_ref, w_ref, x_ref, gmid_ref, gain_ref, feed_vec_ref, piece_ref, *refs
):
    n = BRANCHES - first
    packs, (weight_ref, back_ref, vec_ref, up_ref, proj_ref, down_ref) = refs[:n], refs[n : n + 6]
    acc, mixed, order, terms, recv_core, recv_x, recv_seq, total, feed_total, vecs, vec_recv = refs[n + 6 : n + 17]
    red_send, red_recv, in_send, in_recv, feed_send, feed_recv, vec_send, vec_recv_sems = refs[n + 17 :]
    step = pl.program_id(0)
    last = pl.num_programs(0) - 1
    length = nseg * SEG
    turns = length // ROWS
    end = STEPS + turns
    blocks = terms.shape[1] // CHUNKS
    core = lax.rem(lax.axis_index("fsdp"), 2)
    spread = Spread(blocks, total, Sends(in_send, in_recv))
    reduce = Reduce(
        blocks, terms, terms, lambda xo: 2 * xo + core, recv_core, recv_x, recv_seq, Sends(red_send, red_recv),
        spread.begin,
    )
    feed_spread = Spread(feed_total.shape[0] // CHUNKS, feed_total, Sends(feed_send, feed_recv))
    vec_sends = Sends(vec_send, vec_recv_sems)
    peers = all_peers()

    def vec_copy(i):
        return vec_sends.copy(i, vecs.at[i], vec_recv.at[i], *peers[i])

    def vec_event(i):
        vec_copy(i).wait_recv()
        vecs[i + 1] = vecs[i] + vec_recv[i]
        if i + 1 < len(peers):
            vec_copy(i + 1).start()

    def vec_start():
        vec_copy(0).start()

    @pl.when(step == 0)
    def _():
        meet(peers)
        vecs[0] = jnp.concatenate([jnp.zeros((2, D), F32), feed_vec_ref[...], jnp.zeros((4, D), F32)], axis=0)
        for chunk in reversed(range(CHUNKS)):
            feed_spread.begin(chunk, piece_ref.at[chunk], 0)

    @pl.when((step >= 2) & (step < STEPS))
    def _():
        upper = lax.rem(step, 2) == 1
        for pack, level in zip(packs, range(first, BRANCHES)):
            size = SEG >> level
            for head in range(HEADS // 2):
                rows = slice(head * HEAD_DIM, (head + 1) * HEAD_DIM)
                for seg in range(nseg):
                    start = seg * SEG + (rev4(head) >> (4 - level)) * size
                    piece = pack[0, rows, seg * size : (seg + 1) * size].astype(F32)
                    if level == 4:
                        zero = jnp.zeros_like(piece)
                        piece = jnp.concatenate(
                            [jnp.where(upper, zero, piece), jnp.where(upper, piece, zero)], axis=1
                        )
                    local_ref[0, rows, start : start + piece.shape[1]] += piece

    @pl.when(step < STEPS)
    def _():
        block = local_ref[0].astype(BF16)
        mixed[pl.ds(pl.multiple_of(step * HALF, HALF), HALF), :] = block
        base = lax.div(step, 2) * blocks + lax.rem(step, 2) * 36
        grad_in = dotg(block, inner_ref[...], 1, 1).T.astype(BF16)
        for col in range(3):
            part = grad_in[:, col * 128 : (col + 1) * 128].reshape(4, 12, 16, 128)
            for owner in range(4):
                terms[owner, pl.ds(base + col * 12, 12)] = part[owner]

    def inner_grad(turn):
        lanes = pl.ds(pl.multiple_of(turn * ROWS, ROWS), ROWS)
        acc[lax.rem(turn, 2)] = dotg(w_ref[...], mixed[:, lanes], 1, 0)

    @pl.when(step == STEPS - 1)
    def _():
        inner_grad(step - (STEPS - 1))

    @pl.when((step >= STEPS) & (step < end))
    def _():
        turn = step - STEPS
        inner_grad(lax.rem(turn + 1, turns))
        quarter = lax.rem(turn, 4)
        low = (quarter >> 1) | ((quarter & 1) << 1)
        gain = gain_ref[0:1, :]
        grad = acc[lax.rem(turn, 2)].T
        _, unit, inverse = normalize(x_ref[...].astype(F32), gain, gain)
        back, gain_part, shift_part = normalize_back(grad, unit, inverse, gain)
        vecs[0, 0:1, :] += gain_part[None, :]
        vecs[0, 1:2, :] += shift_part[None, :]
        total_back = gmid_ref[...] + back
        for i in range(4):
            put_residue(order, rev4(i) + low, total_back[i * RUN : (i + 1) * RUN])

        @pl.when(quarter == 3)
        def _():
            back_ref[...] = get_rows(order, 0, SEG)

    events = []
    for chunk in range(CHUNKS):
        for stage in range(feed_spread.stages()):
            events.append((1 + stage, functools.partial(feed_spread.event, stage, chunk)))
    for chunk in range(CHUNKS):
        begin = 2 * chunk + 1
        events.append((begin, functools.partial(reduce.begin, chunk)))
        for stage in range(reduce.stages()):
            when = begin + 1 + (0 if stage == 0 else 3 * chunk + 2 * stage)
            events.append((when, functools.partial(reduce.event, stage, chunk)))
        for stage in range(spread.stages()):
            when = begin + 2 * reduce.stages() + 3 * chunk + 2 * stage
            events.append((when, functools.partial(spread.event, stage, chunk)))
    events.append((end - 1, vec_start))
    for i in range(len(peers)):
        events.append((end + i, functools.partial(vec_event, i)))
    run_schedule(step, last, sorted(events, key=lambda event: event[0]))

    @pl.when(step == end - 2)
    def _():
        for tile in range(TILES):
            cols = slice(tile * 128, (tile + 1) * 128)
            for col in range(4):
                at = col * 72 + tile * 12
                up_ref[:, col * D + tile * 128 : col * D + (tile + 1) * 128] = rows_of(feed_total, at, 12)
            proj_ref[:, cols] = rows_of(feed_total, 288 + tile * 12, 12)
            down_ref[:, cols] = rows_of(feed_total, 360 + tile * 48, 48)

    @pl.when(step == last)
    def _():
        reduce.finish()
        spread.finish()
        feed_spread.finish()
        for i in range(len(peers)):
            vec_copy(i).wait_send()
        vec_ref[...] = vecs[len(peers)]
        for part in range(STEPS):
            for col in range(3):
                at = part // 2 * blocks + part % 2 * 36 + col * 12
                weight_ref[:, part * HALF + col * 128 : part * HALF + (col + 1) * 128] = rows_of(total, at, 12)


def call_inner_back(nseg, first, local, inner, weight, x, gmid, gain, feed_vec, pieces, packs):
    length = nseg * SEG
    turns = length // ROWS
    blocks = padded(IN_BLOCKS)
    if blocks // CHUNKS < 72:
        raise ValueError("blocks")
    bits = seq_bits()
    peers = 2 + bits
    feed_blocks = CHUNKS * (pieces.shape[1] << bits)

    def at(i):
        return jnp.minimum(i, STEPS - 1)

    def turn(i):
        return jnp.clip(i - STEPS, 0, turns - 1)

    return pl.pallas_call(
        functools.partial(inner_back_kernel, nseg, first),
        grid=(STEPS + turns + 1,),
        in_specs=[
            pl.BlockSpec((1, HALF, length), lambda i: (at(i) // 2, at(i) % 2, 0)),
            const_block((D, length)),
            const_block((D, 3 * D)),
            pl.BlockSpec((ROWS, D), lambda i: (turn(i), 0)),
            pl.BlockSpec((ROWS, D), lambda i: (turn(i), 0)),
            const_block((8, D)),
            const_block((2, D)),
            const_block(pieces.shape),
        ]
        + [
            pl.BlockSpec((1, HALF, pack.shape[2]), lambda i: (jnp.maximum(at(i) // 2 - 1, 0), at(i) % 2, 0))
            for pack in packs
        ],
        out_specs=[
            const_block((192, 3 * D)),
            pl.BlockSpec((SEG, D), lambda i: (turn(i) // 4, 0)),
            const_block((8, D)),
            const_block((192, 4 * D)),
            const_block((192, D)),
            const_block((D, D)),
        ],
        out_shape=[
            shape((192, 3 * D), BF16),
            shape((length, D), F32),
            shape((8, D), F32),
            shape((192, 4 * D), BF16),
            shape((192, D), BF16),
            shape((D, D), BF16),
        ],
        scratch_shapes=[
            pltpu.VMEM((2, D, ROWS), F32),
            pltpu.VMEM((3 * D, length), BF16),
            pltpu.VMEM((TILES, SEG, 128), F32),
            pltpu.VMEM((4, blocks, 16, 128), BF16),
            pltpu.VMEM((2, blocks, 16, 128), BF16),
            pltpu.VMEM((blocks, 16, 128), BF16),
            pltpu.VMEM((blocks, 16, 128), BF16),
            pltpu.VMEM((blocks, 16, 128), BF16),
            pltpu.VMEM((feed_blocks, 16, 128), BF16),
            pltpu.VMEM((peers + 1, 8, D), F32),
            pltpu.VMEM((peers, 8, D), F32),
            sems(reduce_copies()),
            sems(reduce_copies()),
            sems(CHUNKS * bits),
            sems(CHUNKS * bits),
            sems(CHUNKS * bits),
            sems(CHUNKS * bits),
            sems(peers),
            sems(peers),
        ],
        compiler_params=talking(3, 60),
        cost_estimate=cost(nseg * 15e-6),
        name="inner_back",
    )(local, inner, weight, x, gmid, gain, feed_vec, pieces, *packs)


def per_device(
    tokens,
    first_gain,
    first_shift,
    project_in,
    project_out,
    second_gain,
    second_shift,
    up_weight,
    down_weight,
    valid_mask,
    cotangent,
):
    length = tokens.shape[1]
    nseg = length // SEG
    first = nseg.bit_length()

    def gather(weight):
        return lax.all_gather(weight, "fsdp", axis=0, tiled=True)

    mask = jnp.sum(valid_mask[0])[None]

    vectors = [vector[None, :] for vector in (first_gain, first_shift, second_gain, second_shift)]
    qkv, x, inner, weight_in, gains, *packs = call_project(nseg, first, mask, tokens[0], vectors, project_in)
    weight_in = weight_in.reshape(D, 3 * D)
    _, *shards = lax.optimization_barrier((gains, project_out, up_weight, down_weight))
    weight_out, weight_up, weight_down = (gather(shard) for shard in shards)
    o_part, l_part, m_part, gathered = call_local_forward(nseg, first, qkv, mask, packs)
    attended, lse = call_remote_forward(nseg, first, qkv, mask, o_part, l_part, m_part, gathered)

    mixed, grad_middle, grad_merged, along, feed_vec, feed_grads = call_feed(
        nseg, mask, attended, x, cotangent[0], weight_out, weight_up, weight_down, gains
    )

    dq_remote, *sent = call_remote_backward(nseg, first, qkv, grad_merged, lse, along, mask, gathered)
    local, returned, pieces = call_local_backward(
        nseg, first, qkv, grad_merged, lse, along, mask, dq_remote, sent, feed_grads
    )
    grad_in, tokens_back, vectors, grad_up, grad_out, grad_down = call_inner_back(
        nseg, first, local, inner, weight_in, x, grad_middle, gains, feed_vec, pieces, returned
    )
    quarter = D // lax.axis_size("fsdp")
    vectors = lax.dynamic_slice_in_dim(vectors, lax.axis_index("fsdp") * quarter, quarter, 1)
    return (
        mixed[None],
        tokens_back[None],
        vectors[0],
        vectors[1],
        grad_in.astype(F32),
        grad_out.astype(F32),
        vectors[2],
        vectors[3],
        grad_up.astype(F32),
        grad_down.astype(F32),
    )


def solution(mesh):
    in_specs = (
        P("fsdp", "seq", None),
        P("fsdp"),
        P("fsdp"),
        P("fsdp", None),
        P("fsdp", None),
        P("fsdp"),
        P("fsdp"),
        P("fsdp", None),
        P("fsdp", None),
        P("fsdp", "seq"),
        P("fsdp", "seq", None),
    )
    out_specs = (
        P("fsdp", "seq", None),
        P("fsdp", "seq", None),
        P("fsdp"),
        P("fsdp"),
        P("fsdp", None),
        P("fsdp", None),
        P("fsdp"),
        P("fsdp"),
        P("fsdp", None),
        P("fsdp", None),
    )
    return jax.shard_map(
        per_device, mesh=mesh, in_specs=in_specs, out_specs=out_specs, check_vma=False
    )
```

```python
import functools
import math

import jax
import jax.numpy as jnp
import ml_dtypes
import numpy as np
from jax import lax
from jax.experimental import pallas as pl
from jax.experimental.pallas import tpu as pltpu
from jax.sharding import PartitionSpec as P

HEADS = 16
HEAD_DIM = 48
SEG = 1024
BRANCHES = 5
RES = 16
RUN = SEG // RES
D = HEADS * HEAD_DIM

EPS = 1e-05
NEG = -1e30
ROOT_HALF = 0.7071067811865476
INV_ROOT_TWO_PI = 0.3989422804014327
F32 = jnp.float32
BF16 = jnp.bfloat16
QUERY_SCALE = math.log2(math.e) * HEAD_DIM ** (-0.5)
VMEM_LIMIT = 56 * 1024 * 1024


def dotg(left, right, left_dim, right_dim):
    return lax.dot_general(
        left, right, (((left_dim,), (right_dim,)), ((), ())), preferred_element_type=F32
    )


def normalize(values, gain, shift):
    mean = jnp.mean(values, axis=-1, keepdims=True)
    centred = values - mean
    spread = jnp.mean(centred * centred, axis=-1, keepdims=True)
    inverse = lax.rsqrt(spread + EPS)
    normed = centred * inverse
    return (normed * gain + shift, normed, inverse)


def normalize_back(grad, normed, inverse, gain):
    scaled = grad * gain
    first = jnp.mean(scaled, axis=-1, keepdims=True)
    second = jnp.mean(scaled * normed, axis=-1, keepdims=True)
    return (
        inverse * (scaled - first - normed * second),
        jnp.sum(grad * normed, axis=0),
        jnp.sum(grad, axis=0),
    )


def reversed_bits(head):
    return ((head & 1) << 3) | ((head & 2) << 1) | ((head & 4) >> 1) | ((head & 8) >> 3)


def near_class(head, low_bits, length):
    lane = lax.broadcasted_iota(jnp.int32, (1, length), 1)
    rho = lax.rem(lane // RUN, 1 << low_bits)
    return rho ^ (reversed_bits(head) & ((1 << low_bits) - 1))


def class_rows(near, length):
    row = lax.broadcasted_iota(jnp.int32, (16, length), 0)
    step = lax.rem(row + 3, 4) + 1
    bound = jnp.where((row >= 5) & (row <= 12), lax.shift_right_logical(RES, step), 0)
    return row, near < bound


def query_rows(head, length, neg_lse=None):
    near = near_class(head, 4, length)
    row, inside = class_rows(near, length)
    out = jnp.where(inside, 1.0, 0.0)
    out = jnp.where(row == 0, 1.0, out)
    out = jnp.where(row == 4, jnp.where(near < 1, 0.0, NEG), out)
    if neg_lse is not None:
        high = neg_lse.astype(BF16).astype(F32)
        rest = neg_lse - high
        mid = rest.astype(BF16).astype(F32)
        low = rest - mid
        out = jnp.where(row == 1, high, jnp.where(row == 2, mid, jnp.where(row == 3, low, out)))
    return out.astype(BF16)


def residue_of(rho):
    return reversed_bits(rho)


def local_keep(count, length):
    lane = lax.broadcasted_iota(jnp.int32, (1, length), 1)
    rho = lax.rem(lane // RUN, RES)
    position = lane // SEG * SEG + lax.rem(lane, RUN) * RES + residue_of(rho)
    return position < count


def packed_keep(count, level, nseg):
    size = SEG >> level
    dims = (HEADS, nseg * size)
    head = lax.broadcasted_iota(jnp.int32, dims, 0)
    lane = lax.broadcasted_iota(jnp.int32, dims, 1)
    rho = (reversed_bits(head) >> (4 - level)) * (size // RUN) + lax.rem(lane, size) // RUN
    position = lane // size * SEG + lax.rem(lane, RUN) * RES + residue_of(rho)
    return jnp.where(position < count, 1.0, 0.0).astype(BF16)


def weight_of(level, step):
    return math.log2((step - level + 1) / (step - level)) if step > level else 0.0


def key_rows(head, level, low_bits, length, keep):
    near = near_class(head, low_bits, length)
    row, inside = class_rows(near, length)
    weight = jnp.zeros((16, length), F32)
    for step in range(level + 1, BRANCHES):
        value = weight_of(level, step)
        high = float(np.asarray(value, ml_dtypes.bfloat16))
        weight = jnp.where(row == 4 + step, high, weight)
        weight = jnp.where(row == 8 + step, value - high, weight)
    out = jnp.where(inside, weight, 0.0)
    out = jnp.where((row >= 1) & (row <= 3), 1.0, out)
    out = jnp.where(row == 0, jnp.where(keep, 0.0, NEG), out)
    if level == BRANCHES - 1:
        out = jnp.where(row == 4, 1.0, out)
    return out.astype(BF16)


def value_rows(length):
    row = lax.broadcasted_iota(jnp.int32, (16, length), 0)
    return jnp.where(row < 2, 1.0, 0.0).astype(BF16)


def join(rows, extra):
    return jnp.concatenate([rows, extra], axis=0)


def kept_start(head, level, seg):
    size = SEG >> level
    block = reversed_bits(head) >> (4 - level)
    return pl.multiple_of(seg * SEG + block * size, min(size, 128))


def partner(axis, distance):
    place = lax.axis_index(axis)
    return {axis: place + distance * (1 - 2 * lax.rem(lax.div(place, distance), 2))}


def seq_bits():
    return lax.axis_size("seq").bit_length() - 1


def meet(peers):
    barrier = pltpu.get_barrier_semaphore()
    for axis, distance in peers:
        pl.semaphore_signal(
            barrier, inc=1, device_id=partner(axis, distance), device_id_type=pl.DeviceIdType.MESH
        )
    pl.semaphore_wait(barrier, len(peers))


class Sends:
    def __init__(self, send_sems, recv_sems):
        self.send_sems, self.recv_sems, self.made = send_sems, recv_sems, {}

    def copy(self, key, source, target, axis, distance):
        index = self.made.setdefault(key, len(self.made))
        return pltpu.make_async_remote_copy(
            src_ref=source,
            dst_ref=target,
            send_sem=self.send_sems.at[index],
            recv_sem=self.recv_sems.at[index],
            device_id=partner(axis, distance),
            device_id_type=pl.DeviceIdType.MESH,
        )


class Gather:
    def __init__(self, nseg, first, packs, gathered, sends):
        self.hops, self.distances = [], set()
        for level, pack, into in zip(range(first, BRANCHES), packs, gathered):
            group = (SEG << (level - 1)) // (nseg * SEG)
            hops = [((level, 0), pack, into.at[0], group)]
            step = 1
            while step < group:
                hops.append(((level, step), into.at[pl.ds(0, step)], into.at[pl.ds(step, step)], step))
                step *= 2
            self.hops.append([sends.copy(k, a, b, "seq", d) for k, a, b, d in hops])
            self.distances |= {hop[3] for hop in hops}

    def peers(self):
        return [("seq", distance) for distance in sorted(self.distances)]

    def start(self):
        for hops in reversed(self.hops):
            hops[0].start()

    def pass_on(self, index, turn):
        hops = self.hops[index]
        hops[turn - 1].wait_recv()
        hops[turn].start()

    def finish(self):
        for hops in self.hops:
            for hop in hops:
                hop.wait_send()
            hops[-1].wait_recv()

    def turns(self):
        events = []
        for index, hops in reversed(list(enumerate(self.hops))):
            for turn in range(1, len(hops)):
                when = 4 * turn + (2 if turn > 1 else 0) + (len(self.hops) - 1 - index)
                events.append((when, functools.partial(self.pass_on, index, turn)))
        return events


class Shards:
    def __init__(self, shards, whole, sends, loads):
        self.copies = []
        me = lax.axis_index("fsdp")
        other = lax.rem(me + 2, 4)
        for i, (shard, into) in enumerate(zip(shards, whole)):
            self.copies.append(
                (
                    pltpu.make_async_copy(shard, into.at[me], loads.at[i]),
                    sends.copy((i, "core"), shard, into.at[me], "fsdp", 1),
                    sends.copy((i, "x"), shard, into.at[me], "fsdp", 2),
                    sends.copy((i, "hand"), into.at[other], into.at[other], "fsdp", 1),
                )
            )

    def start(self):
        for load, core, x, _ in self.copies:
            load.start()
            core.start()
            x.start()

    def hand(self, i):
        _, _, x, hand = self.copies[i]
        x.wait_recv()
        hand.start()

    def finish(self):
        for load, core, x, hand in self.copies:
            load.wait()
            core.wait()
            x.wait_send()
            hand.wait()


class Return:
    def __init__(self, nseg, first, sent, returned, bufs, recvs, local_sems, sends):
        self.plans = []
        for i, level in enumerate(range(first, BRANCHES)):
            group = (SEG << (level - 1)) // (nseg * SEG)
            plan = []
            if group == 1:
                plan.append((None, sends.copy((level, 0), sent[i].at[0], returned[i], "seq", group)))
                self.plans.append((plan, None))
                continue
            buf, recv = bufs.pop(0), recvs.pop(0)
            step = group // 2
            load = pltpu.make_async_copy(sent[i].at[pl.ds(0, step)], buf, local_sems.at[i])
            source, at, add = sent[i].at[pl.ds(step, step)], 0, None
            while step >= 1:
                into = recv.at[pl.ds(at, step)]
                plan.append((add, sends.copy((level, step), source, into, "seq", step)))
                add = (buf, recv, at, step)
                at += step
                step //= 2
                if step:
                    source = buf.at[pl.ds(step, step)]
            plan.append((add, sends.copy((level, 0), buf.at[0], returned[i], "seq", group)))
            self.plans.append((plan, load))

    def start(self, direct):
        for plan, load in reversed(self.plans):
            if direct == (load is None):
                if load is not None:
                    load.start()
                plan[0][1].start()

    def turn(self, number):
        for plan, load in reversed(self.plans):
            if number < len(plan):
                plan[number - 1][1].wait_recv()
                if number == 1 and load is not None:
                    load.wait()
                buf, recv, at, step = plan[number][0]
                for i in range(step):
                    buf[i] = (buf[i].astype(F32) + recv[at + i].astype(F32)).astype(BF16)
                plan[number][1].start()

    def finish(self):
        for plan, load in self.plans:
            for _, copy in plan:
                copy.wait_send()
            plan[-1][1].wait_recv()

    def turns(self):
        return max(len(plan) for plan, _ in self.plans)


def add_blocks(into, at, other, start, count):
    unit = max(u for u in range(1, 13) if count % u == 0)

    def body(i, carry):
        rows = pl.ds(at + i * unit, unit)
        part = other[pl.ds(start + i * unit, unit)].astype(F32)
        into[rows] = (into[rows].astype(F32) + part).astype(BF16)
        return carry

    lax.fori_loop(0, count // unit, body, 0)


def copy_blocks(into, at, other, start, count):
    unit = max(u for u in range(1, 13) if count % u == 0)

    def body(i, carry):
        into[pl.ds(at + i * unit, unit)] = other[pl.ds(start + i * unit, unit)]
        return carry

    lax.fori_loop(0, count // unit, body, 0)


def halving(blocks, order):
    seq = lax.axis_index("seq")
    low, given = [0], []
    for j, distance in enumerate(order):
        bit = lax.rem(lax.div(seq, distance), 2)
        half = blocks >> (j + 1)
        given.append(low[j] + (1 - bit) * half)
        low.append(low[j] + bit * half)
    return low, given


def feed_orders():
    plain = [2**j for j in range(seq_bits())]
    return [plain] * (CHUNKS - 1) + [plain[1:] + plain[:1]]


def inner_orders():
    plain = [2**j for j in range(seq_bits())]
    return [plain] * (CHUNKS - 1) + [[plain[1], plain[0]] + plain[2:]]


def all_peers():
    return [("fsdp", 1), ("fsdp", 2)] + [("seq", 2**j) for j in range(seq_bits())]


class Reduce:
    def __init__(
        self, orders, blocks, source, terms, own, recv_core, recv_x, recv_seq, sends, done, loads=None
    ):
        self.blocks, self.source, self.terms, self.own, self.done = blocks, source, terms, own, done
        self.recv_core, self.recv_x, self.recv_seq = recv_core, recv_x, recv_seq
        self.sends, self.loads = sends, loads
        fsdp = lax.axis_index("fsdp")
        self.core, self.x = lax.rem(fsdp, 2), lax.div(fsdp, 2)
        self.bits = seq_bits()
        self.orders = orders
        self.halves = [halving(blocks, order) for order in self.orders]

    def stages(self):
        return 2 + self.bits

    def core_copy(self, chunk, xo):
        rows = pl.ds(chunk * self.blocks, self.blocks)
        owner = 2 * xo + 1 - self.core
        return self.sends.copy(
            ("core", chunk, xo), self.source.at[owner, rows], self.recv_core.at[xo, rows], "fsdp", 1
        )

    def load_copy(self, chunk, xo):
        rows = pl.ds(chunk * self.blocks, self.blocks)
        return pltpu.make_async_copy(
            self.source.at[2 * xo + self.core, rows], self.terms.at[xo, rows], self.loads.at[2 * chunk + xo]
        )

    def x_copy(self, chunk):
        rows = pl.ds(chunk * self.blocks, self.blocks)
        return self.sends.copy(
            ("x", chunk), self.terms.at[self.own(1 - self.x), rows], self.recv_x.at[rows], "fsdp", 2
        )

    def down_copy(self, chunk, j):
        half = self.blocks >> (j + 1)
        base = chunk * self.blocks
        rows = pl.ds(base + self.halves[chunk][1][j], half)
        into = pl.ds(base + self.blocks - (self.blocks >> j), half)
        return self.sends.copy(
            ("down", chunk, j), self.terms.at[self.own(self.x), rows], self.recv_seq.at[into], "seq",
            self.orders[chunk][j],
        )

    def begin(self, chunk):
        for xo in range(2):
            if self.loads is not None:
                self.load_copy(chunk, xo).start()
            self.core_copy(chunk, xo).start()

    def event(self, stage, chunk):
        base = chunk * self.blocks
        low = self.halves[chunk][0]
        mine = self.terms.at[self.own(self.x)]
        if stage == 0:
            for xo in range(2):
                self.core_copy(chunk, xo).wait_recv()
                if self.loads is not None:
                    self.load_copy(chunk, xo).wait()
                add_blocks(self.terms.at[self.own(xo)], base, self.recv_core.at[xo], base, self.blocks)
            self.x_copy(chunk).start()
            return
        j = stage - 2
        if stage == 1:
            self.x_copy(chunk).wait_recv()
            add_blocks(mine, base, self.recv_x, base, self.blocks)
        else:
            self.down_copy(chunk, j).wait_recv()
            half = self.blocks >> (j + 1)
            add_blocks(mine, base + low[j + 1], self.recv_seq, base + self.blocks - (self.blocks >> j), half)
        if j + 1 < self.bits:
            self.down_copy(chunk, j + 1).start()
        else:
            self.done(chunk, mine, base + low[self.bits])

    def finish(self):
        for chunk in range(CHUNKS):
            for xo in range(2):
                self.core_copy(chunk, xo).wait_send()
            self.x_copy(chunk).wait_send()
            for j in range(self.bits):
                self.down_copy(chunk, j).wait_send()


class Spread:
    def __init__(self, orders, blocks, total, sends):
        self.blocks, self.total, self.sends = blocks, total, sends
        self.bits = seq_bits()
        self.orders = orders
        self.lows = [halving(blocks, order)[0] for order in self.orders]

    def stages(self):
        return self.bits

    def copy(self, chunk, j):
        rows = pl.ds(chunk * self.blocks + self.lows[chunk][j + 1], self.blocks >> (j + 1))
        here = self.total.at[rows]
        return self.sends.copy((chunk, j), here, here, "seq", self.orders[chunk][j])

    def begin(self, chunk, ref, start):
        size = self.blocks >> self.bits
        copy_blocks(self.total, chunk * self.blocks + self.lows[chunk][self.bits], ref, start, size)
        self.copy(chunk, self.bits - 1).start()

    def event(self, stage, chunk):
        j = self.bits - 1 - stage
        self.copy(chunk, j).wait_recv()
        if j:
            self.copy(chunk, j - 1).start()

    def finish(self):
        for chunk in range(CHUNKS):
            for j in range(self.bits):
                self.copy(chunk, j).wait_send()


def run_schedule(step, last, events):
    due = {}
    for when, call in events:
        due.setdefault(min(when, last), []).append(call)
    for when in sorted(due):

        @pl.when(step == when)
        def _():
            for call in due[when]:
                call()


FRONT = 3
KEY_TILE = 128


class State:
    def __init__(self, query, acc=None, top=None):
        self.query, self.acc, self.top = query, acc, top


def attend(items):
    items = list(items)
    ready = []
    for turn in range(len(items) + FRONT):
        if turn < len(items):
            state, key, _ = items[turn]
            ready.append(dotg(key, state.query, 1, 0))
        if turn >= FRONT:
            state, _, value = items[turn - FRONT]
            scores, ready[turn - FRONT] = ready[turn - FRONT], None
            top = jnp.max(scores, axis=0, keepdims=True)
            if state.top is not None:
                top = jnp.maximum(top, state.top)
            probs = jnp.exp2(scores - top).astype(BF16)
            part = dotg(value, probs, 1, 0)
            state.acc = part if state.top is None else state.acc * jnp.exp2(state.top - top) + part
            state.top = top


def key_items(state, key_t, value):
    size = key_t.shape[0]
    tile = min(KEY_TILE, size)
    for start in range(0, size, tile):
        yield state, key_t[start : start + tile], value[:, start : start + tile]


def load_state(query, mine, o_ref, l_ref, m_ref):
    acc = [jnp.concatenate([o_ref[:, at], jnp.broadcast_to(l_ref[0, :, at], (16, at.size))]) for at in mine]
    top = [m_ref[0, :, at] for at in mine]
    return State(query, jnp.concatenate(acc, axis=1), jnp.concatenate(top, axis=1))


def store_state(state, mine, o_ref, l_ref, m_ref):
    start = 0
    for at in mine:
        lanes = slice(start, start + at.size)
        o_ref[:, at] = state.acc[:HEAD_DIM, lanes]
        l_ref[0, :, at] = state.acc[HEAD_DIM : HEAD_DIM + 1, lanes]
        m_ref[0, :, at] = state.top[:, lanes]
        start += at.size


def local_forward(nseg, first, mask_ref, q_ref, k_ref, v_ref, *refs):
    n = BRANCHES - first
    packs, shards, (o_ref, l_ref, m_ref) = refs[:n], refs[n : n + 3], refs[n + 3 : n + 6]
    gathered, whole = refs[n + 6 : 2 * n + 6], refs[2 * n + 6 : 2 * n + 9]
    qa, ka, va, send_sems, recv_sems, shard_send, shard_recv, shard_load = refs[2 * n + 9 :]
    head = pl.program_id(0)
    gather = Gather(nseg, first, packs, gathered, Sends(send_sems, recv_sems))
    fetch = Shards(shards, whole, Sends(shard_send, shard_recv), shard_load)

    def begin():
        meet(gather.peers() + [("fsdp", 1), ("fsdp", 2)])
        gather.start()
        fetch.start()

    def finish():
        gather.finish()
        fetch.hand(2)
        fetch.finish()

    hands = [(3, functools.partial(fetch.hand, 0)), (10, functools.partial(fetch.hand, 1))]
    run_schedule(head, HEADS - 1, [(0, begin)] + sorted(gather.turns() + hands, key=lambda event: event[0]))
    local_forward_core(nseg, mask_ref, q_ref, k_ref, v_ref, o_ref, l_ref, m_ref, qa, ka, va)
    run_schedule(head, HEADS - 1, [(HEADS - 1, finish)])


def local_forward_scratch(nseg):
    length = nseg * SEG
    return [
        pltpu.VMEM((64, length), BF16),
        pltpu.VMEM((nseg, 64, length), BF16),
        pltpu.VMEM((64, length), BF16),
    ]


def local_forward_core(nseg, mask_ref, q_ref, k_ref, v_ref, o_ref, l_ref, m_ref, qa, ka, va):
    head = pl.program_id(0)
    length = nseg * SEG
    keep = local_keep(mask_ref[0], length)
    qa[...] = join(q_ref[0], query_rows(head, length))
    va[...] = join(v_ref[0], value_rows(length))
    ka[0] = join(k_ref[0], key_rows(head, 0, 4, length, keep))
    if nseg == 2:
        ka[1] = join(k_ref[0], key_rows(head, 1, 4, length, keep))
    states, items = [], []
    for seg in range(nseg):
        lanes = slice(seg * SEG, (seg + 1) * SEG)
        states.append(State(qa[:, lanes]))
        items += key_items(states[-1], ka[0, :, lanes].T, va[:, lanes])
    attend(items)
    for seg in range(nseg):
        store_state(states[seg], [pl.ds(seg * SEG, SEG)], o_ref, l_ref, m_ref)
    if nseg == 2:
        kept = [pl.ds(kept_start(head, 1, seg), SEG // 2) for seg in range(2)]
        states = [load_state(qa[:, at], [at], o_ref, l_ref, m_ref) for at in kept]
        items = []
        for seg in range(2):
            items += key_items(states[seg], ka[1, :, kept[1 - seg]].T, va[:, kept[1 - seg]])
        attend(items)
        for seg in range(2):
            store_state(states[seg], [kept[seg]], o_ref, l_ref, m_ref)


def remote_keys(head, level, pack):
    k_ref, v_ref, mask_ref = pack
    pieces = range(k_ref.shape[0])
    key, value, mask = (
        jnp.concatenate([ref[i] for i in pieces], axis=1) for ref in (k_ref, v_ref, mask_ref)
    )
    length = key.shape[1]
    row = lax.broadcasted_iota(jnp.int32, (16, length), 0)
    keep = jnp.sum(jnp.where(row == head, mask.astype(F32), 0.0), axis=0, keepdims=True) > 0.5
    return join(key, key_rows(head, level, 4 - level, length, keep)), join(value, value_rows(length))


def remote_plan(first):
    return [(level,) for level in range(first, 3)] + [(3, 4)]


def remote_forward(nseg, first, mask_ref, q_ref, o_in, l_in, m_in, *refs):
    head = pl.program_id(0)
    levels = range(first, BRANCHES)
    packs = {level: refs[3 * i : 3 * i + 3] for i, level in enumerate(levels)}
    att_ref, lse_ref, o_ref, l_ref, m_ref, qa = refs[3 * len(levels) :]
    length = nseg * SEG
    qa[...] = join(q_ref[0], query_rows(head, length))
    o_ref[...] = o_in[...]
    l_ref[...] = l_in[...]
    m_ref[...] = m_in[...]
    for group in remote_plan(first):
        pairs = [remote_keys(head, level, packs[level]) for level in group]
        key = jnp.concatenate([pair[0] for pair in pairs], axis=1)
        value = jnp.concatenate([pair[1] for pair in pairs], axis=1)
        mine = [pl.ds(kept_start(head, group[0], seg), SEG >> group[0]) for seg in range(nseg)]
        query = jnp.concatenate([qa[:, at] for at in mine], axis=1)
        state = load_state(query, mine, o_ref, l_ref, m_ref)
        attend(key_items(state, key.T, value))
        store_state(state, mine, o_ref, l_ref, m_ref)
    weight = jnp.where(local_keep(mask_ref[0], length), 1.0, 0.0) / l_ref[0]
    att_ref[...] = (o_ref[...] * weight).astype(BF16)
    lse_ref[0] = m_ref[0] + jnp.log2(l_ref[0])


def grad_rows(grad, slope):
    length = grad.shape[1]
    row = lax.broadcasted_iota(jnp.int32, (16, length), 0)
    high = (-slope).astype(BF16).astype(F32)
    low = -slope - high
    extra = jnp.where(row == 0, high, jnp.where(row == 1, low, 0.0)).astype(BF16)
    return join(grad, extra)


AHEAD = 2
QUERY_TILE = 256
BACK_KEYS = 256


class Side:
    def __init__(self, query, grad):
        self.query, self.grad = query[:HEAD_DIM], grad[:HEAD_DIM]
        self.query_t, self.grad_t = query.T, grad.T
        self.dq = None


def attend_back(items, dk_ref, dv_ref, written):
    items = list(items)
    ready = []
    for turn in range(len(items) + AHEAD):
        if turn < len(items):
            side, key, value, _, _ = items[turn]
            ready.append((dotg(side.query_t, key, 1, 0), dotg(side.grad_t, value, 1, 0)))
        if turn >= AHEAD:
            side, key, _, lanes, name = items[turn - AHEAD]
            scores, slope = ready[turn - AHEAD]
            ready[turn - AHEAD] = None
            probs = jnp.exp2(scores)
            dscore = (probs * slope).astype(BF16)
            dv = dotg(side.grad, probs.astype(BF16), 1, 0)
            dk = dotg(side.query, dscore, 1, 0)
            part = dotg(key[:HEAD_DIM], dscore, 1, 1)
            side.dq = part if side.dq is None else side.dq + part
            if name in written:
                dv_ref[:, lanes] += dv
                dk_ref[:, lanes] += dk
            else:
                written.add(name)
                dv_ref[:, lanes] = dv
                dk_ref[:, lanes] = dk


def sides_of(query, grad):
    tile = min(QUERY_TILE, query.shape[1])
    return [
        Side(query[:, start : start + tile], grad[:, start : start + tile])
        for start in range(0, query.shape[1], tile)
    ]


def pairs(sides, key_ref, value_ref, tiles):
    return [
        (side, key_ref[:, lanes], value_ref[:, lanes], lanes, name) for side in sides for name, lanes in tiles
    ]


def joined(sides):
    return jnp.concatenate([side.dq for side in sides], axis=1) if len(sides) > 1 else sides[0].dq


DQ_SCALE = HEAD_DIM ** (-0.5)
DK_SCALE = math.log(2.0)


def neg_total(lse, keep):
    return jnp.where(keep, -lse, NEG)


def local_backward(nseg, first, mask_ref, q_ref, k_ref, v_ref, g_ref, lse_ref, slope_ref, dqr_ref, *refs):
    n = BRANCHES - first
    sent, feed_ref, out_ref = refs[:n], refs[n], refs[n + 1]
    returned, piece_ref = refs[n + 2 : 2 * n + 2], refs[2 * n + 2]
    qa, ga, ka, va, dk, dv = refs[2 * n + 3 : 2 * n + 9]
    rest = list(refs[2 * n + 9 :])
    back_send, back_recv, back_load, red_send, red_recv, red_load = rest[-6:]
    terms, recv_core, recv_x, recv_seq = rest[-10:-6]
    bufs, recvs = rest[: (len(rest) - 10) // 2], rest[(len(rest) - 10) // 2 : -10]
    head = pl.program_id(0)
    last = HEADS - 1

    back = Return(nseg, first, sent, returned, bufs, recvs, back_load, Sends(back_send, back_recv))
    blocks = terms.shape[1] // CHUNKS
    reduce = Reduce(
        feed_orders(), blocks, feed_ref, terms, lambda xo: xo, recv_core, recv_x, recv_seq, Sends(red_send, red_recv),
        lambda chunk, ref, start: copy_blocks(piece_ref.at[chunk], 0, ref, start, blocks >> seq_bits()),
        red_load,
    )

    def begin():
        meet(all_peers())
        back.start(False)
        for chunk in range(CHUNKS):
            reduce.begin(chunk)

    events = [(3 * turn, functools.partial(back.turn, turn)) for turn in range(1, back.turns())]
    events.append((8, functools.partial(back.start, True)))
    for chunk in range(CHUNKS):
        for stage in range(reduce.stages()):
            when = 1 + (chunk + 1) // 2 if stage == 0 else 4 + 3 * chunk + 2 * (stage - 1)
            events.append((when, functools.partial(reduce.event, stage, chunk)))
    run_schedule(head, last, [(0, begin)] + sorted(events, key=lambda event: event[0]))
    local_backward_core(
        nseg, first, mask_ref, q_ref, k_ref, v_ref, g_ref, lse_ref, slope_ref, dqr_ref, out_ref,
        qa, ga, ka, va, dk, dv,
    )

    @pl.when(head == last)
    def _():
        back.finish()
        reduce.finish()


def local_backward_scratch(nseg):
    length = nseg * SEG
    return [
        pltpu.VMEM((64, length), BF16),
        pltpu.VMEM((64, length), BF16),
        pltpu.VMEM((nseg, 64, length), BF16),
        pltpu.VMEM((64, length), BF16),
        pltpu.VMEM((HEAD_DIM, length), F32),
        pltpu.VMEM((HEAD_DIM, length), F32),
    ]


def local_backward_core(
    nseg, first, mask_ref, q_ref, k_ref, v_ref, g_ref, lse_ref, slope_ref, dqr_ref, out_ref,
    qa, ga, ka, va, dk, dv,
):
    head = pl.program_id(0)
    length = nseg * SEG
    keep = local_keep(mask_ref[0], length)
    qa[...] = join(q_ref[0], query_rows(head, length, neg_total(lse_ref[0], keep)))
    ga[...] = grad_rows(g_ref[...], slope_ref[0])
    va[...] = join(v_ref[0], value_rows(length))
    ka[0] = join(k_ref[0], key_rows(head, 0, 4, length, keep))
    if nseg == 2:
        ka[1] = join(k_ref[0], key_rows(head, 1, 4, length, keep))
    items, sides, written = [], [], set()
    for seg in range(nseg):
        lanes = slice(seg * SEG, (seg + 1) * SEG)
        tiles = [
            ((seg, i), slice(seg * SEG + BACK_KEYS * i, seg * SEG + BACK_KEYS * (i + 1)))
            for i in range(SEG // BACK_KEYS)
        ]
        sides.append(sides_of(qa[:, lanes], ga[:, lanes]))
        items += pairs(sides[-1], ka.at[0], va, tiles)
    attend_back(items, dk, dv, written)
    for seg in range(nseg):
        out_ref[0, :, seg * SEG : (seg + 1) * SEG] = joined(sides[seg]) * DQ_SCALE
    if nseg == 2:
        items, sides = [], []
        kept = [pl.ds(kept_start(head, 1, seg), SEG // 2) for seg in range(2)]
        for seg in range(2):
            base = kept_start(head, 1, 1 - seg)
            tile = min(BACK_KEYS, SEG // 2)
            tiles = [
                ((seg, i), pl.ds(pl.multiple_of(base + tile * i, tile), tile)) for i in range(SEG // 2 // tile)
            ]
            sides.append(sides_of(qa[:, kept[seg]], ga[:, kept[seg]]))
            items += pairs(sides[-1], ka.at[1], va, tiles)
        attend_back(items, dk, dv, set(item[4] for item in items))
        for seg in range(2):
            out_ref[0, :, kept[seg]] += joined(sides[seg]) * DQ_SCALE
    size = SEG >> first
    for seg in range(nseg):
        mine = pl.ds(kept_start(head, first, seg), size)
        out_ref[0, :, mine] += dqr_ref[:, seg * size : (seg + 1) * size]
    out_ref[1] = dk[...] * DK_SCALE
    out_ref[2] = dv[...]


def rows_of(total, at, count):
    return total[at : at + count].reshape(count * 16, 128)


def remote_backward(nseg, first, mask_ref, q_ref, g_ref, lse_ref, slope_ref, *refs):
    head = pl.program_id(0)
    levels = range(first, BRANCHES)
    n = len(levels)
    packs = {level: refs[3 * i : 3 * i + 3] for i, level in enumerate(levels)}
    dqr_ref = refs[3 * n]
    outs = {level: refs[3 * n + 1 + i] for i, level in enumerate(levels)}
    qa, ga, ka, va, dk, dv = refs[4 * n + 1 :]
    length = nseg * SEG
    qa[...] = join(q_ref[0], query_rows(head, length, neg_total(lse_ref[0], local_keep(mask_ref[0], length))))
    ga[...] = grad_rows(g_ref[...], slope_ref[0])
    full = SEG >> first
    for group in remote_plan(first):
        for i, level in enumerate(group):
            key, value = remote_keys(head, level, packs[level])
            ka[:, i * 512 : (i + 1) * 512] = key
            va[:, i * 512 : (i + 1) * 512] = value
        size = SEG >> group[0]
        mine = [pl.ds(kept_start(head, group[0], seg), size) for seg in range(nseg)]
        query = jnp.concatenate([qa[:, m] for m in mine], axis=1)
        grad = jnp.concatenate([ga[:, m] for m in mine], axis=1)
        tile = min(BACK_KEYS, 512)
        tiles = [(i, slice(tile * i, tile * (i + 1))) for i in range(512 // tile * len(group))]
        sides = sides_of(query, grad)
        attend_back(pairs(sides, ka, va, tiles), dk, dv, set())
        dq = joined(sides) * DQ_SCALE
        for seg in range(nseg):
            piece = dq[:, seg * size : (seg + 1) * size]
            if group[0] == first:
                dqr_ref[:, seg * full : (seg + 1) * full] = piece
            else:
                inner = (reversed_bits(head) >> (4 - group[0])) & ((1 << (group[0] - first)) - 1)
                lanes = pl.ds(pl.multiple_of(seg * full + inner * size, 128), size)
                dqr_ref[:, lanes] += piece
        for i, level in enumerate(group):
            pieces, _, _, size = outs[level].shape
            for piece in range(pieces):
                lanes = slice(i * 512 + piece * size, i * 512 + (piece + 1) * size)
                outs[level][piece, 0] = (dk[:, lanes] * DK_SCALE).astype(BF16)
                outs[level][piece, 1] = dv[:, lanes].astype(BF16)


def row_block(length):
    return pl.BlockSpec((1, 1, length), lambda h: (h, 0, 0))


def head_block(length):
    return pl.BlockSpec((HEAD_DIM, length), lambda h: (h, 0))


def part_block(part, length):
    return pl.BlockSpec((1, HEAD_DIM, length), lambda h: (part, h, 0))


MASK_BLOCK = pl.BlockSpec(memory_space=pltpu.SMEM)


def pack_specs(pack):
    group, _, length = pack.shape
    return [
        pl.BlockSpec((group, HEAD_DIM, length), lambda h: (0, h, 0)),
        pl.BlockSpec((group, HEAD_DIM, length), lambda h: (0, HEADS + h, 0)),
        pl.BlockSpec((group, 16, length), lambda h: (0, 2 * D // 16, 0)),
    ]


ANY_BLOCK = pl.BlockSpec(memory_space=pl.ANY)


def sems(count):
    return pltpu.SemaphoreType.DMA((count,))


def talking(collective_id, mebibytes=56):
    return pltpu.CompilerParams(
        vmem_limit_bytes=mebibytes * 1024 * 1024, collective_id=collective_id, has_side_effects=True
    )


PARAMS = pltpu.CompilerParams(vmem_limit_bytes=VMEM_LIMIT)


def shape(dims, dtype):
    return jax.ShapeDtypeStruct(dims, dtype)


def cost(seconds):
    return pl.CostEstimate(flops=int(seconds * 1.1e15), transcendentals=0, bytes_accessed=0)


def call_local_forward(nseg, first, qkv, mask, packs, shards):
    length = nseg * SEG
    n = len(packs)
    groups = [(SEG << (level - 1)) // length for level in range(first, BRANCHES)]
    hops = sum(group.bit_length() for group in groups)
    o_part, l_part, m_part, *rest = pl.pallas_call(
        functools.partial(local_forward, nseg, first),
        grid=(HEADS,),
        in_specs=[MASK_BLOCK, part_block(0, length), part_block(1, length), part_block(2, length)]
        + [ANY_BLOCK] * (n + 3),
        out_specs=[head_block(length), row_block(length), row_block(length)] + [ANY_BLOCK] * (n + 3),
        out_shape=[shape((D, length), F32), shape((HEADS, 1, length), F32), shape((HEADS, 1, length), F32)]
        + [shape((group,) + pack.shape, BF16) for group, pack in zip(groups, packs)]
        + [shape((4,) + shard.shape, BF16) for shard in shards],
        scratch_shapes=local_forward_scratch(nseg)
        + [
            sems(hops),
            sems(hops),
            sems(9),
            sems(9),
            sems(3),
        ],
        compiler_params=talking(1),
        cost_estimate=cost(nseg * 37e-6),
        name="local_forward",
    )(mask, qkv, qkv, qkv, *packs, *shards)
    whole = [weight.reshape(4 * weight.shape[1], weight.shape[2]) for weight in rest[n:]]
    return o_part, l_part, m_part, rest[:n], whole


def call_remote_forward(nseg, first, qkv, mask, o_part, l_part, m_part, packs):
    length = nseg * SEG
    args, specs = [], []
    for pack in packs:
        args += [pack] * 3
        specs += pack_specs(pack)
    return pl.pallas_call(
        functools.partial(remote_forward, nseg, first),
        grid=(HEADS,),
        in_specs=[MASK_BLOCK, part_block(0, length), head_block(length), row_block(length), row_block(length)]
        + specs,
        out_specs=[head_block(length), row_block(length)],
        out_shape=[shape((D, length), BF16), shape((HEADS, 1, length), F32)],
        scratch_shapes=[
            pltpu.VMEM((HEAD_DIM, length), F32),
            pltpu.VMEM((1, 1, length), F32),
            pltpu.VMEM((1, 1, length), F32),
            pltpu.VMEM((64, length), BF16),
        ],
        compiler_params=PARAMS,
        cost_estimate=cost(nseg * 24e-6),
        name="remote_forward",
    )(mask, qkv, o_part, l_part, m_part, *args)


def call_remote_backward(nseg, first, qkv, grad, lse, slope, mask, packs):
    length = nseg * SEG
    args, specs = [], []
    for pack in packs:
        args += [pack] * 3
        specs += pack_specs(pack)
    kept = nseg * (SEG >> first)
    return pl.pallas_call(
        functools.partial(remote_backward, nseg, first),
        grid=(HEADS,),
        in_specs=[MASK_BLOCK, part_block(0, length), head_block(length), row_block(length), row_block(length)]
        + specs,
        out_specs=[head_block(kept)]
        + [
            pl.BlockSpec((pack.shape[0], 2, HEAD_DIM, pack.shape[2]), lambda h: (0, 0, h, 0))
            for pack in packs
        ],
        out_shape=[shape((D, kept), F32)]
        + [shape((pack.shape[0], 2, D, pack.shape[2]), BF16) for pack in packs],
        scratch_shapes=[
            pltpu.VMEM((64, length), BF16),
            pltpu.VMEM((64, length), BF16),
            pltpu.VMEM((64, 1024), BF16),
            pltpu.VMEM((64, 1024), BF16),
            pltpu.VMEM((HEAD_DIM, 1024), F32),
            pltpu.VMEM((HEAD_DIM, 1024), F32),
        ],
        compiler_params=PARAMS,
        cost_estimate=cost(nseg * 20e-6),
        name="remote_backward",
    )(mask, qkv, grad, lse, slope, *args)


CHUNKS = 3
FEED_BLOCKS = (4 * D + D + 4 * D) * D // (4 * 16 * 128)
IN_BLOCKS = 3 * D * D // (4 * 16 * 128)


def padded(blocks):
    unit = CHUNKS * lax.axis_size("seq")
    return (blocks + unit - 1) // unit * unit


def reduce_copies():
    return CHUNKS * (3 + seq_bits())


def call_local_backward(nseg, first, qkv, grad, lse, slope, mask, dq_remote, sent, feed_grads):
    length = nseg * SEG
    n = len(sent)
    groups = [part.shape[0] for part in sent]
    hops = sum(group.bit_length() for group in groups)
    blocks = feed_grads.shape[1]
    piece = (CHUNKS, blocks // CHUNKS >> seq_bits(), 16, 128)
    bufs = [pltpu.VMEM((g // 2,) + part.shape[1:], BF16) for g, part in zip(groups, sent) if g > 1]
    recvs = [pltpu.VMEM((g - 1,) + part.shape[1:], BF16) for g, part in zip(groups, sent) if g > 1]
    local, *rest = pl.pallas_call(
        functools.partial(local_backward, nseg, first),
        grid=(HEADS,),
        in_specs=[MASK_BLOCK, part_block(0, length), part_block(1, length), part_block(2, length), head_block(length),
                  row_block(length), row_block(length), head_block(dq_remote.shape[1])]
        + [ANY_BLOCK] * (n + 1),
        out_specs=[pl.BlockSpec((3, HEAD_DIM, length), lambda h: (0, h, 0))]
        + [ANY_BLOCK] * n
        + [const_block(piece)],
        out_shape=[shape((3, D, length), F32)]
        + [shape(part.shape[1:], BF16) for part in sent]
        + [shape(piece, BF16)],
        scratch_shapes=local_backward_scratch(nseg)
        + bufs
        + recvs
        + [
            pltpu.VMEM((2, blocks, 16, 128), BF16),
            pltpu.VMEM((2, blocks, 16, 128), BF16),
            pltpu.VMEM((blocks, 16, 128), BF16),
            pltpu.VMEM((blocks, 16, 128), BF16),
            sems(hops),
            sems(hops),
            sems(n),
            sems(reduce_copies()),
            sems(reduce_copies()),
            sems(2 * CHUNKS),
        ],
        compiler_params=talking(2),
        cost_estimate=cost(nseg * 72e-6),
        name="local_backward",
    )(mask, qkv, qkv, qkv, grad, lse, slope, dq_remote, *sent, feed_grads)
    return local, rest[:n], rest[n]


HALF = D // 2


def const_block(dims):
    return pl.BlockSpec(dims, lambda i: (0,) * len(dims), pipeline_mode=pl.Buffered(1))


def rev4(value):
    return int(reversed_bits(value))


TILES = D // 128


def put_rows(tiled, start, array):
    for tile in range(TILES):
        tiled[tile, start : start + array.shape[0], :] = array[:, tile * 128 : (tile + 1) * 128]


def get_rows(tiled, start, size):
    return jnp.concatenate([tiled[tile, start : start + size, :] for tile in range(TILES)], axis=1)


def get_residue(tiled, start):
    return jnp.concatenate(
        [tiled[tile, pl.ds(start, RUN, stride=RES), :] for tile in range(TILES)], axis=1
    )


def put_residue(tiled, start, array):
    for tile in range(TILES):
        tiled[tile, pl.ds(start, RUN, stride=RES), :] = array[:, tile * 128 : (tile + 1) * 128]


COLUMN_CHUNKS = 3


def project_kernel(nseg, first, mask_ref, tok_ref, *refs):
    n = BRANCHES - first
    vectors, w_ref = refs[:4], refs[4]
    qkv_ref, xp_ref, inner_ref, weight_ref, gains_ref = refs[5:10]
    packs = refs[10 : 10 + n]
    xs, weight, gains, vec_send, vec_recv, w_send, w_recv, w_load, w_store = refs[10 + n :]
    step = pl.program_id(0)
    last = pl.num_programs(0) - 1
    me = lax.axis_index("fsdp")
    sibling = me + 1 - 2 * lax.rem(me, 2)
    across = lax.rem(me + 2, 4)
    sends = Sends(w_send, w_recv)

    def send(source, target, key, other):
        index = sends.made.setdefault(key, len(sends.made))
        return pltpu.make_async_remote_copy(
            src_ref=source, dst_ref=target, send_sem=w_send.at[index], recv_sem=w_recv.at[index],
            device_id={"fsdp": other}, device_id_type=pl.DeviceIdType.MESH,
        )

    def chunk_copies(chunk):
        cols = pl.ds(chunk * D, D)
        mine = w_ref.at[:, cols]
        load = pltpu.make_async_copy(mine, weight.at[me, :, cols], w_load.at[chunk])
        core = send(mine, weight.at[me, :, cols], ("core", chunk), sibling)
        x = send(mine, weight.at[me, :, cols], ("x", chunk), across)
        handed = weight.at[across, :, cols]
        return load, core, x, send(handed, handed, ("hand", chunk), sibling)

    def vec_copies():
        return [
            pltpu.make_async_remote_copy(
                src_ref=gains.at[me], dst_ref=gains.at[me], send_sem=vec_send.at[i], recv_sem=vec_recv.at[i],
                device_id={"fsdp": other}, device_id_type=pl.DeviceIdType.MESH,
            )
            for i, other in enumerate((sibling, across, 3 - me))
        ]

    store = pltpu.make_async_copy(weight, weight_ref, w_store.at[0])

    @pl.when(step == 0)
    def _():
        barrier = pltpu.get_barrier_semaphore()
        for other in (sibling, across, 3 - me):
            pl.semaphore_signal(
                barrier, inc=1, device_id={"fsdp": other}, device_id_type=pl.DeviceIdType.MESH
            )
        for i, vector in enumerate(vectors):
            gains[me, i : i + 1, :192] = vector[...].astype(F32).reshape(1, 192)
        pl.semaphore_wait(barrier, 3)
        for copy in vec_copies():
            copy.start()
        for chunk in range(COLUMN_CHUNKS):
            for copy in chunk_copies(chunk)[:3]:
                copy.start()
        for copy in vec_copies():
            copy.wait_recv()
        full = [
            jnp.concatenate([gains[owner, i : i + 1, :192] for owner in range(4)], axis=1) for i in range(4)
        ]
        gains_ref[...] = jnp.concatenate(full + [jnp.zeros((4, D), F32)], axis=0)
        for seg in range(nseg):
            put_rows(xs, 0, tok_ref[seg * SEG : (seg + 1) * SEG, :].astype(F32))
            for pair in range(RES // 2):
                rows = jnp.concatenate([get_residue(xs, rev4(2 * pair + i)) for i in range(2)], axis=0)
                normed = normalize(rows, full[0], full[1])[0].astype(BF16)
                at = slice(seg * SEG + pair * 2 * RUN, seg * SEG + (pair + 1) * 2 * RUN)
                xp_ref[at, :] = rows.astype(BF16)
                inner_ref[:, at] = normed.T
        for pack, level in zip(packs, range(first, BRANCHES)):
            pack[2 * D :, :] = packed_keep(mask_ref[0], level, nseg)

    for chunk in range(COLUMN_CHUNKS):

        @pl.when(step == 2 * chunk)
        def _():
            load, core, x, hand = chunk_copies(chunk)
            x.wait_recv()
            hand.start()
            load.wait()
            core.wait_recv()
            hand.wait_recv()

    @pl.when(step == 4)
    def _():
        store.start()

    cols = pl.ds(pl.multiple_of(step * HALF, HALF), HALF)
    block = jnp.concatenate([weight[owner, :, cols] for owner in range(4)], axis=0)
    scale = jnp.where(step < 2, QUERY_SCALE, 1.0)
    for start in range(0, nseg * SEG, 512):
        lanes = slice(start, start + 512)
        qkv_ref[0, :, lanes] = (dotg(block, inner_ref[:, lanes], 0, 0) * scale).astype(BF16)

    @pl.when(step >= 2)
    def _():
        upper = lax.rem(step, 2) == 1
        for pack, level in zip(packs, range(first, BRANCHES)):
            size = SEG >> level
            for head in range(HEADS // 2):
                rows = slice(head * HEAD_DIM, (head + 1) * HEAD_DIM)
                pieces = []
                for seg in range(nseg):
                    start = seg * SEG + (rev4(head) >> (4 - level)) * size
                    if level < 4:
                        pieces.append(qkv_ref[0, rows, start : start + size])
                    else:
                        both = qkv_ref[0, rows, start : start + 2 * size]
                        pieces.append(jnp.where(upper, both[:, size:], both[:, :size]))
                into = pl.ds(pl.multiple_of((step - 2) * HALF + head * HEAD_DIM, 16), HEAD_DIM)
                pack[into, :] = jnp.concatenate(pieces, axis=1) if nseg > 1 else pieces[0]

    @pl.when(step == last)
    def _():
        for copy in vec_copies():
            copy.wait_send()
        for chunk in range(COLUMN_CHUNKS):
            for copy in chunk_copies(chunk)[1:]:
                copy.wait_send()
        store.wait()


def call_project(nseg, first, mask, tokens, vectors, weight):
    length = nseg * SEG
    kept = [nseg * (SEG >> level) for level in range(first, BRANCHES)]
    return pl.pallas_call(
        functools.partial(project_kernel, nseg, first),
        grid=(6,),
        in_specs=[MASK_BLOCK, const_block((length, D))] + [const_block((192,))] * 4 + [ANY_BLOCK],
        out_specs=[
            pl.BlockSpec((1, HALF, length), lambda i: (i // 2, i % 2, 0)),
            const_block((length, D)),
            const_block((D, length)),
            ANY_BLOCK,
            const_block((8, D)),
        ]
        + [const_block((2 * D + 16, size)) for size in kept],
        out_shape=[
            shape((3, D, length), BF16),
            shape((length, D), BF16),
            shape((D, length), BF16),
            shape((4, 192, 3 * D), BF16),
            shape((8, D), F32),
        ]
        + [shape((2 * D + 16, size), BF16) for size in kept],
        scratch_shapes=[
            pltpu.VMEM((TILES, SEG, 128), F32),
            pltpu.VMEM((4, 192, 3 * D), BF16),
            pltpu.VMEM((4, 8, 256), F32),
            sems(3),
            sems(3),
            sems(3 * COLUMN_CHUNKS),
            sems(3 * COLUMN_CHUNKS),
            sems(COLUMN_CHUNKS),
            sems(1),
        ],
        compiler_params=talking(4),
        cost_estimate=cost(nseg * 10e-6),
        name="project",
    )(mask, tokens, *vectors, weight)


ROWS = 256


def blocks_of(ref, rows, col):
    part = ref[rows, col * 128 : (col + 1) * 128].astype(BF16)
    return part.reshape(part.shape[0] // 16, 16, 128)


def feed_kernel(
    nseg, mask_ref, att_ref, x_ref, cot_ref, wout_ref, up_ref, down_ref, gains_ref,
    mixed_ref, gmid_ref, gm_ref, along_ref, vec_ref, grads_ref,
    cs, out_acc, up_acc, down_acc, stage, sems,
):
    step = pl.program_id(0)
    quarter = lax.rem(step, 4)
    low = (quarter >> 1) | ((quarter & 1) << 1)

    @pl.when(step == 0)
    def _():
        out_acc[...] = jnp.zeros_like(out_acc)
        up_acc[...] = jnp.zeros_like(up_acc)
        down_acc[...] = jnp.zeros_like(down_acc)
        vec_ref[...] = jnp.zeros_like(vec_ref)

    @pl.when(quarter == 0)
    def _():
        put_rows(cs, 0, cot_ref[...].astype(F32))

    grad = jnp.concatenate([get_residue(cs, rev4(i) + low) for i in range(4)], axis=0)
    grad_b = grad.astype(BF16)
    att = att_ref[...]
    middle = x_ref[...].astype(F32) + dotg(att, wout_ref[...], 0, 0)
    gain = gains_ref[2:3, :]
    normed, unit, inverse = normalize(middle, gain, gains_ref[3:4, :])
    hidden = normed.astype(BF16)
    hidden_t = hidden.T
    final = middle
    grad_hidden = jnp.zeros((ROWS, D), F32)
    for start in range(0, 4 * D, D):
        cols = slice(start, start + D)
        upper = dotg(hidden, up_ref[:, cols], 1, 0)
        grad_active = dotg(grad_b, down_ref[cols, :], 1, 1)
        half = 0.5 * (1.0 + lax.erf(upper * ROOT_HALF))
        slope = half + upper * jnp.exp(-0.5 * upper * upper) * INV_ROOT_TWO_PI
        active = (upper * half).astype(BF16)
        grad_upper = (grad_active * slope).astype(BF16)
        final = final + dotg(active, down_ref[cols, :], 1, 0)
        grad_hidden = grad_hidden + dotg(grad_upper, up_ref[:, cols], 1, 1)
        up_acc[:, cols] += dotg(hidden_t, grad_upper, 1, 0)
        down_acc[cols, :] += dotg(active, grad_b, 0, 0)
    for i in range(4):
        put_residue(cs, rev4(i) + low, final[i * RUN : (i + 1) * RUN])

    @pl.when(quarter == 3)
    def _():
        mixed_ref[...] = get_rows(cs, 0, SEG).astype(BF16)

    back, gain_back, shift_back = normalize_back(grad_hidden, unit, inverse, gain)
    vec_ref[0:1, :] += gain_back[None, :]
    vec_ref[1:2, :] += shift_back[None, :]
    grad_middle = grad + back
    gmid_ref[...] = grad_middle
    branch = grad_middle.astype(BF16)
    out_acc[...] += dotg(att, branch, 1, 0)
    lane = lax.broadcasted_iota(jnp.int32, (1, ROWS), 1)
    position = step // 4 * SEG + lax.rem(lane, RUN) * RES + residue_of(lane // RUN) + low
    keep = position < mask_ref[0]
    merged = jnp.where(keep, dotg(wout_ref[...], branch, 1, 1), 0.0).astype(BF16)
    gm_ref[...] = merged
    product = merged.astype(F32) * att.astype(F32)
    for head in range(HEADS):
        rows = slice(head * HEAD_DIM, (head + 1) * HEAD_DIM)
        along_ref[head] = jnp.sum(product[rows], axis=0, keepdims=True)

    @pl.when(step == pl.num_programs(0) - 1)
    def _():
        copies = []
        for owner in range(4):
            for piece in range(3):
                count = owner * 3 + piece
                slot = count % 2
                if count >= 2:
                    copies[count - 2].wait()
                if piece == 0:
                    rows, offset, size = slice(owner * 192, (owner + 1) * 192), 0, 288
                    for col in range(4 * TILES):
                        stage[slot, col * 12 : (col + 1) * 12] = blocks_of(up_acc, rows, col)
                elif piece == 1:
                    rows, offset, size = slice(owner * 192, (owner + 1) * 192), 288, 72
                    for col in range(TILES):
                        stage[slot, col * 12 : (col + 1) * 12] = blocks_of(out_acc, rows, col)
                else:
                    rows, offset, size = slice(owner * D, (owner + 1) * D), 360, 288
                    for col in range(TILES):
                        stage[slot, col * 48 : (col + 1) * 48] = blocks_of(down_acc, rows, col)
                copy = pltpu.make_async_copy(
                    stage.at[slot, pl.ds(0, size)],
                    grads_ref.at[owner, pl.ds(offset, size)],
                    sems.at[slot],
                )
                copy.start()
                copies.append(copy)
        copies[-2].wait()
        copies[-1].wait()


def call_feed(nseg, mask, att, x, cot, wout, up, down, gains):
    length = nseg * SEG
    return pl.pallas_call(
        functools.partial(feed_kernel, nseg),
        grid=(length // ROWS,),
        in_specs=[
            MASK_BLOCK,
            pl.BlockSpec((D, ROWS), lambda i: (0, i)),
            pl.BlockSpec((ROWS, D), lambda i: (i, 0)),
            pl.BlockSpec((SEG, D), lambda i: (i // 4, 0)),
            const_block((D, D)),
            const_block((D, 4 * D)),
            const_block((4 * D, D)),
            const_block((8, D)),
        ],
        out_specs=[
            pl.BlockSpec((SEG, D), lambda i: (i // 4, 0)),
            pl.BlockSpec((ROWS, D), lambda i: (i, 0)),
            pl.BlockSpec((D, ROWS), lambda i: (0, i)),
            pl.BlockSpec((HEADS, 1, ROWS), lambda i: (0, 0, i)),
            pl.BlockSpec((2, D), lambda i: (0, 0)),
            pl.BlockSpec(memory_space=pl.ANY),
        ],
        out_shape=[
            shape((length, D), BF16),
            shape((length, D), F32),
            shape((D, length), BF16),
            shape((HEADS, 1, length), F32),
            shape((2, D), F32),
            shape((4, padded(FEED_BLOCKS), 16, 128), BF16),
        ],
        scratch_shapes=[
            pltpu.VMEM((TILES, SEG, 128), F32),
            pltpu.VMEM((D, D), F32),
            pltpu.VMEM((D, 4 * D), F32),
            pltpu.VMEM((4 * D, D), F32),
            pltpu.VMEM((2, 288, 16, 128), BF16),
            pltpu.SemaphoreType.DMA((2,)),
        ],
        compiler_params=pltpu.CompilerParams(vmem_limit_bytes=62 * 1024 * 1024),
        cost_estimate=cost(nseg * 45e-6),
        name="feed",
    )(mask, att, x, cot, wout, up, down, gains)


STEPS = 6
INNER_TABLE = (
    (1, "start", 0, 0), (1, "feed", 2, 0), (1, "feed", 1, 0), (2, "feed", 0, 0),
    (2, "reduce", 0, 0), (3, "start", 1, 0), (4, "feed", 2, 1), (4, "feed", 1, 1),
    (4, "reduce", 1, 0), (4, "reduce", 0, 1), (4, "feed", 0, 1), (5, "start", 2, 0),
    (8, "reduce", 1, 1), (8, "reduce", 2, 0), (8, "feed", 2, 2), (8, "feed", 1, 2),
    (9, "reduce", 0, 2), (12, "reduce", 0, 3), (13, "vec_start", 0, 0), (13, "reduce", 2, 1),
    (14, "feed", 0, 2), (14, "reduce", 0, 4), (14, "vec", 0, 0), (14, "reduce", 1, 2),
    (14, "vec", 0, 1), (14, "reduce", 2, 2), (14, "vec", 0, 2), (14, "spread", 0, 0),
    (14, "reduce", 1, 3), (14, "vec", 0, 3), (14, "reduce", 2, 3), (14, "spread", 0, 1),
    (14, "reduce", 1, 4), (14, "vec", 0, 4), (14, "reduce", 2, 4), (14, "spread", 0, 2),
    (14, "spread", 1, 0), (14, "spread", 2, 0), (14, "spread", 1, 1), (14, "spread", 2, 1),
    (14, "spread", 1, 2), (14, "spread", 2, 2),
)


def inner_back_kernel(
    nseg, first, local_ref, inner_ref, w_ref, x_ref, gmid_ref, gain_ref, feed_vec_ref, piece_ref, *refs
):
    n = BRANCHES - first
    packs, (weight_ref, back_ref, vec_ref, up_ref, proj_ref, down_ref) = refs[:n], refs[n : n + 6]
    acc, mixed, order, terms, recv_core, recv_x, recv_seq, total, feed_total, vecs, vec_recv = refs[n + 6 : n + 17]
    red_send, red_recv, in_send, in_recv, feed_send, feed_recv, vec_send, vec_recv_sems = refs[n + 17 :]
    step = pl.program_id(0)
    last = pl.num_programs(0) - 1
    length = nseg * SEG
    turns = length // ROWS
    end = STEPS + turns
    blocks = terms.shape[1] // CHUNKS
    core = lax.rem(lax.axis_index("fsdp"), 2)
    spread = Spread(inner_orders(), blocks, total, Sends(in_send, in_recv))
    reduce = Reduce(
        inner_orders(), blocks, terms, terms, lambda xo: 2 * xo + core, recv_core, recv_x, recv_seq, Sends(red_send, red_recv),
        spread.begin,
    )
    feed_spread = Spread(feed_orders(), feed_total.shape[0] // CHUNKS, feed_total, Sends(feed_send, feed_recv))
    vec_sends = Sends(vec_send, vec_recv_sems)
    peers = all_peers()

    def vec_copy(i):
        return vec_sends.copy(i, vecs.at[i], vec_recv.at[i], *peers[i])

    def vec_event(i):
        vec_copy(i).wait_recv()
        vecs[i + 1] = vecs[i] + vec_recv[i]
        if i + 1 < len(peers):
            vec_copy(i + 1).start()

    def vec_start():
        vec_copy(0).start()

    @pl.when(step == 0)
    def _():
        meet(peers)
        vecs[0] = jnp.concatenate([jnp.zeros((2, D), F32), feed_vec_ref[...], jnp.zeros((4, D), F32)], axis=0)
        for chunk in reversed(range(CHUNKS)):
            feed_spread.begin(chunk, piece_ref.at[chunk], 0)

    @pl.when((step >= 2) & (step < STEPS))
    def _():
        upper = lax.rem(step, 2) == 1
        for pack, level in zip(packs, range(first, BRANCHES)):
            size = SEG >> level
            for head in range(HEADS // 2):
                rows = slice(head * HEAD_DIM, (head + 1) * HEAD_DIM)
                for seg in range(nseg):
                    start = seg * SEG + (rev4(head) >> (4 - level)) * size
                    piece = pack[0, rows, seg * size : (seg + 1) * size].astype(F32)
                    if level == 4:
                        zero = jnp.zeros_like(piece)
                        piece = jnp.concatenate(
                            [jnp.where(upper, zero, piece), jnp.where(upper, piece, zero)], axis=1
                        )
                    local_ref[0, rows, start : start + piece.shape[1]] += piece

    @pl.when(step < STEPS)
    def _():
        block = local_ref[0].astype(BF16)
        mixed[pl.ds(pl.multiple_of(step * HALF, HALF), HALF), :] = block
        base = lax.div(step, 2) * blocks + lax.rem(step, 2) * 36
        grad_in = dotg(block, inner_ref[...], 1, 1).T.astype(BF16)
        for col in range(3):
            part = grad_in[:, col * 128 : (col + 1) * 128].reshape(4, 12, 16, 128)
            for owner in range(4):
                terms[owner, pl.ds(base + col * 12, 12)] = part[owner]

    def inner_grad(turn):
        lanes = pl.ds(pl.multiple_of(turn * ROWS, ROWS), ROWS)
        acc[lax.rem(turn, 2)] = dotg(w_ref[...], mixed[:, lanes], 1, 0)

    @pl.when(step == STEPS - 1)
    def _():
        inner_grad(step - (STEPS - 1))

    @pl.when((step >= STEPS) & (step < end))
    def _():
        turn = step - STEPS
        inner_grad(lax.rem(turn + 1, turns))
        quarter = lax.rem(turn, 4)
        low = (quarter >> 1) | ((quarter & 1) << 1)
        gain = gain_ref[0:1, :]
        grad = acc[lax.rem(turn, 2)].T
        _, unit, inverse = normalize(x_ref[...].astype(F32), gain, gain)
        back, gain_part, shift_part = normalize_back(grad, unit, inverse, gain)
        vecs[0, 0:1, :] += gain_part[None, :]
        vecs[0, 1:2, :] += shift_part[None, :]
        total_back = gmid_ref[...] + back
        for i in range(4):
            put_residue(order, rev4(i) + low, total_back[i * RUN : (i + 1) * RUN])

        @pl.when(quarter == 3)
        def _():
            back_ref[...] = get_rows(order, 0, SEG)

    calls = {
        "start": lambda chunk, stage: reduce.begin(chunk),
        "reduce": lambda chunk, stage: reduce.event(stage, chunk),
        "spread": lambda chunk, stage: spread.event(stage, chunk),
        "feed": lambda chunk, stage: feed_spread.event(stage, chunk),
        "vec_start": lambda chunk, stage: vec_start(),
        "vec": lambda chunk, stage: vec_event(stage),
    }
    if seq_bits() == 3 and turns == 8:
        table = INNER_TABLE
    else:
        table = []
        for chunk in range(CHUNKS):
            begin = 2 * chunk + 1
            late = begin + 2 * reduce.stages() + 3 * chunk
            table += [(1 + 2 * stage, "feed", chunk, stage) for stage in range(feed_spread.stages())]
            table += [(begin, "start", chunk, 0), (begin + 1, "reduce", chunk, 0)]
            table += [
                (begin + 1 + 3 * chunk + 2 * stage, "reduce", chunk, stage)
                for stage in range(1, reduce.stages())
            ]
            table += [(late + 2 * stage, "spread", chunk, stage) for stage in range(spread.stages())]
        table += [(end - 1, "vec_start", 0, 0)]
        table += [(end + stage, "vec", 0, stage) for stage in range(len(peers))]
        table.sort(key=lambda event: event[0])
    events = [(when, functools.partial(calls[name], chunk, stage)) for when, name, chunk, stage in table]
    run_schedule(step, last, events)

    @pl.when(step == last)
    def _():
        for tile in range(TILES):
            cols = slice(tile * 128, (tile + 1) * 128)
            for col in range(4):
                at = col * 72 + tile * 12
                up_ref[:, col * D + tile * 128 : col * D + (tile + 1) * 128] = rows_of(feed_total, at, 12)
            proj_ref[:, cols] = rows_of(feed_total, 288 + tile * 12, 12)
            down_ref[:, cols] = rows_of(feed_total, 360 + tile * 48, 48)

    @pl.when(step == last)
    def _():
        reduce.finish()
        spread.finish()
        feed_spread.finish()
        for i in range(len(peers)):
            vec_copy(i).wait_send()
        vec_ref[...] = vecs[len(peers)]
        for part in range(STEPS):
            for col in range(3):
                at = part // 2 * blocks + part % 2 * 36 + col * 12
                weight_ref[:, part * HALF + col * 128 : part * HALF + (col + 1) * 128] = rows_of(total, at, 12)


def call_inner_back(nseg, first, local, inner, weight, x, gmid, gain, feed_vec, pieces, packs):
    length = nseg * SEG
    turns = length // ROWS
    blocks = padded(IN_BLOCKS)
    if blocks // CHUNKS < 72:
        raise ValueError("blocks")
    bits = seq_bits()
    peers = 2 + bits
    feed_blocks = CHUNKS * (pieces.shape[1] << bits)

    def at(i):
        return jnp.minimum(i, STEPS - 1)

    def turn(i):
        return jnp.clip(i - STEPS, 0, turns - 1)

    return pl.pallas_call(
        functools.partial(inner_back_kernel, nseg, first),
        grid=(STEPS + turns + 1,),
        in_specs=[
            pl.BlockSpec((1, HALF, length), lambda i: (at(i) // 2, at(i) % 2, 0)),
            const_block((D, length)),
            const_block((D, 3 * D)),
            pl.BlockSpec((ROWS, D), lambda i: (turn(i), 0)),
            pl.BlockSpec((ROWS, D), lambda i: (turn(i), 0)),
            const_block((8, D)),
            const_block((2, D)),
            const_block(pieces.shape),
        ]
        + [
            pl.BlockSpec((1, HALF, pack.shape[2]), lambda i: (jnp.maximum(at(i) // 2 - 1, 0), at(i) % 2, 0))
            for pack in packs
        ],
        out_specs=[
            const_block((192, 3 * D)),
            pl.BlockSpec((SEG, D), lambda i: (turn(i) // 4, 0)),
            const_block((8, D)),
            const_block((192, 4 * D)),
            const_block((192, D)),
            const_block((D, D)),
        ],
        out_shape=[
            shape((192, 3 * D), BF16),
            shape((length, D), F32),
            shape((8, D), F32),
            shape((192, 4 * D), BF16),
            shape((192, D), BF16),
            shape((D, D), BF16),
        ],
        scratch_shapes=[
            pltpu.VMEM((2, D, ROWS), F32),
            pltpu.VMEM((3 * D, length), BF16),
            pltpu.VMEM((TILES, SEG, 128), F32),
            pltpu.VMEM((4, blocks, 16, 128), BF16),
            pltpu.VMEM((2, blocks, 16, 128), BF16),
            pltpu.VMEM((blocks, 16, 128), BF16),
            pltpu.VMEM((blocks, 16, 128), BF16),
            pltpu.VMEM((blocks, 16, 128), BF16),
            pltpu.VMEM((feed_blocks, 16, 128), BF16),
            pltpu.VMEM((peers + 1, 8, D), F32),
            pltpu.VMEM((peers, 8, D), F32),
            sems(reduce_copies()),
            sems(reduce_copies()),
            sems(CHUNKS * bits),
            sems(CHUNKS * bits),
            sems(CHUNKS * bits),
            sems(CHUNKS * bits),
            sems(peers),
            sems(peers),
        ],
        compiler_params=talking(3, 60),
        cost_estimate=cost(nseg * 15e-6),
        name="inner_back",
    )(local, inner, weight, x, gmid, gain, feed_vec, pieces, *packs)


def per_device(
    tokens,
    first_gain,
    first_shift,
    project_in,
    project_out,
    second_gain,
    second_shift,
    up_weight,
    down_weight,
    valid_mask,
    cotangent,
):
    length = tokens.shape[1]
    nseg = length // SEG
    first = nseg.bit_length()

    mask = jnp.sum(valid_mask[0])[None]

    vectors = [first_gain, first_shift, second_gain, second_shift]
    qkv, x, inner, weight_in, gains, *packs = call_project(nseg, first, mask, tokens[0], vectors, project_in)
    weight_in = weight_in.reshape(D, 3 * D)
    o_part, l_part, m_part, gathered, (weight_out, weight_up, weight_down) = call_local_forward(
        nseg, first, qkv, mask, packs, (project_out, up_weight, down_weight)
    )
    attended, lse = call_remote_forward(nseg, first, qkv, mask, o_part, l_part, m_part, gathered)

    mixed, grad_middle, grad_merged, along, feed_vec, feed_grads = call_feed(
        nseg, mask, attended, x, cotangent[0], weight_out, weight_up, weight_down, gains
    )

    dq_remote, *sent = call_remote_backward(nseg, first, qkv, grad_merged, lse, along, mask, gathered)
    local, returned, pieces = call_local_backward(
        nseg, first, qkv, grad_merged, lse, along, mask, dq_remote, sent, feed_grads
    )
    grad_in, tokens_back, vectors, grad_up, grad_out, grad_down = call_inner_back(
        nseg, first, local, inner, weight_in, x, grad_middle, gains, feed_vec, pieces, returned
    )
    quarter = D // lax.axis_size("fsdp")
    vectors = lax.dynamic_slice_in_dim(vectors, lax.axis_index("fsdp") * quarter, quarter, 1)
    return (
        mixed[None],
        tokens_back[None],
        vectors[0],
        vectors[1],
        grad_in.astype(F32),
        grad_out.astype(F32),
        vectors[2],
        vectors[3],
        grad_up.astype(F32),
        grad_down.astype(F32),
    )


def solution(mesh):
    in_specs = (
        P("fsdp", "seq", None),
        P("fsdp"),
        P("fsdp"),
        P("fsdp", None),
        P("fsdp", None),
        P("fsdp"),
        P("fsdp"),
        P("fsdp", None),
        P("fsdp", None),
        P("fsdp", "seq"),
        P("fsdp", "seq", None),
    )
    out_specs = (
        P("fsdp", "seq", None),
        P("fsdp", "seq", None),
        P("fsdp"),
        P("fsdp"),
        P("fsdp", None),
        P("fsdp", None),
        P("fsdp"),
        P("fsdp"),
        P("fsdp", None),
        P("fsdp", None),
    )
    return jax.shard_map(
        per_device, mesh=mesh, in_specs=in_specs, out_specs=out_specs, check_vma=False
    )
```

```python
import functools
import math

import jax
import jax.numpy as jnp
import ml_dtypes
import numpy as np
from jax import lax
from jax.experimental import pallas as pl
from jax.experimental.pallas import tpu as pltpu
from jax.sharding import PartitionSpec as P

HEADS = 16
HEAD_DIM = 48
SEG = 1024
BRANCHES = 5
RES = 16
RUN = SEG // RES
D = HEADS * HEAD_DIM

EPS = 1e-05
NEG = -1e30
ROOT_HALF = 0.7071067811865476
INV_ROOT_TWO_PI = 0.3989422804014327
F32 = jnp.float32
BF16 = jnp.bfloat16
QUERY_SCALE = math.log2(math.e) * HEAD_DIM ** (-0.5)
VMEM_LIMIT = 56 * 1024 * 1024


def dotg(left, right, left_dim, right_dim):
    return lax.dot_general(
        left, right, (((left_dim,), (right_dim,)), ((), ())), preferred_element_type=F32
    )


def normalize(values, gain, shift):
    mean = jnp.mean(values, axis=-1, keepdims=True)
    centred = values - mean
    spread = jnp.mean(centred * centred, axis=-1, keepdims=True)
    inverse = lax.rsqrt(spread + EPS)
    normed = centred * inverse
    return (normed * gain + shift, normed, inverse)


def normalize_back(grad, normed, inverse, gain):
    scaled = grad * gain
    first = jnp.mean(scaled, axis=-1, keepdims=True)
    second = jnp.mean(scaled * normed, axis=-1, keepdims=True)
    return (
        inverse * (scaled - first - normed * second),
        jnp.sum(grad * normed, axis=0),
        jnp.sum(grad, axis=0),
    )


def reversed_bits(head):
    return ((head & 1) << 3) | ((head & 2) << 1) | ((head & 4) >> 1) | ((head & 8) >> 3)


def near_class(head, low_bits, length):
    lane = lax.broadcasted_iota(jnp.int32, (1, length), 1)
    rho = lax.rem(lane // RUN, 1 << low_bits)
    return rho ^ (reversed_bits(head) & ((1 << low_bits) - 1))


def class_rows(near, length):
    row = lax.broadcasted_iota(jnp.int32, (16, length), 0)
    step = lax.rem(row + 3, 4) + 1
    bound = jnp.where((row >= 5) & (row <= 12), lax.shift_right_logical(RES, step), 0)
    return row, near < bound


def query_rows(head, length, neg_lse=None):
    near = near_class(head, 4, length)
    row, inside = class_rows(near, length)
    out = jnp.where(inside, 1.0, 0.0)
    out = jnp.where(row == 0, 1.0, out)
    out = jnp.where(row == 4, jnp.where(near < 1, 0.0, NEG), out)
    if neg_lse is not None:
        high = neg_lse.astype(BF16).astype(F32)
        rest = neg_lse - high
        mid = rest.astype(BF16).astype(F32)
        low = rest - mid
        out = jnp.where(row == 1, high, jnp.where(row == 2, mid, jnp.where(row == 3, low, out)))
    return out.astype(BF16)


def residue_of(rho):
    return reversed_bits(rho)


def local_keep(count, length):
    lane = lax.broadcasted_iota(jnp.int32, (1, length), 1)
    rho = lax.rem(lane // RUN, RES)
    position = lane // SEG * SEG + lax.rem(lane, RUN) * RES + residue_of(rho)
    return position < count


def packed_keep(count, level, nseg):
    size = SEG >> level
    dims = (HEADS, nseg * size)
    head = lax.broadcasted_iota(jnp.int32, dims, 0)
    lane = lax.broadcasted_iota(jnp.int32, dims, 1)
    rho = (reversed_bits(head) >> (4 - level)) * (size // RUN) + lax.rem(lane, size) // RUN
    position = lane // size * SEG + lax.rem(lane, RUN) * RES + residue_of(rho)
    return jnp.where(position < count, 1.0, 0.0).astype(BF16)


def weight_of(level, step):
    return math.log2((step - level + 1) / (step - level)) if step > level else 0.0


def key_rows(head, level, low_bits, length, keep):
    near = near_class(head, low_bits, length)
    row, inside = class_rows(near, length)
    weight = jnp.zeros((16, length), F32)
    for step in range(level + 1, BRANCHES):
        value = weight_of(level, step)
        high = float(np.asarray(value, ml_dtypes.bfloat16))
        weight = jnp.where(row == 4 + step, high, weight)
        weight = jnp.where(row == 8 + step, value - high, weight)
    out = jnp.where(inside, weight, 0.0)
    out = jnp.where((row >= 1) & (row <= 3), 1.0, out)
    out = jnp.where(row == 0, jnp.where(keep, 0.0, NEG), out)
    if level == BRANCHES - 1:
        out = jnp.where(row == 4, 1.0, out)
    return out.astype(BF16)


def value_rows(length):
    row = lax.broadcasted_iota(jnp.int32, (16, length), 0)
    return jnp.where(row < 2, 1.0, 0.0).astype(BF16)


def join(rows, extra):
    return jnp.concatenate([rows, extra], axis=0)


def kept_start(head, level, seg):
    size = SEG >> level
    block = reversed_bits(head) >> (4 - level)
    return pl.multiple_of(seg * SEG + block * size, min(size, 128))


def partner(axis, distance):
    place = lax.axis_index(axis)
    return {axis: place + distance * (1 - 2 * lax.rem(lax.div(place, distance), 2))}


def seq_bits():
    return lax.axis_size("seq").bit_length() - 1


def meet(peers):
    barrier = pltpu.get_barrier_semaphore()
    for axis, distance in peers:
        pl.semaphore_signal(
            barrier, inc=1, device_id=partner(axis, distance), device_id_type=pl.DeviceIdType.MESH
        )
    pl.semaphore_wait(barrier, len(peers))


class Sends:
    def __init__(self, send_sems, recv_sems):
        self.send_sems, self.recv_sems, self.made = send_sems, recv_sems, {}

    def copy(self, key, source, target, axis, distance):
        index = self.made.setdefault(key, len(self.made))
        return pltpu.make_async_remote_copy(
            src_ref=source,
            dst_ref=target,
            send_sem=self.send_sems.at[index],
            recv_sem=self.recv_sems.at[index],
            device_id=partner(axis, distance),
            device_id_type=pl.DeviceIdType.MESH,
        )


class Gather:
    def __init__(self, nseg, first, packs, gathered, sends):
        self.hops, self.distances = [], set()
        for level, pack, into in zip(range(first, BRANCHES), packs, gathered):
            group = (SEG << (level - 1)) // (nseg * SEG)
            source = pack if pack.shape[0] == into.shape[1] else pack.at[pl.ds(D, D + 16)]
            hops = [((level, 0), source, into.at[0], group)]
            step = 1
            while step < group:
                hops.append(((level, step), into.at[pl.ds(0, step)], into.at[pl.ds(step, step)], step))
                step *= 2
            self.hops.append([sends.copy(k, a, b, "seq", d) for k, a, b, d in hops])
            self.distances |= {hop[3] for hop in hops}

    def peers(self):
        return [("seq", distance) for distance in sorted(self.distances)]

    def start(self):
        for hops in reversed(self.hops):
            hops[0].start()

    def pass_on(self, index, turn):
        hops = self.hops[index]
        hops[turn - 1].wait_recv()
        hops[turn].start()

    def finish(self):
        for hops in self.hops:
            for hop in hops:
                hop.wait_send()
            hops[-1].wait_recv()

    def turns(self):
        events = []
        for index, hops in reversed(list(enumerate(self.hops))):
            for turn in range(1, len(hops)):
                when = 4 * turn + (2 if turn > 1 else 0) + (len(self.hops) - 1 - index)
                events.append((when, functools.partial(self.pass_on, index, turn)))
        return events


class Shards:
    def __init__(self, shards, whole, sends, loads):
        self.copies = []
        me = lax.axis_index("fsdp")
        other = lax.rem(me + 2, 4)
        for i, (shard, into) in enumerate(zip(shards, whole)):
            self.copies.append(
                (
                    pltpu.make_async_copy(shard, into.at[me], loads.at[i]),
                    sends.copy((i, "core"), shard, into.at[me], "fsdp", 1),
                    sends.copy((i, "x"), shard, into.at[me], "fsdp", 2),
                    sends.copy((i, "hand"), into.at[other], into.at[other], "fsdp", 1),
                )
            )

    def start(self, count):
        for i, (load, core, x, _) in enumerate(self.copies):
            load.start()
            core.start()
            if i < count:
                x.start()

    def hand(self, i):
        _, _, x, hand = self.copies[i]
        x.wait_recv()
        hand.start()
        if i + 1 < len(self.copies):
            self.copies[i + 1][2].start()

    def finish(self):
        for load, core, x, hand in self.copies:
            load.wait()
            core.wait()
            x.wait_send()
            hand.wait()


class Return:
    def __init__(self, nseg, first, sent, returned, bufs, recvs, local_sems, sends):
        self.plans = []
        for i, level in enumerate(range(first, BRANCHES)):
            group = (SEG << (level - 1)) // (nseg * SEG)
            plan = []
            if group == 1:
                plan.append((None, sends.copy((level, 0), sent[i].at[0], returned[i], "seq", group)))
                self.plans.append((plan, None))
                continue
            buf, recv = bufs.pop(0), recvs.pop(0)
            step = group // 2
            load = pltpu.make_async_copy(sent[i].at[pl.ds(0, step)], buf, local_sems.at[i])
            source, at, add = sent[i].at[pl.ds(step, step)], 0, None
            while step >= 1:
                into = recv.at[pl.ds(at, step)]
                plan.append((add, sends.copy((level, step), source, into, "seq", step)))
                add = (buf, recv, at, step)
                at += step
                step //= 2
                if step:
                    source = buf.at[pl.ds(step, step)]
            plan.append((add, sends.copy((level, 0), buf.at[0], returned[i], "seq", group)))
            self.plans.append((plan, load))

    def start(self, direct):
        for plan, load in reversed(self.plans):
            if direct == (load is None):
                if load is not None:
                    load.start()
                plan[0][1].start()

    def turn(self, number):
        for plan, load in reversed(self.plans):
            if number < len(plan):
                plan[number - 1][1].wait_recv()
                if number == 1 and load is not None:
                    load.wait()
                buf, recv, at, step = plan[number][0]
                for i in range(step):
                    buf[i] = (buf[i].astype(F32) + recv[at + i].astype(F32)).astype(BF16)
                plan[number][1].start()

    def finish(self):
        for plan, load in self.plans:
            for _, copy in plan:
                copy.wait_send()
            plan[-1][1].wait_recv()

    def turns(self):
        return max(len(plan) for plan, _ in self.plans)


def add_blocks(into, at, other, start, count):
    unit = max(u for u in range(1, 13) if count % u == 0)

    def body(i, carry):
        rows = pl.ds(at + i * unit, unit)
        part = other[pl.ds(start + i * unit, unit)].astype(F32)
        into[rows] = (into[rows].astype(F32) + part).astype(BF16)
        return carry

    lax.fori_loop(0, count // unit, body, 0)


def copy_blocks(into, at, other, start, count):
    unit = max(u for u in range(1, 13) if count % u == 0)

    def body(i, carry):
        into[pl.ds(at + i * unit, unit)] = other[pl.ds(start + i * unit, unit)]
        return carry

    lax.fori_loop(0, count // unit, body, 0)


def halving(blocks, order):
    seq = lax.axis_index("seq")
    low, given = [0], []
    for j, distance in enumerate(order):
        bit = lax.rem(lax.div(seq, distance), 2)
        half = blocks >> (j + 1)
        given.append(low[j] + (1 - bit) * half)
        low.append(low[j] + bit * half)
    return low, given


def feed_orders():
    plain = [2**j for j in range(seq_bits())]
    return [plain] * (CHUNKS - 1) + [plain[1:] + plain[:1]]


def inner_orders():
    plain = [2**j for j in range(seq_bits())]
    return [plain] * (CHUNKS - 1) + [[plain[1], plain[0]] + plain[2:]]


def all_peers():
    return [("fsdp", 1), ("fsdp", 2)] + [("seq", 2**j) for j in range(seq_bits())]


class Reduce:
    def __init__(
        self, orders, blocks, source, terms, own, recv_core, recv_x, recv_seq, sends, done, loads=None
    ):
        self.blocks, self.source, self.terms, self.own, self.done = blocks, source, terms, own, done
        self.recv_core, self.recv_x, self.recv_seq = recv_core, recv_x, recv_seq
        self.sends, self.loads = sends, loads
        fsdp = lax.axis_index("fsdp")
        self.core, self.x = lax.rem(fsdp, 2), lax.div(fsdp, 2)
        self.bits = seq_bits()
        self.orders = orders
        self.halves = [halving(blocks, order) for order in self.orders]

    def stages(self):
        return 2 + self.bits

    def core_copy(self, chunk, xo):
        rows = pl.ds(chunk * self.blocks, self.blocks)
        owner = 2 * xo + 1 - self.core
        return self.sends.copy(
            ("core", chunk, xo), self.source.at[owner, rows], self.recv_core.at[xo, rows], "fsdp", 1
        )

    def load_copy(self, chunk, xo):
        rows = pl.ds(chunk * self.blocks, self.blocks)
        return pltpu.make_async_copy(
            self.source.at[2 * xo + self.core, rows], self.terms.at[xo, rows], self.loads.at[2 * chunk + xo]
        )

    def x_copy(self, chunk):
        rows = pl.ds(chunk * self.blocks, self.blocks)
        return self.sends.copy(
            ("x", chunk), self.terms.at[self.own(1 - self.x), rows], self.recv_x.at[rows], "fsdp", 2
        )

    def down_copy(self, chunk, j):
        half = self.blocks >> (j + 1)
        base = chunk * self.blocks
        rows = pl.ds(base + self.halves[chunk][1][j], half)
        into = pl.ds(base + self.blocks - (self.blocks >> j), half)
        return self.sends.copy(
            ("down", chunk, j), self.terms.at[self.own(self.x), rows], self.recv_seq.at[into], "seq",
            self.orders[chunk][j],
        )

    def begin(self, chunk):
        for xo in range(2):
            if self.loads is not None:
                self.load_copy(chunk, xo).start()
            self.core_copy(chunk, xo).start()

    def event(self, stage, chunk):
        base = chunk * self.blocks
        low = self.halves[chunk][0]
        mine = self.terms.at[self.own(self.x)]
        if stage == 0:
            for xo in range(2):
                self.core_copy(chunk, xo).wait_recv()
                if self.loads is not None:
                    self.load_copy(chunk, xo).wait()
                add_blocks(self.terms.at[self.own(xo)], base, self.recv_core.at[xo], base, self.blocks)
            self.x_copy(chunk).start()
            return
        j = stage - 2
        if stage == 1:
            self.x_copy(chunk).wait_recv()
            add_blocks(mine, base, self.recv_x, base, self.blocks)
        else:
            self.down_copy(chunk, j).wait_recv()
            half = self.blocks >> (j + 1)
            add_blocks(mine, base + low[j + 1], self.recv_seq, base + self.blocks - (self.blocks >> j), half)
        if j + 1 < self.bits:
            self.down_copy(chunk, j + 1).start()
        else:
            self.done(chunk, mine, base + low[self.bits])

    def finish(self):
        for chunk in range(CHUNKS):
            for xo in range(2):
                self.core_copy(chunk, xo).wait_send()
            self.x_copy(chunk).wait_send()
            for j in range(self.bits):
                self.down_copy(chunk, j).wait_send()


class Spread:
    def __init__(self, orders, blocks, total, sends):
        self.blocks, self.total, self.sends = blocks, total, sends
        self.bits = seq_bits()
        self.orders = orders
        self.lows = [halving(blocks, order)[0] for order in self.orders]

    def stages(self):
        return self.bits

    def copy(self, chunk, j):
        rows = pl.ds(chunk * self.blocks + self.lows[chunk][j + 1], self.blocks >> (j + 1))
        here = self.total.at[rows]
        return self.sends.copy((chunk, j), here, here, "seq", self.orders[chunk][j])

    def begin(self, chunk, ref, start):
        size = self.blocks >> self.bits
        copy_blocks(self.total, chunk * self.blocks + self.lows[chunk][self.bits], ref, start, size)
        self.copy(chunk, self.bits - 1).start()

    def event(self, stage, chunk):
        j = self.bits - 1 - stage
        self.copy(chunk, j).wait_recv()
        if j:
            self.copy(chunk, j - 1).start()

    def finish(self):
        for chunk in range(CHUNKS):
            for j in range(self.bits):
                self.copy(chunk, j).wait_send()


def run_schedule(step, last, events):
    due = {}
    for when, call in events:
        due.setdefault(min(when, last), []).append(call)
    for when in sorted(due):

        @pl.when(step == when)
        def _():
            for call in due[when]:
                call()


FRONT = 3
KEY_TILE = 128


class State:
    def __init__(self, query, acc=None, top=None):
        self.query, self.acc, self.top = query, acc, top


def attend(items):
    items = list(items)
    ready = []
    for turn in range(len(items) + FRONT):
        if turn < len(items):
            state, key, _ = items[turn]
            ready.append(dotg(key, state.query, 1, 0))
        if turn >= FRONT:
            state, _, value = items[turn - FRONT]
            scores, ready[turn - FRONT] = ready[turn - FRONT], None
            top = jnp.max(scores, axis=0, keepdims=True)
            if state.top is not None:
                top = jnp.maximum(top, state.top)
            probs = jnp.exp2(scores - top).astype(BF16)
            part = dotg(value, probs, 1, 0)
            state.acc = part if state.top is None else state.acc * jnp.exp2(state.top - top) + part
            state.top = top


def key_items(state, key_t, value):
    size = key_t.shape[0]
    tile = min(KEY_TILE, size)
    for start in range(0, size, tile):
        yield state, key_t[start : start + tile], value[:, start : start + tile]


def load_state(query, mine, o_ref, l_ref, m_ref):
    acc = [jnp.concatenate([o_ref[:, at], jnp.broadcast_to(l_ref[0, :, at], (16, at.size))]) for at in mine]
    top = [m_ref[0, :, at] for at in mine]
    return State(query, jnp.concatenate(acc, axis=1), jnp.concatenate(top, axis=1))


def store_state(state, mine, o_ref, l_ref, m_ref):
    start = 0
    for at in mine:
        lanes = slice(start, start + at.size)
        o_ref[:, at] = state.acc[:HEAD_DIM, lanes]
        l_ref[0, :, at] = state.acc[HEAD_DIM : HEAD_DIM + 1, lanes]
        m_ref[0, :, at] = state.top[:, lanes]
        start += at.size


def local_forward(nseg, first, mask_ref, q_ref, k_ref, v_ref, *refs):
    n = BRANCHES - first
    packs, shards, (o_ref, l_ref, m_ref) = refs[:n], refs[n : n + 2], refs[n + 2 : n + 5]
    gathered, whole = refs[n + 5 : 2 * n + 5], refs[2 * n + 5 : 2 * n + 7]
    qa, ka, va, send_sems, recv_sems, shard_send, shard_recv, shard_load = refs[2 * n + 7 :]
    head = pl.program_id(0)
    gather = Gather(nseg, first, packs, gathered, Sends(send_sems, recv_sems))
    fetch = Shards(shards, whole, Sends(shard_send, shard_recv), shard_load)

    def begin():
        meet(gather.peers() + [("fsdp", 1), ("fsdp", 2)])
        gather.start()
        fetch.start(1)

    def finish():
        gather.finish()
        fetch.hand(1)
        fetch.finish()

    hands = [(9, functools.partial(fetch.hand, 0))]
    run_schedule(head, HEADS - 1, [(0, begin)] + sorted(gather.turns() + hands, key=lambda event: event[0]))
    local_forward_core(nseg, mask_ref, q_ref, k_ref, v_ref, o_ref, l_ref, m_ref, qa, ka, va)
    run_schedule(head, HEADS - 1, [(HEADS - 1, finish)])


def local_forward_scratch(nseg):
    length = nseg * SEG
    return [
        pltpu.VMEM((64, length), BF16),
        pltpu.VMEM((nseg, 64, length), BF16),
        pltpu.VMEM((64, length), BF16),
    ]


def local_forward_core(nseg, mask_ref, q_ref, k_ref, v_ref, o_ref, l_ref, m_ref, qa, ka, va):
    head = pl.program_id(0)
    length = nseg * SEG
    keep = local_keep(mask_ref[0], length)
    qa[...] = join(q_ref[0], query_rows(head, length))
    va[...] = join(v_ref[0], value_rows(length))
    ka[0] = join(k_ref[0], key_rows(head, 0, 4, length, keep))
    if nseg == 2:
        ka[1] = join(k_ref[0], key_rows(head, 1, 4, length, keep))
    states, items = [], []
    for seg in range(nseg):
        lanes = slice(seg * SEG, (seg + 1) * SEG)
        states.append(State(qa[:, lanes]))
        items += key_items(states[-1], ka[0, :, lanes].T, va[:, lanes])
    attend(items)
    for seg in range(nseg):
        store_state(states[seg], [pl.ds(seg * SEG, SEG)], o_ref, l_ref, m_ref)
    if nseg == 2:
        kept = [pl.ds(kept_start(head, 1, seg), SEG // 2) for seg in range(2)]
        states = [load_state(qa[:, at], [at], o_ref, l_ref, m_ref) for at in kept]
        items = []
        for seg in range(2):
            items += key_items(states[seg], ka[1, :, kept[1 - seg]].T, va[:, kept[1 - seg]])
        attend(items)
        for seg in range(2):
            store_state(states[seg], [kept[seg]], o_ref, l_ref, m_ref)


def remote_keys(head, level, pack):
    k_ref, v_ref, mask_ref = pack
    pieces = range(k_ref.shape[0])
    key, value, mask = (
        jnp.concatenate([ref[i] for i in pieces], axis=1) for ref in (k_ref, v_ref, mask_ref)
    )
    length = key.shape[1]
    row = lax.broadcasted_iota(jnp.int32, (16, length), 0)
    keep = jnp.sum(jnp.where(row == head, mask.astype(F32), 0.0), axis=0, keepdims=True) > 0.5
    return join(key, key_rows(head, level, 4 - level, length, keep)), join(value, value_rows(length))


def remote_plan(first):
    return [(level,) for level in range(first, 3)] + [(3, 4)]


def remote_forward(nseg, first, mask_ref, q_ref, o_in, l_in, m_in, *refs):
    head = pl.program_id(0)
    levels = range(first, BRANCHES)
    packs = {level: refs[3 * i : 3 * i + 3] for i, level in enumerate(levels)}
    att_ref, lse_ref, o_ref, l_ref, m_ref, qa = refs[3 * len(levels) :]
    length = nseg * SEG
    qa[...] = join(q_ref[0], query_rows(head, length))
    o_ref[...] = o_in[...]
    l_ref[...] = l_in[...]
    m_ref[...] = m_in[...]
    for group in remote_plan(first):
        pairs = [remote_keys(head, level, packs[level]) for level in group]
        key = jnp.concatenate([pair[0] for pair in pairs], axis=1)
        value = jnp.concatenate([pair[1] for pair in pairs], axis=1)
        mine = [pl.ds(kept_start(head, group[0], seg), SEG >> group[0]) for seg in range(nseg)]
        query = jnp.concatenate([qa[:, at] for at in mine], axis=1)
        state = load_state(query, mine, o_ref, l_ref, m_ref)
        attend(key_items(state, key.T, value))
        store_state(state, mine, o_ref, l_ref, m_ref)
    weight = jnp.where(local_keep(mask_ref[0], length), 1.0, 0.0) / l_ref[0]
    att_ref[...] = (o_ref[...] * weight).astype(BF16)
    lse_ref[0] = m_ref[0] + jnp.log2(l_ref[0])


def grad_rows(grad, slope):
    length = grad.shape[1]
    row = lax.broadcasted_iota(jnp.int32, (16, length), 0)
    high = (-slope).astype(BF16).astype(F32)
    low = -slope - high
    extra = jnp.where(row == 0, high, jnp.where(row == 1, low, 0.0)).astype(BF16)
    return join(grad, extra)


AHEAD = 2
QUERY_TILE = 256
BACK_KEYS = 256


class Side:
    def __init__(self, query, grad):
        self.query, self.grad = query[:HEAD_DIM], grad[:HEAD_DIM]
        self.query_t, self.grad_t = query.T, grad.T
        self.dq = None


def attend_back(items, dk_ref, dv_ref, written):
    items = list(items)
    ready = []
    for turn in range(len(items) + AHEAD):
        if turn < len(items):
            side, key, value, _, _ = items[turn]
            ready.append((dotg(side.query_t, key, 1, 0), dotg(side.grad_t, value, 1, 0)))
        if turn >= AHEAD:
            side, key, _, lanes, name = items[turn - AHEAD]
            scores, slope = ready[turn - AHEAD]
            ready[turn - AHEAD] = None
            probs = jnp.exp2(scores)
            dscore = (probs * slope).astype(BF16)
            dv = dotg(side.grad, probs.astype(BF16), 1, 0)
            dk = dotg(side.query, dscore, 1, 0)
            part = dotg(key[:HEAD_DIM], dscore, 1, 1)
            side.dq = part if side.dq is None else side.dq + part
            if name in written:
                dv_ref[:, lanes] += dv
                dk_ref[:, lanes] += dk
            else:
                written.add(name)
                dv_ref[:, lanes] = dv
                dk_ref[:, lanes] = dk


def sides_of(query, grad):
    tile = min(QUERY_TILE, query.shape[1])
    return [
        Side(query[:, start : start + tile], grad[:, start : start + tile])
        for start in range(0, query.shape[1], tile)
    ]


def pairs(sides, key_ref, value_ref, tiles):
    return [
        (side, key_ref[:, lanes], value_ref[:, lanes], lanes, name) for side in sides for name, lanes in tiles
    ]


def joined(sides):
    return jnp.concatenate([side.dq for side in sides], axis=1) if len(sides) > 1 else sides[0].dq


DQ_SCALE = HEAD_DIM ** (-0.5)
DK_SCALE = math.log(2.0)


def neg_total(lse, keep):
    return jnp.where(keep, -lse, NEG)


def local_backward(nseg, first, mask_ref, q_ref, k_ref, v_ref, g_ref, lse_ref, slope_ref, dqr_ref, *refs):
    n = BRANCHES - first
    sent, feed_ref, out_ref = refs[:n], refs[n], refs[n + 1]
    returned, piece_ref = refs[n + 2 : 2 * n + 2], refs[2 * n + 2]
    qa, ga, ka, va, dk, dv = refs[2 * n + 3 : 2 * n + 9]
    rest = list(refs[2 * n + 9 :])
    back_send, back_recv, back_load, red_send, red_recv, red_load = rest[-6:]
    terms, recv_core, recv_x, recv_seq = rest[-10:-6]
    bufs, recvs = rest[: (len(rest) - 10) // 2], rest[(len(rest) - 10) // 2 : -10]
    head = pl.program_id(0)
    last = HEADS - 1

    back = Return(nseg, first, sent, returned, bufs, recvs, back_load, Sends(back_send, back_recv))
    blocks = terms.shape[1] // CHUNKS
    reduce = Reduce(
        feed_orders(), blocks, feed_ref, terms, lambda xo: xo, recv_core, recv_x, recv_seq, Sends(red_send, red_recv),
        lambda chunk, ref, start: copy_blocks(piece_ref.at[chunk], 0, ref, start, blocks >> seq_bits()),
        red_load,
    )

    def begin():
        meet(all_peers())
        back.start(False)
        for chunk in range(CHUNKS):
            reduce.begin(chunk)

    events = [(3 * turn, functools.partial(back.turn, turn)) for turn in range(1, back.turns())]
    events.append((8, functools.partial(back.start, True)))
    for chunk in range(CHUNKS):
        for stage in range(reduce.stages()):
            when = 1 + (chunk + 1) // 2 if stage == 0 else 4 + 3 * chunk + 2 * (stage - 1)
            events.append((when, functools.partial(reduce.event, stage, chunk)))
    run_schedule(head, last, [(0, begin)] + sorted(events, key=lambda event: event[0]))
    local_backward_core(
        nseg, first, mask_ref, q_ref, k_ref, v_ref, g_ref, lse_ref, slope_ref, dqr_ref, out_ref,
        qa, ga, ka, va, dk, dv,
    )

    @pl.when(head == last)
    def _():
        back.finish()
        reduce.finish()


def local_backward_scratch(nseg):
    length = nseg * SEG
    return [
        pltpu.VMEM((64, length), BF16),
        pltpu.VMEM((64, length), BF16),
        pltpu.VMEM((nseg, 64, length), BF16),
        pltpu.VMEM((64, length), BF16),
        pltpu.VMEM((HEAD_DIM, length), F32),
        pltpu.VMEM((HEAD_DIM, length), F32),
    ]


def local_backward_core(
    nseg, first, mask_ref, q_ref, k_ref, v_ref, g_ref, lse_ref, slope_ref, dqr_ref, out_ref,
    qa, ga, ka, va, dk, dv,
):
    head = pl.program_id(0)
    length = nseg * SEG
    keep = local_keep(mask_ref[0], length)
    qa[...] = join(q_ref[0], query_rows(head, length, neg_total(lse_ref[0], keep)))
    ga[...] = grad_rows(g_ref[...], slope_ref[0])
    va[...] = join(v_ref[0], value_rows(length))
    ka[0] = join(k_ref[0], key_rows(head, 0, 4, length, keep))
    if nseg == 2:
        ka[1] = join(k_ref[0], key_rows(head, 1, 4, length, keep))
    items, sides, written = [], [], set()
    for seg in range(nseg):
        lanes = slice(seg * SEG, (seg + 1) * SEG)
        tiles = [
            ((seg, i), slice(seg * SEG + BACK_KEYS * i, seg * SEG + BACK_KEYS * (i + 1)))
            for i in range(SEG // BACK_KEYS)
        ]
        sides.append(sides_of(qa[:, lanes], ga[:, lanes]))
        items += pairs(sides[-1], ka.at[0], va, tiles)
    attend_back(items, dk, dv, written)
    for seg in range(nseg):
        out_ref[0, :, seg * SEG : (seg + 1) * SEG] = joined(sides[seg]) * DQ_SCALE
    if nseg == 2:
        items, sides = [], []
        kept = [pl.ds(kept_start(head, 1, seg), SEG // 2) for seg in range(2)]
        for seg in range(2):
            base = kept_start(head, 1, 1 - seg)
            tile = min(BACK_KEYS, SEG // 2)
            tiles = [
                ((seg, i), pl.ds(pl.multiple_of(base + tile * i, tile), tile)) for i in range(SEG // 2 // tile)
            ]
            sides.append(sides_of(qa[:, kept[seg]], ga[:, kept[seg]]))
            items += pairs(sides[-1], ka.at[1], va, tiles)
        attend_back(items, dk, dv, set(item[4] for item in items))
        for seg in range(2):
            out_ref[0, :, kept[seg]] += joined(sides[seg]) * DQ_SCALE
    size = SEG >> first
    for seg in range(nseg):
        mine = pl.ds(kept_start(head, first, seg), size)
        out_ref[0, :, mine] += dqr_ref[:, seg * size : (seg + 1) * size]
    out_ref[1] = dk[...] * DK_SCALE
    out_ref[2] = dv[...]


def rows_of(total, at, count):
    return total[at : at + count].reshape(count * 16, 128)


def remote_backward(nseg, first, mask_ref, q_ref, g_ref, lse_ref, slope_ref, *refs):
    head = pl.program_id(0)
    levels = range(first, BRANCHES)
    n = len(levels)
    packs = {level: refs[3 * i : 3 * i + 3] for i, level in enumerate(levels)}
    dqr_ref = refs[3 * n]
    outs = {level: refs[3 * n + 1 + i] for i, level in enumerate(levels)}
    qa, ga, ka, va, dk, dv = refs[4 * n + 1 :]
    length = nseg * SEG
    qa[...] = join(q_ref[0], query_rows(head, length, neg_total(lse_ref[0], local_keep(mask_ref[0], length))))
    ga[...] = grad_rows(g_ref[...], slope_ref[0])
    full = SEG >> first
    for group in remote_plan(first):
        for i, level in enumerate(group):
            key, value = remote_keys(head, level, packs[level])
            ka[:, i * 512 : (i + 1) * 512] = key
            va[:, i * 512 : (i + 1) * 512] = value
        size = SEG >> group[0]
        mine = [pl.ds(kept_start(head, group[0], seg), size) for seg in range(nseg)]
        query = jnp.concatenate([qa[:, m] for m in mine], axis=1)
        grad = jnp.concatenate([ga[:, m] for m in mine], axis=1)
        tile = min(BACK_KEYS, 512)
        tiles = [(i, slice(tile * i, tile * (i + 1))) for i in range(512 // tile * len(group))]
        sides = sides_of(query, grad)
        attend_back(pairs(sides, ka, va, tiles), dk, dv, set())
        dq = joined(sides) * DQ_SCALE
        for seg in range(nseg):
            piece = dq[:, seg * size : (seg + 1) * size]
            if group[0] == first:
                dqr_ref[:, seg * full : (seg + 1) * full] = piece
            else:
                inner = (reversed_bits(head) >> (4 - group[0])) & ((1 << (group[0] - first)) - 1)
                lanes = pl.ds(pl.multiple_of(seg * full + inner * size, 128), size)
                dqr_ref[:, lanes] += piece
        for i, level in enumerate(group):
            pieces, _, _, size = outs[level].shape
            for piece in range(pieces):
                lanes = slice(i * 512 + piece * size, i * 512 + (piece + 1) * size)
                outs[level][piece, 0] = (dk[:, lanes] * DK_SCALE).astype(BF16)
                outs[level][piece, 1] = dv[:, lanes].astype(BF16)


def row_block(length):
    return pl.BlockSpec((1, 1, length), lambda h: (h, 0, 0))


def head_block(length):
    return pl.BlockSpec((HEAD_DIM, length), lambda h: (h, 0))


def part_block(part, length):
    return pl.BlockSpec((1, HEAD_DIM, length), lambda h: (part, h, 0))


MASK_BLOCK = pl.BlockSpec(memory_space=pltpu.SMEM)


def pack_args(keys, packs):
    args, specs = [], []
    for i, pack in enumerate(packs):
        group, _, length = pack.shape
        ahead = 0 if i == 0 else HEADS
        args += [keys if i == 0 else pack, pack, pack]
        specs += [
            pl.BlockSpec((group, HEAD_DIM, length), lambda h: (0, h, 0)),
            pl.BlockSpec((group, HEAD_DIM, length), lambda h, ahead=ahead: (0, ahead + h, 0)),
            pl.BlockSpec((group, 16, length), lambda h, ahead=ahead: (0, (ahead + HEADS) * 3, 0)),
        ]
    return args, specs


ANY_BLOCK = pl.BlockSpec(memory_space=pl.ANY)


def sems(count):
    return pltpu.SemaphoreType.DMA((count,))


def talking(collective_id, mebibytes=56):
    return pltpu.CompilerParams(
        vmem_limit_bytes=mebibytes * 1024 * 1024, collective_id=collective_id, has_side_effects=True
    )


PARAMS = pltpu.CompilerParams(vmem_limit_bytes=VMEM_LIMIT)


def shape(dims, dtype):
    return jax.ShapeDtypeStruct(dims, dtype)


def cost(seconds):
    return pl.CostEstimate(flops=int(seconds * 1.1e15), transcendentals=0, bytes_accessed=0)


def call_local_forward(nseg, first, qkv, mask, packs, shards):
    length = nseg * SEG
    n = len(packs)
    groups = [(SEG << (level - 1)) // length for level in range(first, BRANCHES)]
    hops = sum(group.bit_length() for group in groups)
    o_part, l_part, m_part, *rest = pl.pallas_call(
        functools.partial(local_forward, nseg, first),
        grid=(HEADS,),
        in_specs=[MASK_BLOCK, part_block(0, length), part_block(1, length), part_block(2, length)]
        + [ANY_BLOCK] * (n + 2),
        out_specs=[head_block(length), row_block(length), row_block(length)] + [ANY_BLOCK] * (n + 2),
        out_shape=[shape((D, length), F32), shape((HEADS, 1, length), F32), shape((HEADS, 1, length), F32)]
        + [
            shape((group, D + 16 if i == 0 else pack.shape[0], pack.shape[1]), BF16)
            for i, (group, pack) in enumerate(zip(groups, packs))
        ]
        + [shape((4,) + shard.shape, BF16) for shard in shards],
        scratch_shapes=local_forward_scratch(nseg)
        + [
            sems(hops),
            sems(hops),
            sems(6),
            sems(6),
            sems(2),
        ],
        compiler_params=talking(1),
        cost_estimate=cost(nseg * 37e-6),
        name="local_forward",
    )(mask, qkv, qkv, qkv, *packs, *shards)
    whole = [weight.reshape(4 * weight.shape[1], weight.shape[2]) for weight in rest[n:]]
    return o_part, l_part, m_part, rest[:n], whole


def call_remote_forward(nseg, first, qkv, mask, o_part, l_part, m_part, keys, packs):
    length = nseg * SEG
    args, specs = pack_args(keys, packs)
    return pl.pallas_call(
        functools.partial(remote_forward, nseg, first),
        grid=(HEADS,),
        in_specs=[MASK_BLOCK, part_block(0, length), head_block(length), row_block(length), row_block(length)]
        + specs,
        out_specs=[head_block(length), row_block(length)],
        out_shape=[shape((D, length), BF16), shape((HEADS, 1, length), F32)],
        scratch_shapes=[
            pltpu.VMEM((HEAD_DIM, length), F32),
            pltpu.VMEM((1, 1, length), F32),
            pltpu.VMEM((1, 1, length), F32),
            pltpu.VMEM((64, length), BF16),
        ],
        compiler_params=PARAMS,
        cost_estimate=cost(nseg * 24e-6),
        name="remote_forward",
    )(mask, qkv, o_part, l_part, m_part, *args)


def call_remote_backward(nseg, first, qkv, grad, lse, slope, mask, keys, packs):
    length = nseg * SEG
    args, specs = pack_args(keys, packs)
    kept = nseg * (SEG >> first)
    return pl.pallas_call(
        functools.partial(remote_backward, nseg, first),
        grid=(HEADS,),
        in_specs=[MASK_BLOCK, part_block(0, length), head_block(length), row_block(length), row_block(length)]
        + specs,
        out_specs=[head_block(kept)]
        + [
            pl.BlockSpec((pack.shape[0], 2, HEAD_DIM, pack.shape[2]), lambda h: (0, 0, h, 0))
            for pack in packs
        ],
        out_shape=[shape((D, kept), F32)]
        + [shape((pack.shape[0], 2, D, pack.shape[2]), BF16) for pack in packs],
        scratch_shapes=[
            pltpu.VMEM((64, length), BF16),
            pltpu.VMEM((64, length), BF16),
            pltpu.VMEM((64, 1024), BF16),
            pltpu.VMEM((64, 1024), BF16),
            pltpu.VMEM((HEAD_DIM, 1024), F32),
            pltpu.VMEM((HEAD_DIM, 1024), F32),
        ],
        compiler_params=PARAMS,
        cost_estimate=cost(nseg * 20e-6),
        name="remote_backward",
    )(mask, qkv, grad, lse, slope, *args)


CHUNKS = 3
FEED_BLOCKS = (4 * D + D + 4 * D) * D // (4 * 16 * 128)
IN_BLOCKS = 3 * D * D // (4 * 16 * 128)


def padded(blocks):
    unit = CHUNKS * lax.axis_size("seq")
    return (blocks + unit - 1) // unit * unit


def reduce_copies():
    return CHUNKS * (3 + seq_bits())


def call_local_backward(nseg, first, qkv, grad, lse, slope, mask, dq_remote, sent, feed_grads):
    length = nseg * SEG
    n = len(sent)
    groups = [part.shape[0] for part in sent]
    hops = sum(group.bit_length() for group in groups)
    blocks = feed_grads.shape[1]
    piece = (CHUNKS, blocks // CHUNKS >> seq_bits(), 16, 128)
    bufs = [pltpu.VMEM((g // 2,) + part.shape[1:], BF16) for g, part in zip(groups, sent) if g > 1]
    recvs = [pltpu.VMEM((g - 1,) + part.shape[1:], BF16) for g, part in zip(groups, sent) if g > 1]
    local, *rest = pl.pallas_call(
        functools.partial(local_backward, nseg, first),
        grid=(HEADS,),
        in_specs=[MASK_BLOCK, part_block(0, length), part_block(1, length), part_block(2, length), head_block(length),
                  row_block(length), row_block(length), head_block(dq_remote.shape[1])]
        + [ANY_BLOCK] * (n + 1),
        out_specs=[pl.BlockSpec((3, HEAD_DIM, length), lambda h: (0, h, 0))]
        + [ANY_BLOCK] * n
        + [const_block(piece)],
        out_shape=[shape((3, D, length), F32)]
        + [shape(part.shape[1:], BF16) for part in sent]
        + [shape(piece, BF16)],
        scratch_shapes=local_backward_scratch(nseg)
        + bufs
        + recvs
        + [
            pltpu.VMEM((2, blocks, 16, 128), BF16),
            pltpu.VMEM((2, blocks, 16, 128), BF16),
            pltpu.VMEM((blocks, 16, 128), BF16),
            pltpu.VMEM((blocks, 16, 128), BF16),
            sems(hops),
            sems(hops),
            sems(n),
            sems(reduce_copies()),
            sems(reduce_copies()),
            sems(2 * CHUNKS),
        ],
        compiler_params=talking(2),
        cost_estimate=cost(nseg * 72e-6),
        name="local_backward",
    )(mask, qkv, qkv, qkv, grad, lse, slope, dq_remote, *sent, feed_grads)
    return local, rest[:n], rest[n]


HALF = D // 2


def const_block(dims):
    return pl.BlockSpec(dims, lambda i: (0,) * len(dims), pipeline_mode=pl.Buffered(1))


def rev4(value):
    return int(reversed_bits(value))


TILES = D // 128


def put_rows(tiled, start, array):
    for tile in range(TILES):
        tiled[tile, start : start + array.shape[0], :] = array[:, tile * 128 : (tile + 1) * 128]


def get_rows(tiled, start, size):
    return jnp.concatenate([tiled[tile, start : start + size, :] for tile in range(TILES)], axis=1)


def get_residue(tiled, start):
    return jnp.concatenate(
        [tiled[tile, pl.ds(start, RUN, stride=RES), :] for tile in range(TILES)], axis=1
    )


def put_residue(tiled, start, array):
    for tile in range(TILES):
        tiled[tile, pl.ds(start, RUN, stride=RES), :] = array[:, tile * 128 : (tile + 1) * 128]


COLUMN_CHUNKS = 3


def project_kernel(nseg, first, mask_ref, tok_ref, *refs):
    n = BRANCHES - first
    vectors, w_ref, out_ref = refs[:4], refs[4], refs[5]
    qkv_ref, xp_ref, inner_ref, weight_ref, gains_ref, whole_ref, keys_ref = refs[6:13]
    packs = refs[13 : 13 + n]
    xs, weight, gains, key_pack, vec_send, vec_recv, w_send, w_recv, w_load, w_store = refs[13 + n : 23 + n]
    key_send, key_recv, out_send, out_recv, out_load = refs[23 + n :]
    step = pl.program_id(0)
    last = pl.num_programs(0) - 1
    me = lax.axis_index("fsdp")
    sibling = me + 1 - 2 * lax.rem(me, 2)
    across = lax.rem(me + 2, 4)
    sends = Sends(w_send, w_recv)

    def send(source, target, key, other):
        index = sends.made.setdefault(key, len(sends.made))
        return pltpu.make_async_remote_copy(
            src_ref=source, dst_ref=target, send_sem=w_send.at[index], recv_sem=w_recv.at[index],
            device_id={"fsdp": other}, device_id_type=pl.DeviceIdType.MESH,
        )

    def chunk_copies(chunk):
        cols = pl.ds(chunk * D, D)
        mine = w_ref.at[:, cols]
        load = pltpu.make_async_copy(mine, weight.at[me, :, cols], w_load.at[chunk])
        core = send(mine, weight.at[me, :, cols], ("core", chunk), sibling)
        x = send(mine, weight.at[me, :, cols], ("x", chunk), across)
        handed = weight.at[across, :, cols]
        return load, core, x, send(handed, handed, ("hand", chunk), sibling)

    def vec_copies():
        return [
            pltpu.make_async_remote_copy(
                src_ref=gains.at[me], dst_ref=gains.at[me], send_sem=vec_send.at[i], recv_sem=vec_recv.at[i],
                device_id={"fsdp": other}, device_id_type=pl.DeviceIdType.MESH,
            )
            for i, other in enumerate((sibling, across, 3 - me))
        ]

    store = pltpu.make_async_copy(weight, weight_ref, w_store.at[0])
    fetch = Shards([out_ref], [whole_ref], Sends(out_send, out_recv), out_load)
    ahead = Sends(key_send, key_recv).copy(0, key_pack, keys_ref, "seq", 1)

    @pl.when(step == 0)
    def _():
        barrier = pltpu.get_barrier_semaphore()
        for other in (sibling, across, 3 - me):
            pl.semaphore_signal(
                barrier, inc=1, device_id={"fsdp": other}, device_id_type=pl.DeviceIdType.MESH
            )
        pl.semaphore_signal(
            barrier, inc=1, device_id=partner("seq", 1), device_id_type=pl.DeviceIdType.MESH
        )
        for i, vector in enumerate(vectors):
            gains[me, i : i + 1, :192] = vector[...].astype(F32).reshape(1, 192)
        pl.semaphore_wait(barrier, 4)
        for copy in vec_copies():
            copy.start()
        for turn in range(COLUMN_CHUNKS):
            for copy in chunk_copies((turn + 1) % COLUMN_CHUNKS)[: 3 if turn == 0 else 2]:
                copy.start()
        fetch.start(1)
        for copy in vec_copies():
            copy.wait_recv()
        full = [
            jnp.concatenate([gains[owner, i : i + 1, :192] for owner in range(4)], axis=1) for i in range(4)
        ]
        gains_ref[...] = jnp.concatenate(full + [jnp.zeros((4, D), F32)], axis=0)
        for seg in range(nseg):
            put_rows(xs, 0, tok_ref[seg * SEG : (seg + 1) * SEG, :].astype(F32))
            for pair in range(RES // 2):
                rows = jnp.concatenate([get_residue(xs, rev4(2 * pair + i)) for i in range(2)], axis=0)
                normed = normalize(rows, full[0], full[1])[0].astype(BF16)
                at = slice(seg * SEG + pair * 2 * RUN, seg * SEG + (pair + 1) * 2 * RUN)
                xp_ref[at, :] = rows.astype(BF16)
                inner_ref[:, at] = normed.T
        for pack, level in zip(packs, range(first, BRANCHES)):
            pack[2 * D :, :] = packed_keep(mask_ref[0], level, nseg)

    for turn in range(COLUMN_CHUNKS):

        @pl.when(step == 2 * turn)
        def _():
            load, core, x, hand = chunk_copies((turn + 1) % COLUMN_CHUNKS)
            x.wait_recv()
            hand.start()
            if turn + 1 < COLUMN_CHUNKS:
                chunk_copies((turn + 2) % COLUMN_CHUNKS)[2].start()
            load.wait()
            core.wait_recv()
            hand.wait_recv()

    @pl.when(step == 2)
    def _():
        fetch.hand(0)

    @pl.when(step == 4)
    def _():
        store.start()

    where = lax.rem(step + 2, 6)
    cols = pl.ds(pl.multiple_of(where * HALF, HALF), HALF)
    block = jnp.concatenate([weight[owner, :, cols] for owner in range(4)], axis=0)
    scale = jnp.where(step >= 4, QUERY_SCALE, 1.0)
    for start in range(0, nseg * SEG, 512):
        lanes = slice(start, start + 512)
        qkv_ref[0, :, lanes] = (dotg(block, inner_ref[:, lanes], 0, 0) * scale).astype(BF16)

    @pl.when(step < 4)
    def _():
        upper = lax.rem(step, 2) == 1
        for pack, level in zip(packs, range(first, BRANCHES)):
            size = SEG >> level
            for head in range(HEADS // 2):
                rows = slice(head * HEAD_DIM, (head + 1) * HEAD_DIM)
                pieces = []
                for seg in range(nseg):
                    start = seg * SEG + (rev4(head) >> (4 - level)) * size
                    if level < 4:
                        pieces.append(qkv_ref[0, rows, start : start + size])
                    else:
                        both = qkv_ref[0, rows, start : start + 2 * size]
                        pieces.append(jnp.where(upper, both[:, size:], both[:, :size]))
                into = pl.ds(pl.multiple_of(step * HALF + head * HEAD_DIM, 16), HEAD_DIM)
                pack[into, :] = jnp.concatenate(pieces, axis=1) if nseg > 1 else pieces[0]

    @pl.when(step == 1)
    def _():
        key_pack[...] = packs[0][:D, :]
        ahead.start()

    @pl.when(step == last)
    def _():
        for copy in vec_copies():
            copy.wait_send()
        for chunk in range(COLUMN_CHUNKS):
            for copy in chunk_copies(chunk)[1:]:
                copy.wait_send()
        store.wait()
        fetch.finish()
        ahead.wait()


def call_project(nseg, first, mask, tokens, vectors, weight, weight_out):
    length = nseg * SEG
    kept = [nseg * (SEG >> level) for level in range(first, BRANCHES)]
    return pl.pallas_call(
        functools.partial(project_kernel, nseg, first),
        grid=(6,),
        in_specs=[MASK_BLOCK, const_block((length, D))] + [const_block((192,))] * 4 + [ANY_BLOCK] * 2,
        out_specs=[
            pl.BlockSpec((1, HALF, length), lambda i: ((i + 2) % 6 // 2, i % 2, 0)),
            const_block((length, D)),
            const_block((D, length)),
            ANY_BLOCK,
            const_block((8, D)),
            ANY_BLOCK,
            ANY_BLOCK,
        ]
        + [const_block((2 * D + 16, size)) for size in kept],
        out_shape=[
            shape((3, D, length), BF16),
            shape((length, D), BF16),
            shape((D, length), BF16),
            shape((4, 192, 3 * D), BF16),
            shape((8, D), F32),
            shape((4, 192, D), BF16),
            shape((D, kept[0]), BF16),
        ]
        + [shape((2 * D + 16, size), BF16) for size in kept],
        scratch_shapes=[
            pltpu.VMEM((TILES, SEG, 128), F32),
            pltpu.VMEM((4, 192, 3 * D), BF16),
            pltpu.VMEM((4, 8, 256), F32),
            pltpu.VMEM((D, kept[0]), BF16),
            sems(3),
            sems(3),
            sems(3 * COLUMN_CHUNKS),
            sems(3 * COLUMN_CHUNKS),
            sems(COLUMN_CHUNKS),
            sems(1),
            sems(1),
            sems(1),
            sems(3),
            sems(3),
            sems(1),
        ],
        compiler_params=talking(4),
        cost_estimate=cost(nseg * 10e-6),
        name="project",
    )(mask, tokens, *vectors, weight, weight_out)


ROWS = 256


def blocks_of(ref, rows, col):
    part = ref[rows, col * 128 : (col + 1) * 128].astype(BF16)
    return part.reshape(part.shape[0] // 16, 16, 128)


def feed_kernel(
    nseg, mask_ref, att_ref, x_ref, cot_ref, wout_ref, up_ref, down_ref, gains_ref,
    mixed_ref, gmid_ref, gm_ref, along_ref, vec_ref, grads_ref,
    cs, out_acc, up_acc, down_acc, stage, sems,
):
    step = pl.program_id(0)
    quarter = lax.rem(step, 4)
    low = (quarter >> 1) | ((quarter & 1) << 1)

    @pl.when(step == 0)
    def _():
        out_acc[...] = jnp.zeros_like(out_acc)
        up_acc[...] = jnp.zeros_like(up_acc)
        down_acc[...] = jnp.zeros_like(down_acc)
        vec_ref[...] = jnp.zeros_like(vec_ref)

    @pl.when(quarter == 0)
    def _():
        put_rows(cs, 0, cot_ref[...].astype(F32))

    grad = jnp.concatenate([get_residue(cs, rev4(i) + low) for i in range(4)], axis=0)
    grad_b = grad.astype(BF16)
    att = att_ref[...]
    middle = x_ref[...].astype(F32) + dotg(att, wout_ref[...], 0, 0)
    gain = gains_ref[2:3, :]
    normed, unit, inverse = normalize(middle, gain, gains_ref[3:4, :])
    hidden = normed.astype(BF16)
    hidden_t = hidden.T
    final = middle
    grad_hidden = jnp.zeros((ROWS, D), F32)
    for start in range(0, 4 * D, D):
        cols = slice(start, start + D)
        upper = dotg(hidden, up_ref[:, cols], 1, 0)
        grad_active = dotg(grad_b, down_ref[cols, :], 1, 1)
        half = 0.5 * (1.0 + lax.erf(upper * ROOT_HALF))
        slope = half + upper * jnp.exp(-0.5 * upper * upper) * INV_ROOT_TWO_PI
        active = (upper * half).astype(BF16)
        grad_upper = (grad_active * slope).astype(BF16)
        final = final + dotg(active, down_ref[cols, :], 1, 0)
        grad_hidden = grad_hidden + dotg(grad_upper, up_ref[:, cols], 1, 1)
        up_acc[:, cols] += dotg(hidden_t, grad_upper, 1, 0)
        down_acc[cols, :] += dotg(active, grad_b, 0, 0)
    for i in range(4):
        put_residue(cs, rev4(i) + low, final[i * RUN : (i + 1) * RUN])

    @pl.when(quarter == 3)
    def _():
        mixed_ref[...] = get_rows(cs, 0, SEG).astype(BF16)

    back, gain_back, shift_back = normalize_back(grad_hidden, unit, inverse, gain)
    vec_ref[0:1, :] += gain_back[None, :]
    vec_ref[1:2, :] += shift_back[None, :]
    grad_middle = grad + back
    gmid_ref[...] = grad_middle
    branch = grad_middle.astype(BF16)
    out_acc[...] += dotg(att, branch, 1, 0)
    lane = lax.broadcasted_iota(jnp.int32, (1, ROWS), 1)
    position = step // 4 * SEG + lax.rem(lane, RUN) * RES + residue_of(lane // RUN) + low
    keep = position < mask_ref[0]
    merged = jnp.where(keep, dotg(wout_ref[...], branch, 1, 1), 0.0).astype(BF16)
    gm_ref[...] = merged
    product = merged.astype(F32) * att.astype(F32)
    for head in range(HEADS):
        rows = slice(head * HEAD_DIM, (head + 1) * HEAD_DIM)
        along_ref[head] = jnp.sum(product[rows], axis=0, keepdims=True)

    @pl.when(step == pl.num_programs(0) - 1)
    def _():
        copies = []
        for owner in range(4):
            for piece in range(3):
                count = owner * 3 + piece
                slot = count % 2
                if count >= 2:
                    copies[count - 2].wait()
                if piece == 0:
                    rows, offset, size = slice(owner * 192, (owner + 1) * 192), 0, 288
                    for col in range(4 * TILES):
                        stage[slot, col * 12 : (col + 1) * 12] = blocks_of(up_acc, rows, col)
                elif piece == 1:
                    rows, offset, size = slice(owner * 192, (owner + 1) * 192), 288, 72
                    for col in range(TILES):
                        stage[slot, col * 12 : (col + 1) * 12] = blocks_of(out_acc, rows, col)
                else:
                    rows, offset, size = slice(owner * D, (owner + 1) * D), 360, 288
                    for col in range(TILES):
                        stage[slot, col * 48 : (col + 1) * 48] = blocks_of(down_acc, rows, col)
                copy = pltpu.make_async_copy(
                    stage.at[slot, pl.ds(0, size)],
                    grads_ref.at[owner, pl.ds(offset, size)],
                    sems.at[slot],
                )
                copy.start()
                copies.append(copy)
        copies[-2].wait()
        copies[-1].wait()


def call_feed(nseg, mask, att, x, cot, wout, up, down, gains):
    length = nseg * SEG
    return pl.pallas_call(
        functools.partial(feed_kernel, nseg),
        grid=(length // ROWS,),
        in_specs=[
            MASK_BLOCK,
            pl.BlockSpec((D, ROWS), lambda i: (0, i)),
            pl.BlockSpec((ROWS, D), lambda i: (i, 0)),
            pl.BlockSpec((SEG, D), lambda i: (i // 4, 0)),
            const_block((D, D)),
            const_block((D, 4 * D)),
            const_block((4 * D, D)),
            const_block((8, D)),
        ],
        out_specs=[
            pl.BlockSpec((SEG, D), lambda i: (i // 4, 0)),
            pl.BlockSpec((ROWS, D), lambda i: (i, 0)),
            pl.BlockSpec((D, ROWS), lambda i: (0, i)),
            pl.BlockSpec((HEADS, 1, ROWS), lambda i: (0, 0, i)),
            pl.BlockSpec((2, D), lambda i: (0, 0)),
            pl.BlockSpec(memory_space=pl.ANY),
        ],
        out_shape=[
            shape((length, D), BF16),
            shape((length, D), F32),
            shape((D, length), BF16),
            shape((HEADS, 1, length), F32),
            shape((2, D), F32),
            shape((4, padded(FEED_BLOCKS), 16, 128), BF16),
        ],
        scratch_shapes=[
            pltpu.VMEM((TILES, SEG, 128), F32),
            pltpu.VMEM((D, D), F32),
            pltpu.VMEM((D, 4 * D), F32),
            pltpu.VMEM((4 * D, D), F32),
            pltpu.VMEM((2, 288, 16, 128), BF16),
            pltpu.SemaphoreType.DMA((2,)),
        ],
        compiler_params=pltpu.CompilerParams(vmem_limit_bytes=62 * 1024 * 1024),
        cost_estimate=cost(nseg * 45e-6),
        name="feed",
    )(mask, att, x, cot, wout, up, down, gains)


STEPS = 6
INNER_TABLE = (
    (1, "start", 0, 0), (1, "feed", 2, 0), (1, "feed", 1, 0), (2, "feed", 0, 0),
    (2, "reduce", 0, 0), (3, "start", 1, 0), (4, "feed", 2, 1), (4, "feed", 1, 1),
    (4, "reduce", 1, 0), (4, "reduce", 0, 1), (4, "feed", 0, 1), (5, "start", 2, 0),
    (8, "reduce", 1, 1), (8, "reduce", 2, 0), (8, "feed", 2, 2), (8, "feed", 1, 2),
    (9, "reduce", 0, 2), (12, "reduce", 0, 3), (13, "vec_start", 0, 0), (13, "reduce", 2, 1),
    (14, "feed", 0, 2), (14, "reduce", 0, 4), (14, "vec", 0, 0), (14, "reduce", 1, 2),
    (14, "vec", 0, 1), (14, "reduce", 2, 2), (14, "vec", 0, 2), (14, "spread", 0, 0),
    (14, "reduce", 1, 3), (14, "vec", 0, 3), (14, "reduce", 2, 3), (14, "spread", 0, 1),
    (14, "reduce", 1, 4), (14, "vec", 0, 4), (14, "reduce", 2, 4), (14, "spread", 0, 2),
    (14, "spread", 1, 0), (14, "spread", 2, 0), (14, "spread", 1, 1), (14, "spread", 2, 1),
    (14, "spread", 1, 2), (14, "spread", 2, 2),
)


def inner_back_kernel(
    nseg, first, local_ref, inner_ref, w_ref, x_ref, gmid_ref, gain_ref, feed_vec_ref, piece_ref, *refs
):
    n = BRANCHES - first
    packs, (weight_ref, back_ref, vec_ref, up_ref, proj_ref, down_ref) = refs[:n], refs[n : n + 6]
    acc, mixed, order, terms, recv_core, recv_x, recv_seq, total, feed_total, vecs, vec_recv = refs[n + 6 : n + 17]
    red_send, red_recv, in_send, in_recv, feed_send, feed_recv, vec_send, vec_recv_sems = refs[n + 17 :]
    step = pl.program_id(0)
    last = pl.num_programs(0) - 1
    length = nseg * SEG
    turns = length // ROWS
    end = STEPS + turns
    blocks = terms.shape[1] // CHUNKS
    core = lax.rem(lax.axis_index("fsdp"), 2)
    spread = Spread(inner_orders(), blocks, total, Sends(in_send, in_recv))
    reduce = Reduce(
        inner_orders(), blocks, terms, terms, lambda xo: 2 * xo + core, recv_core, recv_x, recv_seq, Sends(red_send, red_recv),
        spread.begin,
    )
    feed_spread = Spread(feed_orders(), feed_total.shape[0] // CHUNKS, feed_total, Sends(feed_send, feed_recv))
    vec_sends = Sends(vec_send, vec_recv_sems)
    peers = all_peers()

    def vec_copy(i):
        return vec_sends.copy(i, vecs.at[i], vec_recv.at[i], *peers[i])

    def vec_event(i):
        vec_copy(i).wait_recv()
        vecs[i + 1] = vecs[i] + vec_recv[i]
        if i + 1 < len(peers):
            vec_copy(i + 1).start()

    def vec_start():
        vec_copy(0).start()

    @pl.when(step == 0)
    def _():
        meet(peers)
        vecs[0] = jnp.concatenate([jnp.zeros((2, D), F32), feed_vec_ref[...], jnp.zeros((4, D), F32)], axis=0)
        for chunk in reversed(range(CHUNKS)):
            feed_spread.begin(chunk, piece_ref.at[chunk], 0)

    @pl.when((step >= 2) & (step < STEPS))
    def _():
        upper = lax.rem(step, 2) == 1
        for pack, level in zip(packs, range(first, BRANCHES)):
            size = SEG >> level
            for head in range(HEADS // 2):
                rows = slice(head * HEAD_DIM, (head + 1) * HEAD_DIM)
                for seg in range(nseg):
                    start = seg * SEG + (rev4(head) >> (4 - level)) * size
                    piece = pack[0, rows, seg * size : (seg + 1) * size].astype(F32)
                    if level == 4:
                        zero = jnp.zeros_like(piece)
                        piece = jnp.concatenate(
                            [jnp.where(upper, zero, piece), jnp.where(upper, piece, zero)], axis=1
                        )
                    local_ref[0, rows, start : start + piece.shape[1]] += piece

    @pl.when(step < STEPS)
    def _():
        block = local_ref[0].astype(BF16)
        mixed[pl.ds(pl.multiple_of(step * HALF, HALF), HALF), :] = block
        base = lax.div(step, 2) * blocks + lax.rem(step, 2) * 36
        grad_in = dotg(block, inner_ref[...], 1, 1).T.astype(BF16)
        for col in range(3):
            part = grad_in[:, col * 128 : (col + 1) * 128].reshape(4, 12, 16, 128)
            for owner in range(4):
                terms[owner, pl.ds(base + col * 12, 12)] = part[owner]

    def inner_grad(turn):
        lanes = pl.ds(pl.multiple_of(turn * ROWS, ROWS), ROWS)
        acc[lax.rem(turn, 2)] = dotg(w_ref[...], mixed[:, lanes], 1, 0)

    @pl.when(step == STEPS - 1)
    def _():
        inner_grad(step - (STEPS - 1))

    @pl.when((step >= STEPS) & (step < end))
    def _():
        turn = step - STEPS
        inner_grad(lax.rem(turn + 1, turns))
        quarter = lax.rem(turn, 4)
        low = (quarter >> 1) | ((quarter & 1) << 1)
        gain = gain_ref[0:1, :]
        grad = acc[lax.rem(turn, 2)].T
        _, unit, inverse = normalize(x_ref[...].astype(F32), gain, gain)
        back, gain_part, shift_part = normalize_back(grad, unit, inverse, gain)
        vecs[0, 0:1, :] += gain_part[None, :]
        vecs[0, 1:2, :] += shift_part[None, :]
        total_back = gmid_ref[...] + back
        for i in range(4):
            put_residue(order, rev4(i) + low, total_back[i * RUN : (i + 1) * RUN])

        @pl.when(quarter == 3)
        def _():
            back_ref[...] = get_rows(order, 0, SEG)

    calls = {
        "start": lambda chunk, stage: reduce.begin(chunk),
        "reduce": lambda chunk, stage: reduce.event(stage, chunk),
        "spread": lambda chunk, stage: spread.event(stage, chunk),
        "feed": lambda chunk, stage: feed_spread.event(stage, chunk),
        "vec_start": lambda chunk, stage: vec_start(),
        "vec": lambda chunk, stage: vec_event(stage),
    }
    if seq_bits() == 3 and turns == 8:
        table = INNER_TABLE
    else:
        table = []
        for chunk in range(CHUNKS):
            begin = 2 * chunk + 1
            late = begin + 2 * reduce.stages() + 3 * chunk
            table += [(1 + 2 * stage, "feed", chunk, stage) for stage in range(feed_spread.stages())]
            table += [(begin, "start", chunk, 0), (begin + 1, "reduce", chunk, 0)]
            table += [
                (begin + 1 + 3 * chunk + 2 * stage, "reduce", chunk, stage)
                for stage in range(1, reduce.stages())
            ]
            table += [(late + 2 * stage, "spread", chunk, stage) for stage in range(spread.stages())]
        table += [(end - 1, "vec_start", 0, 0)]
        table += [(end + stage, "vec", 0, stage) for stage in range(len(peers))]
        table.sort(key=lambda event: event[0])
    events = [(when, functools.partial(calls[name], chunk, stage)) for when, name, chunk, stage in table]
    run_schedule(step, last, events)

    @pl.when(step == last)
    def _():
        for tile in range(TILES):
            cols = slice(tile * 128, (tile + 1) * 128)
            for col in range(4):
                at = col * 72 + tile * 12
                up_ref[:, col * D + tile * 128 : col * D + (tile + 1) * 128] = rows_of(feed_total, at, 12)
            proj_ref[:, cols] = rows_of(feed_total, 288 + tile * 12, 12)
            down_ref[:, cols] = rows_of(feed_total, 360 + tile * 48, 48)

    @pl.when(step == last)
    def _():
        reduce.finish()
        spread.finish()
        feed_spread.finish()
        for i in range(len(peers)):
            vec_copy(i).wait_send()
        vec_ref[...] = vecs[len(peers)]
        for part in range(STEPS):
            for col in range(3):
                at = part // 2 * blocks + part % 2 * 36 + col * 12
                weight_ref[:, part * HALF + col * 128 : part * HALF + (col + 1) * 128] = rows_of(total, at, 12)


def call_inner_back(nseg, first, local, inner, weight, x, gmid, gain, feed_vec, pieces, packs):
    length = nseg * SEG
    turns = length // ROWS
    blocks = padded(IN_BLOCKS)
    if blocks // CHUNKS < 72:
        raise ValueError("blocks")
    bits = seq_bits()
    peers = 2 + bits
    feed_blocks = CHUNKS * (pieces.shape[1] << bits)

    def at(i):
        return jnp.minimum(i, STEPS - 1)

    def turn(i):
        return jnp.clip(i - STEPS, 0, turns - 1)

    return pl.pallas_call(
        functools.partial(inner_back_kernel, nseg, first),
        grid=(STEPS + turns + 1,),
        in_specs=[
            pl.BlockSpec((1, HALF, length), lambda i: (at(i) // 2, at(i) % 2, 0)),
            const_block((D, length)),
            const_block((D, 3 * D)),
            pl.BlockSpec((ROWS, D), lambda i: (turn(i), 0)),
            pl.BlockSpec((ROWS, D), lambda i: (turn(i), 0)),
            const_block((8, D)),
            const_block((2, D)),
            const_block(pieces.shape),
        ]
        + [
            pl.BlockSpec((1, HALF, pack.shape[2]), lambda i: (jnp.maximum(at(i) // 2 - 1, 0), at(i) % 2, 0))
            for pack in packs
        ],
        out_specs=[
            const_block((192, 3 * D)),
            pl.BlockSpec((SEG, D), lambda i: (turn(i) // 4, 0)),
            const_block((8, D)),
            const_block((192, 4 * D)),
            const_block((192, D)),
            const_block((D, D)),
        ],
        out_shape=[
            shape((192, 3 * D), BF16),
            shape((length, D), F32),
            shape((8, D), F32),
            shape((192, 4 * D), BF16),
            shape((192, D), BF16),
            shape((D, D), BF16),
        ],
        scratch_shapes=[
            pltpu.VMEM((2, D, ROWS), F32),
            pltpu.VMEM((3 * D, length), BF16),
            pltpu.VMEM((TILES, SEG, 128), F32),
            pltpu.VMEM((4, blocks, 16, 128), BF16),
            pltpu.VMEM((2, blocks, 16, 128), BF16),
            pltpu.VMEM((blocks, 16, 128), BF16),
            pltpu.VMEM((blocks, 16, 128), BF16),
            pltpu.VMEM((blocks, 16, 128), BF16),
            pltpu.VMEM((feed_blocks, 16, 128), BF16),
            pltpu.VMEM((peers + 1, 8, D), F32),
            pltpu.VMEM((peers, 8, D), F32),
            sems(reduce_copies()),
            sems(reduce_copies()),
            sems(CHUNKS * bits),
            sems(CHUNKS * bits),
            sems(CHUNKS * bits),
            sems(CHUNKS * bits),
            sems(peers),
            sems(peers),
        ],
        compiler_params=talking(3, 60),
        cost_estimate=cost(nseg * 15e-6),
        name="inner_back",
    )(local, inner, weight, x, gmid, gain, feed_vec, pieces, *packs)


def per_device(
    tokens,
    first_gain,
    first_shift,
    project_in,
    project_out,
    second_gain,
    second_shift,
    up_weight,
    down_weight,
    valid_mask,
    cotangent,
):
    length = tokens.shape[1]
    nseg = length // SEG
    first = nseg.bit_length()

    mask = jnp.sum(valid_mask[0])[None]

    vectors = [first_gain, first_shift, second_gain, second_shift]
    qkv, x, inner, weight_in, gains, weight_out, keys, *packs = call_project(
        nseg, first, mask, tokens[0], vectors, project_in, project_out
    )
    weight_out, keys = weight_out.reshape(D, D), keys[None]
    weight_in = weight_in.reshape(D, 3 * D)
    o_part, l_part, m_part, gathered, (weight_up, weight_down) = call_local_forward(
        nseg, first, qkv, mask, packs, (up_weight, down_weight)
    )
    attended, lse = call_remote_forward(nseg, first, qkv, mask, o_part, l_part, m_part, keys, gathered)

    mixed, grad_middle, grad_merged, along, feed_vec, feed_grads = call_feed(
        nseg, mask, attended, x, cotangent[0], weight_out, weight_up, weight_down, gains
    )

    dq_remote, *sent = call_remote_backward(nseg, first, qkv, grad_merged, lse, along, mask, keys, gathered)
    local, returned, pieces = call_local_backward(
        nseg, first, qkv, grad_merged, lse, along, mask, dq_remote, sent, feed_grads
    )
    grad_in, tokens_back, vectors, grad_up, grad_out, grad_down = call_inner_back(
        nseg, first, local, inner, weight_in, x, grad_middle, gains, feed_vec, pieces, returned
    )
    quarter = D // lax.axis_size("fsdp")
    vectors = lax.dynamic_slice_in_dim(vectors, lax.axis_index("fsdp") * quarter, quarter, 1)
    return (
        mixed[None],
        tokens_back[None],
        vectors[0],
        vectors[1],
        grad_in.astype(F32),
        grad_out.astype(F32),
        vectors[2],
        vectors[3],
        grad_up.astype(F32),
        grad_down.astype(F32),
    )


def solution(mesh):
    in_specs = (
        P("fsdp", "seq", None),
        P("fsdp"),
        P("fsdp"),
        P("fsdp", None),
        P("fsdp", None),
        P("fsdp"),
        P("fsdp"),
        P("fsdp", None),
        P("fsdp", None),
        P("fsdp", "seq"),
        P("fsdp", "seq", None),
    )
    out_specs = (
        P("fsdp", "seq", None),
        P("fsdp", "seq", None),
        P("fsdp"),
        P("fsdp"),
        P("fsdp", None),
        P("fsdp", None),
        P("fsdp"),
        P("fsdp"),
        P("fsdp", None),
        P("fsdp", None),
    )
    return jax.shard_map(
        per_device, mesh=mesh, in_specs=in_specs, out_specs=out_specs, check_vma=False
    )
```

```python
import functools
import math

import jax
import jax.numpy as jnp
import ml_dtypes
import numpy as np
from jax import lax
from jax.experimental import pallas as pl
from jax.experimental.pallas import tpu as pltpu
from jax.sharding import PartitionSpec as P

HEADS = 16
HEAD_DIM = 48
SEG = 1024
BRANCHES = 5
RES = 16
RUN = SEG // RES
D = HEADS * HEAD_DIM

EPS = 1e-05
NEG = -1e30
ROOT_HALF = 0.7071067811865476
INV_ROOT_TWO_PI = 0.3989422804014327
F32 = jnp.float32
BF16 = jnp.bfloat16
QUERY_SCALE = math.log2(math.e) * HEAD_DIM ** (-0.5)
VMEM_LIMIT = 56 * 1024 * 1024


def dotg(left, right, left_dim, right_dim):
    return lax.dot_general(
        left, right, (((left_dim,), (right_dim,)), ((), ())), preferred_element_type=F32
    )


def normalize(values, gain, shift):
    mean = jnp.mean(values, axis=-1, keepdims=True)
    centred = values - mean
    spread = jnp.mean(centred * centred, axis=-1, keepdims=True)
    inverse = lax.rsqrt(spread + EPS)
    normed = centred * inverse
    return (normed * gain + shift, normed, inverse)


def normalize_back(grad, normed, inverse, gain):
    scaled = grad * gain
    first = jnp.mean(scaled, axis=-1, keepdims=True)
    second = jnp.mean(scaled * normed, axis=-1, keepdims=True)
    return (
        inverse * (scaled - first - normed * second),
        jnp.sum(grad * normed, axis=0),
        jnp.sum(grad, axis=0),
    )


def reversed_bits(head):
    return ((head & 1) << 3) | ((head & 2) << 1) | ((head & 4) >> 1) | ((head & 8) >> 3)


def near_class(head, low_bits, length):
    lane = lax.broadcasted_iota(jnp.int32, (1, length), 1)
    rho = lax.rem(lane // RUN, 1 << low_bits)
    return rho ^ (reversed_bits(head) & ((1 << low_bits) - 1))


def class_rows(near, length):
    row = lax.broadcasted_iota(jnp.int32, (16, length), 0)
    step = lax.rem(row + 3, 4) + 1
    bound = jnp.where((row >= 5) & (row <= 12), lax.shift_right_logical(RES, step), 0)
    return row, near < bound


def query_rows(head, length, neg_lse=None):
    near = near_class(head, 4, length)
    row, inside = class_rows(near, length)
    out = jnp.where(inside, 1.0, 0.0)
    out = jnp.where(row == 0, 1.0, out)
    out = jnp.where(row == 4, jnp.where(near < 1, 0.0, NEG), out)
    if neg_lse is not None:
        high = neg_lse.astype(BF16).astype(F32)
        rest = neg_lse - high
        mid = rest.astype(BF16).astype(F32)
        low = rest - mid
        out = jnp.where(row == 1, high, jnp.where(row == 2, mid, jnp.where(row == 3, low, out)))
    return out.astype(BF16)


def residue_of(rho):
    return reversed_bits(rho)


def local_keep(count, length):
    lane = lax.broadcasted_iota(jnp.int32, (1, length), 1)
    rho = lax.rem(lane // RUN, RES)
    position = lane // SEG * SEG + lax.rem(lane, RUN) * RES + residue_of(rho)
    return position < count


def packed_keep(count, level, nseg):
    size = SEG >> level
    dims = (HEADS, nseg * size)
    head = lax.broadcasted_iota(jnp.int32, dims, 0)
    lane = lax.broadcasted_iota(jnp.int32, dims, 1)
    rho = (reversed_bits(head) >> (4 - level)) * (size // RUN) + lax.rem(lane, size) // RUN
    position = lane // size * SEG + lax.rem(lane, RUN) * RES + residue_of(rho)
    return jnp.where(position < count, 1.0, 0.0).astype(BF16)


def weight_of(level, step):
    return math.log2((step - level + 1) / (step - level)) if step > level else 0.0


def key_rows(head, level, low_bits, length, keep):
    near = near_class(head, low_bits, length)
    row, inside = class_rows(near, length)
    weight = jnp.zeros((16, length), F32)
    for step in range(level + 1, BRANCHES):
        value = weight_of(level, step)
        high = float(np.asarray(value, ml_dtypes.bfloat16))
        weight = jnp.where(row == 4 + step, high, weight)
        weight = jnp.where(row == 8 + step, value - high, weight)
    out = jnp.where(inside, weight, 0.0)
    out = jnp.where((row >= 1) & (row <= 3), 1.0, out)
    out = jnp.where(row == 0, jnp.where(keep, 0.0, NEG), out)
    if level == BRANCHES - 1:
        out = jnp.where(row == 4, 1.0, out)
    return out.astype(BF16)


def value_rows(length):
    row = lax.broadcasted_iota(jnp.int32, (16, length), 0)
    return jnp.where(row < 2, 1.0, 0.0).astype(BF16)


def join(rows, extra):
    return jnp.concatenate([rows, extra], axis=0)


def kept_start(head, level, seg):
    size = SEG >> level
    block = reversed_bits(head) >> (4 - level)
    return pl.multiple_of(seg * SEG + block * size, min(size, 128))


def partner(axis, distance):
    place = lax.axis_index(axis)
    return {axis: place + distance * (1 - 2 * lax.rem(lax.div(place, distance), 2))}


def seq_bits():
    return lax.axis_size("seq").bit_length() - 1


def meet(peers):
    barrier = pltpu.get_barrier_semaphore()
    for axis, distance in peers:
        pl.semaphore_signal(
            barrier, inc=1, device_id=partner(axis, distance), device_id_type=pl.DeviceIdType.MESH
        )
    pl.semaphore_wait(barrier, len(peers))


class Sends:
    def __init__(self, send_sems, recv_sems):
        self.send_sems, self.recv_sems, self.made = send_sems, recv_sems, {}

    def copy(self, key, source, target, axis, distance):
        index = self.made.setdefault(key, len(self.made))
        return pltpu.make_async_remote_copy(
            src_ref=source,
            dst_ref=target,
            send_sem=self.send_sems.at[index],
            recv_sem=self.recv_sems.at[index],
            device_id=partner(axis, distance),
            device_id_type=pl.DeviceIdType.MESH,
        )


class Gather:
    def __init__(self, nseg, first, packs, gathered, sends):
        self.hops, self.distances = [], set()
        for level, pack, into in zip(range(first, BRANCHES), packs, gathered):
            group = (SEG << (level - 1)) // (nseg * SEG)
            source = pack if pack.shape[0] == into.shape[1] else pack.at[pl.ds(D, D + 16)]
            hops = [((level, 0), source, into.at[0], group)]
            step = 1
            while step < group:
                hops.append(((level, step), into.at[pl.ds(0, step)], into.at[pl.ds(step, step)], step))
                step *= 2
            self.hops.append([sends.copy(k, a, b, "seq", d) for k, a, b, d in hops])
            self.distances |= {hop[3] for hop in hops}

    def peers(self):
        return [("seq", distance) for distance in sorted(self.distances)]

    def start(self):
        for hops in reversed(self.hops):
            hops[0].start()

    def pass_on(self, index, turn):
        hops = self.hops[index]
        hops[turn - 1].wait_recv()
        hops[turn].start()

    def finish(self):
        for hops in self.hops:
            for hop in hops:
                hop.wait_send()
            hops[-1].wait_recv()

    def turns(self):
        events = []
        for index, hops in reversed(list(enumerate(self.hops))):
            for turn in range(1, len(hops)):
                when = 5 + 3 * (turn - 1) + (len(self.hops) - 1 - index)
                events.append((when, functools.partial(self.pass_on, index, turn)))
        return events


class Shards:
    def __init__(self, shards, whole, stages, sends, loads):
        self.copies = []
        self.staged = [
            pltpu.make_async_copy(shard, stage, loads.at[i])
            for i, (shard, stage) in enumerate(zip(shards, stages))
        ]
        me = lax.axis_index("fsdp")
        other = lax.rem(me + 2, 4)
        for i, (shard, into) in enumerate(zip(stages, whole)):
            self.copies.append(
                (
                    pltpu.make_async_copy(shard, into.at[me], loads.at[i]),
                    sends.copy((i, "core"), shard, into.at[me], "fsdp", 1),
                    sends.copy((i, "x"), shard, into.at[me], "fsdp", 2),
                    sends.copy((i, "hand"), into.at[other], into.at[other], "fsdp", 1),
                )
            )

    def start(self, count):
        for staged in self.staged:
            staged.start()
        for i, (load, core, x, _) in enumerate(self.copies):
            self.staged[i].wait()
            load.start()
            core.start()
            if i < count:
                x.start()

    def hand(self, i):
        _, _, x, hand = self.copies[i]
        x.wait_recv()
        hand.start()
        if i + 1 < len(self.copies):
            self.copies[i + 1][2].start()

    def finish(self):
        for load, core, x, hand in self.copies:
            load.wait()
            core.wait()
            x.wait_send()
            hand.wait()


class Return:
    def __init__(self, nseg, first, sent, returned, bufs, recvs, local_sems, sends):
        self.plans = []
        for i, level in enumerate(range(first, BRANCHES)):
            group = (SEG << (level - 1)) // (nseg * SEG)
            plan = []
            if group == 1:
                plan.append((None, sends.copy((level, 0), sent[i].at[0], returned[i], "seq", group)))
                self.plans.append((plan, None))
                continue
            buf, recv = bufs.pop(0), recvs.pop(0)
            step = group // 2
            load = pltpu.make_async_copy(sent[i].at[pl.ds(0, step)], buf, local_sems.at[i])
            source, at, add = sent[i].at[pl.ds(step, step)], 0, None
            while step >= 1:
                into = recv.at[pl.ds(at, step)]
                plan.append((add, sends.copy((level, step), source, into, "seq", step)))
                add = (buf, recv, at, step)
                at += step
                step //= 2
                if step:
                    source = buf.at[pl.ds(step, step)]
            plan.append((add, sends.copy((level, 0), buf.at[0], returned[i], "seq", group)))
            self.plans.append((plan, load))

    def start(self, direct):
        for plan, load in reversed(self.plans):
            if direct == (load is None):
                if load is not None:
                    load.start()
                plan[0][1].start()

    def turn(self, number):
        for plan, load in reversed(self.plans):
            if number < len(plan):
                plan[number - 1][1].wait_recv()
                if number == 1 and load is not None:
                    load.wait()
                buf, recv, at, step = plan[number][0]
                for i in range(step):
                    buf[i] = (buf[i].astype(F32) + recv[at + i].astype(F32)).astype(BF16)
                plan[number][1].start()

    def finish(self):
        for plan, load in self.plans:
            for _, copy in plan:
                copy.wait_send()
            plan[-1][1].wait_recv()

    def turns(self):
        return max(len(plan) for plan, _ in self.plans)


def add_blocks(into, at, other, start, count):
    unit = max(u for u in range(1, 13) if count % u == 0)

    def body(i, carry):
        rows = pl.ds(at + i * unit, unit)
        part = other[pl.ds(start + i * unit, unit)].astype(F32)
        into[rows] = (into[rows].astype(F32) + part).astype(BF16)
        return carry

    lax.fori_loop(0, count // unit, body, 0)


def copy_blocks(into, at, other, start, count):
    unit = max(u for u in range(1, 13) if count % u == 0)

    def body(i, carry):
        into[pl.ds(at + i * unit, unit)] = other[pl.ds(start + i * unit, unit)]
        return carry

    lax.fori_loop(0, count // unit, body, 0)


def halving(blocks, order):
    seq = lax.axis_index("seq")
    low, given = [0], []
    for j, distance in enumerate(order):
        bit = lax.rem(lax.div(seq, distance), 2)
        half = blocks >> (j + 1)
        given.append(low[j] + (1 - bit) * half)
        low.append(low[j] + bit * half)
    return low, given


def feed_orders():
    plain = [2**j for j in range(seq_bits())]
    return [plain] * (CHUNKS - 1) + [plain[1:] + plain[:1]]


def inner_orders():
    plain = [2**j for j in range(seq_bits())]
    return [plain] * (CHUNKS - 1) + [[plain[1], plain[0]] + plain[2:]]


def all_peers():
    return [("fsdp", 1), ("fsdp", 2)] + [("seq", 2**j) for j in range(seq_bits())]


class Reduce:
    def __init__(
        self, orders, blocks, source, terms, own, recv_core, recv_x, recv_seq, sends, done, loads=None
    ):
        self.blocks, self.source, self.terms, self.own, self.done = blocks, source, terms, own, done
        self.recv_core, self.recv_x, self.recv_seq = recv_core, recv_x, recv_seq
        self.sends, self.loads = sends, loads
        fsdp = lax.axis_index("fsdp")
        self.core, self.x = lax.rem(fsdp, 2), lax.div(fsdp, 2)
        self.bits = seq_bits()
        self.orders = orders
        self.halves = [halving(blocks, order) for order in self.orders]

    def stages(self):
        return 2 + self.bits

    def core_copy(self, chunk, xo):
        rows = pl.ds(chunk * self.blocks, self.blocks)
        owner = 2 * xo + 1 - self.core
        return self.sends.copy(
            ("core", chunk, xo), self.source.at[owner, rows], self.recv_core.at[xo, rows], "fsdp", 1
        )

    def load_copy(self, chunk, xo):
        rows = pl.ds(chunk * self.blocks, self.blocks)
        return pltpu.make_async_copy(
            self.source.at[2 * xo + self.core, rows], self.terms.at[xo, rows], self.loads.at[2 * chunk + xo]
        )

    def x_copy(self, chunk):
        rows = pl.ds(chunk * self.blocks, self.blocks)
        return self.sends.copy(
            ("x", chunk), self.terms.at[self.own(1 - self.x), rows], self.recv_x.at[rows], "fsdp", 2
        )

    def down_copy(self, chunk, j):
        half = self.blocks >> (j + 1)
        base = chunk * self.blocks
        rows = pl.ds(base + self.halves[chunk][1][j], half)
        into = pl.ds(base + self.blocks - (self.blocks >> j), half)
        return self.sends.copy(
            ("down", chunk, j), self.terms.at[self.own(self.x), rows], self.recv_seq.at[into], "seq",
            self.orders[chunk][j],
        )

    def begin(self, chunk):
        for xo in range(2):
            if self.loads is not None:
                self.load_copy(chunk, xo).start()
            self.core_copy(chunk, xo).start()

    def event(self, stage, chunk):
        base = chunk * self.blocks
        low = self.halves[chunk][0]
        mine = self.terms.at[self.own(self.x)]
        if stage == 0:
            for xo in range(2):
                self.core_copy(chunk, xo).wait_recv()
                if self.loads is not None:
                    self.load_copy(chunk, xo).wait()
                add_blocks(self.terms.at[self.own(xo)], base, self.recv_core.at[xo], base, self.blocks)
            self.x_copy(chunk).start()
            return
        j = stage - 2
        if stage == 1:
            self.x_copy(chunk).wait_recv()
            add_blocks(mine, base, self.recv_x, base, self.blocks)
        else:
            self.down_copy(chunk, j).wait_recv()
            half = self.blocks >> (j + 1)
            add_blocks(mine, base + low[j + 1], self.recv_seq, base + self.blocks - (self.blocks >> j), half)
        if j + 1 < self.bits:
            self.down_copy(chunk, j + 1).start()
        else:
            self.done(chunk, mine, base + low[self.bits])

    def finish(self):
        for chunk in range(CHUNKS):
            for xo in range(2):
                self.core_copy(chunk, xo).wait_send()
            self.x_copy(chunk).wait_send()
            for j in range(self.bits):
                self.down_copy(chunk, j).wait_send()


class Spread:
    def __init__(self, orders, blocks, total, sends):
        self.blocks, self.total, self.sends = blocks, total, sends
        self.bits = seq_bits()
        self.orders = orders
        self.lows = [halving(blocks, order)[0] for order in self.orders]

    def stages(self):
        return self.bits

    def copy(self, chunk, j):
        rows = pl.ds(chunk * self.blocks + self.lows[chunk][j + 1], self.blocks >> (j + 1))
        here = self.total.at[rows]
        return self.sends.copy((chunk, j), here, here, "seq", self.orders[chunk][j])

    def begin(self, chunk, ref, start):
        size = self.blocks >> self.bits
        copy_blocks(self.total, chunk * self.blocks + self.lows[chunk][self.bits], ref, start, size)
        self.copy(chunk, self.bits - 1).start()

    def event(self, stage, chunk):
        j = self.bits - 1 - stage
        self.copy(chunk, j).wait_recv()
        if j:
            self.copy(chunk, j - 1).start()

    def finish(self):
        for chunk in range(CHUNKS):
            for j in range(self.bits):
                self.copy(chunk, j).wait_send()


def run_schedule(step, last, events):
    due = {}
    for when, call in events:
        due.setdefault(min(when, last), []).append(call)
    for when in sorted(due):

        @pl.when(step == when)
        def _():
            for call in due[when]:
                call()


FRONT = 3
KEY_TILE = 128


class State:
    def __init__(self, query, acc=None, top=None):
        self.query, self.acc, self.top = query, acc, top


def attend(items):
    items = list(items)
    ready = []
    for turn in range(len(items) + FRONT):
        if turn < len(items):
            state, key, _ = items[turn]
            ready.append(dotg(key, state.query, 1, 0))
        if turn >= FRONT:
            state, _, value = items[turn - FRONT]
            scores, ready[turn - FRONT] = ready[turn - FRONT], None
            top = jnp.max(scores, axis=0, keepdims=True)
            if state.top is not None:
                top = jnp.maximum(top, state.top)
            probs = jnp.exp2(scores - top).astype(BF16)
            part = dotg(value, probs, 1, 0)
            state.acc = part if state.top is None else state.acc * jnp.exp2(state.top - top) + part
            state.top = top


def key_items(state, key_t, value):
    size = key_t.shape[0]
    tile = min(KEY_TILE, size)
    for start in range(0, size, tile):
        yield state, key_t[start : start + tile], value[:, start : start + tile]


def load_state(query, mine, o_ref, l_ref, m_ref):
    acc = [jnp.concatenate([o_ref[:, at], jnp.broadcast_to(l_ref[0, :, at], (16, at.size))]) for at in mine]
    top = [m_ref[0, :, at] for at in mine]
    return State(query, jnp.concatenate(acc, axis=1), jnp.concatenate(top, axis=1))


def store_state(state, mine, o_ref, l_ref, m_ref):
    start = 0
    for at in mine:
        lanes = slice(start, start + at.size)
        o_ref[:, at] = state.acc[:HEAD_DIM, lanes]
        l_ref[0, :, at] = state.acc[HEAD_DIM : HEAD_DIM + 1, lanes]
        m_ref[0, :, at] = state.top[:, lanes]
        start += at.size


DOWN_FIRST = 384


def local_forward(nseg, first, mask_ref, q_ref, k_ref, v_ref, *refs):
    n = BRANCHES - first
    packs, shards, (o_ref, l_ref, m_ref) = refs[:n], refs[n : n + 2], refs[n + 2 : n + 5]
    gathered, whole = refs[n + 5 : 2 * n + 5], refs[2 * n + 5 : 2 * n + 7]
    qa, ka, va, send_sems, recv_sems, up_stage, down_stage, shard_send, shard_recv, shard_load = refs[2 * n + 7 :]
    head = pl.program_id(0)
    gather = Gather(nseg, first, packs, gathered, Sends(send_sems, recv_sems))
    pieces = [shards[0], shards[1].at[pl.ds(0, DOWN_FIRST)]]
    fetch = Shards(pieces, whole, [up_stage, down_stage], Sends(shard_send, shard_recv), shard_load)

    def begin():
        meet(gather.peers() + [("fsdp", 1), ("fsdp", 2)])
        gather.start()
        fetch.start(1)

    def finish():
        gather.finish()
        fetch.finish()

    hands = [(9, functools.partial(fetch.hand, 0)), (14, functools.partial(fetch.hand, 1))]
    run_schedule(head, HEADS - 1, [(0, begin)] + sorted(gather.turns() + hands, key=lambda event: event[0]))
    local_forward_core(nseg, mask_ref, q_ref, k_ref, v_ref, o_ref, l_ref, m_ref, qa, ka, va)
    run_schedule(head, HEADS - 1, [(HEADS - 1, finish)])


def local_forward_scratch(nseg):
    length = nseg * SEG
    return [
        pltpu.VMEM((64, length), BF16),
        pltpu.VMEM((nseg, 64, length), BF16),
        pltpu.VMEM((64, length), BF16),
    ]


def local_forward_core(nseg, mask_ref, q_ref, k_ref, v_ref, o_ref, l_ref, m_ref, qa, ka, va):
    head = pl.program_id(0)
    length = nseg * SEG
    keep = local_keep(mask_ref[0], length)
    qa[...] = join(q_ref[0], query_rows(head, length))
    va[...] = join(v_ref[0], value_rows(length))
    ka[0] = join(k_ref[0], key_rows(head, 0, 4, length, keep))
    if nseg == 2:
        ka[1] = join(k_ref[0], key_rows(head, 1, 4, length, keep))
    states, items = [], []
    for seg in range(nseg):
        lanes = slice(seg * SEG, (seg + 1) * SEG)
        states.append(State(qa[:, lanes]))
        items += key_items(states[-1], ka[0, :, lanes].T, va[:, lanes])
    attend(items)
    for seg in range(nseg):
        store_state(states[seg], [pl.ds(seg * SEG, SEG)], o_ref, l_ref, m_ref)
    if nseg == 2:
        kept = [pl.ds(kept_start(head, 1, seg), SEG // 2) for seg in range(2)]
        states = [load_state(qa[:, at], [at], o_ref, l_ref, m_ref) for at in kept]
        items = []
        for seg in range(2):
            items += key_items(states[seg], ka[1, :, kept[1 - seg]].T, va[:, kept[1 - seg]])
        attend(items)
        for seg in range(2):
            store_state(states[seg], [kept[seg]], o_ref, l_ref, m_ref)


def remote_keys(head, level, pack):
    k_ref, v_ref, mask_ref = pack
    pieces = range(k_ref.shape[0])
    key, value, mask = (
        jnp.concatenate([ref[i] for i in pieces], axis=1) for ref in (k_ref, v_ref, mask_ref)
    )
    length = key.shape[1]
    row = lax.broadcasted_iota(jnp.int32, (16, length), 0)
    keep = jnp.sum(jnp.where(row == head, mask.astype(F32), 0.0), axis=0, keepdims=True) > 0.5
    return join(key, key_rows(head, level, 4 - level, length, keep)), join(value, value_rows(length))


def remote_plan(first):
    return [(level,) for level in range(first, 3)] + [(3, 4)]


def remote_forward(nseg, first, mask_ref, q_ref, o_in, l_in, m_in, *refs):
    head = pl.program_id(0)
    levels = range(first, BRANCHES)
    packs = {level: refs[3 * i : 3 * i + 3] for i, level in enumerate(levels)}
    shard_ref, att_ref, lse_ref, whole_ref, o_ref, l_ref, m_ref, qa, stage, *shard_sems = refs[
        3 * len(levels) :
    ]
    shard_send, shard_recv, shard_load = shard_sems
    piece = shard_ref.at[pl.ds(DOWN_FIRST, D - DOWN_FIRST)]
    fetch = Shards([piece], [whole_ref], [stage], Sends(shard_send, shard_recv), shard_load)

    def begin():
        meet([("fsdp", 1), ("fsdp", 2)])
        fetch.start(1)

    run_schedule(head, HEADS - 1, [(0, begin), (12, functools.partial(fetch.hand, 0))])
    length = nseg * SEG
    qa[...] = join(q_ref[0], query_rows(head, length))
    o_ref[...] = o_in[...]
    l_ref[...] = l_in[...]
    m_ref[...] = m_in[...]
    for group in remote_plan(first):
        pairs = [remote_keys(head, level, packs[level]) for level in group]
        key = jnp.concatenate([pair[0] for pair in pairs], axis=1)
        value = jnp.concatenate([pair[1] for pair in pairs], axis=1)
        mine = [pl.ds(kept_start(head, group[0], seg), SEG >> group[0]) for seg in range(nseg)]
        query = jnp.concatenate([qa[:, at] for at in mine], axis=1)
        state = load_state(query, mine, o_ref, l_ref, m_ref)
        attend(key_items(state, key.T, value))
        store_state(state, mine, o_ref, l_ref, m_ref)
    weight = jnp.where(local_keep(mask_ref[0], length), 1.0, 0.0) / l_ref[0]
    att_ref[...] = (o_ref[...] * weight).astype(BF16)
    lse_ref[0] = m_ref[0] + jnp.log2(l_ref[0])
    run_schedule(head, HEADS - 1, [(HEADS - 1, fetch.finish)])


def grad_rows(grad, slope):
    length = grad.shape[1]
    row = lax.broadcasted_iota(jnp.int32, (16, length), 0)
    high = (-slope).astype(BF16).astype(F32)
    low = -slope - high
    extra = jnp.where(row == 0, high, jnp.where(row == 1, low, 0.0)).astype(BF16)
    return join(grad, extra)


AHEAD = 2
QUERY_TILE = 256
BACK_KEYS = 256


class Side:
    def __init__(self, query, grad):
        self.query, self.grad = query[:HEAD_DIM], grad[:HEAD_DIM]
        self.query_t, self.grad_t = query.T, grad.T
        self.dq = None


def attend_back(items, dk_ref, dv_ref, written):
    items = list(items)
    ready = []
    for turn in range(len(items) + AHEAD):
        if turn < len(items):
            side, key, value, _, _ = items[turn]
            ready.append((dotg(side.query_t, key, 1, 0), dotg(side.grad_t, value, 1, 0)))
        if turn >= AHEAD:
            side, key, _, lanes, name = items[turn - AHEAD]
            scores, slope = ready[turn - AHEAD]
            ready[turn - AHEAD] = None
            probs = jnp.exp2(scores)
            dscore = (probs * slope).astype(BF16)
            dv = dotg(side.grad, probs.astype(BF16), 1, 0)
            dk = dotg(side.query, dscore, 1, 0)
            part = dotg(key[:HEAD_DIM], dscore, 1, 1)
            side.dq = part if side.dq is None else side.dq + part
            if name in written:
                dv_ref[:, lanes] += dv
                dk_ref[:, lanes] += dk
            else:
                written.add(name)
                dv_ref[:, lanes] = dv
                dk_ref[:, lanes] = dk


def sides_of(query, grad):
    tile = min(QUERY_TILE, query.shape[1])
    return [
        Side(query[:, start : start + tile], grad[:, start : start + tile])
        for start in range(0, query.shape[1], tile)
    ]


def pairs(sides, key_ref, value_ref, tiles):
    return [
        (side, key_ref[:, lanes], value_ref[:, lanes], lanes, name) for side in sides for name, lanes in tiles
    ]


def joined(sides):
    return jnp.concatenate([side.dq for side in sides], axis=1) if len(sides) > 1 else sides[0].dq


DQ_SCALE = HEAD_DIM ** (-0.5)
DK_SCALE = math.log(2.0)


def neg_total(lse, keep):
    return jnp.where(keep, -lse, NEG)


def local_backward(nseg, first, mask_ref, q_ref, k_ref, v_ref, g_ref, lse_ref, slope_ref, dqr_ref, *refs):
    n = BRANCHES - first
    sent, feed_ref, out_ref = refs[:n], refs[n], refs[n + 1]
    returned, piece_ref = refs[n + 2 : 2 * n + 2], refs[2 * n + 2]
    qa, ga, ka, va, dk, dv = refs[2 * n + 3 : 2 * n + 9]
    rest = list(refs[2 * n + 9 :])
    back_send, back_recv, back_load, red_send, red_recv, red_load = rest[-6:]
    terms, recv_core, recv_x, recv_seq = rest[-10:-6]
    bufs, recvs = rest[: (len(rest) - 10) // 2], rest[(len(rest) - 10) // 2 : -10]
    head = pl.program_id(0)
    last = HEADS - 1

    back = Return(nseg, first, sent, returned, bufs, recvs, back_load, Sends(back_send, back_recv))
    blocks = terms.shape[1] // CHUNKS
    reduce = Reduce(
        feed_orders(), blocks, feed_ref, terms, lambda xo: xo, recv_core, recv_x, recv_seq, Sends(red_send, red_recv),
        lambda chunk, ref, start: copy_blocks(piece_ref.at[chunk], 0, ref, start, blocks >> seq_bits()),
        red_load,
    )

    def begin():
        meet(all_peers())
        back.start(False)
        for chunk in range(CHUNKS):
            reduce.begin(chunk)

    events = [(3 * turn, functools.partial(back.turn, turn)) for turn in range(1, back.turns())]
    events.append((8, functools.partial(back.start, True)))
    for chunk in range(CHUNKS):
        for stage in range(reduce.stages()):
            when = 1 + (chunk + 1) // 2 if stage == 0 else 4 + 3 * chunk + 2 * (stage - 1)
            events.append((when, functools.partial(reduce.event, stage, chunk)))
    run_schedule(head, last, [(0, begin)] + sorted(events, key=lambda event: event[0]))
    local_backward_core(
        nseg, first, mask_ref, q_ref, k_ref, v_ref, g_ref, lse_ref, slope_ref, dqr_ref, out_ref,
        qa, ga, ka, va, dk, dv,
    )

    @pl.when(head == last)
    def _():
        back.finish()
        reduce.finish()


def local_backward_scratch(nseg):
    length = nseg * SEG
    return [
        pltpu.VMEM((64, length), BF16),
        pltpu.VMEM((64, length), BF16),
        pltpu.VMEM((nseg, 64, length), BF16),
        pltpu.VMEM((64, length), BF16),
        pltpu.VMEM((HEAD_DIM, length), F32),
        pltpu.VMEM((HEAD_DIM, length), F32),
    ]


def local_backward_core(
    nseg, first, mask_ref, q_ref, k_ref, v_ref, g_ref, lse_ref, slope_ref, dqr_ref, out_ref,
    qa, ga, ka, va, dk, dv,
):
    head = pl.program_id(0)
    length = nseg * SEG
    keep = local_keep(mask_ref[0], length)
    qa[...] = join(q_ref[0], query_rows(head, length, neg_total(lse_ref[0], keep)))
    ga[...] = grad_rows(g_ref[...], slope_ref[0])
    va[...] = join(v_ref[0], value_rows(length))
    ka[0] = join(k_ref[0], key_rows(head, 0, 4, length, keep))
    if nseg == 2:
        ka[1] = join(k_ref[0], key_rows(head, 1, 4, length, keep))
    items, sides, written = [], [], set()
    for seg in range(nseg):
        lanes = slice(seg * SEG, (seg + 1) * SEG)
        tiles = [
            ((seg, i), slice(seg * SEG + BACK_KEYS * i, seg * SEG + BACK_KEYS * (i + 1)))
            for i in range(SEG // BACK_KEYS)
        ]
        sides.append(sides_of(qa[:, lanes], ga[:, lanes]))
        items += pairs(sides[-1], ka.at[0], va, tiles)
    attend_back(items, dk, dv, written)
    for seg in range(nseg):
        out_ref[0, :, seg * SEG : (seg + 1) * SEG] = joined(sides[seg]) * DQ_SCALE
    if nseg == 2:
        items, sides = [], []
        kept = [pl.ds(kept_start(head, 1, seg), SEG // 2) for seg in range(2)]
        for seg in range(2):
            base = kept_start(head, 1, 1 - seg)
            tile = min(BACK_KEYS, SEG // 2)
            tiles = [
                ((seg, i), pl.ds(pl.multiple_of(base + tile * i, tile), tile)) for i in range(SEG // 2 // tile)
            ]
            sides.append(sides_of(qa[:, kept[seg]], ga[:, kept[seg]]))
            items += pairs(sides[-1], ka.at[1], va, tiles)
        attend_back(items, dk, dv, set(item[4] for item in items))
        for seg in range(2):
            out_ref[0, :, kept[seg]] += joined(sides[seg]) * DQ_SCALE
    size = SEG >> first
    for seg in range(nseg):
        mine = pl.ds(kept_start(head, first, seg), size)
        out_ref[0, :, mine] += dqr_ref[:, seg * size : (seg + 1) * size]
    out_ref[1] = dk[...] * DK_SCALE
    out_ref[2] = dv[...]


def rows_of(total, at, count):
    return total[at : at + count].reshape(count * 16, 128)


def remote_backward(nseg, first, mask_ref, q_ref, g_ref, lse_ref, slope_ref, *refs):
    head = pl.program_id(0)
    levels = range(first, BRANCHES)
    n = len(levels)
    packs = {level: refs[3 * i : 3 * i + 3] for i, level in enumerate(levels)}
    dqr_ref = refs[3 * n]
    outs = {level: refs[3 * n + 1 + i] for i, level in enumerate(levels)}
    qa, ga, ka, va, dk, dv = refs[4 * n + 1 :]
    length = nseg * SEG
    qa[...] = join(q_ref[0], query_rows(head, length, neg_total(lse_ref[0], local_keep(mask_ref[0], length))))
    ga[...] = grad_rows(g_ref[...], slope_ref[0])
    full = SEG >> first
    for group in remote_plan(first):
        for i, level in enumerate(group):
            key, value = remote_keys(head, level, packs[level])
            ka[:, i * 512 : (i + 1) * 512] = key
            va[:, i * 512 : (i + 1) * 512] = value
        size = SEG >> group[0]
        mine = [pl.ds(kept_start(head, group[0], seg), size) for seg in range(nseg)]
        query = jnp.concatenate([qa[:, m] for m in mine], axis=1)
        grad = jnp.concatenate([ga[:, m] for m in mine], axis=1)
        tile = min(BACK_KEYS, 512)
        tiles = [(i, slice(tile * i, tile * (i + 1))) for i in range(512 // tile * len(group))]
        sides = sides_of(query, grad)
        attend_back(pairs(sides, ka, va, tiles), dk, dv, set())
        dq = joined(sides) * DQ_SCALE
        for seg in range(nseg):
            piece = dq[:, seg * size : (seg + 1) * size]
            if group[0] == first:
                dqr_ref[:, seg * full : (seg + 1) * full] = piece
            else:
                inner = (reversed_bits(head) >> (4 - group[0])) & ((1 << (group[0] - first)) - 1)
                lanes = pl.ds(pl.multiple_of(seg * full + inner * size, 128), size)
                dqr_ref[:, lanes] += piece
        for i, level in enumerate(group):
            pieces, _, _, size = outs[level].shape
            for piece in range(pieces):
                lanes = slice(i * 512 + piece * size, i * 512 + (piece + 1) * size)
                outs[level][piece, 0] = (dk[:, lanes] * DK_SCALE).astype(BF16)
                outs[level][piece, 1] = dv[:, lanes].astype(BF16)


def row_block(length):
    return pl.BlockSpec((1, 1, length), lambda h: (h, 0, 0))


def head_block(length):
    return pl.BlockSpec((HEAD_DIM, length), lambda h: (h, 0))


def part_block(part, length):
    return pl.BlockSpec((1, HEAD_DIM, length), lambda h: (part, h, 0))


MASK_BLOCK = pl.BlockSpec(memory_space=pltpu.SMEM)


def pack_args(keys, packs):
    args, specs = [], []
    for i, pack in enumerate(packs):
        group, _, length = pack.shape
        ahead = 0 if i == 0 else HEADS
        args += [keys if i == 0 else pack, pack, pack]
        specs += [
            pl.BlockSpec((group, HEAD_DIM, length), lambda h: (0, h, 0)),
            pl.BlockSpec((group, HEAD_DIM, length), lambda h, ahead=ahead: (0, ahead + h, 0)),
            pl.BlockSpec((group, 16, length), lambda h, ahead=ahead: (0, (ahead + HEADS) * 3, 0)),
        ]
    return args, specs


ANY_BLOCK = pl.BlockSpec(memory_space=pl.ANY)


def sems(count):
    return pltpu.SemaphoreType.DMA((count,))


def talking(collective_id, mebibytes=56):
    return pltpu.CompilerParams(
        vmem_limit_bytes=mebibytes * 1024 * 1024, collective_id=collective_id, has_side_effects=True
    )


PARAMS = pltpu.CompilerParams(vmem_limit_bytes=VMEM_LIMIT)


def shape(dims, dtype):
    return jax.ShapeDtypeStruct(dims, dtype)


def cost(seconds):
    return pl.CostEstimate(flops=int(seconds * 1.1e15), transcendentals=0, bytes_accessed=0)


def call_local_forward(nseg, first, qkv, mask, packs, shards):
    length = nseg * SEG
    n = len(packs)
    groups = [(SEG << (level - 1)) // length for level in range(first, BRANCHES)]
    hops = sum(group.bit_length() for group in groups)
    pieces = [shards[0].shape, (DOWN_FIRST, D)]
    o_part, l_part, m_part, *rest = pl.pallas_call(
        functools.partial(local_forward, nseg, first),
        grid=(HEADS,),
        in_specs=[MASK_BLOCK, part_block(0, length), part_block(1, length), part_block(2, length)]
        + [ANY_BLOCK] * (n + 2),
        out_specs=[head_block(length), row_block(length), row_block(length)] + [ANY_BLOCK] * (n + 2),
        out_shape=[shape((D, length), F32), shape((HEADS, 1, length), F32), shape((HEADS, 1, length), F32)]
        + [
            shape((group, D + 16 if i == 0 else pack.shape[0], pack.shape[1]), BF16)
            for i, (group, pack) in enumerate(zip(groups, packs))
        ]
        + [shape((4,) + piece, BF16) for piece in pieces],
        scratch_shapes=local_forward_scratch(nseg)
        + [
            sems(hops),
            sems(hops),
        ]
        + [pltpu.VMEM(piece, BF16) for piece in pieces]
        + [
            sems(6),
            sems(6),
            sems(2),
        ],
        compiler_params=talking(1),
        cost_estimate=cost(nseg * 37e-6),
        name="local_forward",
    )(mask, qkv, qkv, qkv, *packs, *shards)
    whole_up, down_first = rest[n:]
    return o_part, l_part, m_part, rest[:n], whole_up.reshape(D, 4 * D), down_first


def call_remote_forward(nseg, first, qkv, mask, o_part, l_part, m_part, keys, packs, shard):
    length = nseg * SEG
    args, specs = pack_args(keys, packs)
    return pl.pallas_call(
        functools.partial(remote_forward, nseg, first),
        grid=(HEADS,),
        in_specs=[MASK_BLOCK, part_block(0, length), head_block(length), row_block(length), row_block(length)]
        + specs
        + [ANY_BLOCK],
        out_specs=[head_block(length), row_block(length), ANY_BLOCK],
        out_shape=[
            shape((D, length), BF16),
            shape((HEADS, 1, length), F32),
            shape((4, D - DOWN_FIRST, D), BF16),
        ],
        scratch_shapes=[
            pltpu.VMEM((HEAD_DIM, length), F32),
            pltpu.VMEM((1, 1, length), F32),
            pltpu.VMEM((1, 1, length), F32),
            pltpu.VMEM((64, length), BF16),
            pltpu.VMEM((D - DOWN_FIRST, D), BF16),
            sems(3),
            sems(3),
            sems(1),
        ],
        compiler_params=talking(5),
        cost_estimate=cost(nseg * 24e-6),
        name="remote_forward",
    )(mask, qkv, o_part, l_part, m_part, *args, shard)


def call_remote_backward(nseg, first, qkv, grad, lse, slope, mask, keys, packs):
    length = nseg * SEG
    args, specs = pack_args(keys, packs)
    kept = nseg * (SEG >> first)
    return pl.pallas_call(
        functools.partial(remote_backward, nseg, first),
        grid=(HEADS,),
        in_specs=[MASK_BLOCK, part_block(0, length), head_block(length), row_block(length), row_block(length)]
        + specs,
        out_specs=[head_block(kept)]
        + [
            pl.BlockSpec((pack.shape[0], 2, HEAD_DIM, pack.shape[2]), lambda h: (0, 0, h, 0))
            for pack in packs
        ],
        out_shape=[shape((D, kept), F32)]
        + [shape((pack.shape[0], 2, D, pack.shape[2]), BF16) for pack in packs],
        scratch_shapes=[
            pltpu.VMEM((64, length), BF16),
            pltpu.VMEM((64, length), BF16),
            pltpu.VMEM((64, 1024), BF16),
            pltpu.VMEM((64, 1024), BF16),
            pltpu.VMEM((HEAD_DIM, 1024), F32),
            pltpu.VMEM((HEAD_DIM, 1024), F32),
        ],
        compiler_params=PARAMS,
        cost_estimate=cost(nseg * 20e-6),
        name="remote_backward",
    )(mask, qkv, grad, lse, slope, *args)


CHUNKS = 3
FEED_BLOCKS = (4 * D + D + 4 * D) * D // (4 * 16 * 128)
IN_BLOCKS = 3 * D * D // (4 * 16 * 128)


def padded(blocks):
    unit = CHUNKS * lax.axis_size("seq")
    return (blocks + unit - 1) // unit * unit


def reduce_copies():
    return CHUNKS * (3 + seq_bits())


def call_local_backward(nseg, first, qkv, grad, lse, slope, mask, dq_remote, sent, feed_grads):
    length = nseg * SEG
    n = len(sent)
    groups = [part.shape[0] for part in sent]
    hops = sum(group.bit_length() for group in groups)
    blocks = feed_grads.shape[1]
    piece = (CHUNKS, blocks // CHUNKS >> seq_bits(), 16, 128)
    bufs = [pltpu.VMEM((g // 2,) + part.shape[1:], BF16) for g, part in zip(groups, sent) if g > 1]
    recvs = [pltpu.VMEM((g - 1,) + part.shape[1:], BF16) for g, part in zip(groups, sent) if g > 1]
    local, *rest = pl.pallas_call(
        functools.partial(local_backward, nseg, first),
        grid=(HEADS,),
        in_specs=[MASK_BLOCK, part_block(0, length), part_block(1, length), part_block(2, length), head_block(length),
                  row_block(length), row_block(length), head_block(dq_remote.shape[1])]
        + [ANY_BLOCK] * (n + 1),
        out_specs=[pl.BlockSpec((3, HEAD_DIM, length), lambda h: (0, h, 0))]
        + [ANY_BLOCK] * n
        + [const_block(piece)],
        out_shape=[shape((3, D, length), F32)]
        + [shape(part.shape[1:], BF16) for part in sent]
        + [shape(piece, BF16)],
        scratch_shapes=local_backward_scratch(nseg)
        + bufs
        + recvs
        + [
            pltpu.VMEM((2, blocks, 16, 128), BF16),
            pltpu.VMEM((2, blocks, 16, 128), BF16),
            pltpu.VMEM((blocks, 16, 128), BF16),
            pltpu.VMEM((blocks, 16, 128), BF16),
            sems(hops),
            sems(hops),
            sems(n),
            sems(reduce_copies()),
            sems(reduce_copies()),
            sems(2 * CHUNKS),
        ],
        compiler_params=talking(2),
        cost_estimate=cost(nseg * 72e-6),
        name="local_backward",
    )(mask, qkv, qkv, qkv, grad, lse, slope, dq_remote, *sent, feed_grads)
    return local, rest[:n], rest[n]


HALF = D // 2


def const_block(dims):
    return pl.BlockSpec(dims, lambda i: (0,) * len(dims), pipeline_mode=pl.Buffered(1))


def rev4(value):
    return int(reversed_bits(value))


TILES = D // 128


def put_rows(tiled, start, array):
    for tile in range(TILES):
        tiled[tile, start : start + array.shape[0], :] = array[:, tile * 128 : (tile + 1) * 128]


def get_rows(tiled, start, size):
    return jnp.concatenate([tiled[tile, start : start + size, :] for tile in range(TILES)], axis=1)


def get_residue(tiled, start):
    return jnp.concatenate(
        [tiled[tile, pl.ds(start, RUN, stride=RES), :] for tile in range(TILES)], axis=1
    )


def put_residue(tiled, start, array):
    for tile in range(TILES):
        tiled[tile, pl.ds(start, RUN, stride=RES), :] = array[:, tile * 128 : (tile + 1) * 128]


COLUMN_CHUNKS = 3


def project_kernel(nseg, first, mask_ref, tok_ref, *refs):
    n = BRANCHES - first
    vectors, w_ref, out_ref = refs[:4], refs[4], refs[5]
    qkv_ref, xp_ref, inner_ref, weight_ref, gains_ref, whole_ref, keys_ref = refs[6:13]
    packs = refs[13 : 13 + n]
    xs, weight, gains, key_pack, vec_send, vec_recv, w_send, w_recv, w_load, w_store = refs[13 + n : 23 + n]
    key_send, key_recv, out_stage, out_send, out_recv, out_load = refs[23 + n :]
    step = pl.program_id(0)
    last = pl.num_programs(0) - 1
    me = lax.axis_index("fsdp")
    sibling = me + 1 - 2 * lax.rem(me, 2)
    across = lax.rem(me + 2, 4)
    sends = Sends(w_send, w_recv)

    def send(source, target, key, other):
        index = sends.made.setdefault(key, len(sends.made))
        return pltpu.make_async_remote_copy(
            src_ref=source, dst_ref=target, send_sem=w_send.at[index], recv_sem=w_recv.at[index],
            device_id={"fsdp": other}, device_id_type=pl.DeviceIdType.MESH,
        )

    def chunk_copies(chunk):
        cols = pl.ds(chunk * D, D)
        mine = w_ref.at[:, cols]
        load = pltpu.make_async_copy(mine, weight.at[me, :, cols], w_load.at[chunk])
        core = send(mine, weight.at[me, :, cols], ("core", chunk), sibling)
        x = send(mine, weight.at[me, :, cols], ("x", chunk), across)
        handed = weight.at[across, :, cols]
        return load, core, x, send(handed, handed, ("hand", chunk), sibling)

    def vec_copies():
        return [
            pltpu.make_async_remote_copy(
                src_ref=gains.at[me], dst_ref=gains.at[me], send_sem=vec_send.at[i], recv_sem=vec_recv.at[i],
                device_id={"fsdp": other}, device_id_type=pl.DeviceIdType.MESH,
            )
            for i, other in enumerate((sibling, across, 3 - me))
        ]

    store = pltpu.make_async_copy(weight, weight_ref, w_store.at[0])
    fetch = Shards([out_ref], [whole_ref], [out_stage], Sends(out_send, out_recv), out_load)
    ahead = Sends(key_send, key_recv).copy(0, key_pack, keys_ref, "seq", 1)

    @pl.when(step == 0)
    def _():
        barrier = pltpu.get_barrier_semaphore()
        for other in (sibling, across, 3 - me):
            pl.semaphore_signal(
                barrier, inc=1, device_id={"fsdp": other}, device_id_type=pl.DeviceIdType.MESH
            )
        pl.semaphore_signal(
            barrier, inc=1, device_id=partner("seq", 1), device_id_type=pl.DeviceIdType.MESH
        )
        for i, vector in enumerate(vectors):
            gains[me, i : i + 1, :192] = vector[...].astype(F32).reshape(1, 192)
        pl.semaphore_wait(barrier, 4)
        for copy in vec_copies():
            copy.start()
        for turn in range(COLUMN_CHUNKS):
            for copy in chunk_copies((turn + 1) % COLUMN_CHUNKS)[: 3 if turn == 0 else 2]:
                copy.start()
        fetch.start(1)
        for copy in vec_copies():
            copy.wait_recv()
        full = [
            jnp.concatenate([gains[owner, i : i + 1, :192] for owner in range(4)], axis=1) for i in range(4)
        ]
        gains_ref[...] = jnp.concatenate(full + [jnp.zeros((4, D), F32)], axis=0)
        for seg in range(nseg):
            put_rows(xs, 0, tok_ref[seg * SEG : (seg + 1) * SEG, :].astype(F32))
            for pair in range(RES // 2):
                rows = jnp.concatenate([get_residue(xs, rev4(2 * pair + i)) for i in range(2)], axis=0)
                normed = normalize(rows, full[0], full[1])[0].astype(BF16)
                at = slice(seg * SEG + pair * 2 * RUN, seg * SEG + (pair + 1) * 2 * RUN)
                xp_ref[at, :] = rows.astype(BF16)
                inner_ref[:, at] = normed.T
        for pack, level in zip(packs, range(first, BRANCHES)):
            pack[2 * D :, :] = packed_keep(mask_ref[0], level, nseg)

    for turn in range(COLUMN_CHUNKS):

        @pl.when(step == 2 * turn)
        def _():
            load, core, x, hand = chunk_copies((turn + 1) % COLUMN_CHUNKS)
            x.wait_recv()
            hand.start()
            if turn + 1 < COLUMN_CHUNKS:
                chunk_copies((turn + 2) % COLUMN_CHUNKS)[2].start()
            load.wait()
            core.wait_recv()
            hand.wait_recv()

    @pl.when(step == 2)
    def _():
        fetch.hand(0)

    @pl.when(step == 4)
    def _():
        store.start()

    where = lax.rem(step + 2, 6)
    cols = pl.ds(pl.multiple_of(where * HALF, HALF), HALF)
    block = jnp.concatenate([weight[owner, :, cols] for owner in range(4)], axis=0)
    scale = jnp.where(step >= 4, QUERY_SCALE, 1.0)
    for start in range(0, nseg * SEG, 512):
        lanes = slice(start, start + 512)
        qkv_ref[0, :, lanes] = (dotg(block, inner_ref[:, lanes], 0, 0) * scale).astype(BF16)

    @pl.when(step < 4)
    def _():
        upper = lax.rem(step, 2) == 1
        for pack, level in zip(packs, range(first, BRANCHES)):
            size = SEG >> level
            for head in range(HEADS // 2):
                rows = slice(head * HEAD_DIM, (head + 1) * HEAD_DIM)
                pieces = []
                for seg in range(nseg):
                    start = seg * SEG + (rev4(head) >> (4 - level)) * size
                    if level < 4:
                        pieces.append(qkv_ref[0, rows, start : start + size])
                    else:
                        both = qkv_ref[0, rows, start : start + 2 * size]
                        pieces.append(jnp.where(upper, both[:, size:], both[:, :size]))
                into = pl.ds(pl.multiple_of(step * HALF + head * HEAD_DIM, 16), HEAD_DIM)
                pack[into, :] = jnp.concatenate(pieces, axis=1) if nseg > 1 else pieces[0]

    @pl.when(step == 1)
    def _():
        key_pack[...] = packs[0][:D, :]
        ahead.start()

    @pl.when(step == last)
    def _():
        for copy in vec_copies():
            copy.wait_send()
        for chunk in range(COLUMN_CHUNKS):
            for copy in chunk_copies(chunk)[1:]:
                copy.wait_send()
        store.wait()
        fetch.finish()
        ahead.wait()


def call_project(nseg, first, mask, tokens, vectors, weight, weight_out):
    length = nseg * SEG
    kept = [nseg * (SEG >> level) for level in range(first, BRANCHES)]
    return pl.pallas_call(
        functools.partial(project_kernel, nseg, first),
        grid=(6,),
        in_specs=[MASK_BLOCK, const_block((length, D))] + [const_block((192,))] * 4 + [ANY_BLOCK] * 2,
        out_specs=[
            pl.BlockSpec((1, HALF, length), lambda i: ((i + 2) % 6 // 2, i % 2, 0)),
            const_block((length, D)),
            const_block((D, length)),
            ANY_BLOCK,
            const_block((8, D)),
            ANY_BLOCK,
            ANY_BLOCK,
        ]
        + [const_block((2 * D + 16, size)) for size in kept],
        out_shape=[
            shape((3, D, length), BF16),
            shape((length, D), BF16),
            shape((D, length), BF16),
            shape((4, 192, 3 * D), BF16),
            shape((8, D), F32),
            shape((4, 192, D), BF16),
            shape((D, kept[0]), BF16),
        ]
        + [shape((2 * D + 16, size), BF16) for size in kept],
        scratch_shapes=[
            pltpu.VMEM((TILES, SEG, 128), F32),
            pltpu.VMEM((4, 192, 3 * D), BF16),
            pltpu.VMEM((4, 8, 256), F32),
            pltpu.VMEM((D, kept[0]), BF16),
            sems(3),
            sems(3),
            sems(3 * COLUMN_CHUNKS),
            sems(3 * COLUMN_CHUNKS),
            sems(COLUMN_CHUNKS),
            sems(1),
            sems(1),
            sems(1),
            pltpu.VMEM((192, D), BF16),
            sems(3),
            sems(3),
            sems(1),
        ],
        compiler_params=talking(4),
        cost_estimate=cost(nseg * 10e-6),
        name="project",
    )(mask, tokens, *vectors, weight, weight_out)


ROWS = 256


def blocks_of(ref, rows, col):
    part = ref[rows, col * 128 : (col + 1) * 128].astype(BF16)
    return part.reshape(part.shape[0] // 16, 16, 128)


def feed_kernel(
    nseg, mask_ref, att_ref, x_ref, cot_ref, wout_ref, up_ref, down_a, down_b, gains_ref,
    mixed_ref, gmid_ref, gm_ref, along_ref, vec_ref, grads_ref,
    cs, out_acc, up_acc, down_acc, stage, sems,
):
    step = pl.program_id(0)
    quarter = lax.rem(step, 4)
    low = (quarter >> 1) | ((quarter & 1) << 1)

    @pl.when(step == 0)
    def _():
        out_acc[...] = jnp.zeros_like(out_acc)
        up_acc[...] = jnp.zeros_like(up_acc)
        down_acc[...] = jnp.zeros_like(down_acc)
        vec_ref[...] = jnp.zeros_like(vec_ref)

    @pl.when(quarter == 0)
    def _():
        put_rows(cs, 0, cot_ref[...].astype(F32))

    grad = jnp.concatenate([get_residue(cs, rev4(i) + low) for i in range(4)], axis=0)
    grad_b = grad.astype(BF16)
    att = att_ref[...]
    middle = x_ref[...].astype(F32) + dotg(att, wout_ref[...], 0, 0)
    gain = gains_ref[2:3, :]
    normed, unit, inverse = normalize(middle, gain, gains_ref[3:4, :])
    hidden = normed.astype(BF16)
    hidden_t = hidden.T
    final = middle
    grad_hidden = jnp.zeros((ROWS, D), F32)
    for start in range(0, 4 * D, D):
        cols = slice(start, start + D)
        upper = dotg(hidden, up_ref[:, cols], 1, 0)
        down = jnp.concatenate([down_a[start // D], down_b[start // D]], axis=0)
        grad_active = dotg(grad_b, down, 1, 1)
        half = 0.5 * (1.0 + lax.erf(upper * ROOT_HALF))
        slope = half + upper * jnp.exp(-0.5 * upper * upper) * INV_ROOT_TWO_PI
        active = (upper * half).astype(BF16)
        grad_upper = (grad_active * slope).astype(BF16)
        final = final + dotg(active, down, 1, 0)
        grad_hidden = grad_hidden + dotg(grad_upper, up_ref[:, cols], 1, 1)
        up_acc[:, cols] += dotg(hidden_t, grad_upper, 1, 0)
        down_acc[cols, :] += dotg(active, grad_b, 0, 0)
    for i in range(4):
        put_residue(cs, rev4(i) + low, final[i * RUN : (i + 1) * RUN])

    @pl.when(quarter == 3)
    def _():
        mixed_ref[...] = get_rows(cs, 0, SEG).astype(BF16)

    back, gain_back, shift_back = normalize_back(grad_hidden, unit, inverse, gain)
    vec_ref[0:1, :] += gain_back[None, :]
    vec_ref[1:2, :] += shift_back[None, :]
    grad_middle = grad + back
    gmid_ref[...] = grad_middle
    branch = grad_middle.astype(BF16)
    out_acc[...] += dotg(att, branch, 1, 0)
    lane = lax.broadcasted_iota(jnp.int32, (1, ROWS), 1)
    position = step // 4 * SEG + lax.rem(lane, RUN) * RES + residue_of(lane // RUN) + low
    keep = position < mask_ref[0]
    merged = jnp.where(keep, dotg(wout_ref[...], branch, 1, 1), 0.0).astype(BF16)
    gm_ref[...] = merged
    product = merged.astype(F32) * att.astype(F32)
    for head in range(HEADS):
        rows = slice(head * HEAD_DIM, (head + 1) * HEAD_DIM)
        along_ref[head] = jnp.sum(product[rows], axis=0, keepdims=True)

    @pl.when(step == pl.num_programs(0) - 1)
    def _():
        copies = []
        for owner in range(4):
            for piece in range(3):
                count = owner * 3 + piece
                slot = count % 2
                if count >= 2:
                    copies[count - 2].wait()
                if piece == 0:
                    rows, offset, size = slice(owner * 192, (owner + 1) * 192), 0, 288
                    for col in range(4 * TILES):
                        stage[slot, col * 12 : (col + 1) * 12] = blocks_of(up_acc, rows, col)
                elif piece == 1:
                    rows, offset, size = slice(owner * 192, (owner + 1) * 192), 288, 72
                    for col in range(TILES):
                        stage[slot, col * 12 : (col + 1) * 12] = blocks_of(out_acc, rows, col)
                else:
                    rows, offset, size = slice(owner * D, (owner + 1) * D), 360, 288
                    for col in range(TILES):
                        stage[slot, col * 48 : (col + 1) * 48] = blocks_of(down_acc, rows, col)
                copy = pltpu.make_async_copy(
                    stage.at[slot, pl.ds(0, size)],
                    grads_ref.at[owner, pl.ds(offset, size)],
                    sems.at[slot],
                )
                copy.start()
                copies.append(copy)
        copies[-2].wait()
        copies[-1].wait()


def call_feed(nseg, mask, att, x, cot, wout, up, down_a, down_b, gains):
    length = nseg * SEG
    return pl.pallas_call(
        functools.partial(feed_kernel, nseg),
        grid=(length // ROWS,),
        in_specs=[
            MASK_BLOCK,
            pl.BlockSpec((D, ROWS), lambda i: (0, i)),
            pl.BlockSpec((ROWS, D), lambda i: (i, 0)),
            pl.BlockSpec((SEG, D), lambda i: (i // 4, 0)),
            const_block((D, D)),
            const_block((D, 4 * D)),
            const_block((4, DOWN_FIRST, D)),
            const_block((4, D - DOWN_FIRST, D)),
            const_block((8, D)),
        ],
        out_specs=[
            pl.BlockSpec((SEG, D), lambda i: (i // 4, 0)),
            pl.BlockSpec((ROWS, D), lambda i: (i, 0)),
            pl.BlockSpec((D, ROWS), lambda i: (0, i)),
            pl.BlockSpec((HEADS, 1, ROWS), lambda i: (0, 0, i)),
            pl.BlockSpec((2, D), lambda i: (0, 0)),
            pl.BlockSpec(memory_space=pl.ANY),
        ],
        out_shape=[
            shape((length, D), BF16),
            shape((length, D), F32),
            shape((D, length), BF16),
            shape((HEADS, 1, length), F32),
            shape((2, D), F32),
            shape((4, padded(FEED_BLOCKS), 16, 128), BF16),
        ],
        scratch_shapes=[
            pltpu.VMEM((TILES, SEG, 128), F32),
            pltpu.VMEM((D, D), F32),
            pltpu.VMEM((D, 4 * D), F32),
            pltpu.VMEM((4 * D, D), F32),
            pltpu.VMEM((2, 288, 16, 128), BF16),
            pltpu.SemaphoreType.DMA((2,)),
        ],
        compiler_params=pltpu.CompilerParams(vmem_limit_bytes=62 * 1024 * 1024),
        cost_estimate=cost(nseg * 45e-6),
        name="feed",
    )(mask, att, x, cot, wout, up, down_a, down_b, gains)


STEPS = 6
INNER_TABLE = (
    (1, "start", 0, 0), (1, "feed", 2, 0), (1, "feed", 1, 0), (2, "feed", 0, 0),
    (2, "reduce", 0, 0), (3, "start", 1, 0), (4, "feed", 2, 1), (4, "feed", 1, 1),
    (4, "reduce", 1, 0), (4, "reduce", 0, 1), (4, "feed", 0, 1), (5, "start", 2, 0),
    (8, "reduce", 1, 1), (8, "reduce", 2, 0), (8, "feed", 2, 2), (8, "feed", 1, 2),
    (9, "reduce", 0, 2), (12, "reduce", 0, 3), (13, "vec_start", 0, 0), (13, "reduce", 2, 1),
    (14, "feed", 0, 2), (14, "reduce", 0, 4), (14, "vec", 0, 0), (14, "reduce", 1, 2),
    (14, "vec", 0, 1), (14, "reduce", 2, 2), (14, "vec", 0, 2), (14, "spread", 0, 0),
    (14, "reduce", 1, 3), (14, "vec", 0, 3), (14, "reduce", 2, 3), (14, "spread", 0, 1),
    (14, "reduce", 1, 4), (14, "vec", 0, 4), (14, "reduce", 2, 4), (14, "spread", 0, 2),
    (14, "spread", 1, 0), (14, "spread", 2, 0), (14, "spread", 1, 1), (14, "spread", 2, 1),
    (14, "spread", 1, 2), (14, "spread", 2, 2),
)


def inner_back_kernel(
    nseg, first, local_ref, inner_ref, w_ref, x_ref, gmid_ref, gain_ref, feed_vec_ref, piece_ref, *refs
):
    n = BRANCHES - first
    packs, (weight_ref, back_ref, vec_ref, up_ref, proj_ref, down_ref) = refs[:n], refs[n : n + 6]
    acc, mixed, order, terms, recv_core, recv_x, recv_seq, total, feed_total, vecs, vec_recv = refs[n + 6 : n + 17]
    red_send, red_recv, in_send, in_recv, feed_send, feed_recv, vec_send, vec_recv_sems = refs[n + 17 :]
    step = pl.program_id(0)
    last = pl.num_programs(0) - 1
    length = nseg * SEG
    turns = length // ROWS
    end = STEPS + turns
    blocks = terms.shape[1] // CHUNKS
    core = lax.rem(lax.axis_index("fsdp"), 2)
    spread = Spread(inner_orders(), blocks, total, Sends(in_send, in_recv))
    reduce = Reduce(
        inner_orders(), blocks, terms, terms, lambda xo: 2 * xo + core, recv_core, recv_x, recv_seq, Sends(red_send, red_recv),
        spread.begin,
    )
    feed_spread = Spread(feed_orders(), feed_total.shape[0] // CHUNKS, feed_total, Sends(feed_send, feed_recv))
    vec_sends = Sends(vec_send, vec_recv_sems)
    peers = all_peers()

    def vec_copy(i):
        return vec_sends.copy(i, vecs.at[i], vec_recv.at[i], *peers[i])

    def vec_event(i):
        vec_copy(i).wait_recv()
        vecs[i + 1] = vecs[i] + vec_recv[i]
        if i + 1 < len(peers):
            vec_copy(i + 1).start()

    def vec_start():
        vec_copy(0).start()

    @pl.when(step == 0)
    def _():
        meet(peers)
        vecs[0] = jnp.concatenate([jnp.zeros((2, D), F32), feed_vec_ref[...], jnp.zeros((4, D), F32)], axis=0)
        for chunk in reversed(range(CHUNKS)):
            feed_spread.begin(chunk, piece_ref.at[chunk], 0)

    @pl.when((step >= 2) & (step < STEPS))
    def _():
        upper = lax.rem(step, 2) == 1
        for pack, level in zip(packs, range(first, BRANCHES)):
            size = SEG >> level
            for head in range(HEADS // 2):
                rows = slice(head * HEAD_DIM, (head + 1) * HEAD_DIM)
                for seg in range(nseg):
                    start = seg * SEG + (rev4(head) >> (4 - level)) * size
                    piece = pack[0, rows, seg * size : (seg + 1) * size].astype(F32)
                    if level == 4:
                        zero = jnp.zeros_like(piece)
                        piece = jnp.concatenate(
                            [jnp.where(upper, zero, piece), jnp.where(upper, piece, zero)], axis=1
                        )
                    local_ref[0, rows, start : start + piece.shape[1]] += piece

    @pl.when(step < STEPS)
    def _():
        block = local_ref[0].astype(BF16)
        mixed[pl.ds(pl.multiple_of(step * HALF, HALF), HALF), :] = block
        base = lax.div(step, 2) * blocks + lax.rem(step, 2) * 36
        grad_in = dotg(block, inner_ref[...], 1, 1).T.astype(BF16)
        for col in range(3):
            part = grad_in[:, col * 128 : (col + 1) * 128].reshape(4, 12, 16, 128)
            for owner in range(4):
                terms[owner, pl.ds(base + col * 12, 12)] = part[owner]

    def inner_grad(turn):
        lanes = pl.ds(pl.multiple_of(turn * ROWS, ROWS), ROWS)
        acc[lax.rem(turn, 2)] = dotg(w_ref[...], mixed[:, lanes], 1, 0)

    @pl.when(step == STEPS - 1)
    def _():
        inner_grad(step - (STEPS - 1))

    @pl.when((step >= STEPS) & (step < end))
    def _():
        turn = step - STEPS
        inner_grad(lax.rem(turn + 1, turns))
        quarter = lax.rem(turn, 4)
        low = (quarter >> 1) | ((quarter & 1) << 1)
        gain = gain_ref[0:1, :]
        grad = acc[lax.rem(turn, 2)].T
        _, unit, inverse = normalize(x_ref[...].astype(F32), gain, gain)
        back, gain_part, shift_part = normalize_back(grad, unit, inverse, gain)
        vecs[0, 0:1, :] += gain_part[None, :]
        vecs[0, 1:2, :] += shift_part[None, :]
        total_back = gmid_ref[...] + back
        for i in range(4):
            put_residue(order, rev4(i) + low, total_back[i * RUN : (i + 1) * RUN])

        @pl.when(quarter == 3)
        def _():
            back_ref[...] = get_rows(order, 0, SEG)

    calls = {
        "start": lambda chunk, stage: reduce.begin(chunk),
        "reduce": lambda chunk, stage: reduce.event(stage, chunk),
        "spread": lambda chunk, stage: spread.event(stage, chunk),
        "feed": lambda chunk, stage: feed_spread.event(stage, chunk),
        "vec_start": lambda chunk, stage: vec_start(),
        "vec": lambda chunk, stage: vec_event(stage),
    }
    if seq_bits() == 3 and turns == 8:
        table = INNER_TABLE
    else:
        table = []
        for chunk in range(CHUNKS):
            begin = 2 * chunk + 1
            late = begin + 2 * reduce.stages() + 3 * chunk
            table += [(1 + 2 * stage, "feed", chunk, stage) for stage in range(feed_spread.stages())]
            table += [(begin, "start", chunk, 0), (begin + 1, "reduce", chunk, 0)]
            table += [
                (begin + 1 + 3 * chunk + 2 * stage, "reduce", chunk, stage)
                for stage in range(1, reduce.stages())
            ]
            table += [(late + 2 * stage, "spread", chunk, stage) for stage in range(spread.stages())]
        table += [(end - 1, "vec_start", 0, 0)]
        table += [(end + stage, "vec", 0, stage) for stage in range(len(peers))]
        table.sort(key=lambda event: event[0])
    events = [(when, functools.partial(calls[name], chunk, stage)) for when, name, chunk, stage in table]
    run_schedule(step, last, events)

    @pl.when(step == last)
    def _():
        for tile in range(TILES):
            cols = slice(tile * 128, (tile + 1) * 128)
            for col in range(4):
                at = col * 72 + tile * 12
                up_ref[:, col * D + tile * 128 : col * D + (tile + 1) * 128] = rows_of(feed_total, at, 12)
            proj_ref[:, cols] = rows_of(feed_total, 288 + tile * 12, 12)
            down_ref[:, cols] = rows_of(feed_total, 360 + tile * 48, 48)

    @pl.when(step == last)
    def _():
        reduce.finish()
        spread.finish()
        feed_spread.finish()
        for i in range(len(peers)):
            vec_copy(i).wait_send()
        vec_ref[...] = vecs[len(peers)]
        for part in range(STEPS):
            for col in range(3):
                at = part // 2 * blocks + part % 2 * 36 + col * 12
                weight_ref[:, part * HALF + col * 128 : part * HALF + (col + 1) * 128] = rows_of(total, at, 12)


def call_inner_back(nseg, first, local, inner, weight, x, gmid, gain, feed_vec, pieces, packs):
    length = nseg * SEG
    turns = length // ROWS
    blocks = padded(IN_BLOCKS)
    if blocks // CHUNKS < 72:
        raise ValueError("blocks")
    bits = seq_bits()
    peers = 2 + bits
    feed_blocks = CHUNKS * (pieces.shape[1] << bits)

    def at(i):
        return jnp.minimum(i, STEPS - 1)

    def turn(i):
        return jnp.clip(i - STEPS, 0, turns - 1)

    return pl.pallas_call(
        functools.partial(inner_back_kernel, nseg, first),
        grid=(STEPS + turns + 1,),
        in_specs=[
            pl.BlockSpec((1, HALF, length), lambda i: (at(i) // 2, at(i) % 2, 0)),
            const_block((D, length)),
            const_block((D, 3 * D)),
            pl.BlockSpec((ROWS, D), lambda i: (turn(i), 0)),
            pl.BlockSpec((ROWS, D), lambda i: (turn(i), 0)),
            const_block((8, D)),
            const_block((2, D)),
            const_block(pieces.shape),
        ]
        + [
            pl.BlockSpec((1, HALF, pack.shape[2]), lambda i: (jnp.maximum(at(i) // 2 - 1, 0), at(i) % 2, 0))
            for pack in packs
        ],
        out_specs=[
            const_block((192, 3 * D)),
            pl.BlockSpec((SEG, D), lambda i: (turn(i) // 4, 0)),
            const_block((8, D)),
            const_block((192, 4 * D)),
            const_block((192, D)),
            const_block((D, D)),
        ],
        out_shape=[
            shape((192, 3 * D), BF16),
            shape((length, D), F32),
            shape((8, D), F32),
            shape((192, 4 * D), BF16),
            shape((192, D), BF16),
            shape((D, D), BF16),
        ],
        scratch_shapes=[
            pltpu.VMEM((2, D, ROWS), F32),
            pltpu.VMEM((3 * D, length), BF16),
            pltpu.VMEM((TILES, SEG, 128), F32),
            pltpu.VMEM((4, blocks, 16, 128), BF16),
            pltpu.VMEM((2, blocks, 16, 128), BF16),
            pltpu.VMEM((blocks, 16, 128), BF16),
            pltpu.VMEM((blocks, 16, 128), BF16),
            pltpu.VMEM((blocks, 16, 128), BF16),
            pltpu.VMEM((feed_blocks, 16, 128), BF16),
            pltpu.VMEM((peers + 1, 8, D), F32),
            pltpu.VMEM((peers, 8, D), F32),
            sems(reduce_copies()),
            sems(reduce_copies()),
            sems(CHUNKS * bits),
            sems(CHUNKS * bits),
            sems(CHUNKS * bits),
            sems(CHUNKS * bits),
            sems(peers),
            sems(peers),
        ],
        compiler_params=talking(3, 60),
        cost_estimate=cost(nseg * 15e-6),
        name="inner_back",
    )(local, inner, weight, x, gmid, gain, feed_vec, pieces, *packs)


def per_device(
    tokens,
    first_gain,
    first_shift,
    project_in,
    project_out,
    second_gain,
    second_shift,
    up_weight,
    down_weight,
    valid_mask,
    cotangent,
):
    length = tokens.shape[1]
    nseg = length // SEG
    first = nseg.bit_length()

    mask = jnp.sum(valid_mask[0])[None]

    vectors = [first_gain, first_shift, second_gain, second_shift]
    qkv, x, inner, weight_in, gains, weight_out, keys, *packs = call_project(
        nseg, first, mask, tokens[0], vectors, project_in, project_out
    )
    weight_out, keys = weight_out.reshape(D, D), keys[None]
    weight_in = weight_in.reshape(D, 3 * D)
    o_part, l_part, m_part, gathered, weight_up, down_first = call_local_forward(
        nseg, first, qkv, mask, packs, (up_weight, down_weight)
    )
    attended, lse, down_second = call_remote_forward(
        nseg, first, qkv, mask, o_part, l_part, m_part, keys, gathered, down_weight
    )

    mixed, grad_middle, grad_merged, along, feed_vec, feed_grads = call_feed(
        nseg, mask, attended, x, cotangent[0], weight_out, weight_up, down_first, down_second, gains
    )

    dq_remote, *sent = call_remote_backward(nseg, first, qkv, grad_merged, lse, along, mask, keys, gathered)
    local, returned, pieces = call_local_backward(
        nseg, first, qkv, grad_merged, lse, along, mask, dq_remote, sent, feed_grads
    )
    grad_in, tokens_back, vectors, grad_up, grad_out, grad_down = call_inner_back(
        nseg, first, local, inner, weight_in, x, grad_middle, gains, feed_vec, pieces, returned
    )
    quarter = D // lax.axis_size("fsdp")
    vectors = lax.dynamic_slice_in_dim(vectors, lax.axis_index("fsdp") * quarter, quarter, 1)
    return (
        mixed[None],
        tokens_back[None],
        vectors[0],
        vectors[1],
        grad_in.astype(F32),
        grad_out.astype(F32),
        vectors[2],
        vectors[3],
        grad_up.astype(F32),
        grad_down.astype(F32),
    )


def solution(mesh):
    in_specs = (
        P("fsdp", "seq", None),
        P("fsdp"),
        P("fsdp"),
        P("fsdp", None),
        P("fsdp", None),
        P("fsdp"),
        P("fsdp"),
        P("fsdp", None),
        P("fsdp", None),
        P("fsdp", "seq"),
        P("fsdp", "seq", None),
    )
    out_specs = (
        P("fsdp", "seq", None),
        P("fsdp", "seq", None),
        P("fsdp"),
        P("fsdp"),
        P("fsdp", None),
        P("fsdp", None),
        P("fsdp"),
        P("fsdp"),
        P("fsdp", None),
        P("fsdp", None),
    )
    return jax.shard_map(
        per_device, mesh=mesh, in_specs=in_specs, out_specs=out_specs, check_vma=False
    )
```

```python
import functools
import math

import jax
import jax.numpy as jnp
import ml_dtypes
import numpy as np
from jax import lax
from jax.experimental import pallas as pl
from jax.experimental.pallas import tpu as pltpu
from jax.sharding import PartitionSpec as P

HEADS = 16
HEAD_DIM = 48
SEG = 1024
BRANCHES = 5
RES = 16
RUN = SEG // RES
D = HEADS * HEAD_DIM

EPS = 1e-05
NEG = -1e30
ROOT_HALF = 0.7071067811865476
INV_ROOT_TWO_PI = 0.3989422804014327
F32 = jnp.float32
BF16 = jnp.bfloat16
QUERY_SCALE = math.log2(math.e) * HEAD_DIM ** (-0.5)
VMEM_LIMIT = 56 * 1024 * 1024


def dotg(left, right, left_dim, right_dim):
    return lax.dot_general(
        left, right, (((left_dim,), (right_dim,)), ((), ())), preferred_element_type=F32
    )


def normalize(values, gain, shift):
    mean = jnp.mean(values, axis=-1, keepdims=True)
    centred = values - mean
    spread = jnp.mean(centred * centred, axis=-1, keepdims=True)
    inverse = lax.rsqrt(spread + EPS)
    normed = centred * inverse
    return (normed * gain + shift, normed, inverse)


def normalize_back(grad, normed, inverse, gain):
    scaled = grad * gain
    first = jnp.mean(scaled, axis=-1, keepdims=True)
    second = jnp.mean(scaled * normed, axis=-1, keepdims=True)
    return (
        inverse * (scaled - first - normed * second),
        jnp.sum(grad * normed, axis=0),
        jnp.sum(grad, axis=0),
    )


def reversed_bits(head):
    return ((head & 1) << 3) | ((head & 2) << 1) | ((head & 4) >> 1) | ((head & 8) >> 3)


def near_class(head, low_bits, length):
    lane = lax.broadcasted_iota(jnp.int32, (1, length), 1)
    rho = lax.rem(lane // RUN, 1 << low_bits)
    return rho ^ (reversed_bits(head) & ((1 << low_bits) - 1))


def class_rows(near, length):
    row = lax.broadcasted_iota(jnp.int32, (16, length), 0)
    step = lax.rem(row + 3, 4) + 1
    bound = jnp.where((row >= 5) & (row <= 12), lax.shift_right_logical(RES, step), 0)
    return row, near < bound


def query_rows(head, length, neg_lse=None):
    near = near_class(head, 4, length)
    row, inside = class_rows(near, length)
    out = jnp.where(inside, 1.0, 0.0)
    out = jnp.where(row == 0, 1.0, out)
    out = jnp.where(row == 4, jnp.where(near < 1, 0.0, NEG), out)
    if neg_lse is not None:
        high = neg_lse.astype(BF16).astype(F32)
        rest = neg_lse - high
        mid = rest.astype(BF16).astype(F32)
        low = rest - mid
        out = jnp.where(row == 1, high, jnp.where(row == 2, mid, jnp.where(row == 3, low, out)))
    return out.astype(BF16)


def residue_of(rho):
    return reversed_bits(rho)


def local_keep(count, length):
    lane = lax.broadcasted_iota(jnp.int32, (1, length), 1)
    rho = lax.rem(lane // RUN, RES)
    position = lane // SEG * SEG + lax.rem(lane, RUN) * RES + residue_of(rho)
    return position < count


def packed_keep(count, level, nseg):
    size = SEG >> level
    dims = (HEADS, nseg * size)
    head = lax.broadcasted_iota(jnp.int32, dims, 0)
    lane = lax.broadcasted_iota(jnp.int32, dims, 1)
    rho = (reversed_bits(head) >> (4 - level)) * (size // RUN) + lax.rem(lane, size) // RUN
    position = lane // size * SEG + lax.rem(lane, RUN) * RES + residue_of(rho)
    return jnp.where(position < count, 1.0, 0.0).astype(BF16)


def weight_of(level, step):
    return math.log2((step - level + 1) / (step - level)) if step > level else 0.0


def key_rows(head, level, low_bits, length, keep):
    near = near_class(head, low_bits, length)
    row, inside = class_rows(near, length)
    weight = jnp.zeros((16, length), F32)
    for step in range(level + 1, BRANCHES):
        value = weight_of(level, step)
        high = float(np.asarray(value, ml_dtypes.bfloat16))
        weight = jnp.where(row == 4 + step, high, weight)
        weight = jnp.where(row == 8 + step, value - high, weight)
    out = jnp.where(inside, weight, 0.0)
    out = jnp.where((row >= 1) & (row <= 3), 1.0, out)
    out = jnp.where(row == 0, jnp.where(keep, 0.0, NEG), out)
    if level == BRANCHES - 1:
        out = jnp.where(row == 4, 1.0, out)
    return out.astype(BF16)


def value_rows(length):
    row = lax.broadcasted_iota(jnp.int32, (16, length), 0)
    return jnp.where(row < 2, 1.0, 0.0).astype(BF16)


def join(rows, extra):
    return jnp.concatenate([rows, extra], axis=0)


def kept_start(head, level, seg):
    size = SEG >> level
    block = reversed_bits(head) >> (4 - level)
    return pl.multiple_of(seg * SEG + block * size, min(size, 128))


def partner(axis, distance):
    place = lax.axis_index(axis)
    return {axis: place + distance * (1 - 2 * lax.rem(lax.div(place, distance), 2))}


def seq_bits():
    return lax.axis_size("seq").bit_length() - 1


def meet(peers):
    barrier = pltpu.get_barrier_semaphore()
    for axis, distance in peers:
        pl.semaphore_signal(
            barrier, inc=1, device_id=partner(axis, distance), device_id_type=pl.DeviceIdType.MESH
        )
    pl.semaphore_wait(barrier, len(peers))


class Sends:
    def __init__(self, send_sems, recv_sems):
        self.send_sems, self.recv_sems, self.made = send_sems, recv_sems, {}

    def copy(self, key, source, target, axis, distance):
        index = self.made.setdefault(key, len(self.made))
        return pltpu.make_async_remote_copy(
            src_ref=source,
            dst_ref=target,
            send_sem=self.send_sems.at[index],
            recv_sem=self.recv_sems.at[index],
            device_id=partner(axis, distance),
            device_id_type=pl.DeviceIdType.MESH,
        )


class Gather:
    def __init__(self, nseg, first, packs, gathered, sends):
        self.hops, self.distances = [], set()
        for level, pack, into in zip(range(first, BRANCHES), packs, gathered):
            group = (SEG << (level - 1)) // (nseg * SEG)
            source = pack if pack.shape[0] == into.shape[1] else pack.at[pl.ds(D, D + 16)]
            hops = [((level, 0), source, into.at[0], group)]
            step = 1
            while step < group:
                hops.append(((level, step), into.at[pl.ds(0, step)], into.at[pl.ds(step, step)], step))
                step *= 2
            self.hops.append([sends.copy(k, a, b, "seq", d) for k, a, b, d in hops])
            self.distances |= {hop[3] for hop in hops}

    def peers(self):
        return [("seq", distance) for distance in sorted(self.distances)]

    def start(self):
        for hops in reversed(self.hops):
            hops[0].start()

    def pass_on(self, index, turn):
        hops = self.hops[index]
        hops[turn - 1].wait_recv()
        hops[turn].start()

    def finish(self):
        for hops in self.hops:
            for hop in hops:
                hop.wait_send()
            hops[-1].wait_recv()

    def turns(self):
        events = []
        for index, hops in reversed(list(enumerate(self.hops))):
            for turn in range(1, len(hops)):
                when = 6 + 3 * (turn - 1) + 2 * (len(self.hops) - 1 - index)
                events.append((when, functools.partial(self.pass_on, index, turn)))
        return events


class Shards:
    def __init__(self, shards, whole, stages, sends, loads, started=1):
        self.copies, self.started = [], started
        self.staged = [
            pltpu.make_async_copy(shard, stage, loads.at[i])
            for i, (shard, stage) in enumerate(zip(shards, stages))
        ]
        me = lax.axis_index("fsdp")
        other = lax.rem(me + 2, 4)
        for i, (shard, into) in enumerate(zip(stages, whole)):
            self.copies.append(
                (
                    pltpu.make_async_copy(shard, into.at[me], loads.at[i]),
                    sends.copy((i, "core"), shard, into.at[me], "fsdp", 1),
                    sends.copy((i, "x"), shard, into.at[me], "fsdp", 2),
                    sends.copy((i, "hand"), into.at[other], into.at[other], "fsdp", 1),
                )
            )

    def start(self):
        for staged in self.staged:
            staged.start()
        for i, (load, core, x, _) in enumerate(self.copies):
            self.staged[i].wait()
            load.start()
            core.start()
            if i < self.started:
                x.start()

    def hand(self, i):
        _, _, x, hand = self.copies[i]
        x.wait_recv()
        hand.start()
        if self.started <= i + 1 < len(self.copies):
            self.copies[i + 1][2].start()

    def finish(self):
        for load, core, x, hand in self.copies:
            load.wait()
            core.wait()
            x.wait_send()
            hand.wait()


class Return:
    def __init__(self, nseg, first, sent, returned, bufs, recvs, local_sems, sends):
        self.plans = []
        for i, level in enumerate(range(first, BRANCHES)):
            group = (SEG << (level - 1)) // (nseg * SEG)
            plan = []
            if group == 1:
                plan.append((None, sends.copy((level, 0), sent[i].at[0], returned[i], "seq", group)))
                self.plans.append((plan, None))
                continue
            buf, recv = bufs.pop(0), recvs.pop(0)
            step = group // 2
            load = pltpu.make_async_copy(sent[i].at[pl.ds(0, step)], buf, local_sems.at[i])
            source, at, add = sent[i].at[pl.ds(step, step)], 0, None
            while step >= 1:
                into = recv.at[pl.ds(at, step)]
                plan.append((add, sends.copy((level, step), source, into, "seq", step)))
                add = (buf, recv, at, step)
                at += step
                step //= 2
                if step:
                    source = buf.at[pl.ds(step, step)]
            plan.append((add, sends.copy((level, 0), buf.at[0], returned[i], "seq", group)))
            self.plans.append((plan, load))

    def start(self, direct):
        for plan, load in reversed(self.plans):
            if direct == (load is None):
                if load is not None:
                    load.start()
                plan[0][1].start()

    def turn(self, number):
        for plan, load in reversed(self.plans):
            if number < len(plan):
                plan[number - 1][1].wait_recv()
                if number == 1 and load is not None:
                    load.wait()
                buf, recv, at, step = plan[number][0]
                for i in range(step):
                    buf[i] = (buf[i].astype(F32) + recv[at + i].astype(F32)).astype(BF16)
                plan[number][1].start()

    def finish(self):
        for plan, load in self.plans:
            for _, copy in plan:
                copy.wait_send()
            plan[-1][1].wait_recv()

    def turns(self):
        return max(len(plan) for plan, _ in self.plans)


def add_blocks(into, at, other, start, count):
    unit = max(u for u in range(1, 13) if count % u == 0)

    def body(i, carry):
        rows = pl.ds(at + i * unit, unit)
        part = other[pl.ds(start + i * unit, unit)].astype(F32)
        into[rows] = (into[rows].astype(F32) + part).astype(BF16)
        return carry

    lax.fori_loop(0, count // unit, body, 0)


def copy_blocks(into, at, other, start, count):
    unit = max(u for u in range(1, 13) if count % u == 0)

    def body(i, carry):
        into[pl.ds(at + i * unit, unit)] = other[pl.ds(start + i * unit, unit)]
        return carry

    lax.fori_loop(0, count // unit, body, 0)


def halving(blocks, order):
    seq = lax.axis_index("seq")
    low, given = [0], []
    for j, distance in enumerate(order):
        bit = lax.rem(lax.div(seq, distance), 2)
        half = blocks >> (j + 1)
        given.append(low[j] + (1 - bit) * half)
        low.append(low[j] + bit * half)
    return low, given


def feed_orders():
    plain = [2**j for j in range(seq_bits())]
    return [plain] * (CHUNKS - 1) + [plain[1:] + plain[:1]]


def inner_orders():
    plain = [2**j for j in range(seq_bits())]
    return [plain] * (CHUNKS - 1) + [[plain[1], plain[0]] + plain[2:]]


def all_peers():
    return [("fsdp", 1), ("fsdp", 2)] + [("seq", 2**j) for j in range(seq_bits())]


class Reduce:
    def __init__(
        self, orders, blocks, source, terms, own, recv_core, recv_x, recv_seq, sends, done, loads=None
    ):
        self.blocks, self.source, self.terms, self.own, self.done = blocks, source, terms, own, done
        self.recv_core, self.recv_x, self.recv_seq = recv_core, recv_x, recv_seq
        self.sends, self.loads = sends, loads
        fsdp = lax.axis_index("fsdp")
        self.core, self.x = lax.rem(fsdp, 2), lax.div(fsdp, 2)
        self.bits = seq_bits()
        self.orders = orders
        self.halves = [halving(blocks, order) for order in self.orders]

    def stages(self):
        return 2 + self.bits

    def core_copy(self, chunk, xo):
        rows = pl.ds(chunk * self.blocks, self.blocks)
        owner = 2 * xo + 1 - self.core
        return self.sends.copy(
            ("core", chunk, xo), self.source.at[owner, rows], self.recv_core.at[xo, rows], "fsdp", 1
        )

    def load_copy(self, chunk, xo):
        rows = pl.ds(chunk * self.blocks, self.blocks)
        return pltpu.make_async_copy(
            self.source.at[2 * xo + self.core, rows], self.terms.at[xo, rows], self.loads.at[2 * chunk + xo]
        )

    def x_copy(self, chunk):
        rows = pl.ds(chunk * self.blocks, self.blocks)
        return self.sends.copy(
            ("x", chunk), self.terms.at[self.own(1 - self.x), rows], self.recv_x.at[rows], "fsdp", 2
        )

    def down_copy(self, chunk, j):
        half = self.blocks >> (j + 1)
        base = chunk * self.blocks
        rows = pl.ds(base + self.halves[chunk][1][j], half)
        into = pl.ds(base + self.blocks - (self.blocks >> j), half)
        return self.sends.copy(
            ("down", chunk, j), self.terms.at[self.own(self.x), rows], self.recv_seq.at[into], "seq",
            self.orders[chunk][j],
        )

    def begin(self, chunk):
        for xo in range(2):
            if self.loads is not None:
                self.load_copy(chunk, xo).start()
            self.core_copy(chunk, xo).start()

    def event(self, stage, chunk):
        base = chunk * self.blocks
        low = self.halves[chunk][0]
        mine = self.terms.at[self.own(self.x)]
        if stage == 0:
            for xo in range(2):
                self.core_copy(chunk, xo).wait_recv()
                if self.loads is not None:
                    self.load_copy(chunk, xo).wait()
                add_blocks(self.terms.at[self.own(xo)], base, self.recv_core.at[xo], base, self.blocks)
            self.x_copy(chunk).start()
            return
        j = stage - 2
        if stage == 1:
            self.x_copy(chunk).wait_recv()
            add_blocks(mine, base, self.recv_x, base, self.blocks)
        else:
            self.down_copy(chunk, j).wait_recv()
            half = self.blocks >> (j + 1)
            add_blocks(mine, base + low[j + 1], self.recv_seq, base + self.blocks - (self.blocks >> j), half)
        if j + 1 < self.bits:
            self.down_copy(chunk, j + 1).start()
        else:
            self.done(chunk, mine, base + low[self.bits])

    def finish(self):
        for chunk in range(CHUNKS):
            for xo in range(2):
                self.core_copy(chunk, xo).wait_send()
            self.x_copy(chunk).wait_send()
            for j in range(self.bits):
                self.down_copy(chunk, j).wait_send()


class Spread:
    def __init__(self, orders, blocks, total, sends):
        self.blocks, self.total, self.sends = blocks, total, sends
        self.bits = seq_bits()
        self.orders = orders
        self.lows = [halving(blocks, order)[0] for order in self.orders]

    def stages(self):
        return self.bits

    def copy(self, chunk, j):
        rows = pl.ds(chunk * self.blocks + self.lows[chunk][j + 1], self.blocks >> (j + 1))
        here = self.total.at[rows]
        return self.sends.copy((chunk, j), here, here, "seq", self.orders[chunk][j])

    def begin(self, chunk, ref, start):
        size = self.blocks >> self.bits
        copy_blocks(self.total, chunk * self.blocks + self.lows[chunk][self.bits], ref, start, size)
        self.copy(chunk, self.bits - 1).start()

    def event(self, stage, chunk):
        j = self.bits - 1 - stage
        self.copy(chunk, j).wait_recv()
        if j:
            self.copy(chunk, j - 1).start()

    def finish(self):
        for chunk in range(CHUNKS):
            for j in range(self.bits):
                self.copy(chunk, j).wait_send()


def run_schedule(step, last, events):
    due = {}
    for when, call in events:
        due.setdefault(min(when, last), []).append(call)
    for when in sorted(due):

        @pl.when(step == when)
        def _():
            for call in due[when]:
                call()


FRONT = 3
KEY_TILE = 128


class State:
    def __init__(self, query, acc=None, top=None):
        self.query, self.acc, self.top = query, acc, top


def attend(items):
    items = list(items)
    ready = []
    for turn in range(len(items) + FRONT):
        if turn < len(items):
            state, key, _ = items[turn]
            ready.append(dotg(key, state.query, 1, 0))
        if turn >= FRONT:
            state, _, value = items[turn - FRONT]
            scores, ready[turn - FRONT] = ready[turn - FRONT], None
            top = jnp.max(scores, axis=0, keepdims=True)
            if state.top is not None:
                top = jnp.maximum(top, state.top)
            probs = jnp.exp2(scores - top).astype(BF16)
            part = dotg(value, probs, 1, 0)
            state.acc = part if state.top is None else state.acc * jnp.exp2(state.top - top) + part
            state.top = top


def key_items(state, key_t, value):
    size = key_t.shape[0]
    tile = min(KEY_TILE, size)
    for start in range(0, size, tile):
        yield state, key_t[start : start + tile], value[:, start : start + tile]


def load_state(query, mine, o_ref, l_ref, m_ref):
    acc = [jnp.concatenate([o_ref[:, at], jnp.broadcast_to(l_ref[0, :, at], (16, at.size))]) for at in mine]
    top = [m_ref[0, :, at] for at in mine]
    return State(query, jnp.concatenate(acc, axis=1), jnp.concatenate(top, axis=1))


def store_state(state, mine, o_ref, l_ref, m_ref):
    start = 0
    for at in mine:
        lanes = slice(start, start + at.size)
        o_ref[:, at] = state.acc[:HEAD_DIM, lanes]
        l_ref[0, :, at] = state.acc[HEAD_DIM : HEAD_DIM + 1, lanes]
        m_ref[0, :, at] = state.top[:, lanes]
        start += at.size


DOWN_FIRST = 384


def local_forward(nseg, first, mask_ref, q_ref, k_ref, v_ref, *refs):
    n = BRANCHES - first
    packs, shards, (o_ref, l_ref, m_ref) = refs[:n], refs[n : n + 3], refs[n + 3 : n + 6]
    gathered, whole = refs[n + 6 : 2 * n + 6], refs[2 * n + 6 : 2 * n + 9]
    qa, ka, va, send_sems, recv_sems, *stages, shard_send, shard_recv, shard_load = refs[2 * n + 9 :]
    head = pl.program_id(0)
    gather = Gather(nseg, first, packs, gathered, Sends(send_sems, recv_sems))
    pieces = [shards[0], shards[1], shards[2].at[pl.ds(0, DOWN_FIRST)]]
    fetch = Shards(pieces, whole, stages, Sends(shard_send, shard_recv), shard_load, 2)

    def begin():
        meet(gather.peers() + [("fsdp", 1), ("fsdp", 2)])
        gather.start()
        fetch.start()

    def finish():
        gather.finish()
        fetch.finish()

    hands = [(when, functools.partial(fetch.hand, i)) for i, when in enumerate((11, 11, 15))]
    run_schedule(head, HEADS - 1, [(0, begin)] + sorted(gather.turns() + hands, key=lambda event: event[0]))
    local_forward_core(nseg, mask_ref, q_ref, k_ref, v_ref, o_ref, l_ref, m_ref, qa, ka, va)
    run_schedule(head, HEADS - 1, [(HEADS - 1, finish)])


def local_forward_scratch(nseg):
    length = nseg * SEG
    return [
        pltpu.VMEM((64, length), BF16),
        pltpu.VMEM((nseg, 64, length), BF16),
        pltpu.VMEM((64, length), BF16),
    ]


def local_forward_core(nseg, mask_ref, q_ref, k_ref, v_ref, o_ref, l_ref, m_ref, qa, ka, va):
    head = pl.program_id(0)
    length = nseg * SEG
    keep = local_keep(mask_ref[0], length)
    qa[...] = join(q_ref[0], query_rows(head, length))
    va[...] = join(v_ref[0], value_rows(length))
    ka[0] = join(k_ref[0], key_rows(head, 0, 4, length, keep))
    if nseg == 2:
        ka[1] = join(k_ref[0], key_rows(head, 1, 4, length, keep))
    states, items = [], []
    for seg in range(nseg):
        lanes = slice(seg * SEG, (seg + 1) * SEG)
        states.append(State(qa[:, lanes]))
        items += key_items(states[-1], ka[0, :, lanes].T, va[:, lanes])
    attend(items)
    for seg in range(nseg):
        store_state(states[seg], [pl.ds(seg * SEG, SEG)], o_ref, l_ref, m_ref)
    if nseg == 2:
        kept = [pl.ds(kept_start(head, 1, seg), SEG // 2) for seg in range(2)]
        states = [load_state(qa[:, at], [at], o_ref, l_ref, m_ref) for at in kept]
        items = []
        for seg in range(2):
            items += key_items(states[seg], ka[1, :, kept[1 - seg]].T, va[:, kept[1 - seg]])
        attend(items)
        for seg in range(2):
            store_state(states[seg], [kept[seg]], o_ref, l_ref, m_ref)


def remote_keys(head, level, pack):
    k_ref, v_ref, mask_ref = pack
    pieces = range(k_ref.shape[0])
    key, value, mask = (
        jnp.concatenate([ref[i] for i in pieces], axis=1) for ref in (k_ref, v_ref, mask_ref)
    )
    length = key.shape[1]
    row = lax.broadcasted_iota(jnp.int32, (16, length), 0)
    keep = jnp.sum(jnp.where(row == head, mask.astype(F32), 0.0), axis=0, keepdims=True) > 0.5
    return join(key, key_rows(head, level, 4 - level, length, keep)), join(value, value_rows(length))


def remote_plan(first):
    return [(level,) for level in range(first, 3)] + [(3, 4)]


def remote_forward(nseg, first, mask_ref, q_ref, o_in, l_in, m_in, *refs):
    head = pl.program_id(0)
    levels = range(first, BRANCHES)
    packs = {level: refs[3 * i : 3 * i + 3] for i, level in enumerate(levels)}
    shard_ref, att_ref, lse_ref, whole_ref, o_ref, l_ref, m_ref, qa, stage, *shard_sems = refs[
        3 * len(levels) :
    ]
    shard_send, shard_recv, shard_load = shard_sems
    piece = shard_ref.at[pl.ds(DOWN_FIRST, D - DOWN_FIRST)]
    fetch = Shards([piece], [whole_ref], [stage], Sends(shard_send, shard_recv), shard_load)

    def begin():
        meet([("fsdp", 1), ("fsdp", 2)])
        fetch.start()

    run_schedule(head, HEADS - 1, [(0, begin), (12, functools.partial(fetch.hand, 0))])
    length = nseg * SEG
    qa[...] = join(q_ref[0], query_rows(head, length))
    o_ref[...] = o_in[...]
    l_ref[...] = l_in[...]
    m_ref[...] = m_in[...]
    for group in remote_plan(first):
        pairs = [remote_keys(head, level, packs[level]) for level in group]
        key = jnp.concatenate([pair[0] for pair in pairs], axis=1)
        value = jnp.concatenate([pair[1] for pair in pairs], axis=1)
        mine = [pl.ds(kept_start(head, group[0], seg), SEG >> group[0]) for seg in range(nseg)]
        query = jnp.concatenate([qa[:, at] for at in mine], axis=1)
        state = load_state(query, mine, o_ref, l_ref, m_ref)
        attend(key_items(state, key.T, value))
        store_state(state, mine, o_ref, l_ref, m_ref)
    weight = jnp.where(local_keep(mask_ref[0], length), 1.0, 0.0) / l_ref[0]
    att_ref[...] = (o_ref[...] * weight).astype(BF16)
    lse_ref[0] = m_ref[0] + jnp.log2(l_ref[0])
    run_schedule(head, HEADS - 1, [(HEADS - 1, fetch.finish)])


def grad_rows(grad, slope):
    length = grad.shape[1]
    row = lax.broadcasted_iota(jnp.int32, (16, length), 0)
    high = (-slope).astype(BF16).astype(F32)
    low = -slope - high
    extra = jnp.where(row == 0, high, jnp.where(row == 1, low, 0.0)).astype(BF16)
    return join(grad, extra)


AHEAD = 2
QUERY_TILE = 256
BACK_KEYS = 256


class Side:
    def __init__(self, query, grad):
        self.query, self.grad = query[:HEAD_DIM], grad[:HEAD_DIM]
        self.query_t, self.grad_t = query.T, grad.T
        self.dq = None


def attend_back(items, dk_ref, dv_ref, written):
    items = list(items)
    ready = []
    for turn in range(len(items) + AHEAD):
        if turn < len(items):
            side, key, value, _, _ = items[turn]
            ready.append((dotg(side.query_t, key, 1, 0), dotg(side.grad_t, value, 1, 0)))
        if turn >= AHEAD:
            side, key, _, lanes, name = items[turn - AHEAD]
            scores, slope = ready[turn - AHEAD]
            ready[turn - AHEAD] = None
            probs = jnp.exp2(scores)
            dscore = (probs * slope).astype(BF16)
            dv = dotg(side.grad, probs.astype(BF16), 1, 0)
            dk = dotg(side.query, dscore, 1, 0)
            part = dotg(key[:HEAD_DIM], dscore, 1, 1)
            side.dq = part if side.dq is None else side.dq + part
            if name in written:
                dv_ref[:, lanes] += dv
                dk_ref[:, lanes] += dk
            else:
                written.add(name)
                dv_ref[:, lanes] = dv
                dk_ref[:, lanes] = dk


def sides_of(query, grad):
    tile = min(QUERY_TILE, query.shape[1])
    return [
        Side(query[:, start : start + tile], grad[:, start : start + tile])
        for start in range(0, query.shape[1], tile)
    ]


def pairs(sides, key_ref, value_ref, tiles):
    return [
        (side, key_ref[:, lanes], value_ref[:, lanes], lanes, name) for side in sides for name, lanes in tiles
    ]


def joined(sides):
    return jnp.concatenate([side.dq for side in sides], axis=1) if len(sides) > 1 else sides[0].dq


DQ_SCALE = HEAD_DIM ** (-0.5)
DK_SCALE = math.log(2.0)


def neg_total(lse, keep):
    return jnp.where(keep, -lse, NEG)


def local_backward(nseg, first, mask_ref, q_ref, k_ref, v_ref, g_ref, lse_ref, slope_ref, dqr_ref, *refs):
    n = BRANCHES - first
    sent, feed_ref, out_ref = refs[:n], refs[n], refs[n + 1]
    returned, piece_ref = refs[n + 2 : 2 * n + 2], refs[2 * n + 2]
    qa, ga, ka, va, dk, dv = refs[2 * n + 3 : 2 * n + 9]
    rest = list(refs[2 * n + 9 :])
    back_send, back_recv, back_load, red_send, red_recv, red_load = rest[-6:]
    terms, recv_core, recv_x, recv_seq = rest[-10:-6]
    bufs, recvs = rest[: (len(rest) - 10) // 2], rest[(len(rest) - 10) // 2 : -10]
    head = pl.program_id(0)
    last = HEADS - 1

    back = Return(nseg, first, sent, returned, bufs, recvs, back_load, Sends(back_send, back_recv))
    blocks = terms.shape[1] // CHUNKS
    reduce = Reduce(
        feed_orders(), blocks, feed_ref, terms, lambda xo: xo, recv_core, recv_x, recv_seq, Sends(red_send, red_recv),
        lambda chunk, ref, start: copy_blocks(piece_ref.at[chunk], 0, ref, start, blocks >> seq_bits()),
        red_load,
    )

    def begin():
        meet(all_peers())
        back.start(False)
        for chunk in range(CHUNKS):
            reduce.begin(chunk)

    events = [(3 * turn, functools.partial(back.turn, turn)) for turn in range(1, back.turns())]
    events.append((8, functools.partial(back.start, True)))
    for chunk in range(CHUNKS):
        for stage in range(reduce.stages()):
            when = 1 + (chunk + 1) // 2 if stage == 0 else 4 + 3 * chunk + 2 * (stage - 1)
            events.append((when, functools.partial(reduce.event, stage, chunk)))
    run_schedule(head, last, [(0, begin)] + sorted(events, key=lambda event: event[0]))
    local_backward_core(
        nseg, first, mask_ref, q_ref, k_ref, v_ref, g_ref, lse_ref, slope_ref, dqr_ref, out_ref,
        qa, ga, ka, va, dk, dv,
    )

    @pl.when(head == last)
    def _():
        back.finish()
        reduce.finish()


def local_backward_scratch(nseg):
    length = nseg * SEG
    return [
        pltpu.VMEM((64, length), BF16),
        pltpu.VMEM((64, length), BF16),
        pltpu.VMEM((nseg, 64, length), BF16),
        pltpu.VMEM((64, length), BF16),
        pltpu.VMEM((HEAD_DIM, length), F32),
        pltpu.VMEM((HEAD_DIM, length), F32),
    ]


def local_backward_core(
    nseg, first, mask_ref, q_ref, k_ref, v_ref, g_ref, lse_ref, slope_ref, dqr_ref, out_ref,
    qa, ga, ka, va, dk, dv,
):
    head = pl.program_id(0)
    length = nseg * SEG
    keep = local_keep(mask_ref[0], length)
    qa[...] = join(q_ref[0], query_rows(head, length, neg_total(lse_ref[0], keep)))
    ga[...] = grad_rows(g_ref[...], slope_ref[0])
    va[...] = join(v_ref[0], value_rows(length))
    ka[0] = join(k_ref[0], key_rows(head, 0, 4, length, keep))
    if nseg == 2:
        ka[1] = join(k_ref[0], key_rows(head, 1, 4, length, keep))
    items, sides, written = [], [], set()
    for seg in range(nseg):
        lanes = slice(seg * SEG, (seg + 1) * SEG)
        tiles = [
            ((seg, i), slice(seg * SEG + BACK_KEYS * i, seg * SEG + BACK_KEYS * (i + 1)))
            for i in range(SEG // BACK_KEYS)
        ]
        sides.append(sides_of(qa[:, lanes], ga[:, lanes]))
        items += pairs(sides[-1], ka.at[0], va, tiles)
    attend_back(items, dk, dv, written)
    for seg in range(nseg):
        out_ref[0, :, seg * SEG : (seg + 1) * SEG] = joined(sides[seg]) * DQ_SCALE
    if nseg == 2:
        items, sides = [], []
        kept = [pl.ds(kept_start(head, 1, seg), SEG // 2) for seg in range(2)]
        for seg in range(2):
            base = kept_start(head, 1, 1 - seg)
            tile = min(BACK_KEYS, SEG // 2)
            tiles = [
                ((seg, i), pl.ds(pl.multiple_of(base + tile * i, tile), tile)) for i in range(SEG // 2 // tile)
            ]
            sides.append(sides_of(qa[:, kept[seg]], ga[:, kept[seg]]))
            items += pairs(sides[-1], ka.at[1], va, tiles)
        attend_back(items, dk, dv, set(item[4] for item in items))
        for seg in range(2):
            out_ref[0, :, kept[seg]] += joined(sides[seg]) * DQ_SCALE
    size = SEG >> first
    for seg in range(nseg):
        mine = pl.ds(kept_start(head, first, seg), size)
        out_ref[0, :, mine] += dqr_ref[:, seg * size : (seg + 1) * size]
    out_ref[1] = dk[...] * DK_SCALE
    out_ref[2] = dv[...]


def rows_of(total, at, count):
    return total[at : at + count].reshape(count * 16, 128)


def remote_backward(nseg, first, mask_ref, q_ref, g_ref, lse_ref, slope_ref, *refs):
    head = pl.program_id(0)
    levels = range(first, BRANCHES)
    n = len(levels)
    packs = {level: refs[3 * i : 3 * i + 3] for i, level in enumerate(levels)}
    dqr_ref = refs[3 * n]
    outs = {level: refs[3 * n + 1 + i] for i, level in enumerate(levels)}
    qa, ga, ka, va, dk, dv = refs[4 * n + 1 :]
    length = nseg * SEG
    qa[...] = join(q_ref[0], query_rows(head, length, neg_total(lse_ref[0], local_keep(mask_ref[0], length))))
    ga[...] = grad_rows(g_ref[...], slope_ref[0])
    full = SEG >> first
    for group in remote_plan(first):
        for i, level in enumerate(group):
            key, value = remote_keys(head, level, packs[level])
            ka[:, i * 512 : (i + 1) * 512] = key
            va[:, i * 512 : (i + 1) * 512] = value
        size = SEG >> group[0]
        mine = [pl.ds(kept_start(head, group[0], seg), size) for seg in range(nseg)]
        query = jnp.concatenate([qa[:, m] for m in mine], axis=1)
        grad = jnp.concatenate([ga[:, m] for m in mine], axis=1)
        tile = min(BACK_KEYS, 512)
        tiles = [(i, slice(tile * i, tile * (i + 1))) for i in range(512 // tile * len(group))]
        sides = sides_of(query, grad)
        attend_back(pairs(sides, ka, va, tiles), dk, dv, set())
        dq = joined(sides) * DQ_SCALE
        for seg in range(nseg):
            piece = dq[:, seg * size : (seg + 1) * size]
            if group[0] == first:
                dqr_ref[:, seg * full : (seg + 1) * full] = piece
            else:
                inner = (reversed_bits(head) >> (4 - group[0])) & ((1 << (group[0] - first)) - 1)
                lanes = pl.ds(pl.multiple_of(seg * full + inner * size, 128), size)
                dqr_ref[:, lanes] += piece
        for i, level in enumerate(group):
            pieces, _, _, size = outs[level].shape
            for piece in range(pieces):
                lanes = slice(i * 512 + piece * size, i * 512 + (piece + 1) * size)
                outs[level][piece, 0] = (dk[:, lanes] * DK_SCALE).astype(BF16)
                outs[level][piece, 1] = dv[:, lanes].astype(BF16)


def row_block(length):
    return pl.BlockSpec((1, 1, length), lambda h: (h, 0, 0))


def head_block(length):
    return pl.BlockSpec((HEAD_DIM, length), lambda h: (h, 0))


def part_block(part, length):
    return pl.BlockSpec((1, HEAD_DIM, length), lambda h: (part, h, 0))


MASK_BLOCK = pl.BlockSpec(memory_space=pltpu.SMEM)


def pack_args(keys, packs):
    args, specs = [], []
    for i, pack in enumerate(packs):
        group, _, length = pack.shape
        ahead = 0 if i == 0 else HEADS
        args += [keys if i == 0 else pack, pack, pack]
        specs += [
            pl.BlockSpec((group, HEAD_DIM, length), lambda h: (0, h, 0)),
            pl.BlockSpec((group, HEAD_DIM, length), lambda h, ahead=ahead: (0, ahead + h, 0)),
            pl.BlockSpec((group, 16, length), lambda h, ahead=ahead: (0, (ahead + HEADS) * 3, 0)),
        ]
    return args, specs


ANY_BLOCK = pl.BlockSpec(memory_space=pl.ANY)


def sems(count):
    return pltpu.SemaphoreType.DMA((count,))


def talking(collective_id, mebibytes=56):
    return pltpu.CompilerParams(
        vmem_limit_bytes=mebibytes * 1024 * 1024, collective_id=collective_id, has_side_effects=True
    )


PARAMS = pltpu.CompilerParams(vmem_limit_bytes=VMEM_LIMIT)


def shape(dims, dtype):
    return jax.ShapeDtypeStruct(dims, dtype)


def cost(seconds):
    return pl.CostEstimate(flops=int(seconds * 1.1e15), transcendentals=0, bytes_accessed=0)


def call_local_forward(nseg, first, qkv, mask, packs, shards):
    length = nseg * SEG
    n = len(packs)
    groups = [(SEG << (level - 1)) // length for level in range(first, BRANCHES)]
    hops = sum(group.bit_length() for group in groups)
    pieces = [shards[0].shape, shards[1].shape, (DOWN_FIRST, D)]
    o_part, l_part, m_part, *rest = pl.pallas_call(
        functools.partial(local_forward, nseg, first),
        grid=(HEADS,),
        in_specs=[MASK_BLOCK, part_block(0, length), part_block(1, length), part_block(2, length)]
        + [ANY_BLOCK] * (n + 3),
        out_specs=[head_block(length), row_block(length), row_block(length)] + [ANY_BLOCK] * (n + 3),
        out_shape=[shape((D, length), F32), shape((HEADS, 1, length), F32), shape((HEADS, 1, length), F32)]
        + [
            shape((group, D + 16 if i == 0 else pack.shape[0], pack.shape[1]), BF16)
            for i, (group, pack) in enumerate(zip(groups, packs))
        ]
        + [shape((4,) + piece, BF16) for piece in pieces],
        scratch_shapes=local_forward_scratch(nseg)
        + [
            sems(hops),
            sems(hops),
        ]
        + [pltpu.VMEM(piece, BF16) for piece in pieces]
        + [
            sems(9),
            sems(9),
            sems(3),
        ],
        compiler_params=talking(1),
        cost_estimate=cost(nseg * 37e-6),
        name="local_forward",
    )(mask, qkv, qkv, qkv, *packs, *shards)
    whole_out, whole_up, down_first = rest[n:]
    return (
        o_part, l_part, m_part, rest[:n], whole_out.reshape(D, D), whole_up.reshape(D, 4 * D), down_first
    )


def call_remote_forward(nseg, first, qkv, mask, o_part, l_part, m_part, keys, packs, shard):
    length = nseg * SEG
    args, specs = pack_args(keys, packs)
    return pl.pallas_call(
        functools.partial(remote_forward, nseg, first),
        grid=(HEADS,),
        in_specs=[MASK_BLOCK, part_block(0, length), head_block(length), row_block(length), row_block(length)]
        + specs
        + [ANY_BLOCK],
        out_specs=[head_block(length), row_block(length), ANY_BLOCK],
        out_shape=[
            shape((D, length), BF16),
            shape((HEADS, 1, length), F32),
            shape((4, D - DOWN_FIRST, D), BF16),
        ],
        scratch_shapes=[
            pltpu.VMEM((HEAD_DIM, length), F32),
            pltpu.VMEM((1, 1, length), F32),
            pltpu.VMEM((1, 1, length), F32),
            pltpu.VMEM((64, length), BF16),
            pltpu.VMEM((D - DOWN_FIRST, D), BF16),
            sems(3),
            sems(3),
            sems(1),
        ],
        compiler_params=talking(5),
        cost_estimate=cost(nseg * 24e-6),
        name="remote_forward",
    )(mask, qkv, o_part, l_part, m_part, *args, shard)


def call_remote_backward(nseg, first, qkv, grad, lse, slope, mask, keys, packs):
    length = nseg * SEG
    args, specs = pack_args(keys, packs)
    kept = nseg * (SEG >> first)
    return pl.pallas_call(
        functools.partial(remote_backward, nseg, first),
        grid=(HEADS,),
        in_specs=[MASK_BLOCK, part_block(0, length), head_block(length), row_block(length), row_block(length)]
        + specs,
        out_specs=[head_block(kept)]
        + [
            pl.BlockSpec((pack.shape[0], 2, HEAD_DIM, pack.shape[2]), lambda h: (0, 0, h, 0))
            for pack in packs
        ],
        out_shape=[shape((D, kept), F32)]
        + [shape((pack.shape[0], 2, D, pack.shape[2]), BF16) for pack in packs],
        scratch_shapes=[
            pltpu.VMEM((64, length), BF16),
            pltpu.VMEM((64, length), BF16),
            pltpu.VMEM((64, 1024), BF16),
            pltpu.VMEM((64, 1024), BF16),
            pltpu.VMEM((HEAD_DIM, 1024), F32),
            pltpu.VMEM((HEAD_DIM, 1024), F32),
        ],
        compiler_params=PARAMS,
        cost_estimate=cost(nseg * 20e-6),
        name="remote_backward",
    )(mask, qkv, grad, lse, slope, *args)


CHUNKS = 3
FEED_BLOCKS = (4 * D + D + 4 * D) * D // (4 * 16 * 128)
IN_BLOCKS = 3 * D * D // (4 * 16 * 128)


def padded(blocks):
    unit = CHUNKS * lax.axis_size("seq")
    return (blocks + unit - 1) // unit * unit


def reduce_copies():
    return CHUNKS * (3 + seq_bits())


def call_local_backward(nseg, first, qkv, grad, lse, slope, mask, dq_remote, sent, feed_grads):
    length = nseg * SEG
    n = len(sent)
    groups = [part.shape[0] for part in sent]
    hops = sum(group.bit_length() for group in groups)
    blocks = feed_grads.shape[1]
    piece = (CHUNKS, blocks // CHUNKS >> seq_bits(), 16, 128)
    bufs = [pltpu.VMEM((g // 2,) + part.shape[1:], BF16) for g, part in zip(groups, sent) if g > 1]
    recvs = [pltpu.VMEM((g - 1,) + part.shape[1:], BF16) for g, part in zip(groups, sent) if g > 1]
    local, *rest = pl.pallas_call(
        functools.partial(local_backward, nseg, first),
        grid=(HEADS,),
        in_specs=[MASK_BLOCK, part_block(0, length), part_block(1, length), part_block(2, length), head_block(length),
                  row_block(length), row_block(length), head_block(dq_remote.shape[1])]
        + [ANY_BLOCK] * (n + 1),
        out_specs=[pl.BlockSpec((3, HEAD_DIM, length), lambda h: (0, h, 0))]
        + [ANY_BLOCK] * n
        + [const_block(piece)],
        out_shape=[shape((3, D, length), F32)]
        + [shape(part.shape[1:], BF16) for part in sent]
        + [shape(piece, BF16)],
        scratch_shapes=local_backward_scratch(nseg)
        + bufs
        + recvs
        + [
            pltpu.VMEM((2, blocks, 16, 128), BF16),
            pltpu.VMEM((2, blocks, 16, 128), BF16),
            pltpu.VMEM((blocks, 16, 128), BF16),
            pltpu.VMEM((blocks, 16, 128), BF16),
            sems(hops),
            sems(hops),
            sems(n),
            sems(reduce_copies()),
            sems(reduce_copies()),
            sems(2 * CHUNKS),
        ],
        compiler_params=talking(2),
        cost_estimate=cost(nseg * 72e-6),
        name="local_backward",
    )(mask, qkv, qkv, qkv, grad, lse, slope, dq_remote, *sent, feed_grads)
    return local, rest[:n], rest[n]


HALF = D // 2


def const_block(dims):
    return pl.BlockSpec(dims, lambda i: (0,) * len(dims), pipeline_mode=pl.Buffered(1))


def rev4(value):
    return int(reversed_bits(value))


TILES = D // 128


def put_rows(tiled, start, array):
    for tile in range(TILES):
        tiled[tile, start : start + array.shape[0], :] = array[:, tile * 128 : (tile + 1) * 128]


def get_rows(tiled, start, size):
    return jnp.concatenate([tiled[tile, start : start + size, :] for tile in range(TILES)], axis=1)


def get_residue(tiled, start):
    return jnp.concatenate(
        [tiled[tile, pl.ds(start, RUN, stride=RES), :] for tile in range(TILES)], axis=1
    )


def put_residue(tiled, start, array):
    for tile in range(TILES):
        tiled[tile, pl.ds(start, RUN, stride=RES), :] = array[:, tile * 128 : (tile + 1) * 128]


COLUMN_CHUNKS = 3


def project_kernel(nseg, first, mask_ref, tok_ref, *refs):
    n = BRANCHES - first
    vectors, w_ref = refs[:4], refs[4]
    qkv_ref, xp_ref, inner_ref, weight_ref, gains_ref, keys_ref = refs[5:11]
    packs = refs[11 : 11 + n]
    xs, weight, gains, key_pack, vec_send, vec_recv, w_send, w_recv, w_load, w_store = refs[11 + n : 21 + n]
    key_send, key_recv = refs[21 + n :]
    step = pl.program_id(0)
    last = pl.num_programs(0) - 1
    me = lax.axis_index("fsdp")
    sibling = me + 1 - 2 * lax.rem(me, 2)
    across = lax.rem(me + 2, 4)
    sends = Sends(w_send, w_recv)

    def send(source, target, key, other):
        index = sends.made.setdefault(key, len(sends.made))
        return pltpu.make_async_remote_copy(
            src_ref=source, dst_ref=target, send_sem=w_send.at[index], recv_sem=w_recv.at[index],
            device_id={"fsdp": other}, device_id_type=pl.DeviceIdType.MESH,
        )

    def chunk_copies(chunk):
        cols = pl.ds(chunk * D, D)
        mine = w_ref.at[:, cols]
        load = pltpu.make_async_copy(mine, weight.at[me, :, cols], w_load.at[chunk])
        core = send(mine, weight.at[me, :, cols], ("core", chunk), sibling)
        x = send(mine, weight.at[me, :, cols], ("x", chunk), across)
        handed = weight.at[across, :, cols]
        return load, core, x, send(handed, handed, ("hand", chunk), sibling)

    def vec_copies():
        return [
            pltpu.make_async_remote_copy(
                src_ref=gains.at[me], dst_ref=gains.at[me], send_sem=vec_send.at[i], recv_sem=vec_recv.at[i],
                device_id={"fsdp": other}, device_id_type=pl.DeviceIdType.MESH,
            )
            for i, other in enumerate((sibling, across, 3 - me))
        ]

    store = pltpu.make_async_copy(weight, weight_ref, w_store.at[0])
    key_sends = Sends(key_send, key_recv)

    def ahead(half):
        rows = pl.ds(half * HALF, HALF)
        return key_sends.copy(half, key_pack.at[rows], keys_ref.at[rows], "seq", 1)


    @pl.when(step == 0)
    def _():
        barrier = pltpu.get_barrier_semaphore()
        for other in (sibling, across, 3 - me):
            pl.semaphore_signal(
                barrier, inc=1, device_id={"fsdp": other}, device_id_type=pl.DeviceIdType.MESH
            )
        pl.semaphore_signal(
            barrier, inc=1, device_id=partner("seq", 1), device_id_type=pl.DeviceIdType.MESH
        )
        for i, vector in enumerate(vectors):
            gains[me, i : i + 1, :192] = vector[...].astype(F32).reshape(1, 192)
        pl.semaphore_wait(barrier, 4)
        for copy in vec_copies():
            copy.start()
        for turn in range(COLUMN_CHUNKS):
            for copy in chunk_copies((turn + 1) % COLUMN_CHUNKS)[: 3 if turn == 0 else 2]:
                copy.start()
        for copy in vec_copies():
            copy.wait_recv()
        full = [
            jnp.concatenate([gains[owner, i : i + 1, :192] for owner in range(4)], axis=1) for i in range(4)
        ]
        gains_ref[...] = jnp.concatenate(full + [jnp.zeros((4, D), F32)], axis=0)
        for seg in range(nseg):
            put_rows(xs, 0, tok_ref[seg * SEG : (seg + 1) * SEG, :].astype(F32))
            for pair in range(RES // 2):
                rows = jnp.concatenate([get_residue(xs, rev4(2 * pair + i)) for i in range(2)], axis=0)
                normed = normalize(rows, full[0], full[1])[0].astype(BF16)
                at = slice(seg * SEG + pair * 2 * RUN, seg * SEG + (pair + 1) * 2 * RUN)
                xp_ref[at, :] = rows.astype(BF16)
                inner_ref[:, at] = normed.T
        for pack, level in zip(packs, range(first, BRANCHES)):
            pack[2 * D :, :] = packed_keep(mask_ref[0], level, nseg)

    for turn in range(COLUMN_CHUNKS):

        @pl.when(step == 2 * turn)
        def _():
            load, core, x, hand = chunk_copies((turn + 1) % COLUMN_CHUNKS)
            x.wait_recv()
            hand.start()
            if turn + 1 < COLUMN_CHUNKS:
                chunk_copies((turn + 2) % COLUMN_CHUNKS)[2].start()
            load.wait()
            core.wait_recv()
            hand.wait_recv()

    @pl.when(step == 4)
    def _():
        store.start()

    where = lax.rem(step + 2, 6)
    cols = pl.ds(pl.multiple_of(where * HALF, HALF), HALF)
    block = jnp.concatenate([weight[owner, :, cols] for owner in range(4)], axis=0)
    scale = jnp.where(step >= 4, QUERY_SCALE, 1.0)
    for start in range(0, nseg * SEG, 512):
        lanes = slice(start, start + 512)
        qkv_ref[0, :, lanes] = (dotg(block, inner_ref[:, lanes], 0, 0) * scale).astype(BF16)

    @pl.when(step < 4)
    def _():
        upper = lax.rem(step, 2) == 1
        for pack, level in zip(packs, range(first, BRANCHES)):
            size = SEG >> level
            for head in range(HEADS // 2):
                rows = slice(head * HEAD_DIM, (head + 1) * HEAD_DIM)
                pieces = []
                for seg in range(nseg):
                    start = seg * SEG + (rev4(head) >> (4 - level)) * size
                    if level < 4:
                        pieces.append(qkv_ref[0, rows, start : start + size])
                    else:
                        both = qkv_ref[0, rows, start : start + 2 * size]
                        pieces.append(jnp.where(upper, both[:, size:], both[:, :size]))
                into = pl.ds(pl.multiple_of(step * HALF + head * HEAD_DIM, 16), HEAD_DIM)
                pack[into, :] = jnp.concatenate(pieces, axis=1) if nseg > 1 else pieces[0]

    for half in range(2):

        @pl.when(step == half)
        def _():
            rows = slice(half * HALF, (half + 1) * HALF)
            key_pack[rows, :] = packs[0][rows, :]
            ahead(half).start()

    @pl.when(step == last)
    def _():
        for copy in vec_copies():
            copy.wait_send()
        for chunk in range(COLUMN_CHUNKS):
            for copy in chunk_copies(chunk)[1:]:
                copy.wait_send()
        store.wait()
        for half in range(2):
            ahead(half).wait()


def call_project(nseg, first, mask, tokens, vectors, weight):
    length = nseg * SEG
    kept = [nseg * (SEG >> level) for level in range(first, BRANCHES)]
    return pl.pallas_call(
        functools.partial(project_kernel, nseg, first),
        grid=(6,),
        in_specs=[MASK_BLOCK, const_block((length, D))] + [const_block((192,))] * 4 + [ANY_BLOCK],
        out_specs=[
            pl.BlockSpec((1, HALF, length), lambda i: ((i + 2) % 6 // 2, i % 2, 0)),
            const_block((length, D)),
            const_block((D, length)),
            ANY_BLOCK,
            const_block((8, D)),
            ANY_BLOCK,
        ]
        + [const_block((2 * D + 16, size)) for size in kept],
        out_shape=[
            shape((3, D, length), BF16),
            shape((length, D), BF16),
            shape((D, length), BF16),
            shape((4, 192, 3 * D), BF16),
            shape((8, D), F32),
            shape((D, kept[0]), BF16),
        ]
        + [shape((2 * D + 16, size), BF16) for size in kept],
        scratch_shapes=[
            pltpu.VMEM((TILES, SEG, 128), F32),
            pltpu.VMEM((4, 192, 3 * D), BF16),
            pltpu.VMEM((4, 8, 256), F32),
            pltpu.VMEM((D, kept[0]), BF16),
            sems(3),
            sems(3),
            sems(3 * COLUMN_CHUNKS),
            sems(3 * COLUMN_CHUNKS),
            sems(COLUMN_CHUNKS),
            sems(1),
            sems(2),
            sems(2),
        ],
        compiler_params=talking(4),
        cost_estimate=cost(nseg * 10e-6),
        name="project",
    )(mask, tokens, *vectors, weight)


ROWS = 256


def blocks_of(ref, rows, col):
    part = ref[rows, col * 128 : (col + 1) * 128].astype(BF16)
    return part.reshape(part.shape[0] // 16, 16, 128)


def feed_kernel(
    nseg, mask_ref, att_ref, x_ref, cot_ref, wout_ref, up_ref, down_a, down_b, gains_ref,
    mixed_ref, gmid_ref, gm_ref, along_ref, vec_ref, grads_ref,
    cs, out_acc, up_acc, down_acc, stage, sems,
):
    step = pl.program_id(0)
    quarter = lax.rem(step, 4)
    low = (quarter >> 1) | ((quarter & 1) << 1)

    @pl.when(step == 0)
    def _():
        out_acc[...] = jnp.zeros_like(out_acc)
        up_acc[...] = jnp.zeros_like(up_acc)
        down_acc[...] = jnp.zeros_like(down_acc)
        vec_ref[...] = jnp.zeros_like(vec_ref)

    @pl.when(quarter == 0)
    def _():
        put_rows(cs, 0, cot_ref[...].astype(F32))

    grad = jnp.concatenate([get_residue(cs, rev4(i) + low) for i in range(4)], axis=0)
    grad_b = grad.astype(BF16)
    att = att_ref[...]
    middle = x_ref[...].astype(F32) + dotg(att, wout_ref[...], 0, 0)
    gain = gains_ref[2:3, :]
    normed, unit, inverse = normalize(middle, gain, gains_ref[3:4, :])
    hidden = normed.astype(BF16)
    hidden_t = hidden.T
    final = middle
    grad_hidden = jnp.zeros((ROWS, D), F32)
    for start in range(0, 4 * D, D):
        cols = slice(start, start + D)
        upper = dotg(hidden, up_ref[:, cols], 1, 0)
        down = jnp.concatenate([down_a[start // D], down_b[start // D]], axis=0)
        grad_active = dotg(grad_b, down, 1, 1)
        half = 0.5 * (1.0 + lax.erf(upper * ROOT_HALF))
        slope = half + upper * jnp.exp(-0.5 * upper * upper) * INV_ROOT_TWO_PI
        active = (upper * half).astype(BF16)
        grad_upper = (grad_active * slope).astype(BF16)
        final = final + dotg(active, down, 1, 0)
        grad_hidden = grad_hidden + dotg(grad_upper, up_ref[:, cols], 1, 1)
        up_acc[:, cols] += dotg(hidden_t, grad_upper, 1, 0)
        down_acc[cols, :] += dotg(active, grad_b, 0, 0)
    for i in range(4):
        put_residue(cs, rev4(i) + low, final[i * RUN : (i + 1) * RUN])

    @pl.when(quarter == 3)
    def _():
        mixed_ref[...] = get_rows(cs, 0, SEG).astype(BF16)

    back, gain_back, shift_back = normalize_back(grad_hidden, unit, inverse, gain)
    vec_ref[0:1, :] += gain_back[None, :]
    vec_ref[1:2, :] += shift_back[None, :]
    grad_middle = grad + back
    gmid_ref[...] = grad_middle
    branch = grad_middle.astype(BF16)
    out_acc[...] += dotg(att, branch, 1, 0)
    lane = lax.broadcasted_iota(jnp.int32, (1, ROWS), 1)
    position = step // 4 * SEG + lax.rem(lane, RUN) * RES + residue_of(lane // RUN) + low
    keep = position < mask_ref[0]
    merged = jnp.where(keep, dotg(wout_ref[...], branch, 1, 1), 0.0).astype(BF16)
    gm_ref[...] = merged
    product = merged.astype(F32) * att.astype(F32)
    for head in range(HEADS):
        rows = slice(head * HEAD_DIM, (head + 1) * HEAD_DIM)
        along_ref[head] = jnp.sum(product[rows], axis=0, keepdims=True)

    @pl.when(step == pl.num_programs(0) - 1)
    def _():
        copies = []
        for owner in range(4):
            for piece in range(3):
                count = owner * 3 + piece
                slot = count % 2
                if count >= 2:
                    copies[count - 2].wait()
                if piece == 0:
                    rows, offset, size = slice(owner * 192, (owner + 1) * 192), 0, 288
                    for col in range(4 * TILES):
                        stage[slot, col * 12 : (col + 1) * 12] = blocks_of(up_acc, rows, col)
                elif piece == 1:
                    rows, offset, size = slice(owner * 192, (owner + 1) * 192), 288, 72
                    for col in range(TILES):
                        stage[slot, col * 12 : (col + 1) * 12] = blocks_of(out_acc, rows, col)
                else:
                    rows, offset, size = slice(owner * D, (owner + 1) * D), 360, 288
                    for col in range(TILES):
                        stage[slot, col * 48 : (col + 1) * 48] = blocks_of(down_acc, rows, col)
                copy = pltpu.make_async_copy(
                    stage.at[slot, pl.ds(0, size)],
                    grads_ref.at[owner, pl.ds(offset, size)],
                    sems.at[slot],
                )
                copy.start()
                copies.append(copy)
        copies[-2].wait()
        copies[-1].wait()


def call_feed(nseg, mask, att, x, cot, wout, up, down_a, down_b, gains):
    length = nseg * SEG
    return pl.pallas_call(
        functools.partial(feed_kernel, nseg),
        grid=(length // ROWS,),
        in_specs=[
            MASK_BLOCK,
            pl.BlockSpec((D, ROWS), lambda i: (0, i)),
            pl.BlockSpec((ROWS, D), lambda i: (i, 0)),
            pl.BlockSpec((SEG, D), lambda i: (i // 4, 0)),
            const_block((D, D)),
            const_block((D, 4 * D)),
            const_block((4, DOWN_FIRST, D)),
            const_block((4, D - DOWN_FIRST, D)),
            const_block((8, D)),
        ],
        out_specs=[
            pl.BlockSpec((SEG, D), lambda i: (i // 4, 0)),
            pl.BlockSpec((ROWS, D), lambda i: (i, 0)),
            pl.BlockSpec((D, ROWS), lambda i: (0, i)),
            pl.BlockSpec((HEADS, 1, ROWS), lambda i: (0, 0, i)),
            pl.BlockSpec((2, D), lambda i: (0, 0)),
            pl.BlockSpec(memory_space=pl.ANY),
        ],
        out_shape=[
            shape((length, D), BF16),
            shape((length, D), F32),
            shape((D, length), BF16),
            shape((HEADS, 1, length), F32),
            shape((2, D), F32),
            shape((4, padded(FEED_BLOCKS), 16, 128), BF16),
        ],
        scratch_shapes=[
            pltpu.VMEM((TILES, SEG, 128), F32),
            pltpu.VMEM((D, D), F32),
            pltpu.VMEM((D, 4 * D), F32),
            pltpu.VMEM((4 * D, D), F32),
            pltpu.VMEM((2, 288, 16, 128), BF16),
            pltpu.SemaphoreType.DMA((2,)),
        ],
        compiler_params=pltpu.CompilerParams(vmem_limit_bytes=62 * 1024 * 1024),
        cost_estimate=cost(nseg * 45e-6),
        name="feed",
    )(mask, att, x, cot, wout, up, down_a, down_b, gains)


STEPS = 6
INNER_TABLE = (
    (1, "start", 0, 0), (1, "feed", 2, 0), (1, "feed", 1, 0), (2, "feed", 0, 0),
    (2, "reduce", 0, 0), (3, "start", 1, 0), (4, "feed", 2, 1), (4, "feed", 1, 1),
    (4, "reduce", 1, 0), (4, "reduce", 0, 1), (4, "feed", 0, 1), (5, "start", 2, 0),
    (8, "reduce", 1, 1), (8, "reduce", 2, 0), (8, "feed", 2, 2), (8, "feed", 1, 2),
    (9, "reduce", 0, 2), (12, "reduce", 0, 3), (13, "vec_start", 0, 0), (13, "reduce", 2, 1),
    (14, "feed", 0, 2), (14, "reduce", 0, 4), (14, "vec", 0, 0), (14, "reduce", 1, 2),
    (14, "vec", 0, 1), (14, "reduce", 2, 2), (14, "vec", 0, 2), (14, "spread", 0, 0),
    (14, "reduce", 1, 3), (14, "vec", 0, 3), (14, "reduce", 2, 3), (14, "spread", 0, 1),
    (14, "reduce", 1, 4), (14, "vec", 0, 4), (14, "reduce", 2, 4), (14, "spread", 0, 2),
    (14, "spread", 1, 0), (14, "spread", 2, 0), (14, "spread", 1, 1), (14, "spread", 2, 1),
    (14, "spread", 1, 2), (14, "spread", 2, 2),
)


def inner_back_kernel(
    nseg, first, local_ref, inner_ref, w_ref, x_ref, gmid_ref, gain_ref, feed_vec_ref, piece_ref, *refs
):
    n = BRANCHES - first
    packs, (weight_ref, back_ref, vec_ref, up_ref, proj_ref, down_ref) = refs[:n], refs[n : n + 6]
    acc, mixed, order, terms, recv_core, recv_x, recv_seq, total, feed_total, vecs, vec_recv = refs[n + 6 : n + 17]
    red_send, red_recv, in_send, in_recv, feed_send, feed_recv, vec_send, vec_recv_sems = refs[n + 17 :]
    step = pl.program_id(0)
    last = pl.num_programs(0) - 1
    length = nseg * SEG
    turns = length // ROWS
    end = STEPS + turns
    blocks = terms.shape[1] // CHUNKS
    core = lax.rem(lax.axis_index("fsdp"), 2)
    spread = Spread(inner_orders(), blocks, total, Sends(in_send, in_recv))
    reduce = Reduce(
        inner_orders(), blocks, terms, terms, lambda xo: 2 * xo + core, recv_core, recv_x, recv_seq, Sends(red_send, red_recv),
        spread.begin,
    )
    feed_spread = Spread(feed_orders(), feed_total.shape[0] // CHUNKS, feed_total, Sends(feed_send, feed_recv))
    vec_sends = Sends(vec_send, vec_recv_sems)
    peers = all_peers()

    def vec_copy(i):
        return vec_sends.copy(i, vecs.at[i], vec_recv.at[i], *peers[i])

    def vec_event(i):
        vec_copy(i).wait_recv()
        vecs[i + 1] = vecs[i] + vec_recv[i]
        if i + 1 < len(peers):
            vec_copy(i + 1).start()

    def vec_start():
        vec_copy(0).start()

    @pl.when(step == 0)
    def _():
        meet(peers)
        vecs[0] = jnp.concatenate([jnp.zeros((2, D), F32), feed_vec_ref[...], jnp.zeros((4, D), F32)], axis=0)
        for chunk in reversed(range(CHUNKS)):
            feed_spread.begin(chunk, piece_ref.at[chunk], 0)

    @pl.when((step >= 2) & (step < STEPS))
    def _():
        upper = lax.rem(step, 2) == 1
        for pack, level in zip(packs, range(first, BRANCHES)):
            size = SEG >> level
            for head in range(HEADS // 2):
                rows = slice(head * HEAD_DIM, (head + 1) * HEAD_DIM)
                for seg in range(nseg):
                    start = seg * SEG + (rev4(head) >> (4 - level)) * size
                    piece = pack[0, rows, seg * size : (seg + 1) * size].astype(F32)
                    if level == 4:
                        zero = jnp.zeros_like(piece)
                        piece = jnp.concatenate(
                            [jnp.where(upper, zero, piece), jnp.where(upper, piece, zero)], axis=1
                        )
                    local_ref[0, rows, start : start + piece.shape[1]] += piece

    @pl.when(step < STEPS)
    def _():
        block = local_ref[0].astype(BF16)
        mixed[pl.ds(pl.multiple_of(step * HALF, HALF), HALF), :] = block
        base = lax.div(step, 2) * blocks + lax.rem(step, 2) * 36
        grad_in = dotg(block, inner_ref[...], 1, 1).T.astype(BF16)
        for col in range(3):
            part = grad_in[:, col * 128 : (col + 1) * 128].reshape(4, 12, 16, 128)
            for owner in range(4):
                terms[owner, pl.ds(base + col * 12, 12)] = part[owner]

    def inner_grad(turn):
        lanes = pl.ds(pl.multiple_of(turn * ROWS, ROWS), ROWS)
        acc[lax.rem(turn, 2)] = dotg(w_ref[...], mixed[:, lanes], 1, 0)

    @pl.when(step == STEPS - 1)
    def _():
        inner_grad(step - (STEPS - 1))

    @pl.when((step >= STEPS) & (step < end))
    def _():
        turn = step - STEPS
        inner_grad(lax.rem(turn + 1, turns))
        quarter = lax.rem(turn, 4)
        low = (quarter >> 1) | ((quarter & 1) << 1)
        gain = gain_ref[0:1, :]
        grad = acc[lax.rem(turn, 2)].T
        _, unit, inverse = normalize(x_ref[...].astype(F32), gain, gain)
        back, gain_part, shift_part = normalize_back(grad, unit, inverse, gain)
        vecs[0, 0:1, :] += gain_part[None, :]
        vecs[0, 1:2, :] += shift_part[None, :]
        total_back = gmid_ref[...] + back
        for i in range(4):
            put_residue(order, rev4(i) + low, total_back[i * RUN : (i + 1) * RUN])

        @pl.when(quarter == 3)
        def _():
            back_ref[...] = get_rows(order, 0, SEG)

    calls = {
        "start": lambda chunk, stage: reduce.begin(chunk),
        "reduce": lambda chunk, stage: reduce.event(stage, chunk),
        "spread": lambda chunk, stage: spread.event(stage, chunk),
        "feed": lambda chunk, stage: feed_spread.event(stage, chunk),
        "vec_start": lambda chunk, stage: vec_start(),
        "vec": lambda chunk, stage: vec_event(stage),
    }
    if seq_bits() == 3 and turns == 8:
        table = INNER_TABLE
    else:
        table = []
        for chunk in range(CHUNKS):
            begin = 2 * chunk + 1
            late = begin + 2 * reduce.stages() + 3 * chunk
            table += [(1 + 2 * stage, "feed", chunk, stage) for stage in range(feed_spread.stages())]
            table += [(begin, "start", chunk, 0), (begin + 1, "reduce", chunk, 0)]
            table += [
                (begin + 1 + 3 * chunk + 2 * stage, "reduce", chunk, stage)
                for stage in range(1, reduce.stages())
            ]
            table += [(late + 2 * stage, "spread", chunk, stage) for stage in range(spread.stages())]
        table += [(end - 1, "vec_start", 0, 0)]
        table += [(end + stage, "vec", 0, stage) for stage in range(len(peers))]
        table.sort(key=lambda event: event[0])
    events = [(when, functools.partial(calls[name], chunk, stage)) for when, name, chunk, stage in table]
    run_schedule(step, last, events)

    @pl.when(step == last)
    def _():
        for tile in range(TILES):
            cols = slice(tile * 128, (tile + 1) * 128)
            for col in range(4):
                at = col * 72 + tile * 12
                up_ref[:, col * D + tile * 128 : col * D + (tile + 1) * 128] = rows_of(feed_total, at, 12)
            proj_ref[:, cols] = rows_of(feed_total, 288 + tile * 12, 12)
            down_ref[:, cols] = rows_of(feed_total, 360 + tile * 48, 48)

    @pl.when(step == last)
    def _():
        reduce.finish()
        spread.finish()
        feed_spread.finish()
        for i in range(len(peers)):
            vec_copy(i).wait_send()
        vec_ref[...] = vecs[len(peers)]
        for part in range(STEPS):
            for col in range(3):
                at = part // 2 * blocks + part % 2 * 36 + col * 12
                weight_ref[:, part * HALF + col * 128 : part * HALF + (col + 1) * 128] = rows_of(total, at, 12)


def call_inner_back(nseg, first, local, inner, weight, x, gmid, gain, feed_vec, pieces, packs):
    length = nseg * SEG
    turns = length // ROWS
    blocks = padded(IN_BLOCKS)
    if blocks // CHUNKS < 72:
        raise ValueError("blocks")
    bits = seq_bits()
    peers = 2 + bits
    feed_blocks = CHUNKS * (pieces.shape[1] << bits)

    def at(i):
        return jnp.minimum(i, STEPS - 1)

    def turn(i):
        return jnp.clip(i - STEPS, 0, turns - 1)

    return pl.pallas_call(
        functools.partial(inner_back_kernel, nseg, first),
        grid=(STEPS + turns + 1,),
        in_specs=[
            pl.BlockSpec((1, HALF, length), lambda i: (at(i) // 2, at(i) % 2, 0)),
            const_block((D, length)),
            const_block((D, 3 * D)),
            pl.BlockSpec((ROWS, D), lambda i: (turn(i), 0)),
            pl.BlockSpec((ROWS, D), lambda i: (turn(i), 0)),
            const_block((8, D)),
            const_block((2, D)),
            const_block(pieces.shape),
        ]
        + [
            pl.BlockSpec((1, HALF, pack.shape[2]), lambda i: (jnp.maximum(at(i) // 2 - 1, 0), at(i) % 2, 0))
            for pack in packs
        ],
        out_specs=[
            const_block((192, 3 * D)),
            pl.BlockSpec((SEG, D), lambda i: (turn(i) // 4, 0)),
            const_block((8, D)),
            const_block((192, 4 * D)),
            const_block((192, D)),
            const_block((D, D)),
        ],
        out_shape=[
            shape((192, 3 * D), BF16),
            shape((length, D), F32),
            shape((8, D), F32),
            shape((192, 4 * D), BF16),
            shape((192, D), BF16),
            shape((D, D), BF16),
        ],
        scratch_shapes=[
            pltpu.VMEM((2, D, ROWS), F32),
            pltpu.VMEM((3 * D, length), BF16),
            pltpu.VMEM((TILES, SEG, 128), F32),
            pltpu.VMEM((4, blocks, 16, 128), BF16),
            pltpu.VMEM((2, blocks, 16, 128), BF16),
            pltpu.VMEM((blocks, 16, 128), BF16),
            pltpu.VMEM((blocks, 16, 128), BF16),
            pltpu.VMEM((blocks, 16, 128), BF16),
            pltpu.VMEM((feed_blocks, 16, 128), BF16),
            pltpu.VMEM((peers + 1, 8, D), F32),
            pltpu.VMEM((peers, 8, D), F32),
            sems(reduce_copies()),
            sems(reduce_copies()),
            sems(CHUNKS * bits),
            sems(CHUNKS * bits),
            sems(CHUNKS * bits),
            sems(CHUNKS * bits),
            sems(peers),
            sems(peers),
        ],
        compiler_params=talking(3, 60),
        cost_estimate=cost(nseg * 15e-6),
        name="inner_back",
    )(local, inner, weight, x, gmid, gain, feed_vec, pieces, *packs)


def per_device(
    tokens,
    first_gain,
    first_shift,
    project_in,
    project_out,
    second_gain,
    second_shift,
    up_weight,
    down_weight,
    valid_mask,
    cotangent,
):
    length = tokens.shape[1]
    nseg = length // SEG
    first = nseg.bit_length()

    mask = jnp.sum(valid_mask[0])[None]

    vectors = [first_gain, first_shift, second_gain, second_shift]
    qkv, x, inner, weight_in, gains, keys, *packs = call_project(
        nseg, first, mask, tokens[0], vectors, project_in
    )
    keys = keys[None]
    weight_in = weight_in.reshape(D, 3 * D)
    o_part, l_part, m_part, gathered, weight_out, weight_up, down_first = call_local_forward(
        nseg, first, qkv, mask, packs, (project_out, up_weight, down_weight)
    )
    attended, lse, down_second = call_remote_forward(
        nseg, first, qkv, mask, o_part, l_part, m_part, keys, gathered, down_weight
    )

    mixed, grad_middle, grad_merged, along, feed_vec, feed_grads = call_feed(
        nseg, mask, attended, x, cotangent[0], weight_out, weight_up, down_first, down_second, gains
    )

    dq_remote, *sent = call_remote_backward(nseg, first, qkv, grad_merged, lse, along, mask, keys, gathered)
    local, returned, pieces = call_local_backward(
        nseg, first, qkv, grad_merged, lse, along, mask, dq_remote, sent, feed_grads
    )
    grad_in, tokens_back, vectors, grad_up, grad_out, grad_down = call_inner_back(
        nseg, first, local, inner, weight_in, x, grad_middle, gains, feed_vec, pieces, returned
    )
    quarter = D // lax.axis_size("fsdp")
    vectors = lax.dynamic_slice_in_dim(vectors, lax.axis_index("fsdp") * quarter, quarter, 1)
    return (
        mixed[None],
        tokens_back[None],
        vectors[0],
        vectors[1],
        grad_in.astype(F32),
        grad_out.astype(F32),
        vectors[2],
        vectors[3],
        grad_up.astype(F32),
        grad_down.astype(F32),
    )


def solution(mesh):
    in_specs = (
        P("fsdp", "seq", None),
        P("fsdp"),
        P("fsdp"),
        P("fsdp", None),
        P("fsdp", None),
        P("fsdp"),
        P("fsdp"),
        P("fsdp", None),
        P("fsdp", None),
        P("fsdp", "seq"),
        P("fsdp", "seq", None),
    )
    out_specs = (
        P("fsdp", "seq", None),
        P("fsdp", "seq", None),
        P("fsdp"),
        P("fsdp"),
        P("fsdp", None),
        P("fsdp", None),
        P("fsdp"),
        P("fsdp"),
        P("fsdp", None),
        P("fsdp", None),
    )
    return jax.shard_map(
        per_device, mesh=mesh, in_specs=in_specs, out_specs=out_specs, check_vma=False
    )
```

```python
import functools
import math

import jax
import jax.numpy as jnp
import ml_dtypes
import numpy as np
from jax import lax
from jax.experimental import pallas as pl
from jax.experimental.pallas import tpu as pltpu
from jax.sharding import PartitionSpec as P

HEADS = 16
HEAD_DIM = 48
SEG = 1024
BRANCHES = 5
RES = 16
RUN = SEG // RES
D = HEADS * HEAD_DIM

EPS = 1e-05
NEG = -1e30
ROOT_HALF = 0.7071067811865476
INV_ROOT_TWO_PI = 0.3989422804014327
F32 = jnp.float32
BF16 = jnp.bfloat16
QUERY_SCALE = math.log2(math.e) * HEAD_DIM ** (-0.5)
VMEM_LIMIT = 56 * 1024 * 1024


def dotg(left, right, left_dim, right_dim):
    return lax.dot_general(
        left, right, (((left_dim,), (right_dim,)), ((), ())), preferred_element_type=F32
    )


def normalize(values, gain, shift):
    mean = jnp.mean(values, axis=-1, keepdims=True)
    centred = values - mean
    spread = jnp.mean(centred * centred, axis=-1, keepdims=True)
    inverse = lax.rsqrt(spread + EPS)
    normed = centred * inverse
    return (normed * gain + shift, normed, inverse)


def normalize_back(grad, normed, inverse, gain):
    scaled = grad * gain
    first = jnp.mean(scaled, axis=-1, keepdims=True)
    second = jnp.mean(scaled * normed, axis=-1, keepdims=True)
    return (
        inverse * (scaled - first - normed * second),
        jnp.sum(grad * normed, axis=0),
        jnp.sum(grad, axis=0),
    )


def reversed_bits(head):
    return ((head & 1) << 3) | ((head & 2) << 1) | ((head & 4) >> 1) | ((head & 8) >> 3)


def near_class(head, low_bits, length):
    lane = lax.broadcasted_iota(jnp.int32, (1, length), 1)
    rho = lax.rem(lane // RUN, 1 << low_bits)
    return rho ^ (reversed_bits(head) & ((1 << low_bits) - 1))


def class_rows(near, length):
    row = lax.broadcasted_iota(jnp.int32, (16, length), 0)
    step = lax.rem(row + 3, 4) + 1
    bound = jnp.where((row >= 5) & (row <= 12), lax.shift_right_logical(RES, step), 0)
    return row, near < bound


def query_rows(head, length, neg_lse=None):
    near = near_class(head, 4, length)
    row, inside = class_rows(near, length)
    out = jnp.where(inside, 1.0, 0.0)
    out = jnp.where(row == 0, 1.0, out)
    out = jnp.where(row == 4, jnp.where(near < 1, 0.0, NEG), out)
    if neg_lse is not None:
        high = neg_lse.astype(BF16).astype(F32)
        rest = neg_lse - high
        mid = rest.astype(BF16).astype(F32)
        low = rest - mid
        out = jnp.where(row == 1, high, jnp.where(row == 2, mid, jnp.where(row == 3, low, out)))
    return out.astype(BF16)


def residue_of(rho):
    return reversed_bits(rho)


def local_keep(count, length):
    lane = lax.broadcasted_iota(jnp.int32, (1, length), 1)
    rho = lax.rem(lane // RUN, RES)
    position = lane // SEG * SEG + lax.rem(lane, RUN) * RES + residue_of(rho)
    return position < count


def packed_keep(count, level, nseg):
    size = SEG >> level
    dims = (HEADS, nseg * size)
    head = lax.broadcasted_iota(jnp.int32, dims, 0)
    lane = lax.broadcasted_iota(jnp.int32, dims, 1)
    rho = (reversed_bits(head) >> (4 - level)) * (size // RUN) + lax.rem(lane, size) // RUN
    position = lane // size * SEG + lax.rem(lane, RUN) * RES + residue_of(rho)
    return jnp.where(position < count, 1.0, 0.0).astype(BF16)


def weight_of(level, step):
    return math.log2((step - level + 1) / (step - level)) if step > level else 0.0


def key_rows(head, level, low_bits, length, keep):
    near = near_class(head, low_bits, length)
    row, inside = class_rows(near, length)
    weight = jnp.zeros((16, length), F32)
    for step in range(level + 1, BRANCHES):
        value = weight_of(level, step)
        high = float(np.asarray(value, ml_dtypes.bfloat16))
        weight = jnp.where(row == 4 + step, high, weight)
        weight = jnp.where(row == 8 + step, value - high, weight)
    out = jnp.where(inside, weight, 0.0)
    out = jnp.where((row >= 1) & (row <= 3), 1.0, out)
    out = jnp.where(row == 0, jnp.where(keep, 0.0, NEG), out)
    if level == BRANCHES - 1:
        out = jnp.where(row == 4, 1.0, out)
    return out.astype(BF16)


def value_rows(length):
    row = lax.broadcasted_iota(jnp.int32, (16, length), 0)
    return jnp.where(row < 2, 1.0, 0.0).astype(BF16)


def join(rows, extra):
    return jnp.concatenate([rows, extra], axis=0)


def kept_start(head, level, seg):
    size = SEG >> level
    block = reversed_bits(head) >> (4 - level)
    return pl.multiple_of(seg * SEG + block * size, min(size, 128))


def partner(axis, distance):
    place = lax.axis_index(axis)
    return {axis: place + distance * (1 - 2 * lax.rem(lax.div(place, distance), 2))}


def seq_bits():
    return lax.axis_size("seq").bit_length() - 1


def meet(peers):
    barrier = pltpu.get_barrier_semaphore()
    for axis, distance in peers:
        pl.semaphore_signal(
            barrier, inc=1, device_id=partner(axis, distance), device_id_type=pl.DeviceIdType.MESH
        )
    pl.semaphore_wait(barrier, len(peers))


class Sends:
    def __init__(self, send_sems, recv_sems):
        self.send_sems, self.recv_sems, self.made = send_sems, recv_sems, {}

    def copy(self, key, source, target, axis, distance):
        index = self.made.setdefault(key, len(self.made))
        return pltpu.make_async_remote_copy(
            src_ref=source,
            dst_ref=target,
            send_sem=self.send_sems.at[index],
            recv_sem=self.recv_sems.at[index],
            device_id=partner(axis, distance),
            device_id_type=pl.DeviceIdType.MESH,
        )


class Gather:
    def __init__(self, nseg, first, packs, gathered, sends):
        self.hops, self.distances = [], set()
        for level, pack, into in zip(range(first, BRANCHES), packs, gathered):
            group = (SEG << (level - 1)) // (nseg * SEG)
            source = pack if pack.shape[0] == into.shape[1] else pack.at[pl.ds(D, D + 16)]
            hops = [((level, 0), source, into.at[0], group)]
            step = 1
            while step < group:
                hops.append(((level, step), into.at[pl.ds(0, step)], into.at[pl.ds(step, step)], step))
                step *= 2
            self.hops.append([sends.copy(k, a, b, "seq", d) for k, a, b, d in hops])
            self.distances |= {hop[3] for hop in hops}

    def peers(self):
        return [("seq", distance) for distance in sorted(self.distances)]

    def start(self):
        for hops in reversed(self.hops):
            hops[0].start()

    def pass_on(self, index, turn):
        hops = self.hops[index]
        hops[turn - 1].wait_recv()
        hops[turn].start()

    def finish(self):
        for hops in self.hops:
            for hop in hops:
                hop.wait_send()
            hops[-1].wait_recv()

    def turns(self):
        events = []
        for index, hops in reversed(list(enumerate(self.hops))):
            for turn in range(1, len(hops)):
                when = 6 + 3 * (turn - 1) + 2 * (len(self.hops) - 1 - index)
                events.append((when, functools.partial(self.pass_on, index, turn)))
        return events


class Shards:
    def __init__(self, shards, whole, stages, sends, loads, started=1):
        self.copies, self.started = [], started
        self.staged = [
            pltpu.make_async_copy(shard, stage, loads.at[i])
            for i, (shard, stage) in enumerate(zip(shards, stages))
        ]
        me = lax.axis_index("fsdp")
        other = lax.rem(me + 2, 4)
        for i, (shard, into) in enumerate(zip(stages, whole)):
            self.copies.append(
                (
                    pltpu.make_async_copy(shard, into.at[me], loads.at[i]),
                    sends.copy((i, "core"), shard, into.at[me], "fsdp", 1),
                    sends.copy((i, "x"), shard, into.at[me], "fsdp", 2),
                    sends.copy((i, "hand"), into.at[other], into.at[other], "fsdp", 1),
                )
            )

    def start(self):
        for staged in self.staged:
            staged.start()
        for i, (load, core, x, _) in enumerate(self.copies):
            self.staged[i].wait()
            load.start()
            core.start()
            if i < self.started:
                x.start()

    def hand(self, i):
        _, _, x, hand = self.copies[i]
        x.wait_recv()
        hand.start()
        if self.started <= i + 1 < len(self.copies):
            self.copies[i + 1][2].start()

    def finish(self):
        for load, core, x, hand in self.copies:
            load.wait()
            core.wait()
            x.wait_send()
            hand.wait()


class Return:
    def __init__(self, nseg, first, sent, returned, bufs, recvs, local_sems, sends):
        self.plans = []
        for i, level in enumerate(range(first, BRANCHES)):
            group = (SEG << (level - 1)) // (nseg * SEG)
            plan = []
            if group == 1:
                plan.append((None, sends.copy((level, 0), sent[i].at[0], returned[i], "seq", group)))
                self.plans.append((plan, None))
                continue
            buf, recv = bufs.pop(0), recvs.pop(0)
            step = group // 2
            load = pltpu.make_async_copy(sent[i].at[pl.ds(0, step)], buf, local_sems.at[i])
            source, at, add = sent[i].at[pl.ds(step, step)], 0, None
            while step >= 1:
                into = recv.at[pl.ds(at, step)]
                plan.append((add, sends.copy((level, step), source, into, "seq", step)))
                add = (buf, recv, at, step)
                at += step
                step //= 2
                if step:
                    source = buf.at[pl.ds(step, step)]
            plan.append((add, sends.copy((level, 0), buf.at[0], returned[i], "seq", group)))
            self.plans.append((plan, load))

    def start(self, direct):
        for plan, load in reversed(self.plans):
            if direct == (load is None):
                if load is not None:
                    load.start()
                plan[0][1].start()

    def turn(self, number):
        for plan, load in reversed(self.plans):
            if number < len(plan):
                plan[number - 1][1].wait_recv()
                if number == 1 and load is not None:
                    load.wait()
                buf, recv, at, step = plan[number][0]
                for i in range(step):
                    buf[i] = (buf[i].astype(F32) + recv[at + i].astype(F32)).astype(BF16)
                plan[number][1].start()

    def finish(self):
        for plan, load in self.plans:
            for _, copy in plan:
                copy.wait_send()
            plan[-1][1].wait_recv()

    def turns(self):
        return max(len(plan) for plan, _ in self.plans)


def add_blocks(into, at, other, start, count):
    unit = max(u for u in range(1, 13) if count % u == 0)

    def body(i, carry):
        rows = pl.ds(at + i * unit, unit)
        part = other[pl.ds(start + i * unit, unit)].astype(F32)
        into[rows] = (into[rows].astype(F32) + part).astype(BF16)
        return carry

    lax.fori_loop(0, count // unit, body, 0)


def copy_blocks(into, at, other, start, count):
    unit = max(u for u in range(1, 13) if count % u == 0)

    def body(i, carry):
        into[pl.ds(at + i * unit, unit)] = other[pl.ds(start + i * unit, unit)]
        return carry

    lax.fori_loop(0, count // unit, body, 0)


def halving(blocks, order):
    seq = lax.axis_index("seq")
    low, given = [0], []
    for j, distance in enumerate(order):
        bit = lax.rem(lax.div(seq, distance), 2)
        half = blocks >> (j + 1)
        given.append(low[j] + (1 - bit) * half)
        low.append(low[j] + bit * half)
    return low, given


def feed_orders():
    plain = [2**j for j in range(seq_bits())]
    return [plain] * (CHUNKS - 1) + [plain[1:] + plain[:1]]


def inner_orders():
    plain = [2**j for j in range(seq_bits())]
    return [plain] * (CHUNKS - 1) + [[plain[1], plain[0]] + plain[2:]]


def all_peers():
    return [("fsdp", 1), ("fsdp", 2)] + [("seq", 2**j) for j in range(seq_bits())]


class Reduce:
    def __init__(
        self, orders, blocks, source, terms, own, recv_core, recv_x, recv_seq, sends, done, loads=None
    ):
        self.blocks, self.source, self.terms, self.own, self.done = blocks, source, terms, own, done
        self.recv_core, self.recv_x, self.recv_seq = recv_core, recv_x, recv_seq
        self.sends, self.loads = sends, loads
        fsdp = lax.axis_index("fsdp")
        self.core, self.x = lax.rem(fsdp, 2), lax.div(fsdp, 2)
        self.bits = seq_bits()
        self.orders = orders
        self.halves = [halving(blocks, order) for order in self.orders]

    def stages(self):
        return 2 + self.bits

    def core_copy(self, chunk, xo):
        rows = pl.ds(chunk * self.blocks, self.blocks)
        owner = 2 * xo + 1 - self.core
        return self.sends.copy(
            ("core", chunk, xo), self.source.at[owner, rows], self.recv_core.at[xo, rows], "fsdp", 1
        )

    def load_copy(self, chunk, xo):
        rows = pl.ds(chunk * self.blocks, self.blocks)
        return pltpu.make_async_copy(
            self.source.at[2 * xo + self.core, rows], self.terms.at[xo, rows], self.loads.at[2 * chunk + xo]
        )

    def x_copy(self, chunk):
        rows = pl.ds(chunk * self.blocks, self.blocks)
        return self.sends.copy(
            ("x", chunk), self.terms.at[self.own(1 - self.x), rows], self.recv_x.at[rows], "fsdp", 2
        )

    def down_copy(self, chunk, j):
        half = self.blocks >> (j + 1)
        base = chunk * self.blocks
        rows = pl.ds(base + self.halves[chunk][1][j], half)
        into = pl.ds(base + self.blocks - (self.blocks >> j), half)
        return self.sends.copy(
            ("down", chunk, j), self.terms.at[self.own(self.x), rows], self.recv_seq.at[into], "seq",
            self.orders[chunk][j],
        )

    def begin(self, chunk):
        for xo in range(2):
            if self.loads is not None:
                self.load_copy(chunk, xo).start()
            self.core_copy(chunk, xo).start()

    def event(self, stage, chunk):
        base = chunk * self.blocks
        low = self.halves[chunk][0]
        mine = self.terms.at[self.own(self.x)]
        if stage == 0:
            for xo in range(2):
                self.core_copy(chunk, xo).wait_recv()
                if self.loads is not None:
                    self.load_copy(chunk, xo).wait()
                add_blocks(self.terms.at[self.own(xo)], base, self.recv_core.at[xo], base, self.blocks)
            self.x_copy(chunk).start()
            return
        j = stage - 2
        if stage == 1:
            self.x_copy(chunk).wait_recv()
            add_blocks(mine, base, self.recv_x, base, self.blocks)
        else:
            self.down_copy(chunk, j).wait_recv()
            half = self.blocks >> (j + 1)
            add_blocks(mine, base + low[j + 1], self.recv_seq, base + self.blocks - (self.blocks >> j), half)
        if j + 1 < self.bits:
            self.down_copy(chunk, j + 1).start()
        else:
            self.done(chunk, mine, base + low[self.bits])

    def finish(self):
        for chunk in range(CHUNKS):
            for xo in range(2):
                self.core_copy(chunk, xo).wait_send()
            self.x_copy(chunk).wait_send()
            for j in range(self.bits):
                self.down_copy(chunk, j).wait_send()


class Spread:
    def __init__(self, orders, blocks, total, sends):
        self.blocks, self.total, self.sends = blocks, total, sends
        self.bits = seq_bits()
        self.orders = orders
        self.lows = [halving(blocks, order)[0] for order in self.orders]

    def stages(self):
        return self.bits

    def copy(self, chunk, j):
        rows = pl.ds(chunk * self.blocks + self.lows[chunk][j + 1], self.blocks >> (j + 1))
        here = self.total.at[rows]
        return self.sends.copy((chunk, j), here, here, "seq", self.orders[chunk][j])

    def begin(self, chunk, ref, start):
        size = self.blocks >> self.bits
        copy_blocks(self.total, chunk * self.blocks + self.lows[chunk][self.bits], ref, start, size)
        self.copy(chunk, self.bits - 1).start()

    def event(self, stage, chunk):
        j = self.bits - 1 - stage
        self.copy(chunk, j).wait_recv()
        if j:
            self.copy(chunk, j - 1).start()

    def finish(self):
        for chunk in range(CHUNKS):
            for j in range(self.bits):
                self.copy(chunk, j).wait_send()


def run_schedule(step, last, events):
    due = {}
    for when, call in events:
        due.setdefault(min(when, last), []).append(call)
    for when in sorted(due):

        @pl.when(step == when)
        def _():
            for call in due[when]:
                call()


FRONT = 3
KEY_TILE = 128


class State:
    def __init__(self, query, acc=None, top=None):
        self.query, self.acc, self.top = query, acc, top


def attend(items):
    items = list(items)
    ready = []
    for turn in range(len(items) + FRONT):
        if turn < len(items):
            state, key, _ = items[turn]
            ready.append(dotg(key, state.query, 1, 0))
        if turn >= FRONT:
            state, _, value = items[turn - FRONT]
            scores, ready[turn - FRONT] = ready[turn - FRONT], None
            top = jnp.max(scores, axis=0, keepdims=True)
            if state.top is not None:
                top = jnp.maximum(top, state.top)
            probs = jnp.exp2(scores - top).astype(BF16)
            part = dotg(value, probs, 1, 0)
            state.acc = part if state.top is None else state.acc * jnp.exp2(state.top - top) + part
            state.top = top


def key_items(state, key_t, value):
    size = key_t.shape[0]
    tile = min(KEY_TILE, size)
    for start in range(0, size, tile):
        yield state, key_t[start : start + tile], value[:, start : start + tile]


def load_state(query, mine, o_ref, l_ref, m_ref):
    acc = [jnp.concatenate([o_ref[:, at], jnp.broadcast_to(l_ref[0, :, at], (16, at.size))]) for at in mine]
    top = [m_ref[0, :, at] for at in mine]
    return State(query, jnp.concatenate(acc, axis=1), jnp.concatenate(top, axis=1))


def store_state(state, mine, o_ref, l_ref, m_ref):
    start = 0
    for at in mine:
        lanes = slice(start, start + at.size)
        o_ref[:, at] = state.acc[:HEAD_DIM, lanes]
        l_ref[0, :, at] = state.acc[HEAD_DIM : HEAD_DIM + 1, lanes]
        m_ref[0, :, at] = state.top[:, lanes]
        start += at.size


DOWN_FIRST = 384


def local_forward(nseg, first, mask_ref, q_ref, k_ref, v_ref, *refs):
    n = BRANCHES - first
    packs, shards, (o_ref, l_ref, m_ref) = refs[:n], refs[n : n + 3], refs[n + 3 : n + 6]
    gathered, whole = refs[n + 6 : 2 * n + 6], refs[2 * n + 6 : 2 * n + 9]
    qa, ka, va, send_sems, recv_sems, *stages, shard_send, shard_recv, shard_load = refs[2 * n + 9 :]
    head = pl.program_id(0)
    gather = Gather(nseg, first, packs, gathered, Sends(send_sems, recv_sems))
    pieces = [shards[0], shards[1], shards[2].at[pl.ds(0, DOWN_FIRST)]]
    fetch = Shards(pieces, whole, stages, Sends(shard_send, shard_recv), shard_load, 2)

    def begin():
        meet(gather.peers() + [("fsdp", 1), ("fsdp", 2)])
        gather.start()
        fetch.start()

    def finish():
        gather.finish()
        fetch.finish()

    hands = [(when, functools.partial(fetch.hand, i)) for i, when in enumerate((11, 11, 15))]
    run_schedule(head, HEADS - 1, [(0, begin)] + sorted(gather.turns() + hands, key=lambda event: event[0]))
    local_forward_core(nseg, mask_ref, q_ref, k_ref, v_ref, o_ref, l_ref, m_ref, qa, ka, va)
    run_schedule(head, HEADS - 1, [(HEADS - 1, finish)])


def local_forward_scratch(nseg):
    length = nseg * SEG
    return [
        pltpu.VMEM((64, length), BF16),
        pltpu.VMEM((nseg, 64, length), BF16),
        pltpu.VMEM((64, length), BF16),
    ]


def local_forward_core(nseg, mask_ref, q_ref, k_ref, v_ref, o_ref, l_ref, m_ref, qa, ka, va):
    head = pl.program_id(0)
    length = nseg * SEG
    keep = local_keep(mask_ref[0], length)
    qa[...] = join(q_ref[0], query_rows(head, length))
    va[...] = join(v_ref[0], value_rows(length))
    ka[0] = join(k_ref[0], key_rows(head, 0, 4, length, keep))
    if nseg == 2:
        ka[1] = join(k_ref[0], key_rows(head, 1, 4, length, keep))
    states, items = [], []
    for seg in range(nseg):
        lanes = slice(seg * SEG, (seg + 1) * SEG)
        states.append(State(qa[:, lanes]))
        items += key_items(states[-1], ka[0, :, lanes].T, va[:, lanes])
    attend(items)
    for seg in range(nseg):
        store_state(states[seg], [pl.ds(seg * SEG, SEG)], o_ref, l_ref, m_ref)
    if nseg == 2:
        kept = [pl.ds(kept_start(head, 1, seg), SEG // 2) for seg in range(2)]
        states = [load_state(qa[:, at], [at], o_ref, l_ref, m_ref) for at in kept]
        items = []
        for seg in range(2):
            items += key_items(states[seg], ka[1, :, kept[1 - seg]].T, va[:, kept[1 - seg]])
        attend(items)
        for seg in range(2):
            store_state(states[seg], [kept[seg]], o_ref, l_ref, m_ref)


def remote_keys(head, level, pack):
    k_ref, v_ref, mask_ref = pack
    pieces = range(k_ref.shape[0])
    key, value, mask = (
        jnp.concatenate([ref[i] for i in pieces], axis=1) for ref in (k_ref, v_ref, mask_ref)
    )
    length = key.shape[1]
    row = lax.broadcasted_iota(jnp.int32, (16, length), 0)
    keep = jnp.sum(jnp.where(row == head, mask.astype(F32), 0.0), axis=0, keepdims=True) > 0.5
    return join(key, key_rows(head, level, 4 - level, length, keep)), join(value, value_rows(length))


def remote_plan(first):
    return [(level,) for level in range(first, 3)] + [(3, 4)]


def remote_forward(nseg, first, mask_ref, q_ref, o_in, l_in, m_in, *refs):
    head = pl.program_id(0)
    levels = range(first, BRANCHES)
    packs = {level: refs[3 * i : 3 * i + 3] for i, level in enumerate(levels)}
    shard_ref, att_ref, lse_ref, whole_ref, o_ref, l_ref, m_ref, qa, stage, *shard_sems = refs[
        3 * len(levels) :
    ]
    shard_send, shard_recv, shard_load = shard_sems
    piece = shard_ref.at[pl.ds(DOWN_FIRST, D - DOWN_FIRST)]
    fetch = Shards([piece], [whole_ref], [stage], Sends(shard_send, shard_recv), shard_load)

    def begin():
        meet([("fsdp", 1), ("fsdp", 2)])
        fetch.start()

    run_schedule(head, HEADS - 1, [(0, begin), (12, functools.partial(fetch.hand, 0))])
    length = nseg * SEG
    qa[...] = join(q_ref[0], query_rows(head, length))
    o_ref[...] = o_in[...]
    l_ref[...] = l_in[...]
    m_ref[...] = m_in[...]
    for group in remote_plan(first):
        pairs = [remote_keys(head, level, packs[level]) for level in group]
        key = jnp.concatenate([pair[0] for pair in pairs], axis=1)
        value = jnp.concatenate([pair[1] for pair in pairs], axis=1)
        mine = [pl.ds(kept_start(head, group[0], seg), SEG >> group[0]) for seg in range(nseg)]
        query = jnp.concatenate([qa[:, at] for at in mine], axis=1)
        state = load_state(query, mine, o_ref, l_ref, m_ref)
        attend(key_items(state, key.T, value))
        store_state(state, mine, o_ref, l_ref, m_ref)
    weight = jnp.where(local_keep(mask_ref[0], length), 1.0, 0.0) / l_ref[0]
    att_ref[...] = (o_ref[...] * weight).astype(BF16)
    lse_ref[0] = m_ref[0] + jnp.log2(l_ref[0])
    run_schedule(head, HEADS - 1, [(HEADS - 1, fetch.finish)])


def grad_rows(grad, slope):
    length = grad.shape[1]
    row = lax.broadcasted_iota(jnp.int32, (16, length), 0)
    high = (-slope).astype(BF16).astype(F32)
    low = -slope - high
    extra = jnp.where(row == 0, high, jnp.where(row == 1, low, 0.0)).astype(BF16)
    return join(grad, extra)


AHEAD = 2
QUERY_TILE = 256
BACK_KEYS = 256


class Side:
    def __init__(self, query, grad):
        self.query, self.grad = query[:HEAD_DIM], grad[:HEAD_DIM]
        self.query_t, self.grad_t = query.T, grad.T
        self.dq = None


def attend_back(items, dk_ref, dv_ref, written):
    items = list(items)
    ready = []
    for turn in range(len(items) + AHEAD):
        if turn < len(items):
            side, key, value, _, _ = items[turn]
            ready.append((dotg(side.query_t, key, 1, 0), dotg(side.grad_t, value, 1, 0)))
        if turn >= AHEAD:
            side, key, _, lanes, name = items[turn - AHEAD]
            scores, slope = ready[turn - AHEAD]
            ready[turn - AHEAD] = None
            probs = jnp.exp2(scores)
            dscore = (probs * slope).astype(BF16)
            dv = dotg(side.grad, probs.astype(BF16), 1, 0)
            dk = dotg(side.query, dscore, 1, 0)
            part = dotg(key[:HEAD_DIM], dscore, 1, 1)
            side.dq = part if side.dq is None else side.dq + part
            if name in written:
                dv_ref[:, lanes] += dv
                dk_ref[:, lanes] += dk
            else:
                written.add(name)
                dv_ref[:, lanes] = dv
                dk_ref[:, lanes] = dk


def sides_of(query, grad):
    tile = min(QUERY_TILE, query.shape[1])
    return [
        Side(query[:, start : start + tile], grad[:, start : start + tile])
        for start in range(0, query.shape[1], tile)
    ]


def pairs(sides, key_ref, value_ref, tiles):
    return [
        (side, key_ref[:, lanes], value_ref[:, lanes], lanes, name) for side in sides for name, lanes in tiles
    ]


def joined(sides):
    return jnp.concatenate([side.dq for side in sides], axis=1) if len(sides) > 1 else sides[0].dq


DQ_SCALE = HEAD_DIM ** (-0.5)
DK_SCALE = math.log(2.0)


def neg_total(lse, keep):
    return jnp.where(keep, -lse, NEG)


def local_backward(nseg, first, mask_ref, q_ref, k_ref, v_ref, g_ref, lse_ref, slope_ref, dqr_ref, *refs):
    n = BRANCHES - first
    sent, feed_ref, out_ref = refs[:n], refs[n], refs[n + 1]
    returned, piece_ref = refs[n + 2 : 2 * n + 2], refs[2 * n + 2]
    qa, ga, ka, va, dk, dv = refs[2 * n + 3 : 2 * n + 9]
    rest = list(refs[2 * n + 9 :])
    back_send, back_recv, back_load, red_send, red_recv, red_load = rest[-6:]
    terms, recv_core, recv_x, recv_seq = rest[-10:-6]
    bufs, recvs = rest[: (len(rest) - 10) // 2], rest[(len(rest) - 10) // 2 : -10]
    head = pl.program_id(0)
    last = HEADS - 1

    back = Return(nseg, first, sent, returned, bufs, recvs, back_load, Sends(back_send, back_recv))
    blocks = terms.shape[1] // CHUNKS
    reduce = Reduce(
        feed_orders(), blocks, feed_ref, terms, lambda xo: xo, recv_core, recv_x, recv_seq, Sends(red_send, red_recv),
        lambda chunk, ref, start: copy_blocks(piece_ref.at[chunk], 0, ref, start, blocks >> seq_bits()),
        red_load,
    )

    def begin():
        meet(all_peers())
        back.start(False)
        for chunk in range(CHUNKS):
            reduce.begin(chunk)

    events = [(3 * turn, functools.partial(back.turn, turn)) for turn in range(1, back.turns())]
    events.append((9, functools.partial(back.start, True)))
    for chunk in range(CHUNKS):
        for stage in range(reduce.stages()):
            when = 1 + (chunk + 1) // 2 if stage == 0 else 4 + 3 * chunk + 2 * (stage - 1)
            events.append((when, functools.partial(reduce.event, stage, chunk)))
    run_schedule(head, last, [(0, begin)] + sorted(events, key=lambda event: event[0]))
    local_backward_core(
        nseg, first, mask_ref, q_ref, k_ref, v_ref, g_ref, lse_ref, slope_ref, dqr_ref, out_ref,
        qa, ga, ka, va, dk, dv,
    )

    @pl.when(head == last)
    def _():
        back.finish()
        reduce.finish()


def local_backward_scratch(nseg):
    length = nseg * SEG
    return [
        pltpu.VMEM((64, length), BF16),
        pltpu.VMEM((64, length), BF16),
        pltpu.VMEM((nseg, 64, length), BF16),
        pltpu.VMEM((64, length), BF16),
        pltpu.VMEM((HEAD_DIM, length), F32),
        pltpu.VMEM((HEAD_DIM, length), F32),
    ]


def local_backward_core(
    nseg, first, mask_ref, q_ref, k_ref, v_ref, g_ref, lse_ref, slope_ref, dqr_ref, out_ref,
    qa, ga, ka, va, dk, dv,
):
    head = pl.program_id(0)
    length = nseg * SEG
    keep = local_keep(mask_ref[0], length)
    qa[...] = join(q_ref[0], query_rows(head, length, neg_total(lse_ref[0], keep)))
    ga[...] = grad_rows(g_ref[...], slope_ref[0])
    va[...] = join(v_ref[0], value_rows(length))
    ka[0] = join(k_ref[0], key_rows(head, 0, 4, length, keep))
    if nseg == 2:
        ka[1] = join(k_ref[0], key_rows(head, 1, 4, length, keep))
    items, sides, written = [], [], set()
    for seg in range(nseg):
        lanes = slice(seg * SEG, (seg + 1) * SEG)
        tiles = [
            ((seg, i), slice(seg * SEG + BACK_KEYS * i, seg * SEG + BACK_KEYS * (i + 1)))
            for i in range(SEG // BACK_KEYS)
        ]
        sides.append(sides_of(qa[:, lanes], ga[:, lanes]))
        items += pairs(sides[-1], ka.at[0], va, tiles)
    attend_back(items, dk, dv, written)
    for seg in range(nseg):
        out_ref[0, :, seg * SEG : (seg + 1) * SEG] = joined(sides[seg]) * DQ_SCALE
    if nseg == 2:
        items, sides = [], []
        kept = [pl.ds(kept_start(head, 1, seg), SEG // 2) for seg in range(2)]
        for seg in range(2):
            base = kept_start(head, 1, 1 - seg)
            tile = min(BACK_KEYS, SEG // 2)
            tiles = [
                ((seg, i), pl.ds(pl.multiple_of(base + tile * i, tile), tile)) for i in range(SEG // 2 // tile)
            ]
            sides.append(sides_of(qa[:, kept[seg]], ga[:, kept[seg]]))
            items += pairs(sides[-1], ka.at[1], va, tiles)
        attend_back(items, dk, dv, set(item[4] for item in items))
        for seg in range(2):
            out_ref[0, :, kept[seg]] += joined(sides[seg]) * DQ_SCALE
    size = SEG >> first
    for seg in range(nseg):
        mine = pl.ds(kept_start(head, first, seg), size)
        out_ref[0, :, mine] += dqr_ref[:, seg * size : (seg + 1) * size]
    out_ref[1] = dk[...] * DK_SCALE
    out_ref[2] = dv[...]


def rows_of(total, at, count):
    return total[at : at + count].reshape(count * 16, 128)


def remote_backward(nseg, first, mask_ref, q_ref, g_ref, lse_ref, slope_ref, *refs):
    head = pl.program_id(0)
    levels = range(first, BRANCHES)
    n = len(levels)
    packs = {level: refs[3 * i : 3 * i + 3] for i, level in enumerate(levels)}
    dqr_ref = refs[3 * n]
    outs = {level: refs[3 * n + 1 + i] for i, level in enumerate(levels)}
    qa, ga, ka, va, dk, dv = refs[4 * n + 1 :]
    length = nseg * SEG
    qa[...] = join(q_ref[0], query_rows(head, length, neg_total(lse_ref[0], local_keep(mask_ref[0], length))))
    ga[...] = grad_rows(g_ref[...], slope_ref[0])
    full = SEG >> first
    for group in remote_plan(first):
        for i, level in enumerate(group):
            key, value = remote_keys(head, level, packs[level])
            ka[:, i * 512 : (i + 1) * 512] = key
            va[:, i * 512 : (i + 1) * 512] = value
        size = SEG >> group[0]
        mine = [pl.ds(kept_start(head, group[0], seg), size) for seg in range(nseg)]
        query = jnp.concatenate([qa[:, m] for m in mine], axis=1)
        grad = jnp.concatenate([ga[:, m] for m in mine], axis=1)
        tile = min(BACK_KEYS, 512)
        tiles = [(i, slice(tile * i, tile * (i + 1))) for i in range(512 // tile * len(group))]
        sides = sides_of(query, grad)
        attend_back(pairs(sides, ka, va, tiles), dk, dv, set())
        dq = joined(sides) * DQ_SCALE
        for seg in range(nseg):
            piece = dq[:, seg * size : (seg + 1) * size]
            if group[0] == first:
                dqr_ref[:, seg * full : (seg + 1) * full] = piece
            else:
                inner = (reversed_bits(head) >> (4 - group[0])) & ((1 << (group[0] - first)) - 1)
                lanes = pl.ds(pl.multiple_of(seg * full + inner * size, 128), size)
                dqr_ref[:, lanes] += piece
        for i, level in enumerate(group):
            pieces, _, _, size = outs[level].shape
            for piece in range(pieces):
                lanes = slice(i * 512 + piece * size, i * 512 + (piece + 1) * size)
                outs[level][piece, 0] = (dk[:, lanes] * DK_SCALE).astype(BF16)
                outs[level][piece, 1] = dv[:, lanes].astype(BF16)


def row_block(length):
    return pl.BlockSpec((1, 1, length), lambda h: (h, 0, 0))


def head_block(length):
    return pl.BlockSpec((HEAD_DIM, length), lambda h: (h, 0))


def part_block(part, length):
    return pl.BlockSpec((1, HEAD_DIM, length), lambda h: (part, h, 0))


MASK_BLOCK = pl.BlockSpec(memory_space=pltpu.SMEM)


def pack_args(keys, packs):
    args, specs = [], []
    for i, pack in enumerate(packs):
        group, _, length = pack.shape
        ahead = 0 if i == 0 else HEADS
        args += [keys if i == 0 else pack, pack, pack]
        specs += [
            pl.BlockSpec((group, HEAD_DIM, length), lambda h: (0, h, 0)),
            pl.BlockSpec((group, HEAD_DIM, length), lambda h, ahead=ahead: (0, ahead + h, 0)),
            pl.BlockSpec((group, 16, length), lambda h, ahead=ahead: (0, (ahead + HEADS) * 3, 0)),
        ]
    return args, specs


ANY_BLOCK = pl.BlockSpec(memory_space=pl.ANY)


def sems(count):
    return pltpu.SemaphoreType.DMA((count,))


def talking(collective_id, mebibytes=56):
    return pltpu.CompilerParams(
        vmem_limit_bytes=mebibytes * 1024 * 1024, collective_id=collective_id, has_side_effects=True
    )


PARAMS = pltpu.CompilerParams(vmem_limit_bytes=VMEM_LIMIT)


def shape(dims, dtype):
    return jax.ShapeDtypeStruct(dims, dtype)


def cost(seconds):
    return pl.CostEstimate(flops=int(seconds * 1.1e15), transcendentals=0, bytes_accessed=0)


def call_local_forward(nseg, first, qkv, mask, packs, shards):
    length = nseg * SEG
    n = len(packs)
    groups = [(SEG << (level - 1)) // length for level in range(first, BRANCHES)]
    hops = sum(group.bit_length() for group in groups)
    pieces = [shards[0].shape, shards[1].shape, (DOWN_FIRST, D)]
    o_part, l_part, m_part, *rest = pl.pallas_call(
        functools.partial(local_forward, nseg, first),
        grid=(HEADS,),
        in_specs=[MASK_BLOCK, part_block(0, length), part_block(1, length), part_block(2, length)]
        + [ANY_BLOCK] * (n + 3),
        out_specs=[head_block(length), row_block(length), row_block(length)] + [ANY_BLOCK] * (n + 3),
        out_shape=[shape((D, length), F32), shape((HEADS, 1, length), F32), shape((HEADS, 1, length), F32)]
        + [
            shape((group, D + 16 if i == 0 else pack.shape[0], pack.shape[1]), BF16)
            for i, (group, pack) in enumerate(zip(groups, packs))
        ]
        + [shape((4,) + piece, BF16) for piece in pieces],
        scratch_shapes=local_forward_scratch(nseg)
        + [
            sems(hops),
            sems(hops),
        ]
        + [pltpu.VMEM(piece, BF16) for piece in pieces]
        + [
            sems(9),
            sems(9),
            sems(3),
        ],
        compiler_params=talking(1),
        cost_estimate=cost(nseg * 37e-6),
        name="local_forward",
    )(mask, qkv, qkv, qkv, *packs, *shards)
    whole_out, whole_up, down_first = rest[n:]
    return (
        o_part, l_part, m_part, rest[:n], whole_out.reshape(D, D), whole_up.reshape(D, 4 * D), down_first
    )


def call_remote_forward(nseg, first, qkv, mask, o_part, l_part, m_part, keys, packs, shard):
    length = nseg * SEG
    args, specs = pack_args(keys, packs)
    return pl.pallas_call(
        functools.partial(remote_forward, nseg, first),
        grid=(HEADS,),
        in_specs=[MASK_BLOCK, part_block(0, length), head_block(length), row_block(length), row_block(length)]
        + specs
        + [ANY_BLOCK],
        out_specs=[head_block(length), row_block(length), ANY_BLOCK],
        out_shape=[
            shape((D, length), BF16),
            shape((HEADS, 1, length), F32),
            shape((4, D - DOWN_FIRST, D), BF16),
        ],
        scratch_shapes=[
            pltpu.VMEM((HEAD_DIM, length), F32),
            pltpu.VMEM((1, 1, length), F32),
            pltpu.VMEM((1, 1, length), F32),
            pltpu.VMEM((64, length), BF16),
            pltpu.VMEM((D - DOWN_FIRST, D), BF16),
            sems(3),
            sems(3),
            sems(1),
        ],
        compiler_params=talking(5),
        cost_estimate=cost(nseg * 24e-6),
        name="remote_forward",
    )(mask, qkv, o_part, l_part, m_part, *args, shard)


def call_remote_backward(nseg, first, qkv, grad, lse, slope, mask, keys, packs):
    length = nseg * SEG
    args, specs = pack_args(keys, packs)
    kept = nseg * (SEG >> first)
    return pl.pallas_call(
        functools.partial(remote_backward, nseg, first),
        grid=(HEADS,),
        in_specs=[MASK_BLOCK, part_block(0, length), head_block(length), row_block(length), row_block(length)]
        + specs,
        out_specs=[head_block(kept)]
        + [
            pl.BlockSpec((pack.shape[0], 2, HEAD_DIM, pack.shape[2]), lambda h: (0, 0, h, 0))
            for pack in packs
        ],
        out_shape=[shape((D, kept), F32)]
        + [shape((pack.shape[0], 2, D, pack.shape[2]), BF16) for pack in packs],
        scratch_shapes=[
            pltpu.VMEM((64, length), BF16),
            pltpu.VMEM((64, length), BF16),
            pltpu.VMEM((64, 1024), BF16),
            pltpu.VMEM((64, 1024), BF16),
            pltpu.VMEM((HEAD_DIM, 1024), F32),
            pltpu.VMEM((HEAD_DIM, 1024), F32),
        ],
        compiler_params=PARAMS,
        cost_estimate=cost(nseg * 20e-6),
        name="remote_backward",
    )(mask, qkv, grad, lse, slope, *args)


CHUNKS = 3
FEED_BLOCKS = (4 * D + D + 4 * D) * D // (4 * 16 * 128)
IN_BLOCKS = 3 * D * D // (4 * 16 * 128)


def padded(blocks):
    unit = CHUNKS * lax.axis_size("seq")
    return (blocks + unit - 1) // unit * unit


def reduce_copies():
    return CHUNKS * (3 + seq_bits())


def call_local_backward(nseg, first, qkv, grad, lse, slope, mask, dq_remote, sent, feed_grads):
    length = nseg * SEG
    n = len(sent)
    groups = [part.shape[0] for part in sent]
    hops = sum(group.bit_length() for group in groups)
    blocks = feed_grads.shape[1]
    piece = (CHUNKS, blocks // CHUNKS >> seq_bits(), 16, 128)
    bufs = [pltpu.VMEM((g // 2,) + part.shape[1:], BF16) for g, part in zip(groups, sent) if g > 1]
    recvs = [pltpu.VMEM((g - 1,) + part.shape[1:], BF16) for g, part in zip(groups, sent) if g > 1]
    local, *rest = pl.pallas_call(
        functools.partial(local_backward, nseg, first),
        grid=(HEADS,),
        in_specs=[MASK_BLOCK, part_block(0, length), part_block(1, length), part_block(2, length), head_block(length),
                  row_block(length), row_block(length), head_block(dq_remote.shape[1])]
        + [ANY_BLOCK] * (n + 1),
        out_specs=[pl.BlockSpec((3, HEAD_DIM, length), lambda h: (0, h, 0))]
        + [ANY_BLOCK] * n
        + [const_block(piece)],
        out_shape=[shape((3, D, length), F32)]
        + [shape(part.shape[1:], BF16) for part in sent]
        + [shape(piece, BF16)],
        scratch_shapes=local_backward_scratch(nseg)
        + bufs
        + recvs
        + [
            pltpu.VMEM((2, blocks, 16, 128), BF16),
            pltpu.VMEM((2, blocks, 16, 128), BF16),
            pltpu.VMEM((blocks, 16, 128), BF16),
            pltpu.VMEM((blocks, 16, 128), BF16),
            sems(hops),
            sems(hops),
            sems(n),
            sems(reduce_copies()),
            sems(reduce_copies()),
            sems(2 * CHUNKS),
        ],
        compiler_params=talking(2),
        cost_estimate=cost(nseg * 72e-6),
        name="local_backward",
    )(mask, qkv, qkv, qkv, grad, lse, slope, dq_remote, *sent, feed_grads)
    return local, rest[:n], rest[n]


HALF = D // 2


def const_block(dims):
    return pl.BlockSpec(dims, lambda i: (0,) * len(dims), pipeline_mode=pl.Buffered(1))


def rev4(value):
    return int(reversed_bits(value))


TILES = D // 128


def put_rows(tiled, start, array):
    for tile in range(TILES):
        tiled[tile, start : start + array.shape[0], :] = array[:, tile * 128 : (tile + 1) * 128]


def get_rows(tiled, start, size):
    return jnp.concatenate([tiled[tile, start : start + size, :] for tile in range(TILES)], axis=1)


def get_residue(tiled, start):
    return jnp.concatenate(
        [tiled[tile, pl.ds(start, RUN, stride=RES), :] for tile in range(TILES)], axis=1
    )


def put_residue(tiled, start, array):
    for tile in range(TILES):
        tiled[tile, pl.ds(start, RUN, stride=RES), :] = array[:, tile * 128 : (tile + 1) * 128]


COLUMN_CHUNKS = 3


def project_kernel(nseg, first, mask_ref, tok_ref, *refs):
    n = BRANCHES - first
    vectors, w_ref = refs[:4], refs[4]
    qkv_ref, xp_ref, inner_ref, weight_ref, gains_ref, keys_ref = refs[5:11]
    packs = refs[11 : 11 + n]
    xs, weight, gains, key_pack, vec_send, vec_recv, w_send, w_recv, w_load, w_store = refs[11 + n : 21 + n]
    key_send, key_recv = refs[21 + n :]
    step = pl.program_id(0)
    last = pl.num_programs(0) - 1
    me = lax.axis_index("fsdp")
    sibling = me + 1 - 2 * lax.rem(me, 2)
    across = lax.rem(me + 2, 4)
    sends = Sends(w_send, w_recv)

    def send(source, target, key, other):
        index = sends.made.setdefault(key, len(sends.made))
        return pltpu.make_async_remote_copy(
            src_ref=source, dst_ref=target, send_sem=w_send.at[index], recv_sem=w_recv.at[index],
            device_id={"fsdp": other}, device_id_type=pl.DeviceIdType.MESH,
        )

    def chunk_copies(chunk):
        cols = pl.ds(chunk * D, D)
        mine = w_ref.at[:, cols]
        load = pltpu.make_async_copy(mine, weight.at[me, :, cols], w_load.at[chunk])
        core = send(mine, weight.at[me, :, cols], ("core", chunk), sibling)
        x = send(mine, weight.at[me, :, cols], ("x", chunk), across)
        handed = weight.at[across, :, cols]
        return load, core, x, send(handed, handed, ("hand", chunk), sibling)

    def vec_copies():
        return [
            pltpu.make_async_remote_copy(
                src_ref=gains.at[me], dst_ref=gains.at[me], send_sem=vec_send.at[i], recv_sem=vec_recv.at[i],
                device_id={"fsdp": other}, device_id_type=pl.DeviceIdType.MESH,
            )
            for i, other in enumerate((sibling, across, 3 - me))
        ]

    store = pltpu.make_async_copy(weight, weight_ref, w_store.at[0])
    key_sends = Sends(key_send, key_recv)

    def ahead(half):
        rows = pl.ds(half * HALF, HALF)
        return key_sends.copy(half, key_pack.at[rows], keys_ref.at[rows], "seq", 1)


    @pl.when(step == 0)
    def _():
        barrier = pltpu.get_barrier_semaphore()
        for other in (sibling, across, 3 - me):
            pl.semaphore_signal(
                barrier, inc=1, device_id={"fsdp": other}, device_id_type=pl.DeviceIdType.MESH
            )
        pl.semaphore_signal(
            barrier, inc=1, device_id=partner("seq", 1), device_id_type=pl.DeviceIdType.MESH
        )
        for i, vector in enumerate(vectors):
            gains[me, i : i + 1, :192] = vector[...].astype(F32).reshape(1, 192)
        pl.semaphore_wait(barrier, 4)
        for copy in vec_copies():
            copy.start()
        for turn in range(COLUMN_CHUNKS):
            for copy in chunk_copies((turn + 1) % COLUMN_CHUNKS)[: 3 if turn == 0 else 2]:
                copy.start()
        for copy in vec_copies():
            copy.wait_recv()
        full = [
            jnp.concatenate([gains[owner, i : i + 1, :192] for owner in range(4)], axis=1) for i in range(4)
        ]
        gains_ref[...] = jnp.concatenate(full + [jnp.zeros((4, D), F32)], axis=0)
        for seg in range(nseg):
            put_rows(xs, 0, tok_ref[seg * SEG : (seg + 1) * SEG, :].astype(F32))
            for pair in range(RES // 2):
                rows = jnp.concatenate([get_residue(xs, rev4(2 * pair + i)) for i in range(2)], axis=0)
                normed = normalize(rows, full[0], full[1])[0].astype(BF16)
                at = slice(seg * SEG + pair * 2 * RUN, seg * SEG + (pair + 1) * 2 * RUN)
                xp_ref[at, :] = rows.astype(BF16)
                inner_ref[:, at] = normed.T
        for pack, level in zip(packs, range(first, BRANCHES)):
            pack[2 * D :, :] = packed_keep(mask_ref[0], level, nseg)

    for turn in range(COLUMN_CHUNKS):

        @pl.when(step == 2 * turn)
        def _():
            load, core, x, hand = chunk_copies((turn + 1) % COLUMN_CHUNKS)
            x.wait_recv()
            hand.start()
            if turn + 1 < COLUMN_CHUNKS:
                chunk_copies((turn + 2) % COLUMN_CHUNKS)[2].start()
            load.wait()
            core.wait_recv()
            hand.wait_recv()

    @pl.when(step == 4)
    def _():
        store.start()

    where = lax.rem(step + 2, 6)
    cols = pl.ds(pl.multiple_of(where * HALF, HALF), HALF)
    block = jnp.concatenate([weight[owner, :, cols] for owner in range(4)], axis=0)
    scale = jnp.where(step >= 4, QUERY_SCALE, 1.0)
    for start in range(0, nseg * SEG, 512):
        lanes = slice(start, start + 512)
        qkv_ref[0, :, lanes] = (dotg(block, inner_ref[:, lanes], 0, 0) * scale).astype(BF16)

    @pl.when(step < 4)
    def _():
        upper = lax.rem(step, 2) == 1
        for pack, level in zip(packs, range(first, BRANCHES)):
            size = SEG >> level
            for head in range(HEADS // 2):
                rows = slice(head * HEAD_DIM, (head + 1) * HEAD_DIM)
                pieces = []
                for seg in range(nseg):
                    start = seg * SEG + (rev4(head) >> (4 - level)) * size
                    if level < 4:
                        pieces.append(qkv_ref[0, rows, start : start + size])
                    else:
                        both = qkv_ref[0, rows, start : start + 2 * size]
                        pieces.append(jnp.where(upper, both[:, size:], both[:, :size]))
                into = pl.ds(pl.multiple_of(step * HALF + head * HEAD_DIM, 16), HEAD_DIM)
                pack[into, :] = jnp.concatenate(pieces, axis=1) if nseg > 1 else pieces[0]

    for half in range(2):

        @pl.when(step == half)
        def _():
            rows = slice(half * HALF, (half + 1) * HALF)
            key_pack[rows, :] = packs[0][rows, :]
            ahead(half).start()

    @pl.when(step == last)
    def _():
        for copy in vec_copies():
            copy.wait_send()
        for chunk in range(COLUMN_CHUNKS):
            for copy in chunk_copies(chunk)[1:]:
                copy.wait_send()
        store.wait()
        for half in range(2):
            ahead(half).wait()


def call_project(nseg, first, mask, tokens, vectors, weight):
    length = nseg * SEG
    kept = [nseg * (SEG >> level) for level in range(first, BRANCHES)]
    return pl.pallas_call(
        functools.partial(project_kernel, nseg, first),
        grid=(6,),
        in_specs=[MASK_BLOCK, const_block((length, D))] + [const_block((192,))] * 4 + [ANY_BLOCK],
        out_specs=[
            pl.BlockSpec((1, HALF, length), lambda i: ((i + 2) % 6 // 2, i % 2, 0)),
            const_block((length, D)),
            const_block((D, length)),
            ANY_BLOCK,
            const_block((8, D)),
            ANY_BLOCK,
        ]
        + [const_block((2 * D + 16, size)) for size in kept],
        out_shape=[
            shape((3, D, length), BF16),
            shape((length, D), BF16),
            shape((D, length), BF16),
            shape((4, 192, 3 * D), BF16),
            shape((8, D), F32),
            shape((D, kept[0]), BF16),
        ]
        + [shape((2 * D + 16, size), BF16) for size in kept],
        scratch_shapes=[
            pltpu.VMEM((TILES, SEG, 128), F32),
            pltpu.VMEM((4, 192, 3 * D), BF16),
            pltpu.VMEM((4, 8, 256), F32),
            pltpu.VMEM((D, kept[0]), BF16),
            sems(3),
            sems(3),
            sems(3 * COLUMN_CHUNKS),
            sems(3 * COLUMN_CHUNKS),
            sems(COLUMN_CHUNKS),
            sems(1),
            sems(2),
            sems(2),
        ],
        compiler_params=talking(4),
        cost_estimate=cost(nseg * 10e-6),
        name="project",
    )(mask, tokens, *vectors, weight)


ROWS = 256


def blocks_of(ref, rows, col):
    part = ref[rows, col * 128 : (col + 1) * 128].astype(BF16)
    return part.reshape(part.shape[0] // 16, 16, 128)


def feed_kernel(
    nseg, mask_ref, att_ref, x_ref, cot_ref, wout_ref, up_ref, down_a, down_b, gains_ref,
    mixed_ref, gmid_ref, gm_ref, along_ref, vec_ref, grads_ref,
    cs, out_acc, up_acc, down_acc, stage, sems,
):
    step = pl.program_id(0)
    quarter = lax.rem(step, 4)
    low = (quarter >> 1) | ((quarter & 1) << 1)

    @pl.when(step == 0)
    def _():
        out_acc[...] = jnp.zeros_like(out_acc)
        up_acc[...] = jnp.zeros_like(up_acc)
        down_acc[...] = jnp.zeros_like(down_acc)
        vec_ref[...] = jnp.zeros_like(vec_ref)

    @pl.when(quarter == 0)
    def _():
        put_rows(cs, 0, cot_ref[...].astype(F32))

    grad = jnp.concatenate([get_residue(cs, rev4(i) + low) for i in range(4)], axis=0)
    grad_b = grad.astype(BF16)
    att = att_ref[...]
    middle = x_ref[...].astype(F32) + dotg(att, wout_ref[...], 0, 0)
    gain = gains_ref[2:3, :]
    normed, unit, inverse = normalize(middle, gain, gains_ref[3:4, :])
    hidden = normed.astype(BF16)
    hidden_t = hidden.T
    final = middle
    grad_hidden = jnp.zeros((ROWS, D), F32)
    for start in range(0, 4 * D, D):
        cols = slice(start, start + D)
        upper = dotg(hidden, up_ref[:, cols], 1, 0)
        down = jnp.concatenate([down_a[start // D], down_b[start // D]], axis=0)
        grad_active = dotg(grad_b, down, 1, 1)
        half = 0.5 * (1.0 + lax.erf(upper * ROOT_HALF))
        slope = half + upper * jnp.exp(-0.5 * upper * upper) * INV_ROOT_TWO_PI
        active = (upper * half).astype(BF16)
        grad_upper = (grad_active * slope).astype(BF16)
        final = final + dotg(active, down, 1, 0)
        grad_hidden = grad_hidden + dotg(grad_upper, up_ref[:, cols], 1, 1)
        up_acc[:, cols] += dotg(hidden_t, grad_upper, 1, 0)
        down_acc[cols, :] += dotg(active, grad_b, 0, 0)
    for i in range(4):
        put_residue(cs, rev4(i) + low, final[i * RUN : (i + 1) * RUN])

    @pl.when(quarter == 3)
    def _():
        mixed_ref[...] = get_rows(cs, 0, SEG).astype(BF16)

    back, gain_back, shift_back = normalize_back(grad_hidden, unit, inverse, gain)
    vec_ref[0:1, :] += gain_back[None, :]
    vec_ref[1:2, :] += shift_back[None, :]
    grad_middle = grad + back
    gmid_ref[...] = grad_middle
    branch = grad_middle.astype(BF16)
    out_acc[...] += dotg(att, branch, 1, 0)
    lane = lax.broadcasted_iota(jnp.int32, (1, ROWS), 1)
    position = step // 4 * SEG + lax.rem(lane, RUN) * RES + residue_of(lane // RUN) + low
    keep = position < mask_ref[0]
    merged = jnp.where(keep, dotg(wout_ref[...], branch, 1, 1), 0.0).astype(BF16)
    gm_ref[...] = merged
    product = merged.astype(F32) * att.astype(F32)
    for head in range(HEADS):
        rows = slice(head * HEAD_DIM, (head + 1) * HEAD_DIM)
        along_ref[head] = jnp.sum(product[rows], axis=0, keepdims=True)

    @pl.when(step == pl.num_programs(0) - 1)
    def _():
        copies = []
        for owner in range(4):
            for piece in range(3):
                count = owner * 3 + piece
                slot = count % 2
                if count >= 2:
                    copies[count - 2].wait()
                if piece == 0:
                    rows, offset, size = slice(owner * 192, (owner + 1) * 192), 0, 288
                    for col in range(4 * TILES):
                        stage[slot, col * 12 : (col + 1) * 12] = blocks_of(up_acc, rows, col)
                elif piece == 1:
                    rows, offset, size = slice(owner * 192, (owner + 1) * 192), 288, 72
                    for col in range(TILES):
                        stage[slot, col * 12 : (col + 1) * 12] = blocks_of(out_acc, rows, col)
                else:
                    rows, offset, size = slice(owner * D, (owner + 1) * D), 360, 288
                    for col in range(TILES):
                        stage[slot, col * 48 : (col + 1) * 48] = blocks_of(down_acc, rows, col)
                copy = pltpu.make_async_copy(
                    stage.at[slot, pl.ds(0, size)],
                    grads_ref.at[owner, pl.ds(offset, size)],
                    sems.at[slot],
                )
                copy.start()
                copies.append(copy)
        copies[-2].wait()
        copies[-1].wait()


def call_feed(nseg, mask, att, x, cot, wout, up, down_a, down_b, gains):
    length = nseg * SEG
    return pl.pallas_call(
        functools.partial(feed_kernel, nseg),
        grid=(length // ROWS,),
        in_specs=[
            MASK_BLOCK,
            pl.BlockSpec((D, ROWS), lambda i: (0, i)),
            pl.BlockSpec((ROWS, D), lambda i: (i, 0)),
            pl.BlockSpec((SEG, D), lambda i: (i // 4, 0)),
            const_block((D, D)),
            const_block((D, 4 * D)),
            const_block((4, DOWN_FIRST, D)),
            const_block((4, D - DOWN_FIRST, D)),
            const_block((8, D)),
        ],
        out_specs=[
            pl.BlockSpec((SEG, D), lambda i: (i // 4, 0)),
            pl.BlockSpec((ROWS, D), lambda i: (i, 0)),
            pl.BlockSpec((D, ROWS), lambda i: (0, i)),
            pl.BlockSpec((HEADS, 1, ROWS), lambda i: (0, 0, i)),
            pl.BlockSpec((2, D), lambda i: (0, 0)),
            pl.BlockSpec(memory_space=pl.ANY),
        ],
        out_shape=[
            shape((length, D), BF16),
            shape((length, D), F32),
            shape((D, length), BF16),
            shape((HEADS, 1, length), F32),
            shape((2, D), F32),
            shape((4, padded(FEED_BLOCKS), 16, 128), BF16),
        ],
        scratch_shapes=[
            pltpu.VMEM((TILES, SEG, 128), F32),
            pltpu.VMEM((D, D), F32),
            pltpu.VMEM((D, 4 * D), F32),
            pltpu.VMEM((4 * D, D), F32),
            pltpu.VMEM((2, 288, 16, 128), BF16),
            pltpu.SemaphoreType.DMA((2,)),
        ],
        compiler_params=pltpu.CompilerParams(vmem_limit_bytes=62 * 1024 * 1024),
        cost_estimate=cost(nseg * 45e-6),
        name="feed",
    )(mask, att, x, cot, wout, up, down_a, down_b, gains)


STEPS = 6
INNER_TABLE = (
    (1, "start", 0, 0),
    (1, "feed", 2, 0),
    (1, "feed", 1, 0),
    (2, "feed", 0, 0),
    (2, "reduce", 0, 0),
    (3, "start", 1, 0),
    (4, "reduce", 1, 0),
    (5, "reduce", 0, 1),
    (5, "start", 2, 0),
    (6, "feed", 2, 1),
    (6, "feed", 1, 1),
    (6, "feed", 0, 1),
    (6, "reduce", 2, 0),
    (8, "reduce", 1, 1),
    (9, "reduce", 0, 2),
    (11, "feed", 2, 2),
    (11, "feed", 1, 2),
    (12, "reduce", 0, 3),
    (13, "vec_start", 0, 0),
    (13, "reduce", 2, 1),
    (14, "feed", 0, 2),
    (14, "reduce", 0, 4),
    (14, "vec", 0, 0),
    (14, "reduce", 1, 2),
    (14, "vec", 0, 1),
    (14, "reduce", 2, 2),
    (14, "vec", 0, 2),
    (14, "spread", 0, 0),
    (14, "reduce", 1, 3),
    (14, "vec", 0, 3),
    (14, "reduce", 2, 3),
    (14, "spread", 0, 1),
    (14, "reduce", 1, 4),
    (14, "vec", 0, 4),
    (14, "reduce", 2, 4),
    (14, "spread", 0, 2),
    (14, "spread", 1, 0),
    (14, "spread", 2, 0),
    (14, "spread", 1, 1),
    (14, "spread", 2, 1),
    (14, "spread", 1, 2),
    (14, "spread", 2, 2),
)


def inner_back_kernel(
    nseg, first, local_ref, inner_ref, w_ref, x_ref, gmid_ref, gain_ref, feed_vec_ref, piece_ref, *refs
):
    n = BRANCHES - first
    packs, (weight_ref, back_ref, vec_ref, up_ref, proj_ref, down_ref) = refs[:n], refs[n : n + 6]
    acc, mixed, order, terms, recv_core, recv_x, recv_seq, total, feed_total, vecs, vec_recv = refs[n + 6 : n + 17]
    red_send, red_recv, in_send, in_recv, feed_send, feed_recv, vec_send, vec_recv_sems = refs[n + 17 :]
    step = pl.program_id(0)
    last = pl.num_programs(0) - 1
    length = nseg * SEG
    turns = length // ROWS
    end = STEPS + turns
    blocks = terms.shape[1] // CHUNKS
    core = lax.rem(lax.axis_index("fsdp"), 2)
    spread = Spread(inner_orders(), blocks, total, Sends(in_send, in_recv))
    reduce = Reduce(
        inner_orders(), blocks, terms, terms, lambda xo: 2 * xo + core, recv_core, recv_x, recv_seq, Sends(red_send, red_recv),
        spread.begin,
    )
    feed_spread = Spread(feed_orders(), feed_total.shape[0] // CHUNKS, feed_total, Sends(feed_send, feed_recv))
    vec_sends = Sends(vec_send, vec_recv_sems)
    peers = all_peers()

    def vec_copy(i):
        return vec_sends.copy(i, vecs.at[i], vec_recv.at[i], *peers[i])

    def vec_event(i):
        vec_copy(i).wait_recv()
        vecs[i + 1] = vecs[i] + vec_recv[i]
        if i + 1 < len(peers):
            vec_copy(i + 1).start()

    def vec_start():
        vec_copy(0).start()

    @pl.when(step == 0)
    def _():
        meet(peers)
        vecs[0] = jnp.concatenate([jnp.zeros((2, D), F32), feed_vec_ref[...], jnp.zeros((4, D), F32)], axis=0)
        for chunk in reversed(range(CHUNKS)):
            feed_spread.begin(chunk, piece_ref.at[chunk], 0)

    @pl.when((step >= 2) & (step < STEPS))
    def _():
        upper = lax.rem(step, 2) == 1
        for pack, level in zip(packs, range(first, BRANCHES)):
            size = SEG >> level
            for head in range(HEADS // 2):
                rows = slice(head * HEAD_DIM, (head + 1) * HEAD_DIM)
                for seg in range(nseg):
                    start = seg * SEG + (rev4(head) >> (4 - level)) * size
                    piece = pack[0, rows, seg * size : (seg + 1) * size].astype(F32)
                    if level == 4:
                        zero = jnp.zeros_like(piece)
                        piece = jnp.concatenate(
                            [jnp.where(upper, zero, piece), jnp.where(upper, piece, zero)], axis=1
                        )
                    local_ref[0, rows, start : start + piece.shape[1]] += piece

    @pl.when(step < STEPS)
    def _():
        block = local_ref[0].astype(BF16)
        mixed[pl.ds(pl.multiple_of(step * HALF, HALF), HALF), :] = block
        base = lax.div(step, 2) * blocks + lax.rem(step, 2) * 36
        grad_in = dotg(block, inner_ref[...], 1, 1).T.astype(BF16)
        for col in range(3):
            part = grad_in[:, col * 128 : (col + 1) * 128].reshape(4, 12, 16, 128)
            for owner in range(4):
                terms[owner, pl.ds(base + col * 12, 12)] = part[owner]

    def inner_grad(turn):
        lanes = pl.ds(pl.multiple_of(turn * ROWS, ROWS), ROWS)
        acc[lax.rem(turn, 2)] = dotg(w_ref[...], mixed[:, lanes], 1, 0)

    @pl.when(step == STEPS - 1)
    def _():
        inner_grad(step - (STEPS - 1))

    @pl.when((step >= STEPS) & (step < end))
    def _():
        turn = step - STEPS
        inner_grad(lax.rem(turn + 1, turns))
        quarter = lax.rem(turn, 4)
        low = (quarter >> 1) | ((quarter & 1) << 1)
        gain = gain_ref[0:1, :]
        grad = acc[lax.rem(turn, 2)].T
        _, unit, inverse = normalize(x_ref[...].astype(F32), gain, gain)
        back, gain_part, shift_part = normalize_back(grad, unit, inverse, gain)
        vecs[0, 0:1, :] += gain_part[None, :]
        vecs[0, 1:2, :] += shift_part[None, :]
        total_back = gmid_ref[...] + back
        for i in range(4):
            put_residue(order, rev4(i) + low, total_back[i * RUN : (i + 1) * RUN])

        @pl.when(quarter == 3)
        def _():
            back_ref[...] = get_rows(order, 0, SEG)

    calls = {
        "start": lambda chunk, stage: reduce.begin(chunk),
        "reduce": lambda chunk, stage: reduce.event(stage, chunk),
        "spread": lambda chunk, stage: spread.event(stage, chunk),
        "feed": lambda chunk, stage: feed_spread.event(stage, chunk),
        "vec_start": lambda chunk, stage: vec_start(),
        "vec": lambda chunk, stage: vec_event(stage),
    }
    if seq_bits() == 3 and turns == 8:
        table = INNER_TABLE
    else:
        table = []
        for chunk in range(CHUNKS):
            begin = 2 * chunk + 1
            late = begin + 2 * reduce.stages() + 3 * chunk
            table += [(1 + 2 * stage, "feed", chunk, stage) for stage in range(feed_spread.stages())]
            table += [(begin, "start", chunk, 0), (begin + 1, "reduce", chunk, 0)]
            table += [
                (begin + 1 + 3 * chunk + 2 * stage, "reduce", chunk, stage)
                for stage in range(1, reduce.stages())
            ]
            table += [(late + 2 * stage, "spread", chunk, stage) for stage in range(spread.stages())]
        table += [(end - 1, "vec_start", 0, 0)]
        table += [(end + stage, "vec", 0, stage) for stage in range(len(peers))]
        table.sort(key=lambda event: event[0])
    events = [(when, functools.partial(calls[name], chunk, stage)) for when, name, chunk, stage in table]
    run_schedule(step, last, events)

    @pl.when(step == last)
    def _():
        for tile in range(TILES):
            cols = slice(tile * 128, (tile + 1) * 128)
            for col in range(4):
                at = col * 72 + tile * 12
                up_ref[:, col * D + tile * 128 : col * D + (tile + 1) * 128] = rows_of(feed_total, at, 12)
            proj_ref[:, cols] = rows_of(feed_total, 288 + tile * 12, 12)
            down_ref[:, cols] = rows_of(feed_total, 360 + tile * 48, 48)

    @pl.when(step == last)
    def _():
        reduce.finish()
        spread.finish()
        feed_spread.finish()
        for i in range(len(peers)):
            vec_copy(i).wait_send()
        vec_ref[...] = vecs[len(peers)]
        for part in range(STEPS):
            for col in range(3):
                at = part // 2 * blocks + part % 2 * 36 + col * 12
                weight_ref[:, part * HALF + col * 128 : part * HALF + (col + 1) * 128] = rows_of(total, at, 12)


def call_inner_back(nseg, first, local, inner, weight, x, gmid, gain, feed_vec, pieces, packs):
    length = nseg * SEG
    turns = length // ROWS
    blocks = padded(IN_BLOCKS)
    if blocks // CHUNKS < 72:
        raise ValueError("blocks")
    bits = seq_bits()
    peers = 2 + bits
    feed_blocks = CHUNKS * (pieces.shape[1] << bits)

    def at(i):
        return jnp.minimum(i, STEPS - 1)

    def turn(i):
        return jnp.clip(i - STEPS, 0, turns - 1)

    return pl.pallas_call(
        functools.partial(inner_back_kernel, nseg, first),
        grid=(STEPS + turns + 1,),
        in_specs=[
            pl.BlockSpec((1, HALF, length), lambda i: (at(i) // 2, at(i) % 2, 0)),
            const_block((D, length)),
            const_block((D, 3 * D)),
            pl.BlockSpec((ROWS, D), lambda i: (turn(i), 0)),
            pl.BlockSpec((ROWS, D), lambda i: (turn(i), 0)),
            const_block((8, D)),
            const_block((2, D)),
            const_block(pieces.shape),
        ]
        + [
            pl.BlockSpec((1, HALF, pack.shape[2]), lambda i: (jnp.maximum(at(i) // 2 - 1, 0), at(i) % 2, 0))
            for pack in packs
        ],
        out_specs=[
            const_block((192, 3 * D)),
            pl.BlockSpec((SEG, D), lambda i: (turn(i) // 4, 0)),
            const_block((8, D)),
            const_block((192, 4 * D)),
            const_block((192, D)),
            const_block((D, D)),
        ],
        out_shape=[
            shape((192, 3 * D), BF16),
            shape((length, D), F32),
            shape((8, D), F32),
            shape((192, 4 * D), BF16),
            shape((192, D), BF16),
            shape((D, D), BF16),
        ],
        scratch_shapes=[
            pltpu.VMEM((2, D, ROWS), F32),
            pltpu.VMEM((3 * D, length), BF16),
            pltpu.VMEM((TILES, SEG, 128), F32),
            pltpu.VMEM((4, blocks, 16, 128), BF16),
            pltpu.VMEM((2, blocks, 16, 128), BF16),
            pltpu.VMEM((blocks, 16, 128), BF16),
            pltpu.VMEM((blocks, 16, 128), BF16),
            pltpu.VMEM((blocks, 16, 128), BF16),
            pltpu.VMEM((feed_blocks, 16, 128), BF16),
            pltpu.VMEM((peers + 1, 8, D), F32),
            pltpu.VMEM((peers, 8, D), F32),
            sems(reduce_copies()),
            sems(reduce_copies()),
            sems(CHUNKS * bits),
            sems(CHUNKS * bits),
            sems(CHUNKS * bits),
            sems(CHUNKS * bits),
            sems(peers),
            sems(peers),
        ],
        compiler_params=talking(3, 60),
        cost_estimate=cost(nseg * 15e-6),
        name="inner_back",
    )(local, inner, weight, x, gmid, gain, feed_vec, pieces, *packs)


def per_device(
    tokens,
    first_gain,
    first_shift,
    project_in,
    project_out,
    second_gain,
    second_shift,
    up_weight,
    down_weight,
    valid_mask,
    cotangent,
):
    length = tokens.shape[1]
    nseg = length // SEG
    first = nseg.bit_length()

    mask = jnp.sum(valid_mask[0])[None]

    vectors = [first_gain, first_shift, second_gain, second_shift]
    qkv, x, inner, weight_in, gains, keys, *packs = call_project(
        nseg, first, mask, tokens[0], vectors, project_in
    )
    keys = keys[None]
    weight_in = weight_in.reshape(D, 3 * D)
    o_part, l_part, m_part, gathered, weight_out, weight_up, down_first = call_local_forward(
        nseg, first, qkv, mask, packs, (project_out, up_weight, down_weight)
    )
    attended, lse, down_second = call_remote_forward(
        nseg, first, qkv, mask, o_part, l_part, m_part, keys, gathered, down_weight
    )

    mixed, grad_middle, grad_merged, along, feed_vec, feed_grads = call_feed(
        nseg, mask, attended, x, cotangent[0], weight_out, weight_up, down_first, down_second, gains
    )

    dq_remote, *sent = call_remote_backward(nseg, first, qkv, grad_merged, lse, along, mask, keys, gathered)
    local, returned, pieces = call_local_backward(
        nseg, first, qkv, grad_merged, lse, along, mask, dq_remote, sent, feed_grads
    )
    grad_in, tokens_back, vectors, grad_up, grad_out, grad_down = call_inner_back(
        nseg, first, local, inner, weight_in, x, grad_middle, gains, feed_vec, pieces, returned
    )
    quarter = D // lax.axis_size("fsdp")
    vectors = lax.dynamic_slice_in_dim(vectors, lax.axis_index("fsdp") * quarter, quarter, 1)
    return (
        mixed[None],
        tokens_back[None],
        vectors[0],
        vectors[1],
        grad_in.astype(F32),
        grad_out.astype(F32),
        vectors[2],
        vectors[3],
        grad_up.astype(F32),
        grad_down.astype(F32),
    )


def solution(mesh):
    in_specs = (
        P("fsdp", "seq", None),
        P("fsdp"),
        P("fsdp"),
        P("fsdp", None),
        P("fsdp", None),
        P("fsdp"),
        P("fsdp"),
        P("fsdp", None),
        P("fsdp", None),
        P("fsdp", "seq"),
        P("fsdp", "seq", None),
    )
    out_specs = (
        P("fsdp", "seq", None),
        P("fsdp", "seq", None),
        P("fsdp"),
        P("fsdp"),
        P("fsdp", None),
        P("fsdp", None),
        P("fsdp"),
        P("fsdp"),
        P("fsdp", None),
        P("fsdp", None),
    )
    return jax.shard_map(
        per_device, mesh=mesh, in_specs=in_specs, out_specs=out_specs, check_vma=False
    )
```
